32 devices in a mesh: seq: 8 (over z, y), head: 4 (over x, core).
Axes of the slice: x: 2, y: 2, z: 4, core: 2. Of those that a mesh axis runs over, the one named last changes fastest.
Arguments:
- tokens: bfloat16 [3072, 2048], P('seq'), may hold values from -6 to 6
- cotangent: bfloat16 [3072, 2048], P('seq'), may hold values from -6 to 6
- attn_width: int32 [3072], P('seq'), may hold values from 1 to 4
- ffn_width: int32 [3072], P('seq'), may hold values from 1 to 4
- seq_lengths: int32 [4], replicated, may hold values from 1 to 2304, 3072 in all
- tile_order: int32 [4, 96], P('head'), may hold values from 0 to 95, as said below
- master: float32 [4, 96, 256, 512], P('head', 'seq')
- first_moment: float32 [4, 96, 256, 512], P('head', 'seq')
- second_moment: float32 [4, 96, 256, 512], P('head', 'seq')
- left_basis: float32 [4, 96, 256, 256], P('head', 'seq'), may hold values from -1 to 1
- right_basis: float32 [4, 96, 512, 512], P('head', 'seq'), may hold values from -1 to 1
- small_master: float32 [24576], P('seq')
- small_first: float32 [24576], P('seq')
- small_second: float32 [24576], P('seq')
Outputs:
- output: bfloat16 [3072, 2048], P('seq')
- input_grad: float32 [3072, 2048], P('seq')
- new_first: float32 [4, 96, 256, 512], P('head', 'seq')
- new_second: float32 [4, 96, 256, 512], P('head', 'seq')
- new_master: float32 [4, 96, 256, 512], P('head', 'seq')
- new_weights: bfloat16 [4, 96, 256, 512], P('head', 'seq')
- small_first_new: float32 [24576], P('seq')
- small_second_new: float32 [24576], P('seq')
- small_master_new: float32 [24576], P('seq')
The draws below stay inside these ranges and needn't reach their ends.
Inputs may be any that keep to these rules, and one draw needn't show every extreme that they name: Each row of tile_order is a permutation of 0 to 95.
All inputs are finite; a program needn't handle non-finite values.
Results may differ from the reference program's by a relative error of at most 0.019.
Values may be sent and summed in bfloat16 or wider, within the bound.
No kernel may reach another device: no remote copies, remote signals or barrier semaphores. Data moves between devices by JAX's collectives and lax.ppermute only.
A program may use at most 320 MiB of HBM per device.

```python
import math
import jax
import jax.numpy as jnp
import numpy as np
from jax import lax

D = 2048
HEADS = 16
HD = 128
FF = 8192
WIDTHS = 4
TR = 256
TC = 512
STEP = 10
NSEQ = 4
TOKENS = 3072
SEQ_MAX = 2304
KBLK = 1024
HPG = 4
HG = 512
FG = 2048
TILES = 96
SMALL = 24576


MOMENT_SHARE = 0.05 / 0.95


def slot_matrix(key):
    streams = jax.random.split(jax.random.fold_in(key, 11), WIDTHS)
    return jax.vmap(lambda stream: jax.random.permutation(stream, TILES))(streams).astype(jnp.int32)


def kind_index(order):
    count_in = D // TR * (HG // TC)
    count_out = HG // TR * (D // TC)
    count_up = D // TR * (FG // TC)
    edges = jnp.array([count_in, 2 * count_in, 3 * count_in, 3 * count_in + count_out, 3 * count_in + count_out + count_up], jnp.int32)
    return jnp.sum((order[..., None] >= edges).astype(jnp.int32), axis=-1)


def kind_scale(key, table):
    order = slot_matrix(key)
    values = jnp.asarray(np.array(table, np.float32))
    return values[kind_index(order)][:, :, None, None]


def grad_table():
    root = math.sqrt(TOKENS)
    return [root, root, root * 0.3, root * 0.1, root * 0.5, root]


def draw_tile_order(key, part):
    return slot_matrix(key)


def draw_master(key, part):
    table = [D ** (-0.5), D ** (-0.5), D ** (-0.5), 8.0 * D ** (-0.5), D ** (-0.5), FF ** (-0.5)]
    noise = jax.random.truncated_normal(jax.random.fold_in(key, 1), -4.0, 4.0, (WIDTHS, TILES, TR, TC), jnp.float32)
    return noise * kind_scale(key, table)


def draw_first_moment(key, part):
    noise = jax.random.truncated_normal(jax.random.fold_in(key, 2), -4.0, 4.0, (WIDTHS, TILES, TR, TC), jnp.float32)
    return noise * MOMENT_SHARE * kind_scale(key, grad_table())


def draw_second_moment(key, part):
    factor = jax.random.uniform(jax.random.fold_in(key, 3), (WIDTHS, TILES, TR, TC), jnp.float32, 1.0, 4.0)
    scale_sq = kind_scale(key, [entry * entry for entry in grad_table()])
    return factor * MOMENT_SHARE * scale_sq


def basis_draw(key, size):
    number = WIDTHS * TILES
    streams = jax.random.split(key, number)
    picked = jax.vmap(lambda stream: jax.random.permutation(stream, size))(streams).astype(jnp.int32)
    signs = (jax.random.randint(jax.random.fold_in(key, 3), (number, size), 0, 2) * 2 - 1).astype(jnp.float32)
    columns = jnp.arange(size, dtype=jnp.int32)
    phase = (2 * columns[None, None, :] + 1) * picked[:, :, None] % (4 * size)
    weight_norm = jnp.where(picked == 0, math.sqrt(1.0 / size), math.sqrt(2.0 / size)).astype(jnp.float32)
    table = jnp.cos(phase.astype(jnp.float32) * (math.pi / (2 * size))) * (weight_norm * signs)[:, :, None]
    return table.reshape(WIDTHS, TILES, size, size)


def draw_left_basis(key, part):
    return basis_draw(jax.random.fold_in(key, 21), TR)


def draw_right_basis(key, part):
    return basis_draw(jax.random.fold_in(key, 22), TC)


def small_zones():
    places = jnp.arange(SMALL, dtype=jnp.int32)
    gain_zone = (places < D) | (places >= 2 * D) & (places < 3 * D)
    bias_zone = (places >= D) & (places < 2 * D) | (places >= 3 * D) & (places < 4 * D)
    return (gain_zone, bias_zone)


def draw_small_master(key, part):
    gain_zone, bias_zone = small_zones()
    uniform_part = jax.random.uniform(jax.random.fold_in(key, 31), (SMALL,), jnp.float32, 0.6, 1.4)
    normal_part = jax.random.truncated_normal(jax.random.fold_in(key, 32), -4.0, 4.0, (SMALL,), jnp.float32)
    return jnp.where(gain_zone, uniform_part, jnp.where(bias_zone, 0.3 * normal_part, 0.7 * D ** (-0.5) * normal_part))


def small_grad_scale():
    gain_zone, bias_zone = small_zones()
    root = math.sqrt(TOKENS)
    return jnp.where(gain_zone | bias_zone, 3.0 * root, 30.0 * root).astype(jnp.float32)


def draw_small_first(key, part):
    noise = jax.random.truncated_normal(jax.random.fold_in(key, 33), -4.0, 4.0, (SMALL,), jnp.float32)
    return noise * MOMENT_SHARE * small_grad_scale()


def draw_small_second(key, part):
    factor = jax.random.uniform(jax.random.fold_in(key, 34), (SMALL,), jnp.float32, 1.0, 4.0)
    scale_base = small_grad_scale()
    return factor * MOMENT_SHARE * scale_base * scale_base


def with_ends(values, stream_key, least, top_value):
    extent = values.shape
    spot = [jax.random.randint(jax.random.fold_in(stream_key, axis), (), 0, extent[axis]) for axis in range(len(extent))]
    values = values.at[tuple(spot)].set(least)
    longest = extent.index(max(extent))
    spot[longest] = (spot[longest] + 1) % extent[longest]
    return values.at[tuple(spot)].set(top_value)


def block_levels(stream_key, shape, pieces, smallest, top_value):
    def one(dim, shards_of):
        steps = jax.random.uniform(jax.random.fold_in(jax.random.fold_in(stream_key, 6), dim), (shards_of,), jnp.float32, smallest / len(pieces), top_value / len(pieces))
        return jnp.repeat(jnp.exp(steps), shape[dim] // shards_of).reshape((-1,) + (1,) * (len(shape) - dim - 1))

    loudness = one(*pieces[0])
    for cut in pieces[1:]:
        loudness = loudness * one(*cut)
    return loudness


def profile(amount, total, limit, lean):
    loads = [(1 << 20) // math.isqrt(grade ** lean) + 1 for grade in range(2, amount + 1)]
    surplus, holding = total - limit - (amount - 1), [1] * (amount - 1)
    while surplus > 0:
        candidates = [i for i in range(amount - 1) if holding[i] < limit]
        whole, remaining = sum([loads[i] for i in candidates]), surplus
        for i in candidates:
            more = min(limit - holding[i], max(1, remaining * loads[i] // whole), surplus)
            holding[i] = holding[i] + more
            surplus = surplus - more
    return np.array([limit] + holding)


def ragged(stream_key, number_of, total, limit, slope):
    if number_of == 2:
        one = jax.random.randint(stream_key, (), max(1, total - limit), min(limit, total - 1) + 1)
        return jnp.stack([one, total - one])
    tallies = jnp.asarray(profile(number_of, total, limit, slope), jnp.int32)
    twos = (number_of - 1) // 2
    giver, receiver = tallies[1:1 + 2 * twos:2], tallies[2:2 + 2 * twos:2]
    room = jnp.minimum(giver - 1, limit - receiver)
    shifted = jax.random.randint(jax.random.fold_in(stream_key, 1), (twos,), 0, 1 << 20) % (room + 1)
    tallies = tallies.at[1:1 + 2 * twos:2].set(giver - shifted).at[2:2 + 2 * twos:2].set(receiver + shifted)
    return tallies[jax.random.permutation(jax.random.fold_in(stream_key, 2), number_of)]


def scatter_about(key, dims, deviation, limit, cuts=(), kind=jnp.bfloat16):
    loudness = block_levels(key, dims, cuts, -0.22, 0.18) if cuts else 1.0
    drawn = jax.random.normal(key, dims, jnp.float32) * deviation * loudness
    return jnp.minimum(jnp.maximum(drawn, -limit), limit).astype(kind)


def setup_inputs(seed: int = 0) -> dict:
    seeds = jax.random.split(jax.random.key(seed), 15)
    return {
        "tokens": scatter_about(seeds[0], (TOKENS, D), 1.0, 6.0, ((0, 8),)),
        "cotangent": scatter_about(seeds[1], (TOKENS, D), 1.0, 6.0, ((0, 8),)),
        "attn_width": with_ends(jax.random.randint(seeds[2], (TOKENS,), 1, WIDTHS + 1), jax.random.fold_in(seeds[2], 1), 1, WIDTHS).astype(jnp.int32),
        "ffn_width": with_ends(jax.random.randint(seeds[3], (TOKENS,), 1, WIDTHS + 1), jax.random.fold_in(seeds[3], 1), 1, WIDTHS).astype(jnp.int32),
        "seq_lengths": ragged(seeds[4], NSEQ, TOKENS, SEQ_MAX, 0).astype(jnp.int32),
        "tile_order": draw_tile_order(jax.random.fold_in(seeds[14], 71), 0),
        "master": draw_master(jax.random.fold_in(seeds[14], 71), 0),
        "first_moment": draw_first_moment(jax.random.fold_in(seeds[14], 71), 0),
        "second_moment": draw_second_moment(jax.random.fold_in(seeds[14], 71), 0),
        "left_basis": draw_left_basis(jax.random.fold_in(seeds[14], 71), 0),
        "right_basis": draw_right_basis(jax.random.fold_in(seeds[14], 71), 0),
        "small_master": draw_small_master(jax.random.fold_in(seeds[14], 71), 0),
        "small_first": draw_small_first(jax.random.fold_in(seeds[14], 71), 0),
        "small_second": draw_small_second(jax.random.fold_in(seeds[14], 71), 0),
    }


PRECISE = lax.Precision.HIGHEST
EPS_NORM = 1e-05
BETA_ONE = 0.95
BETA_TWO = 0.95
ADAM_EPS = 1e-08
DECAY_RATE = 0.01
RATE_TILE = 0.15
RATE_SMALL = 1.0
ROPE_BASE = 10000.0
NEG_FILL = -1e+30

@jax.custom_vjp
def low(v):
    return lax.optimization_barrier(v.astype(jnp.bfloat16)).astype(jnp.float32)

@jax.custom_vjp
def low_back(v):
    return v

def low_keep(v):
    return (low(v), None)

def low_pass(kept, grad):
    return (grad,)

def back_keep(v):
    return (v, None)

def back_low(kept, grad):
    return (low(grad),)
low.defvjp(low_keep, low_pass)
low_back.defvjp(back_keep, back_low)

def layer_norm(values, weight_gain, weight_bias):
    center = values - lax.optimization_barrier(jnp.mean(values, axis=1, keepdims=True))
    spread = lax.optimization_barrier(jnp.mean(center * center, axis=1, keepdims=True))
    return center * lax.rsqrt(spread + EPS_NORM) * weight_gain + weight_bias

def rotary_tables(places):
    middle = HD // 2
    frequency = ROPE_BASE ** (-(jnp.arange(middle, dtype=jnp.float32) * 2.0) / HD)
    angles = places.astype(jnp.float32)[:, None] * frequency[None, :]
    cosine_half = jnp.cos(angles)
    sine_half = jnp.sin(angles)
    return (jnp.concatenate([cosine_half, cosine_half], axis=1), jnp.concatenate([sine_half, sine_half], axis=1))

def rotary(values, cosine_table, sine_table):
    middle = HD // 2
    turned = jnp.concatenate([-values[..., middle:], values[..., :middle]], axis=-1)
    return values * cosine_table[:, None, :] + turned * sine_table[:, None, :]

def token_layout(seq_lengths):
    places = jnp.arange(TOKENS, dtype=jnp.int32)
    bounds = jnp.cumsum(seq_lengths).astype(jnp.int32)
    passed = places[:, None] >= bounds[None, :]
    segment = lax.optimization_barrier(jnp.sum(passed.astype(jnp.int32), axis=1)).astype(jnp.int32)
    offset = places - lax.optimization_barrier(jnp.sum(jnp.where(passed, seq_lengths[None, :], 0), axis=1)).astype(jnp.int32)
    return (places, segment, offset)

def from_tiles(tile_stack, rows_total, cols_total):
    return tile_stack.reshape(rows_total // TR, cols_total // TC, TR, TC).transpose(0, 2, 1, 3).reshape(rows_total, cols_total)

def group_maps(tile_stack):
    count_in = D // TR * (HG // TC)
    count_out = HG // TR * (D // TC)
    count_up = D // TR * (FG // TC)
    edge_out = 3 * count_in
    edge_up = edge_out + count_out
    edge_down = edge_up + count_up
    query_map = from_tiles(tile_stack[:count_in], D, HG)
    key_map = from_tiles(tile_stack[count_in:2 * count_in], D, HG)
    value_map = from_tiles(tile_stack[2 * count_in:edge_out], D, HG)
    output_map = from_tiles(tile_stack[edge_out:edge_up], HG, D)
    up_map = from_tiles(tile_stack[edge_up:edge_down], D, FG)
    down_map = from_tiles(tile_stack[edge_down:], FG, D)
    return (query_map, key_map, value_map, output_map, up_map, down_map)

def attend_rows(queries, token_index, segment, key_low, value_low, all_index, all_segment):
    raw_scores = jnp.einsum('qhd,khd->hqk', queries, key_low, precision=PRECISE)
    scores = low_back(raw_scores) * HD ** (-0.5)
    allowed = (all_segment[None, :] == segment[:, None]) & (all_index[None, :] <= token_index[:, None])
    scores = jnp.where(allowed[None], scores, NEG_FILL)
    running_max = lax.optimization_barrier(jnp.max(scores, axis=2, keepdims=True))
    expd = jnp.exp(scores - running_max)
    weights_p = expd / lax.optimization_barrier(jnp.sum(expd, axis=2, keepdims=True))
    return jnp.einsum('hqk,khd->qhd', low(weights_p), value_low, precision=PRECISE)

def router_scale(acts_low, router_map, chosen):
    logits = jnp.dot(acts_low, router_map, precision=PRECISE)
    probs_all = jax.nn.softmax(logits, axis=1)
    picked = (chosen[:, None] - 1 == jnp.arange(WIDTHS)[None, :]).astype(jnp.float32)
    return WIDTHS * lax.optimization_barrier(jnp.sum(probs_all * picked, axis=1))

def forward(weights, smalls, residual, attn_width, ffn_width, back_order, token_index, segment, offset):
    lowered = low(weights)
    ordered = jax.vmap(lambda stacked, order_row: stacked[order_row])(lowered, back_order)
    maps = [group_maps(ordered[group_id]) for group_id in range(WIDTHS)]
    query_map = jnp.concatenate([entry[0] for entry in maps], axis=1)
    key_map = jnp.concatenate([entry[1] for entry in maps], axis=1)
    value_map = jnp.concatenate([entry[2] for entry in maps], axis=1)
    output_map = jnp.concatenate([entry[3] for entry in maps], axis=0)
    up_map = jnp.concatenate([entry[4] for entry in maps], axis=1)
    down_map = jnp.concatenate([entry[5] for entry in maps], axis=0)
    small_low = low(smalls)
    gain_one = small_low[0:D]
    bias_one = small_low[D:2 * D]
    gain_two = small_low[2 * D:3 * D]
    bias_two = small_low[3 * D:4 * D]
    routers = small_low[4 * D:].reshape(D, 2 * WIDTHS)
    router_attn = routers[:, :WIDTHS]
    router_ffn = routers[:, WIDTHS:]
    act_one = low(layer_norm(residual, gain_one, bias_one))
    scale_attn = router_scale(act_one, router_attn, attn_width)
    cosine_table, sine_table = rotary_tables(offset)
    query_pre = low_back(jnp.dot(act_one, query_map, precision=PRECISE)).reshape(TOKENS, HEADS, HD)
    key_pre = low_back(jnp.dot(act_one, key_map, precision=PRECISE)).reshape(TOKENS, HEADS, HD)
    value_pre = low_back(jnp.dot(act_one, value_map, precision=PRECISE)).reshape(TOKENS, HEADS, HD)
    query_low = low(rotary(query_pre, cosine_table, sine_table))
    key_low = low(rotary(key_pre, cosine_table, sine_table))
    value_low = low(value_pre)
    row_block = KBLK // 4
    blocks = TOKENS // row_block
    attend = jax.checkpoint(lambda packed: attend_rows(packed[0], packed[1], packed[2], key_low, value_low, token_index, segment))
    context = lax.map(attend, (query_low.reshape(blocks, row_block, HEADS, HD), token_index.reshape(blocks, row_block), segment.reshape(blocks, row_block)))
    context = low_back(context.reshape(TOKENS, HEADS, HD))
    head_group = jnp.arange(HEADS) // HPG
    head_mask = (head_group[None, :] < attn_width[:, None]).astype(jnp.float32)
    ctx_low = low(context * head_mask[:, :, None]).reshape(TOKENS, HEADS * HD)
    attn_out = low_back(jnp.dot(ctx_low, output_map, precision=PRECISE))
    middle_res = residual + scale_attn[:, None] * attn_out
    act_two = low(layer_norm(middle_res, gain_two, bias_two))
    scale_ffn = router_scale(act_two, router_ffn, ffn_width)
    pre_act = low_back(jnp.dot(act_two, up_map, precision=PRECISE))
    unit_mask = ((jnp.arange(FF) // FG)[None, :] < ffn_width[:, None]).astype(jnp.float32)
    hidden_low = low(jnp.square(jnp.maximum(pre_act, 0.0)) * unit_mask)
    ffn_out = low_back(jnp.dot(hidden_low, down_map, precision=PRECISE))
    return middle_res + scale_ffn[:, None] * ffn_out

def reference(tokens, cotangent, attn_width, ffn_width, seq_lengths, tile_order, master, first_moment, second_moment, left_basis, right_basis, small_master, small_first, small_second):
    residual = tokens.astype(jnp.float32)
    back_order = jnp.argsort(tile_order, axis=1).astype(jnp.int32)
    token_index, segment, offset = token_layout(seq_lengths)

    def layer(weights, smalls, inputs):
        return forward(weights, smalls, inputs, attn_width, ffn_width, back_order, token_index, segment, offset)
    result, pull = jax.vjp(layer, master, small_master, residual)
    grad_tiles, grad_small, input_grad = pull(cotangent.astype(jnp.float32))
    turned = jnp.einsum('wnri,wnrc->wnic', left_basis, grad_tiles, precision=PRECISE)
    turned = jnp.einsum('wnic,wncj->wnij', turned, right_basis, precision=PRECISE)
    new_first = BETA_ONE * first_moment + (1.0 - BETA_ONE) * turned
    new_second = BETA_TWO * second_moment + (1.0 - BETA_TWO) * turned * turned
    rotated_step = new_first / (1.0 - BETA_ONE ** STEP) / (jnp.sqrt(new_second / (1.0 - BETA_TWO ** STEP)) + ADAM_EPS)
    back_step = jnp.einsum('wnri,wnij->wnrj', left_basis, rotated_step, precision=PRECISE)
    back_step = jnp.einsum('wnrj,wncj->wnrc', back_step, right_basis, precision=PRECISE)
    new_master = master - RATE_TILE * (back_step + DECAY_RATE * master)
    small_first_new = BETA_ONE * small_first + (1.0 - BETA_ONE) * grad_small
    small_second_new = BETA_TWO * small_second + (1.0 - BETA_TWO) * grad_small * grad_small
    small_step = small_first_new / (1.0 - BETA_ONE ** STEP) / (jnp.sqrt(small_second_new / (1.0 - BETA_TWO ** STEP)) + ADAM_EPS)
    small_master_new = small_master - RATE_SMALL * (small_step + DECAY_RATE * small_master)
    return (result.astype(jnp.bfloat16), input_grad, new_first, new_second, new_master, new_master.astype(jnp.bfloat16), small_first_new, small_second_new, small_master_new)
```

```python
import functools

import jax
import jax.numpy as jnp
from jax import lax
from jax.experimental import pallas as pl
from jax.experimental.pallas import tpu as pltpu
from jax.sharding import PartitionSpec as P

D = 2048
HD = 128
WIDTHS = 4
TR = 256
TC = 512
TILES = 96
STEP = 10
KB_CAP = 1024
HPG = 4
HG = 512
FG = 2048

PRECISE = lax.Precision.HIGHEST
EPS_NORM = 1e-05
BETA_ONE = 0.95
BETA_TWO = 0.95
ADAM_EPS = 1e-08
DECAY_RATE = 0.01
RATE_TILE = 0.15
RATE_SMALL = 1.0
ROPE_BASE = 10000.0
NEG_FILL = -1e30
SCORE_SCALE = HD ** (-0.5)
F32 = jnp.float32
BF16 = jnp.bfloat16
AXES = ("seq", "head")
VMEM_BIG = 56 << 20


def nt(a, b):
    return lax.dot_general(a, b, (((1,), (1,)), ((), ())), preferred_element_type=F32)


def nn(a, b):
    return lax.dot_general(a, b, (((1,), (0,)), ((), ())), preferred_element_type=F32)


def tn(a, b):
    return lax.dot_general(a, b, (((0,), (0,)), ((), ())), preferred_element_type=F32)


VM = pl.BlockSpec(memory_space=pltpu.VMEM)
SM = pl.BlockSpec(memory_space=pltpu.SMEM)
HBM = pl.BlockSpec(memory_space=pl.ANY)


def sds(shape, dtype):
    return jax.ShapeDtypeStruct(shape, dtype)


def params():
    return pltpu.CompilerParams(vmem_limit_bytes=VMEM_BIG)


def cost(flops, nbytes):
    return pl.CostEstimate(flops=int(flops), bytes_accessed=int(nbytes), transcendentals=0)


def flat_call(body, scalars, arrays, outs, scratch=(), flops=0, name=None):
    nbytes = sum(a.size * a.dtype.itemsize for a in arrays)
    nbytes += sum(int(jnp.dtype(o.dtype).itemsize) * o.size for o in outs)
    return pl.pallas_call(
        body,
        out_shape=outs,
        in_specs=[SM] + [VM] * len(arrays),
        out_specs=[VM] * len(outs),
        scratch_shapes=list(scratch),
        compiler_params=params(),
        cost_estimate=cost(flops, nbytes),
        name=name,
    )(scalars, *arrays)


def rows_of(ref, index, rows):
    return ref[pl.ds(pl.multiple_of(index * rows, rows), rows), :]


def put_rows(ref, index, rows, value):
    ref[pl.ds(pl.multiple_of(index * rows, rows), rows), :] = value


def store_pieces(acc_ref, piece, rows, outs):
    outs[0][...] = rows_of(acc_ref, piece, rows)
    for k in range(1, 4):
        outs[k][...] = rows_of(acc_ref, piece ^ k, rows).astype(BF16)


def row_stats(values):
    center = values - jnp.mean(values, axis=1, keepdims=True)
    rstd = lax.rsqrt(jnp.mean(center * center, axis=1, keepdims=True) + EPS_NORM)
    return center * rstd, rstd


def route_level(logits, width_col):
    lane = lax.broadcasted_iota(jnp.int32, logits.shape, 1)
    live = lane < WIDTHS
    top = jnp.max(jnp.where(live, logits, NEG_FILL), axis=1, keepdims=True)
    raised = jnp.where(live, jnp.exp(jnp.where(live, logits, NEG_FILL) - top), 0.0)
    probs = raised / jnp.sum(raised, axis=1, keepdims=True)
    picked = (lane == width_col - 1).astype(F32)
    chosen = jnp.sum(probs * picked, axis=1, keepdims=True)
    return WIDTHS * chosen, WIDTHS * chosen * (picked - probs)


def split_dot(values, right_low):
    high = values.astype(BF16)
    rest = (values - high.astype(F32)).astype(BF16)
    return nn(high, right_low) + nn(rest, right_low)


def norm_one_body(sc, tok, gain, bias, router, width, a1, a1p, tokp, rap, coefp, ra_s, coef_s):
    rows = a1p.shape[0]
    piece = sc[1]
    xhat, _ = row_stats(tok[...].astype(F32))
    low = (xhat * gain[...] + bias[...]).astype(BF16)
    a1[...] = low
    scale, coef = route_level(nn(low, router[...]), width[...])
    ra_s[...] = scale
    coef_s[...] = coef
    a1p[...] = rows_of(a1, piece, rows)
    tokp[...] = rows_of(tok, piece, rows)
    rap[...] = rows_of(ra_s, piece, rows)
    coefp[...] = rows_of(coef_s, piece, rows)


def turn(values, cosine, signed_sine):
    return values * cosine + pltpu.roll(values, HD // 2, 1) * signed_sine


def turn_back(values, cosine, signed_sine):
    return values * cosine - pltpu.roll(values, HD // 2, 1) * signed_sine


def project_body(sc, a1, weights, cosine, sine, o0, o1, o2, o3, heads_s):
    step = pl.program_id(0)
    spot = sc[0]
    out = nn(a1[...], weights[...].reshape(D, HG))
    plain = step == 2
    cos_v = jnp.where(plain, 1.0, cosine[0])
    sin_v = jnp.where(plain, 0.0, sine[0])
    for head in range(HPG):
        heads_s[head] = turn(out[:, head * HD : (head + 1) * HD], cos_v, sin_v).astype(BF16)
    for k, ref in enumerate((o0, o1, o2, o3)):
        ref[0] = heads_s[spot ^ k]


def attend_body(
    sc, start_col, r0, r1, r2, r3, c0, c1, c2, c3,
    o0, o1, o2, o3, ctx, lse, q_all, k_all, v_all, m_s, l_s, acc_s,
):
    spot, core = sc[0], sc[2]
    rows = r0.shape[1]

    def block_of(source, side):
        return (2 * (source // 2) + side) * 2 + source % 2

    for k, (own, other) in enumerate(((r0, c0), (r1, c1), (r2, c2), (r3, c3))):
        mine = block_of(spot ^ k, core)
        theirs = block_of(spot ^ k, 1 - core)
        q_all[k] = own[0]
        k_all[mine] = own[1]
        v_all[mine] = own[2]
        k_all[theirs] = other[1]
        v_all[theirs] = other[2]

    def per_query(k, unused):
        block = block_of(spot ^ k, core)
        query = q_all[k]
        first = start_col[block]
        where_q = block * rows + lax.broadcasted_iota(jnp.int32, (rows, rows), 0)
        lane = lax.broadcasted_iota(jnp.int32, (rows, rows), 1)
        m_s[...] = jnp.full(m_s.shape, NEG_FILL, F32)
        l_s[...] = jnp.zeros(l_s.shape, F32)
        acc_s[...] = jnp.zeros(acc_s.shape, F32)

        def per_key(kb, unused_two):
            where_k = kb * rows + lane
            scores = nt(query, k_all[kb]) * SCORE_SCALE
            scores = jnp.where((where_k <= where_q) & (where_k >= first), scores, NEG_FILL)
            old = m_s[...]
            new = jnp.maximum(old, jnp.max(scores, axis=1, keepdims=True))
            weight = jnp.exp(scores - new)
            fade = jnp.exp(old - new)
            l_s[...] = l_s[...] * fade + jnp.sum(weight, axis=1, keepdims=True)
            acc_s[...] = acc_s[...] * fade + nn(weight.astype(BF16), v_all[kb])
            m_s[...] = new
            return 0

        lax.fori_loop(sc[4 + block], block + 1, per_key, 0)
        ctx[k] = acc_s[...] / l_s[...]
        lse[k] = m_s[...] + jnp.log(l_s[...])
        return 0

    lax.fori_loop(0, 4, per_query, 0)
    for k, ref in enumerate((o0, o1, o2, o3)):
        ref[...] = ctx[k].astype(BF16)


def output_body(sc, r0, r1, r2, r3, width, weights, cb, o0, o1, o2, o3, acc_s):
    spot, piece, group = sc[0], sc[1], sc[3]
    keep = width[...] > group
    for k, ref in enumerate((r0, r1, r2, r3)):
        at = pl.ds(pl.multiple_of((spot ^ k) * HD, HD), HD)
        cb[:, at] = jnp.where(keep, ref[...], jnp.zeros_like(ref[...]))
    for col in range(D // TC):
        acc_s[:, col * TC : (col + 1) * TC] = nn(cb[:, :TR], weights[0, col]) + nn(
            cb[:, TR:], weights[1, col]
        )
    store_pieces(acc_s, piece, o1.shape[0], (o0, o1, o2, o3))


def norm_two_body(sc, own, r1, r2, r3, tokp, rap, gain, bias, attn, h1, a2p):
    total = own[...] + r1[...].astype(F32) + r2[...].astype(F32) + r3[...].astype(F32)
    attn[...] = total
    middle = tokp[...].astype(F32) + rap[...] * total
    h1[...] = middle
    xhat, _ = row_stats(middle)
    a2p[...] = (xhat * gain[...] + bias[...]).astype(BF16)


def ffn_body(
    sc, p0, p1, p2, p3, dy, width, router, w_up, w_down,
    a2, act, relu, gffn, dlog, rfp, o0, o1, o2, o3, acc_s, coef_s, rf_s,
):
    step = pl.program_id(0)
    piece, group = sc[1], sc[3]
    rows = p0.shape[0]

    @pl.when(step == 0)
    def _():
        for k, ref in enumerate((p0, p1, p2, p3)):
            put_rows(a2, piece ^ k, rows, ref[...])
        scale, coef = route_level(nn(a2[...], router[...]), width[...])
        rf_s[...] = scale
        coef_s[...] = coef
        gffn[...] = (scale * dy[...].astype(F32)).astype(BF16)
        rfp[...] = rows_of(rf_s, piece, rows)

    up = jnp.maximum(nn(a2[...], w_up[...].reshape(D, TC)), 0.0)
    up = jnp.where(width[...] > group, up, 0.0)
    relu[...] = up.astype(BF16)
    low = (up * up).astype(BF16)
    act[...] = low
    for col in range(D // TC):
        at = slice(col * TC, (col + 1) * TC)
        part = nn(low[:, :TR], w_down[0, col]) + nn(low[:, TR:], w_down[1, col])

        @pl.when(step == 0)
        def _(part=part, at=at):
            acc_s[:, at] = part

        @pl.when(step > 0)
        def _(part=part, at=at):
            acc_s[:, at] += part

    @pl.when(step == pl.num_programs(0) - 1)
    def _():
        drf = jnp.sum(acc_s[...] * dy[...].astype(F32), axis=1, keepdims=True)
        dlog[...] = drf * coef_s[...]
        store_pieces(acc_s, piece, rows, (o0, o1, o2, o3))


def ffn_back_body(sc, gffn, relu, dlog, router_t, w_up, w_down, gpre, o0, o1, o2, o3, acc_s):
    step = pl.program_id(0)
    piece = sc[1]
    halves = []
    for row in range(2):
        total = nt(gffn[:, :TC], w_down[row, 0])
        for col in range(1, D // TC):
            total += nt(gffn[:, col * TC : (col + 1) * TC], w_down[row, col])
        halves.append(total)
    gact = jnp.concatenate(halves, axis=1)
    low = (gact * 2.0 * relu[...].astype(F32)).astype(BF16)
    gpre[...] = low
    part = nt(low, w_up[...].reshape(D, TC))

    @pl.when(step == 0)
    def _():
        acc_s[...] = part + split_dot(dlog[...], router_t[...])

    @pl.when(step > 0)
    def _():
        acc_s[...] += part

    @pl.when(step == pl.num_programs(0) - 1)
    def _():
        store_pieces(acc_s, piece, o1.shape[0], (o0, o1, o2, o3))


def norm_grad(grad, values, gain):
    xhat, rstd = row_stats(values)
    scaled = grad * gain
    inner = scaled - jnp.mean(scaled, axis=1, keepdims=True)
    inner = inner - xhat * jnp.mean(scaled * xhat, axis=1, keepdims=True)
    gain_grad = jnp.sum(grad * xhat, axis=0, keepdims=True)
    return inner * rstd, gain_grad, jnp.sum(grad, axis=0, keepdims=True)


def norm_two_back_body(
    sc, own, r1, r2, r3, h1, attn, dyp, rap, coefp, gain, dh1, gattnp, dlogp, ggain, gbias
):
    grad = own[...] + r1[...].astype(F32) + r2[...].astype(F32) + r3[...].astype(F32)
    back, gain_grad, bias_grad = norm_grad(grad, h1[...], gain[...])
    middle = dyp[...].astype(F32) + back
    dh1[...] = middle
    gattnp[...] = (rap[...] * middle).astype(BF16)
    dra = jnp.sum(middle * attn[...], axis=1, keepdims=True)
    dlogp[...] = dra * coefp[...]
    ggain[...] = gain_grad
    gbias[...] = bias_grad


def gout_body(sc, p0, p1, p2, p3, width, weights, gattn, o0, o1, o2, o3, heads_s):
    spot, piece, group = sc[0], sc[1], sc[3]
    rows = p0.shape[0]
    for k, ref in enumerate((p0, p1, p2, p3)):
        put_rows(gattn, piece ^ k, rows, ref[...])
    keep = width[...] > group
    for row in range(2):
        total = nt(gattn[:, :TC], weights[row, 0])
        for col in range(1, D // TC):
            total += nt(gattn[:, col * TC : (col + 1) * TC], weights[row, col])
        low = jnp.where(keep, total, 0.0).astype(BF16)
        heads_s[2 * row] = low[:, :HD]
        heads_s[2 * row + 1] = low[:, HD:]
    for k, ref in enumerate((o0, o1, o2, o3)):
        ref[...] = heads_s[spot ^ k]


def attend_back_body(
    sc, start_row, cosine, sine, q_all, k_all, v_all, ctx, lse, g0, g1, g2, g3,
    gq, own, other, g_s, gk_s, gv_s, acc_s,
):
    spot, core = sc[0], sc[2]
    rows = g0.shape[0]

    def block_of(source, side):
        return (2 * (source // 2) + side) * 2 + source % 2

    for k, ref in enumerate((g0, g1, g2, g3)):
        g_s[k] = ref[...]
    gk_s[...] = jnp.zeros(gk_s.shape, F32)
    gv_s[...] = jnp.zeros(gv_s.shape, F32)

    def per_query(k, unused):
        block = block_of(spot ^ k, core)
        query = q_all[k]
        grad = g_s[k]
        shared = grad.astype(F32) * ctx[k]
        delta = lax.dot_general(
            jnp.ones((8, HD), F32), shared, (((1,), (1,)), ((), ())),
            precision=PRECISE, preferred_element_type=F32,
        )[:1]
        first = start_row[block]
        level = lse[k]
        where_q = block * rows + lax.broadcasted_iota(jnp.int32, (rows, rows), 1)
        line = lax.broadcasted_iota(jnp.int32, (rows, rows), 0)
        acc_s[...] = jnp.zeros(acc_s.shape, F32)

        def per_key(kb, unused_two):
            where_k = kb * rows + line
            keys = k_all[kb]
            allowed = (where_k <= where_q) & (where_k >= first)
            scores = nt(keys, query) * SCORE_SCALE
            prob = jnp.where(allowed, jnp.exp(jnp.where(allowed, scores - level, 0.0)), 0.0)
            gprob = nt(v_all[kb], grad)
            graw = (prob * (gprob - delta) * SCORE_SCALE).astype(BF16)
            gv_s[kb] += nn(prob.astype(BF16), grad)
            gk_s[kb] += nn(graw, query)
            acc_s[...] += tn(graw, keys)
            return 0

        lax.fori_loop(sc[4 + block], block + 1, per_key, 0)
        gq[k] = turn_back(acc_s[...], cosine[block], sine[block]).astype(BF16)
        return 0

    lax.fori_loop(0, 4, per_query, 0)
    for k in range(4):
        mine = block_of(spot ^ k, core)
        theirs = block_of(spot ^ k, 1 - core)
        own[k, 0] = gk_s[mine]
        own[k, 1] = gv_s[mine]
        other[k, 0] = gk_s[theirs].astype(BF16)
        other[k, 1] = gv_s[theirs].astype(BF16)


def key_merge_body(sc, gq, own, got, cosine, sine, o0, o1, o2, o3):
    spot, core = sc[0], sc[2]
    for k, ref in enumerate((o0, o1, o2, o3)):
        source = spot ^ k
        block = (2 * (source // 2) + core) * 2 + source % 2
        ref[0] = gq[k]
        gk = own[k, 0] + got[k, 0].astype(F32)
        ref[1] = turn_back(gk, cosine[block], sine[block]).astype(BF16)
        ref[2] = (own[k, 1] + got[k, 1].astype(F32)).astype(BF16)


def input_back_body(sc, r0, r1, r2, r3, weights, gin, o0, o1, o2, o3, acc_s):
    step = pl.program_id(0)
    spot, piece = sc[0], sc[1]

    @pl.when(step == 0)
    def _():
        for k, ref in enumerate((r0, r1, r2, r3)):
            for member in range(3):
                at = pl.ds(pl.multiple_of(member * HG + (spot ^ k) * HD, HD), HD)
                gin[:, at] = ref[member]

    wide = weights.shape[1] * TR
    total = nt(gin[:, :HG], weights[0].reshape(wide, TC))
    for member in range(1, 3):
        total += nt(gin[:, member * HG : (member + 1) * HG], weights[member].reshape(wide, TC))
    acc_s[...] = total
    store_pieces(acc_s, piece, o1.shape[0], (o0, o1, o2, o3))


def norm_one_back_body(sc, own, r1, r2, r3, tokp, dh1, dlogp, router_t, gain, ing, ggain, gbias):
    grad = own[...] + r1[...].astype(F32) + r2[...].astype(F32) + r3[...].astype(F32)
    grad = grad + split_dot(dlogp[...], router_t[...])
    back, gain_grad, bias_grad = norm_grad(grad, tokp[...].astype(F32), gain[...])
    ing[...] = dh1[...] + back
    ggain[...] = gain_grad
    gbias[...] = bias_grad


def place_tiles(ids, chunks, held):
    count = sum(c.shape[0] for c in chunks)

    def body(ids_ref, *refs):
        parts = refs[: len(chunks)]
        out = refs[len(chunks) + (0 if held is None else 1)]
        buf, in_sems, out_sems = refs[-3:]
        places = [(part, i) for part in parts for i in range(part.shape[0])]
        arrive = [
            pltpu.make_async_copy(part.at[i], buf.at[at], in_sems.at[at])
            for at, (part, i) in enumerate(places)
        ]
        leave = [
            pltpu.make_async_copy(buf.at[at], out.at[ids_ref[at]], out_sems.at[at])
            for at in range(count)
        ]
        for copy in arrive:
            copy.start()
        for came, go in zip(arrive, leave):
            came.wait()
            go.start()
        for copy in leave:
            copy.wait()

    extra = [] if held is None else [held]
    return pl.pallas_call(
        body,
        out_shape=sds((TILES, TR, TC), BF16),
        in_specs=[SM] + [HBM] * (len(chunks) + len(extra)),
        out_specs=HBM,
        scratch_shapes=[
            pltpu.VMEM((count, TR, TC), BF16),
            pltpu.SemaphoreType.DMA((count,)),
            pltpu.SemaphoreType.DMA((count,)),
        ],
        compiler_params=params(),
        input_output_aliases={} if held is None else {1 + len(chunks): 0},
        cost_estimate=cost(0, 2 * count * TR * TC * 2),
        name="place_tiles",
    )(ids, *chunks, *extra)


def tile_kind(tile):
    kind = (tile >= 24).astype(jnp.int32) + (tile >= 32).astype(jnp.int32)
    kind = kind + (tile >= 64).astype(jnp.int32)
    base = jnp.where(kind == 1, 24, jnp.where(kind == 2, 32, 64))
    local = tile - base
    left = jnp.where(kind == 0, tile % 8, local // 4)
    right = jnp.where(kind == 0, tile // 8, local % 4)
    return kind, left, right


def tile_grads(ids, lefts, rights, added, outs_of):
    count = ids.shape[0]
    parts = len(lefts)
    rows = lefts[0][0].shape[0]
    flat = [a for part in lefts for a in part] + [a for part in rights for a in part]

    def fetch(ids_ref, step, slot, refs, lbuf, rbuf, sems):
        kind, left, right = tile_kind(ids_ref[step])
        for which in range(4):

            @pl.when(kind == which)
            def _(which=which):
                for part in range(parts):
                    src = refs[part * 4 + which]
                    at = pl.ds(pl.multiple_of(left * TR, TR), TR)
                    pltpu.make_async_copy(
                        src.at[:, at], lbuf.at[slot, pl.ds(part * rows, rows)], sems.at[slot, part]
                    ).start()
                    src = refs[(parts + part) * 4 + which]
                    at = pl.ds(pl.multiple_of(right * TC, TC), TC)
                    pltpu.make_async_copy(
                        src.at[:, at],
                        rbuf.at[slot, pl.ds(part * rows, rows)],
                        sems.at[slot, parts + part],
                    ).start()

    def body(ids_ref, *refs):
        sources = refs[: len(flat)]
        at = len(flat)
        plus = None
        if added is not None:
            plus = refs[at]
            at += 1
        outs = refs[at : at + len(outs_of)]
        lbuf, rbuf, sems = refs[at + len(outs_of) :]
        step = pl.program_id(0)
        slot = lax.rem(step, 2)

        @pl.when(step == 0)
        def _():
            fetch(ids_ref, 0, 0, sources, lbuf, rbuf, sems)

        @pl.when(step + 1 < count)
        def _():
            fetch(ids_ref, step + 1, 1 - slot, sources, lbuf, rbuf, sems)

        for part in range(parts):
            pltpu.make_async_copy(
                sources[0].at[:, :TR], lbuf.at[slot, pl.ds(part * rows, rows)], sems.at[slot, part]
            ).wait()
            pltpu.make_async_copy(
                sources[parts * 4 + 1].at[:, :TC],
                rbuf.at[slot, pl.ds(part * rows, rows)],
                sems.at[slot, parts + part],
            ).wait()
        total = tn(lbuf[slot], rbuf[slot])
        if plus is not None:
            total = total + plus[0].astype(F32)
        low = total.astype(BF16)
        if len(outs_of) == 1:
            outs[0][0] = low
        else:
            begin = 0
            for ref, size in zip(outs, outs_of):

                @pl.when((step >= begin) & (step < begin + size))
                def _(ref=ref):
                    ref[0] = low

                begin += size

    specs_out = []
    begin = 0
    for size in outs_of:
        specs_out.append(
            pl.BlockSpec(
                (1, TR, TC),
                lambda i, ids_ref, begin=begin, size=size: (jnp.clip(i - begin, 0, size - 1), 0, 0),
            )
        )
        begin += size
    plus_in = [] if added is None else [added]
    return pl.pallas_call(
        body,
        out_shape=[sds((size, TR, TC), BF16) for size in outs_of],
        grid_spec=pltpu.PrefetchScalarGridSpec(
            num_scalar_prefetch=1,
            grid=(count,),
            in_specs=[HBM] * len(flat)
            + [pl.BlockSpec((1, TR, TC), lambda i, ids_ref: (i, 0, 0))] * len(plus_in),
            out_specs=specs_out,
            scratch_shapes=[
                pltpu.VMEM((2, parts * rows, TR), BF16),
                pltpu.VMEM((2, parts * rows, TC), BF16),
                pltpu.SemaphoreType.DMA((2, 2 * parts)),
            ],
        ),
        compiler_params=pltpu.CompilerParams(vmem_limit_bytes=32 << 20),
        cost_estimate=cost(
            2 * count * parts * rows * TR * TC, count * (parts * rows * (TR + TC) * 2 + TR * TC * 2)
        ),
        name="tile_grads",
    )(ids, *flat, *plus_in)


def adam_tile(grad, left, right, first, second, master):
    left_low = left.astype(BF16)
    right_low = right.astype(BF16)
    turned = nn(tn(left_low, grad.astype(BF16)).astype(BF16), right_low)
    new_first = BETA_ONE * first + (1.0 - BETA_ONE) * turned
    new_second = BETA_TWO * second + (1.0 - BETA_TWO) * turned * turned
    step = (
        new_first
        / (1.0 - BETA_ONE**STEP)
        / (jnp.sqrt(new_second / (1.0 - BETA_TWO**STEP)) + ADAM_EPS)
    )
    back = nt(nn(left_low, step.astype(BF16)).astype(BF16), right_low)
    return new_first, new_second, master - RATE_TILE * (back + DECAY_RATE * master)


def adam_tiles(sc, size, half, grads, bases, state, held):
    sides = len(grads)
    counts = [len(g) for g in grads]
    flat = [a for g in grads for a in g]

    def slot(i, sc_ref):
        side = i // size
        which = sc_ref[0] if sides == 1 else jnp.where(side == 0, sc_ref[0], 1 - sc_ref[0])
        return which * half + sc_ref[1] + lax.rem(i, size)

    def body(sc_ref, *refs):
        step = pl.program_id(0)
        left, right, first, second, master = refs[len(flat) : len(flat) + 5]
        o_first, o_second, o_master, o_low = refs[-5:-1]
        grad_s = refs[-1]
        at = 0
        for side in range(sides):
            members = refs[at : at + counts[side]]
            at += counts[side]

            @pl.when(step // size == side)
            def _(members=members, side=side):
                total = members[0][0].astype(F32)
                if side == 0:
                    total = jnp.where(sc_ref[2] > 0, total, 0.0)
                for ref in members[1:]:
                    total = total + ref[0].astype(F32)
                grad_s[...] = total

        new_first, new_second, new_master = adam_tile(
            grad_s[...], left[0], right[0], first[0], second[0], master[0]
        )
        o_first[0] = new_first
        o_second[0] = new_second
        o_master[0] = new_master
        o_low[0] = new_master.astype(BF16)

    specs = []
    for side in range(sides):
        for _ in range(counts[side]):
            specs.append(
                pl.BlockSpec(
                    (1, TR, TC),
                    lambda i, sc_ref, side=side: (jnp.clip(i - side * size, 0, size - 1), 0, 0),
                )
            )

    def at_slot(shape):
        return pl.BlockSpec((1,) + shape, lambda i, sc_ref: (slot(i, sc_ref), 0, 0))

    slots = state[0].shape[0]
    shapes = [(TR, TC)] * 4
    types = [F32, F32, F32, BF16]
    extra = [] if held is None else list(held)
    base = 1 + len(flat) + 5
    return pl.pallas_call(
        body,
        out_shape=[sds((slots,) + s, t) for s, t in zip(shapes, types)],
        grid_spec=pltpu.PrefetchScalarGridSpec(
            num_scalar_prefetch=1,
            grid=(sides * size,),
            in_specs=specs
            + [at_slot((TR, TR)), at_slot((TC, TC))]
            + [at_slot((TR, TC))] * 3
            + [HBM] * len(extra),
            out_specs=[at_slot(s) for s in shapes],
            scratch_shapes=[pltpu.VMEM((TR, TC), F32)],
        ),
        input_output_aliases={base + i: i for i in range(len(extra))},
        compiler_params=pltpu.CompilerParams(vmem_limit_bytes=40 << 20),
        cost_estimate=cost(sides * size * 8 * TR * TC * TC, sides * size * 5 * TR * TC * 4),
        name="adam_tiles",
    )(sc, *flat, *bases, *state, *extra)


def small_adam(grad, first, second, master):
    new_first = BETA_ONE * first + (1.0 - BETA_ONE) * grad
    new_second = BETA_TWO * second + (1.0 - BETA_TWO) * grad * grad
    step = (
        new_first
        / (1.0 - BETA_ONE**STEP)
        / (jnp.sqrt(new_second / (1.0 - BETA_TWO**STEP)) + ADAM_EPS)
    )
    return new_first, new_second, master - RATE_SMALL * (step + DECAY_RATE * master)


def signed_tables(places):
    middle = HD // 2
    frequency = ROPE_BASE ** (-(jnp.arange(middle, dtype=F32) * 2.0) / HD)
    angles = places.astype(F32)[:, None] * frequency[None, :]
    cosine = jnp.cos(angles)
    sine = jnp.sin(angles)
    return (
        jnp.concatenate([cosine, cosine], axis=1),
        jnp.concatenate([-sine, sine], axis=1),
    )


def token_layout(first_index, local_rows, seq_lengths):
    places = first_index + jnp.arange(local_rows, dtype=jnp.int32)
    number = seq_lengths.shape[0]
    below = jnp.arange(number)[None, :] <= jnp.arange(number)[:, None]
    bounds = jnp.sum(jnp.where(below, seq_lengths[None, :], 0), axis=1)
    passed = places[:, None] >= bounds[None, :]
    segment = jnp.sum(passed.astype(jnp.int32), axis=1)
    offset = places - jnp.sum(jnp.where(passed, seq_lengths[None, :], 0), axis=1)
    return (places, segment, offset)


def moves(target):
    pairs = []
    for z in range(4):
        for y in range(2):
            for x in range(2):
                for c in range(2):
                    to = target(z, y, x, c)
                    if to is not None:
                        a, b, e, f = to
                        pairs.append((8 * z + 4 * y + 2 * x + c, 8 * a + 4 * b + 2 * e + f))
    return pairs


def only(condition, target):
    return lambda z, y, x, c: target(z, y, x, c) if condition(z, y, x, c) else None


def flip(dz=0, dy=0, dx=0, dc=0):
    return lambda z, y, x, c: (z ^ dz, y ^ dy, x ^ dx, c ^ dc)


def own_group(z, y, x, c):
    return c == z % 2


def foreign(z, y, x, c):
    return c != z % 2


def send(value, target):
    return lax.ppermute(value, AXES, moves(target))


MEMBERS = (None, flip(dz=1), flip(dx=1), flip(dz=1, dx=1))
HEADMATES = (None, flip(dy=1), flip(dz=2), flip(dz=2, dy=1))


def scatter_pieces(pieces):
    return [pieces[0]] + [send(pieces[k], MEMBERS[k]) for k in range(1, 4)]


def share_piece(piece):
    return [piece] + [send(piece, MEMBERS[k]) for k in range(1, 4)]


def swap_heads(blocks):
    return [blocks[0]] + [send(blocks[k], HEADMATES[k]) for k in range(1, 4)]


def gather_small(values, z, y):
    for bit, target in ((y, flip(dy=1)), (z % 2, flip(dz=1)), (z // 2, flip(dz=2))):
        other = send(values, target)
        values = jnp.where(
            bit == 0, jnp.concatenate([values, other]), jnp.concatenate([other, values])
        )
    return values


def reduce_small(terms, z, y):
    terms = terms.reshape(8, -1)
    for bit, target in ((z // 2, flip(dz=2)), (z % 2, flip(dz=1)), (y, flip(dy=1))):
        halves = terms.reshape(2, terms.shape[0] // 2, terms.shape[1])
        keep = jnp.where(bit == 0, halves[0], halves[1])
        away = jnp.where(bit == 0, halves[1], halves[0])
        terms = keep + send(away, target)
    terms = terms.reshape(-1)
    terms = terms + send(terms, flip(dx=1))
    return terms + send(terms, flip(dc=1))


def after(value, *others):
    return lax.optimization_barrier((value,) + others)[0]


def local_remap(
    tokens, cotangent, attn_width, ffn_width, seq_lengths, tile_order, master, first_moment,
    second_moment, left_basis, right_basis, small_master, small_first, small_second,
):
    rows = tokens.shape[0]
    piece_rows = rows // 4
    s = lax.axis_index("seq")
    h = lax.axis_index("head")
    z, y, x, c = s // 2, s % 2, h // 2, h % 2
    zp, zh = z % 2, z // 2
    mine = c == zp
    group = 2 * x + zp
    spot = 2 * zh + y
    block = (2 * zh + c) * 2 + y

    slots = master.shape[1]
    half = slots // 2
    low = master[0].astype(BF16)
    first_half, second_half = low[:half], low[half:]
    same = jnp.where(c == 0, first_half, second_half)
    cross = jnp.where(c == 0, second_half, first_half)
    order = tile_order[0]
    order = jnp.where(mine, order, send(order, flip(dc=1)))
    u0 = jnp.where(mine, same, send(cross, only(own_group, flip(dc=1))))
    u1 = jnp.where(
        mine, send(same, only(foreign, flip(dz=1))), send(cross, only(foreign, flip(dz=1, dc=1)))
    )
    v0 = send(u0, flip(dz=2))
    u0y = send(u0, flip(dy=1))
    small_all = gather_small(small_master.astype(BF16), z, y)
    v1 = send(after(u1, v0), flip(dz=2))
    u1y = send(u1, flip(dy=1))
    v0y = send(v0, flip(dy=1))
    v1y = send(v1, flip(dy=1))
    early = [(u0, s), (u1, s ^ 2), (u0y, s ^ 1), (u1y, s ^ 3), (v0, s ^ 4), (v0y, s ^ 5)]
    late = [(v1, s ^ 6), (v1y, s ^ 7)]

    def ids_at(owner, side):
        return lax.dynamic_slice_in_dim(order, owner * slots + side * half, half, 0)

    tiles = None
    for some in (early, late):
        chunks = [v for v, _ in some] + [send(v, flip(dc=1)) for v, _ in some]
        ids = [ids_at(o, c) for _, o in some] + [ids_at(o, 1 - c) for _, o in some]
        tiles = place_tiles(jnp.concatenate(ids), chunks, tiles)
    by_row = tiles.reshape(TILES // 4, 4, TR, TC)
    by_map = tiles.reshape(TILES // 8, 8, TR, TC)

    to_pair = only(own_group, flip(dz=1))

    def fetch(value):
        return jnp.where(mine, value, send(value, to_pair))

    tok = fetch(tokens)
    widths = fetch(jnp.stack([attn_width, ffn_width]))
    width_a, width_f = widths[0][:, None], widths[1][:, None]
    dy = fetch(cotangent)
    dyp = lax.dynamic_slice_in_dim(dy, group * piece_rows, piece_rows, 0)

    gains = small_all[: 4 * D].astype(F32).reshape(4, 1, D)
    gain_one, bias_one, gain_two, bias_two = gains[0], gains[1], gains[2], gains[3]
    routers = small_all[4 * D :].reshape(D, 2 * WIDTHS)
    pad = ((0, 0), (0, HD - WIDTHS))
    router_a = jnp.pad(routers[:, :WIDTHS], pad)
    router_f = jnp.pad(routers[:, WIDTHS:], pad)

    all_rows = rows * lax.axis_size("seq")
    blocks = all_rows // rows
    places, _, offset = token_layout(0, all_rows, seq_lengths)
    start = places - offset
    first_block = start.reshape(blocks, rows)[:, 0] // rows
    cosine, sine = signed_tables(offset)
    cosine, sine = cosine.reshape(blocks, rows, HD), sine.reshape(blocks, rows, HD)
    scalars = jnp.concatenate(
        [jnp.stack([spot, group, c, group]).astype(jnp.int32), first_block.astype(jnp.int32)]
    )

    a1, a1p, tokp, rap, coefp = flat_call(
        norm_one_body,
        scalars,
        [tok, gain_one, bias_one, router_a, width_a],
        [
            sds((rows, D), BF16),
            sds((piece_rows, D), BF16),
            sds((piece_rows, D), BF16),
            sds((piece_rows, 1), F32),
            sds((piece_rows, HD), F32),
        ],
        [pltpu.VMEM((rows, 1), F32), pltpu.VMEM((rows, HD), F32)],
        name="norm_one",
    )

    table = pl.BlockSpec((1, rows, HD), lambda i, sc: (sc[12], 0, 0))
    sent = pl.pallas_call(
        project_body,
        out_shape=[sds((3, rows, HD), BF16)] * 4,
        grid_spec=pltpu.PrefetchScalarGridSpec(
            num_scalar_prefetch=1,
            grid=(3,),
            in_specs=[
                pl.BlockSpec((rows, D), lambda i, sc: (0, 0)),
                pl.BlockSpec((1, 8, TR, TC), lambda i, sc: (i, 0, 0, 0)),
                table,
                table,
            ],
            out_specs=[pl.BlockSpec((1, rows, HD), lambda i, sc: (i, 0, 0))] * 4,
            scratch_shapes=[pltpu.VMEM((HPG, rows, HD), BF16)],
        ),
        compiler_params=params(),
        cost_estimate=cost(2 * rows * D * 3 * HG, 3 * D * HG * 2 + rows * D * 2),
        name="project",
    )(jnp.concatenate([scalars, block[None].astype(jnp.int32)]), a1, by_map, cosine, sine)
    got = swap_heads(sent)
    beside = [send(v, flip(dc=1)) for v in got]

    pairs_cost = 4 * 4 * rows * rows * HD * 2
    out = flat_call(
        attend_body,
        scalars,
        [start.reshape(blocks, rows, 1)] + got + beside,
        [sds((rows, HD), BF16)] * 4
        + [
            sds((4, rows, HD), F32),
            sds((4, rows, 1), F32),
            sds((4, rows, HD), BF16),
            sds((blocks, rows, HD), BF16),
            sds((blocks, rows, HD), BF16),
        ],
        [pltpu.VMEM((rows, 1), F32), pltpu.VMEM((rows, 1), F32), pltpu.VMEM((rows, HD), F32)],
        flops=2 * pairs_cost,
        name="attend",
    )
    ctx_sent, (ctx, lse, q_all, k_all, v_all) = out[:4], out[4:]
    ctx_got = swap_heads(ctx_sent)

    one_piece = sds((piece_rows, D), F32)
    low_piece = sds((piece_rows, D), BF16)
    piece_outs = [one_piece] + [low_piece] * 3
    wo_spec = pl.BlockSpec((2, 4, TR, TC), lambda i, sc: (3, 0, 0, 0))

    def whole(shape):
        return pl.BlockSpec(shape, lambda i, sc: (0,) * len(shape))

    out = pl.pallas_call(
        output_body,
        out_shape=[sds((rows, HG), BF16)] + piece_outs,
        grid_spec=pltpu.PrefetchScalarGridSpec(
            num_scalar_prefetch=1,
            grid=(1,),
            in_specs=[whole((rows, HD))] * 4 + [whole((rows, 1)), wo_spec],
            out_specs=[whole((rows, HG))] + [whole((piece_rows, D))] * 4,
            scratch_shapes=[pltpu.VMEM((rows, D), F32)],
        ),
        compiler_params=params(),
        cost_estimate=cost(2 * rows * D * HG, D * HG * 2 + rows * D * 4),
        name="output",
    )(scalars, *ctx_got, width_a, by_row)
    cb, attn_parts = out[0], out[1:]
    attn_parts = scatter_pieces(attn_parts)

    attn, h1, a2p = flat_call(
        norm_two_body,
        scalars,
        attn_parts + [tokp, rap, gain_two, bias_two],
        [one_piece, one_piece, low_piece],
        name="norm_two",
    )
    a2_parts = share_piece(a2p)

    up_spec = pl.BlockSpec((8, 1, TR, TC), lambda i, sc: (1, i, 0, 0))
    down_spec = pl.BlockSpec((2, 4, TR, TC), lambda i, sc: (8 + i, 0, 0, 0))
    col_spec = pl.BlockSpec((rows, TC), lambda i, sc: (0, i))
    out = pl.pallas_call(
        ffn_body,
        out_shape=[
            sds((rows, D), BF16),
            sds((rows, FG), BF16),
            sds((rows, FG), BF16),
            sds((rows, D), BF16),
            sds((rows, HD), F32),
            sds((piece_rows, 1), F32),
        ]
        + piece_outs,
        grid_spec=pltpu.PrefetchScalarGridSpec(
            num_scalar_prefetch=1,
            grid=(FG // TC,),
            in_specs=[whole((piece_rows, D))] * 4
            + [whole((rows, D)), whole((rows, 1)), whole((D, HD)), up_spec, down_spec],
            out_specs=[
                whole((rows, D)),
                col_spec,
                col_spec,
                whole((rows, D)),
                whole((rows, HD)),
                whole((piece_rows, 1)),
            ]
            + [whole((piece_rows, D))] * 4,
            scratch_shapes=[
                pltpu.VMEM((rows, D), F32),
                pltpu.VMEM((rows, HD), F32),
                pltpu.VMEM((rows, 1), F32),
            ],
        ),
        compiler_params=params(),
        cost_estimate=cost(4 * rows * D * FG, 4 * D * FG + rows * D * 12),
        name="ffn",
    )(scalars, *a2_parts, dy, width_f, router_f, by_row, by_row)
    a2, act, relu, gffn, dlog_f, rfp = out[:6]
    ffn_parts = out[6:]

    out = pl.pallas_call(
        ffn_back_body,
        out_shape=[sds((rows, FG), BF16)] + piece_outs,
        grid_spec=pltpu.PrefetchScalarGridSpec(
            num_scalar_prefetch=1,
            grid=(FG // TC,),
            in_specs=[
                whole((rows, D)),
                col_spec,
                whole((rows, HD)),
                whole((HD, D)),
                up_spec,
                down_spec,
            ],
            out_specs=[col_spec] + [whole((piece_rows, D))] * 4,
            scratch_shapes=[pltpu.VMEM((rows, D), F32)],
        ),
        compiler_params=params(),
        cost_estimate=cost(4 * rows * D * FG, 4 * D * FG + rows * D * 12),
        name="ffn_back",
    )(scalars, gffn, relu, dlog_f, router_f.T, by_row, by_row)
    gpre, ga2_parts = out[0], scatter_pieces(out[1:])
    ffn_parts = scatter_pieces(ffn_parts)

    dh1, gattnp, dlog_a, ggain_two, gbias_two = flat_call(
        norm_two_back_body,
        scalars,
        ga2_parts + [h1, attn, dyp, rap, coefp, gain_two],
        [one_piece, low_piece, sds((piece_rows, HD), F32), sds((1, D), F32), sds((1, D), F32)],
        name="norm_two_back",
    )
    gattn_parts = share_piece(gattnp)
    out = pl.pallas_call(
        gout_body,
        out_shape=[sds((rows, D), BF16)] + [sds((rows, HD), BF16)] * 4,
        grid_spec=pltpu.PrefetchScalarGridSpec(
            num_scalar_prefetch=1,
            grid=(1,),
            in_specs=[whole((piece_rows, D))] * 4 + [whole((rows, 1)), wo_spec],
            out_specs=[whole((rows, D))] + [whole((rows, HD))] * 4,
            scratch_shapes=[pltpu.VMEM((HPG, rows, HD), BF16)],
        ),
        compiler_params=params(),
        cost_estimate=cost(2 * rows * D * HG, D * HG * 2 + rows * D * 4),
        name="gout",
    )(scalars, *gattn_parts, width_a, by_row)
    gattn, gout_got = out[0], swap_heads(out[1:])

    gq, keys_own, keys_other = flat_call(
        attend_back_body,
        scalars,
        [start.reshape(blocks, 1, rows), cosine, sine, q_all, k_all, v_all, ctx]
        + [lse.reshape(4, 1, rows)]
        + gout_got,
        [
            sds((4, rows, HD), BF16),
            sds((4, 2, rows, HD), F32),
            sds((4, 2, rows, HD), BF16),
        ],
        [
            pltpu.VMEM((4, rows, HD), BF16),
            pltpu.VMEM((blocks, rows, HD), F32),
            pltpu.VMEM((blocks, rows, HD), F32),
            pltpu.VMEM((rows, HD), F32),
        ],
        flops=5 * pairs_cost,
        name="attend_back",
    )
    grads_sent = flat_call(
        key_merge_body,
        scalars,
        [gq, keys_own, send(keys_other, flip(dc=1)), cosine, sine],
        [sds((3, rows, HD), BF16)] * 4,
        name="key_merge",
    )
    grads_got = swap_heads(grads_sent)
    half_cols = D // 2
    half_piece = pl.BlockSpec((piece_rows, half_cols), lambda i, sc: (0, i))
    out = pl.pallas_call(
        input_back_body,
        out_shape=[sds((rows, 3 * HG), BF16)] + piece_outs,
        grid_spec=pltpu.PrefetchScalarGridSpec(
            num_scalar_prefetch=1,
            grid=(2,),
            in_specs=[whole((3, rows, HD))] * 4
            + [pl.BlockSpec((3, 4, TR, TC), lambda i, sc: (0, i, 0, 0))],
            out_specs=[whole((rows, 3 * HG))] + [half_piece] * 4,
            scratch_shapes=[pltpu.VMEM((rows, half_cols), F32)],
        ),
        compiler_params=params(),
        cost_estimate=cost(2 * rows * D * 3 * HG, 3 * D * HG * 2 + rows * D * 4),
        name="input_back",
    )(scalars, *grads_got, by_map)
    gin, ga1_parts = out[0], scatter_pieces(out[1:])

    ingp, ggain_one, gbias_one = flat_call(
        norm_one_back_body,
        scalars,
        ga1_parts + [tokp, dh1, dlog_a, router_a.T, gain_one],
        [one_piece, sds((1, D), F32), sds((1, D), F32)],
        name="norm_one_back",
    )
    outp = ffn_parts[0]
    for part in ffn_parts[1:]:
        outp = outp + part.astype(F32)
    outp = (h1 + rfp * outp).astype(BF16)

    def deliver(piece):
        full = jnp.zeros((rows, D), piece.dtype)
        full = lax.dynamic_update_slice_in_dim(full, piece, group * piece_rows, 0)
        for k, target in (
            (1, only(foreign, flip(dz=1))),
            (2, only(own_group, flip(dx=1))),
            (3, only(foreign, flip(dz=1, dx=1))),
        ):
            full = lax.dynamic_update_slice_in_dim(
                full, send(piece, target), (group ^ k) * piece_rows, 0
            )
        return jnp.where(mine, full, send(full, only(own_group, flip(dc=1))))

    output = deliver(outp)
    input_grad = deliver(ingp)

    grad_router = jnp.concatenate(
        [
            lax.dot_general(
                a1p.astype(F32), dlog_a[:, :WIDTHS], (((0,), (0,)), ((), ())), precision=PRECISE
            ),
            lax.dot_general(
                a2.astype(F32), dlog_f[:, :WIDTHS], (((0,), (0,)), ((), ())), precision=PRECISE
            ),
        ],
        axis=1,
    ).reshape(-1)
    small_terms = jnp.concatenate(
        [ggain_one[0], gbias_one[0], ggain_two[0], gbias_two[0], grad_router]
    )
    small_grad = reduce_small(small_terms, z, y)
    small_outs = small_adam(small_grad, small_first, small_second, small_master)

    lefts = [[a1, cb, a2, act]]
    rights = [[gin, gattn, gpre, gffn]]
    lefts.append([send(v, flip(dc=1)) for v in lefts[0]])
    rights.append([send(v, flip(dc=1)) for v in rights[0]])
    chunk = CHUNK
    relative = (0, 2, 4, 6)

    def grad_ids(flip_y, begin):
        return jnp.concatenate(
            [
                lax.dynamic_slice_in_dim(
                    order, ((s ^ flip_y) ^ r) * slots + c * half + begin, chunk, 0
                )
                for r in relative
            ]
        )

    bases = (left_basis[0], right_basis[0])
    state = (first_moment[0], second_moment[0], master[0])
    held = None
    for begin in range(0, half, chunk):
        away = tile_grads(grad_ids(1, begin), lefts, rights, None, [4 * chunk])[0]
        back = send(away, flip(dy=1))
        here = tile_grads(grad_ids(0, begin), lefts, rights, back, [chunk] * 4)
        to_owner = [None, flip(dz=1), flip(dz=2), flip(dz=3)]
        same_side = [here[0]] + [send(here[r], only(own_group, to_owner[r])) for r in (1, 2, 3)]
        other_side = [send(here[0], only(foreign, flip(dc=1)))] + [
            send(
                here[r],
                only(
                    foreign,
                    lambda z, y, x, c, t=to_owner[r]: t(z, y, x, 1 - c),
                ),
            )
            for r in (1, 2, 3)
        ]
        sc = jnp.stack([c, jnp.int32(begin), mine.astype(jnp.int32)]).astype(jnp.int32)
        held = adam_tiles(sc, chunk, half, [same_side, other_side], bases, state, held)
    return (
        output,
        input_grad,
        held[0][None],
        held[1][None],
        held[2][None],
        held[3][None],
        *small_outs,
    )


CHUNK = 2


def layer_norm(values, weight_gain, weight_bias):
    center = values - jnp.mean(values, axis=1, keepdims=True)
    spread = jnp.mean(center * center, axis=1, keepdims=True)
    return center * lax.rsqrt(spread + EPS_NORM) * weight_gain + weight_bias


def rotary_tables(places):
    middle = HD // 2
    frequency = ROPE_BASE ** (-(jnp.arange(middle, dtype=jnp.float32) * 2.0) / HD)
    angles = places.astype(jnp.float32)[:, None] * frequency[None, :]
    cosine_half = jnp.cos(angles)
    sine_half = jnp.sin(angles)
    return (
        jnp.concatenate([cosine_half, cosine_half], axis=1),
        jnp.concatenate([sine_half, sine_half], axis=1),
    )


def rotary(values, cosine_table, sine_table):
    middle = HD // 2
    turned = jnp.concatenate([-values[..., middle:], values[..., :middle]], axis=-1)
    return values * cosine_table[:, None, :] + turned * sine_table[:, None, :]


def rotary_back(gradients, cosine_table, sine_table):
    middle = HD // 2
    scaled = gradients * sine_table[:, None, :]
    turned = jnp.concatenate([scaled[..., middle:], -scaled[..., :middle]], axis=-1)
    return gradients * cosine_table[:, None, :] + turned


def from_tiles(tile_stack, rows_total, cols_total):
    return (
        tile_stack.reshape(rows_total // TR, cols_total // TC, TR, TC)
        .transpose(0, 2, 1, 3)
        .reshape(rows_total, cols_total)
    )


def unpack(tile_stack):
    count_in = D // TR * (HG // TC)
    count_out = HG // TR * (D // TC)
    count_up = D // TR * (FG // TC)
    edge_out = 3 * count_in
    edge_up = edge_out + count_out
    edge_down = edge_up + count_up
    w_inputs = jnp.concatenate(
        [
            from_tiles(tile_stack[:count_in], D, HG),
            from_tiles(tile_stack[count_in : 2 * count_in], D, HG),
            from_tiles(tile_stack[2 * count_in : edge_out], D, HG),
        ],
        axis=1,
    )
    w_output = from_tiles(tile_stack[edge_out:edge_up], HG, D)
    w_up = from_tiles(tile_stack[edge_up:edge_down], D, FG)
    w_down = from_tiles(tile_stack[edge_down:], FG, D)
    return (w_inputs, w_output, w_up, w_down)


def router_scale(acts_low, router_map, chosen):
    logits = jnp.dot(acts_low.astype(jnp.float32), router_map, precision=PRECISE)
    probs_all = jax.nn.softmax(logits, axis=1)
    picked = (chosen[:, None] - 1 == jnp.arange(WIDTHS)[None, :]).astype(jnp.float32)
    return (WIDTHS * jnp.sum(probs_all * picked, axis=1), probs_all, picked)


def router_back(grad_scale, probs_all, picked):
    chosen_prob = jnp.sum(probs_all * picked, axis=1)
    return (WIDTHS * grad_scale * chosen_prob)[:, None] * (picked - probs_all)


def scores_of(queries, key_block, query_index, query_segment, key_index, key_segment):
    raw_scores = jnp.einsum(
        "qhd,khd->hqk", queries, key_block, preferred_element_type=jnp.float32
    ) * HD ** (-0.5)
    allowed = (key_segment[None, :] == query_segment[:, None]) & (
        key_index[None, :] <= query_index[:, None]
    )
    return (raw_scores, allowed[None])


def fetch_block(packed_all, all_index, all_segment, number, block_rows):
    start = number * block_rows
    piece_rows = lax.dynamic_slice_in_dim(packed_all, start, block_rows, 0)
    key_index = lax.dynamic_slice_in_dim(all_index, start, block_rows, 0)
    key_segment = lax.dynamic_slice_in_dim(all_segment, start, block_rows, 0)
    first_half = piece_rows[:, :HG].reshape(block_rows, HPG, HD)
    second_half = piece_rows[:, HG:].reshape(block_rows, HPG, HD)
    return (first_half, second_half, key_index, key_segment)


def attend_forward(queries, token_index, segment, packed_all, all_index, all_segment, block_rows):
    local_rows = queries.shape[0]
    blocks = packed_all.shape[0] // block_rows

    def first_pass(carried, number):
        running_max, running_sum = carried
        key_block, value_block, key_index, key_segment = fetch_block(
            packed_all, all_index, all_segment, number, block_rows
        )
        raw_scores, allowed = scores_of(
            queries, key_block, token_index, segment, key_index, key_segment
        )
        masked = jnp.where(allowed, raw_scores, NEG_FILL)
        fresh_max = jnp.maximum(running_max, jnp.max(masked, axis=2))
        running_sum = running_sum * jnp.exp(running_max - fresh_max) + jnp.sum(
            jnp.exp(masked - fresh_max[:, :, None]), axis=2
        )
        return ((fresh_max, running_sum), None)

    start_state = (
        jnp.full((HPG, local_rows), NEG_FILL, jnp.float32),
        jnp.zeros((HPG, local_rows), jnp.float32),
    )
    (running_max, running_sum), unused = lax.scan(first_pass, start_state, jnp.arange(blocks))
    log_sum = running_max + jnp.log(running_sum)

    def second_pass(carried, number):
        key_block, value_block, key_index, key_segment = fetch_block(
            packed_all, all_index, all_segment, number, block_rows
        )
        raw_scores, allowed = scores_of(
            queries, key_block, token_index, segment, key_index, key_segment
        )
        weights_p = jnp.where(allowed, jnp.exp(raw_scores - log_sum[:, :, None]), 0.0)
        update = jnp.einsum(
            "hqk,khd->qhd",
            weights_p.astype(jnp.bfloat16),
            value_block,
            preferred_element_type=jnp.float32,
        )
        return (carried + update, None)

    context, unused = lax.scan(
        second_pass, jnp.zeros((local_rows, HPG, HD), jnp.float32), jnp.arange(blocks)
    )
    return (log_sum, context)


def pair_grads(
    queries,
    grad_out,
    log_sum,
    delta,
    query_index,
    query_segment,
    key_block,
    value_block,
    key_index,
    key_segment,
):
    raw_scores, allowed = scores_of(
        queries, key_block, query_index, query_segment, key_index, key_segment
    )
    weights_p = jnp.where(allowed, jnp.exp(raw_scores - log_sum[:, :, None]), 0.0)
    grad_value = jnp.einsum(
        "hqk,qhd->khd", weights_p.astype(jnp.bfloat16), grad_out, preferred_element_type=jnp.float32
    )
    grad_probs = jnp.einsum(
        "qhd,khd->hqk", grad_out, value_block, preferred_element_type=jnp.float32
    )
    grad_raw = (weights_p * (grad_probs - delta[:, :, None]) * HD ** (-0.5)).astype(jnp.bfloat16)
    grad_query = jnp.einsum("hqk,khd->qhd", grad_raw, key_block, preferred_element_type=jnp.float32)
    grad_key = jnp.einsum("hqk,qhd->khd", grad_raw, queries, preferred_element_type=jnp.float32)
    return (grad_query, grad_key, grad_value)


def local_plain(
    tokens,
    cotangent,
    attn_width,
    ffn_width,
    seq_lengths,
    tile_order,
    master,
    first_moment,
    second_moment,
    left_basis,
    right_basis,
    small_master,
    small_first,
    small_second,
):
    local_rows = tokens.shape[0]
    shards = lax.axis_size("seq")
    all_rows = local_rows * shards
    block_rows = min(KB_CAP, all_rows)
    blocks = all_rows // block_rows
    group_id = lax.axis_index("head")
    slot_order = tile_order[0]
    weights_all, small_all = (
        lax.all_gather(master[0].astype(jnp.bfloat16), "seq", axis=0, tiled=True),
        lax.all_gather(small_master.astype(jnp.bfloat16), "seq", axis=0, tiled=True),
    )
    w_inputs, w_output, w_up, w_down = unpack(place_tiles(slot_order, [weights_all], None))
    small_vals = small_all.astype(jnp.float32)
    gain_one = small_vals[0:D]
    bias_one = small_vals[D : 2 * D]
    gain_two = small_vals[2 * D : 3 * D]
    bias_two = small_vals[3 * D : 4 * D]
    routers = small_vals[4 * D :].reshape(D, 2 * WIDTHS)
    router_attn = routers[:, :WIDTHS]
    router_ffn = routers[:, WIDTHS:]
    first_row = lax.axis_index("seq") * local_rows
    token_index, segment, offset = token_layout(first_row, local_rows, seq_lengths)
    residual = tokens.astype(jnp.float32)
    ln_one, pull_one = jax.vjp(layer_norm, residual, gain_one, bias_one)
    act_one = ln_one.astype(jnp.bfloat16)
    scale_attn, probs_attn, picked_attn = router_scale(act_one, router_attn, attn_width)
    projected = jnp.dot(act_one, w_inputs, preferred_element_type=jnp.float32)
    cosine_table, sine_table = rotary_tables(offset)
    query_low = rotary(
        projected[:, :HG].reshape(local_rows, HPG, HD), cosine_table, sine_table
    ).astype(jnp.bfloat16)
    key_low = rotary(
        projected[:, HG : 2 * HG].reshape(local_rows, HPG, HD), cosine_table, sine_table
    ).astype(jnp.bfloat16)
    value_low = projected[:, 2 * HG :].astype(jnp.bfloat16)
    packed = jnp.concatenate([key_low.reshape(local_rows, HG), value_low], axis=1)
    packed_all = lax.all_gather(packed, "seq", axis=0, tiled=True)
    all_index, all_segment, all_offset = token_layout(0, all_rows, seq_lengths)
    log_sum, context = attend_forward(
        query_low, token_index, segment, packed_all, all_index, all_segment, block_rows
    )
    head_mask = (group_id < attn_width).astype(jnp.float32)
    ctx_low = (context * head_mask[:, None, None]).astype(jnp.bfloat16).reshape(local_rows, HG)
    attn_out = lax.psum(
        jnp.dot(ctx_low, w_output, preferred_element_type=jnp.float32).astype(jnp.bfloat16), "head"
    ).astype(jnp.float32)
    middle_res = residual + scale_attn[:, None] * attn_out
    ln_two, pull_two = jax.vjp(layer_norm, middle_res, gain_two, bias_two)
    act_two = ln_two.astype(jnp.bfloat16)
    scale_ffn, probs_ffn, picked_ffn = router_scale(act_two, router_ffn, ffn_width)
    pre_act = jnp.dot(act_two, w_up, preferred_element_type=jnp.float32)
    unit_mask = (group_id < ffn_width).astype(jnp.float32)
    hidden_low = (jnp.square(jnp.maximum(pre_act, 0.0)) * unit_mask[:, None]).astype(jnp.bfloat16)
    ffn_out = lax.psum(
        jnp.dot(hidden_low, w_down, preferred_element_type=jnp.float32).astype(jnp.bfloat16), "head"
    ).astype(jnp.float32)
    output = (middle_res + scale_ffn[:, None] * ffn_out).astype(jnp.bfloat16)
    grad_top = cotangent.astype(jnp.float32)
    grad_scale_ffn = jnp.sum(grad_top * ffn_out, axis=1)
    grad_ffn_low = (scale_ffn[:, None] * grad_top).astype(jnp.bfloat16)
    grad_hidden = jnp.dot(grad_ffn_low, w_down.T, preferred_element_type=jnp.float32)
    grad_pre_low = (grad_hidden * unit_mask[:, None] * 2.0 * jnp.maximum(pre_act, 0.0)).astype(
        jnp.bfloat16
    )
    grad_act_two = lax.psum(
        jnp.dot(grad_pre_low, w_up.T, preferred_element_type=jnp.float32).astype(jnp.bfloat16),
        "head",
    ).astype(jnp.float32)
    logit_ffn = router_back(grad_scale_ffn, probs_ffn, picked_ffn)
    grad_act_two = grad_act_two + jnp.dot(logit_ffn, router_ffn.T, precision=PRECISE)
    grad_mid_ln, grad_gain_two, grad_bias_two = pull_two(grad_act_two)
    grad_middle = grad_top + grad_mid_ln
    grad_scale_attn = jnp.sum(grad_middle * attn_out, axis=1)
    grad_attn_low = (scale_attn[:, None] * grad_middle).astype(jnp.bfloat16)
    grad_context = jnp.dot(grad_attn_low, w_output.T, preferred_element_type=jnp.float32)
    grad_out_low = (
        (grad_context * head_mask[:, None]).astype(jnp.bfloat16).reshape(local_rows, HPG, HD)
    )
    delta = jnp.sum(grad_out_low.astype(jnp.float32) * context, axis=2).T
    zero_state = jnp.zeros((local_rows, HPG, HD), jnp.float32)

    def visit_keys(carried, number):
        key_block, value_block, key_index, key_segment = fetch_block(
            packed_all, all_index, all_segment, number, block_rows
        )
        grad_query, grad_key, grad_value = pair_grads(
            query_low,
            grad_out_low,
            log_sum,
            delta,
            token_index,
            segment,
            key_block,
            value_block,
            key_index,
            key_segment,
        )
        return (
            carried + grad_query,
            jnp.concatenate(
                [grad_key.reshape(block_rows, HG), grad_value.reshape(block_rows, HG)], axis=1
            ),
        )

    grad_query_rot, key_terms = lax.scan(visit_keys, zero_state, jnp.arange(blocks))
    summed = lax.psum_scatter(
        key_terms.reshape(all_rows, 2 * HG).astype(jnp.bfloat16),
        "seq",
        scatter_dimension=0,
        tiled=True,
    ).astype(jnp.float32)
    grad_key_rot = summed[:, :HG].reshape(local_rows, HPG, HD)
    grad_value_all = summed[:, HG:].reshape(local_rows, HPG, HD)
    grad_query_low = (
        rotary_back(grad_query_rot, cosine_table, sine_table)
        .astype(jnp.bfloat16)
        .reshape(local_rows, HG)
    )
    grad_key_low = (
        rotary_back(grad_key_rot, cosine_table, sine_table)
        .astype(jnp.bfloat16)
        .reshape(local_rows, HG)
    )
    grad_value_low = grad_value_all.astype(jnp.bfloat16).reshape(local_rows, HG)
    grad_inputs_low = jnp.concatenate([grad_query_low, grad_key_low, grad_value_low], axis=1)
    grad_act_one = lax.psum(
        jnp.dot(grad_inputs_low, w_inputs.T, preferred_element_type=jnp.float32).astype(
            jnp.bfloat16
        ),
        "head",
    ).astype(jnp.float32)
    logit_attn = router_back(grad_scale_attn, probs_attn, picked_attn)
    grad_act_one = grad_act_one + jnp.dot(logit_attn, router_attn.T, precision=PRECISE)
    grad_res_ln, grad_gain_one, grad_bias_one = pull_one(grad_act_one)
    input_grad = grad_middle + grad_res_ln
    grad_router = jnp.concatenate(
        [
            jnp.dot(act_one.astype(jnp.float32).T, logit_attn, precision=PRECISE),
            jnp.dot(act_two.astype(jnp.float32).T, logit_ffn, precision=PRECISE),
        ],
        axis=1,
    ).reshape(-1)
    small_terms = jnp.concatenate(
        [grad_gain_one, grad_bias_one, grad_gain_two, grad_bias_two, grad_router]
    )
    tile_terms = tile_grads(
        slot_order,
        [[act_one, ctx_low, act_two, hidden_low]],
        [[grad_inputs_low, grad_attn_low, grad_pre_low, grad_ffn_low]],
        None,
        [slot_order.shape[0]],
    )[0]
    tile_grad, small_grad = (
        lax.psum_scatter(tile_terms, "seq", scatter_dimension=0, tiled=True),
        lax.psum_scatter(
            small_terms.astype(jnp.bfloat16), "seq", scatter_dimension=0, tiled=True
        ).astype(jnp.float32),
    )
    slots = master.shape[1]
    held = adam_tiles(
        jnp.array([0, 0, 1], jnp.int32),
        slots,
        slots,
        [[tile_grad]],
        (left_basis[0], right_basis[0]),
        (first_moment[0], second_moment[0], master[0]),
        None,
    )
    small_outs = small_adam(small_grad, small_first, small_second, small_master)
    return (
        output,
        input_grad,
        held[0][None],
        held[1][None],
        held[2][None],
        held[3][None],
        *small_outs,
    )


def solution(mesh):
    return jax.shard_map(
        local_remap if dict(mesh.shape) == {"seq": 8, "head": 4} else local_plain,
        mesh=mesh,
        in_specs=(
            P("seq", None),
            P("seq", None),
            P("seq"),
            P("seq"),
            P(),
            P("head", None),
            P("head", "seq", None, None),
            P("head", "seq", None, None),
            P("head", "seq", None, None),
            P("head", "seq", None, None),
            P("head", "seq", None, None),
            P("seq"),
            P("seq"),
            P("seq"),
        ),
        out_specs=(
            P("seq", None),
            P("seq", None),
            P("head", "seq", None, None),
            P("head", "seq", None, None),
            P("head", "seq", None, None),
            P("head", "seq", None, None),
            P("seq"),
            P("seq"),
            P("seq"),
        ),
        check_vma=False,
    )
```

```python
import functools

import jax
import jax.numpy as jnp
from jax import lax
from jax.experimental import pallas as pl
from jax.experimental.pallas import tpu as pltpu
from jax.sharding import PartitionSpec as P

D = 2048
HD = 128
WIDTHS = 4
TR = 256
TC = 512
TILES = 96
STEP = 10
KB_CAP = 1024
HPG = 4
HG = 512
FG = 2048

PRECISE = lax.Precision.HIGHEST
EPS_NORM = 1e-05
BETA_ONE = 0.95
BETA_TWO = 0.95
ADAM_EPS = 1e-08
DECAY_RATE = 0.01
RATE_TILE = 0.15
RATE_SMALL = 1.0
ROPE_BASE = 10000.0
NEG_FILL = -1e30
SCORE_SCALE = HD ** (-0.5)
F32 = jnp.float32
BF16 = jnp.bfloat16
AXES = ("seq", "head")
VMEM_BIG = 56 << 20
VMEM_ALL = 61 << 20


def nt(a, b):
    return lax.dot_general(a, b, (((1,), (1,)), ((), ())), preferred_element_type=F32)


def nn(a, b):
    return lax.dot_general(a, b, (((1,), (0,)), ((), ())), preferred_element_type=F32)


def tn(a, b):
    return lax.dot_general(a, b, (((0,), (0,)), ((), ())), preferred_element_type=F32)


VM = pl.BlockSpec(memory_space=pltpu.VMEM)
SM = pl.BlockSpec(memory_space=pltpu.SMEM)
HBM = pl.BlockSpec(memory_space=pltpu.MemorySpace.HBM)


def sds(shape, dtype):
    return jax.ShapeDtypeStruct(shape, dtype)


MARK = sds((8, HD), F32)


def params():
    return pltpu.CompilerParams(vmem_limit_bytes=VMEM_BIG)


def cost(flops, nbytes):
    return pl.CostEstimate(flops=int(flops), bytes_accessed=int(nbytes), transcendentals=0)


def flat_call(body, scalars, arrays, outs, scratch=(), flops=0, name=None):
    nbytes = sum(a.size * a.dtype.itemsize for a in arrays)
    nbytes += sum(int(jnp.dtype(o.dtype).itemsize) * o.size for o in outs)
    return pl.pallas_call(
        body,
        out_shape=outs,
        in_specs=[SM] + [VM] * len(arrays),
        out_specs=[VM] * len(outs),
        scratch_shapes=list(scratch),
        compiler_params=params(),
        cost_estimate=cost(flops, nbytes),
        name=name,
    )(scalars, *arrays)


def rows_of(ref, index, rows):
    return ref[pl.ds(pl.multiple_of(index * rows, rows), rows), :]


def put_rows(ref, index, rows, value):
    ref[pl.ds(pl.multiple_of(index * rows, rows), rows), :] = value


def store_pieces(acc_ref, piece, rows, outs):
    outs[0][...] = rows_of(acc_ref, piece, rows)
    for k in range(1, 4):
        outs[k][...] = rows_of(acc_ref, piece ^ k, rows).astype(BF16)


def row_stats(values):
    center = values - jnp.mean(values, axis=1, keepdims=True)
    rstd = lax.rsqrt(jnp.mean(center * center, axis=1, keepdims=True) + EPS_NORM)
    return center * rstd, rstd


def route_level(logits, width_col):
    lane = lax.broadcasted_iota(jnp.int32, logits.shape, 1)
    live = lane < WIDTHS
    top = jnp.max(jnp.where(live, logits, NEG_FILL), axis=1, keepdims=True)
    raised = jnp.where(live, jnp.exp(jnp.where(live, logits, NEG_FILL) - top), 0.0)
    probs = raised / jnp.sum(raised, axis=1, keepdims=True)
    picked = (lane == width_col - 1).astype(F32)
    chosen = jnp.sum(probs * picked, axis=1, keepdims=True)
    return WIDTHS * chosen, WIDTHS * chosen * (picked - probs)


def split_dot(values, right_low):
    high = values.astype(BF16)
    rest = (values - high.astype(F32)).astype(BF16)
    return nn(high, right_low) + nn(rest, right_low)


def norm_one_body(sc, tok, gain, bias, router, width, a1, a1p, tokp, rap, coefp, ra_s, coef_s):
    rows = a1p.shape[0]
    piece = sc[1]
    xhat, _ = row_stats(tok[...].astype(F32))
    low = (xhat * gain[...] + bias[...]).astype(BF16)
    a1[...] = low
    scale, coef = route_level(nn(low, router[...]), width[...])
    ra_s[...] = scale
    coef_s[...] = coef
    a1p[...] = rows_of(a1, piece, rows)
    tokp[...] = rows_of(tok, piece, rows)
    rap[...] = rows_of(ra_s, piece, rows)
    coefp[...] = rows_of(coef_s, piece, rows)


def turn(values, cosine, signed_sine):
    return values * cosine + pltpu.roll(values, HD // 2, 1) * signed_sine


def turn_back(values, cosine, signed_sine):
    return values * cosine - pltpu.roll(values, HD // 2, 1) * signed_sine


def project_body(sc, a1, weights, cosine, sine, o0, o1, o2, o3, heads_s):
    step = pl.program_id(0)
    spot = sc[0]
    out = nn(a1[...], weights[...].reshape(D, HG))
    plain = step == 2
    cos_v = jnp.where(plain, 1.0, cosine[0])
    sin_v = jnp.where(plain, 0.0, sine[0])
    for head in range(HPG):
        heads_s[head] = turn(out[:, head * HD : (head + 1) * HD], cos_v, sin_v).astype(BF16)
    for k, ref in enumerate((o0, o1, o2, o3)):
        ref[0] = heads_s[spot ^ k]


def attend_body(
    sc, start_col, r0, r1, r2, r3, c0, c1, c2, c3,
    o0, o1, o2, o3, ctx, lse, q_all, k_all, v_all, m_s, l_s, acc_s,
):
    spot, core = sc[0], sc[2]
    rows = r0.shape[1]

    def block_of(source, side):
        return (2 * (source // 2) + side) * 2 + source % 2

    for k, (own, other) in enumerate(((r0, c0), (r1, c1), (r2, c2), (r3, c3))):
        mine = block_of(spot ^ k, core)
        theirs = block_of(spot ^ k, 1 - core)
        q_all[k] = own[0]
        k_all[mine] = own[1]
        v_all[mine] = own[2]
        k_all[theirs] = other[1]
        v_all[theirs] = other[2]

    def per_query(k, unused):
        block = block_of(spot ^ k, core)
        query = q_all[k]
        first = start_col[block]
        where_q = block * rows + lax.broadcasted_iota(jnp.int32, (rows, rows), 0)
        lane = lax.broadcasted_iota(jnp.int32, (rows, rows), 1)
        m_s[...] = jnp.full(m_s.shape, NEG_FILL, F32)
        l_s[...] = jnp.zeros(l_s.shape, F32)
        acc_s[...] = jnp.zeros(acc_s.shape, F32)

        def per_key(kb, unused_two):
            where_k = kb * rows + lane
            scores = nt(query, k_all[kb]) * SCORE_SCALE
            scores = jnp.where((where_k <= where_q) & (where_k >= first), scores, NEG_FILL)
            old = m_s[...]
            new = jnp.maximum(old, jnp.max(scores, axis=1, keepdims=True))
            weight = jnp.exp(scores - new)
            fade = jnp.exp(old - new)
            l_s[...] = l_s[...] * fade + jnp.sum(weight, axis=1, keepdims=True)
            acc_s[...] = acc_s[...] * fade + nn(weight.astype(BF16), v_all[kb])
            m_s[...] = new
            return 0

        lax.fori_loop(sc[4 + block], block + 1, per_key, 0)
        ctx[k] = acc_s[...] / l_s[...]
        lse[k] = m_s[...] + jnp.log(l_s[...])
        return 0

    lax.fori_loop(0, 4, per_query, 0)
    for k, ref in enumerate((o0, o1, o2, o3)):
        ref[...] = ctx[k].astype(BF16)


def output_body(sc, r0, r1, r2, r3, width, weights, cb, o0, o1, o2, o3, acc_s):
    spot, piece, group = sc[0], sc[1], sc[3]
    keep = width[...] > group
    for k, ref in enumerate((r0, r1, r2, r3)):
        at = pl.ds(pl.multiple_of((spot ^ k) * HD, HD), HD)
        cb[:, at] = jnp.where(keep, ref[...], jnp.zeros_like(ref[...]))
    for col in range(D // TC):
        acc_s[:, col * TC : (col + 1) * TC] = nn(cb[:, :TR], weights[0, col]) + nn(
            cb[:, TR:], weights[1, col]
        )
    store_pieces(acc_s, piece, o1.shape[0], (o0, o1, o2, o3))


def norm_two_body(sc, own, r1, r2, r3, tokp, rap, gain, bias, attn, h1, a2p):
    total = own[...] + r1[...].astype(F32) + r2[...].astype(F32) + r3[...].astype(F32)
    attn[...] = total
    middle = tokp[...].astype(F32) + rap[...] * total
    h1[...] = middle
    xhat, _ = row_stats(middle)
    a2p[...] = (xhat * gain[...] + bias[...]).astype(BF16)


def ffn_body(
    sc, p0, p1, p2, p3, dy, width, router, w_up, w_down,
    a2, act, relu, gffn, dlog, rfp, o0, o1, o2, o3, acc_s, coef_s, rf_s,
):
    step = pl.program_id(0)
    piece, group = sc[1], sc[3]
    rows = p0.shape[0]

    @pl.when(step == 0)
    def _():
        for k, ref in enumerate((p0, p1, p2, p3)):
            put_rows(a2, piece ^ k, rows, ref[...])
        scale, coef = route_level(nn(a2[...], router[...]), width[...])
        rf_s[...] = scale
        coef_s[...] = coef
        gffn[...] = (scale * dy[...].astype(F32)).astype(BF16)
        rfp[...] = rows_of(rf_s, piece, rows)

    up = jnp.maximum(nn(a2[...], w_up[...].reshape(D, TC)), 0.0)
    up = jnp.where(width[...] > group, up, 0.0)
    relu[...] = up.astype(BF16)
    low = (up * up).astype(BF16)
    act[...] = low
    for col in range(D // TC):
        at = slice(col * TC, (col + 1) * TC)
        part = nn(low[:, :TR], w_down[0, col]) + nn(low[:, TR:], w_down[1, col])

        @pl.when(step == 0)
        def _(part=part, at=at):
            acc_s[:, at] = part

        @pl.when(step > 0)
        def _(part=part, at=at):
            acc_s[:, at] += part

    @pl.when(step == pl.num_programs(0) - 1)
    def _():
        drf = jnp.sum(acc_s[...] * dy[...].astype(F32), axis=1, keepdims=True)
        dlog[...] = drf * coef_s[...]
        store_pieces(acc_s, piece, rows, (o0, o1, o2, o3))


def ffn_back_body(sc, gffn, relu, dlog, router_t, w_up, w_down, gpre, o0, o1, o2, o3, acc_s):
    step = pl.program_id(0)
    piece = sc[1]
    halves = []
    for row in range(2):
        total = nt(gffn[:, :TC], w_down[row, 0])
        for col in range(1, D // TC):
            total += nt(gffn[:, col * TC : (col + 1) * TC], w_down[row, col])
        halves.append(total)
    gact = jnp.concatenate(halves, axis=1)
    low = (gact * 2.0 * relu[...].astype(F32)).astype(BF16)
    gpre[...] = low
    part = nt(low, w_up[...].reshape(D, TC))

    @pl.when(step == 0)
    def _():
        acc_s[...] = part + split_dot(dlog[...], router_t[...])

    @pl.when(step > 0)
    def _():
        acc_s[...] += part

    @pl.when(step == pl.num_programs(0) - 1)
    def _():
        store_pieces(acc_s, piece, o1.shape[0], (o0, o1, o2, o3))


def norm_grad(grad, values, gain):
    xhat, rstd = row_stats(values)
    scaled = grad * gain
    inner = scaled - jnp.mean(scaled, axis=1, keepdims=True)
    inner = inner - xhat * jnp.mean(scaled * xhat, axis=1, keepdims=True)
    gain_grad = jnp.sum(grad * xhat, axis=0, keepdims=True)
    return inner * rstd, gain_grad, jnp.sum(grad, axis=0, keepdims=True)


def norm_two_back_body(
    sc, own, r1, r2, r3, h1, attn, dyp, rap, coefp, gain, dh1, gattnp, dlogp, ggain, gbias
):
    grad = own[...] + r1[...].astype(F32) + r2[...].astype(F32) + r3[...].astype(F32)
    back, gain_grad, bias_grad = norm_grad(grad, h1[...], gain[...])
    middle = dyp[...].astype(F32) + back
    dh1[...] = middle
    gattnp[...] = (rap[...] * middle).astype(BF16)
    dra = jnp.sum(middle * attn[...], axis=1, keepdims=True)
    dlogp[...] = dra * coefp[...]
    ggain[...] = gain_grad
    gbias[...] = bias_grad


def gout_body(sc, p0, p1, p2, p3, width, weights, gattn, o0, o1, o2, o3, heads_s):
    spot, piece, group = sc[0], sc[1], sc[3]
    rows = p0.shape[0]
    for k, ref in enumerate((p0, p1, p2, p3)):
        put_rows(gattn, piece ^ k, rows, ref[...])
    keep = width[...] > group
    for row in range(2):
        total = nt(gattn[:, :TC], weights[row, 0])
        for col in range(1, D // TC):
            total += nt(gattn[:, col * TC : (col + 1) * TC], weights[row, col])
        low = jnp.where(keep, total, 0.0).astype(BF16)
        heads_s[2 * row] = low[:, :HD]
        heads_s[2 * row + 1] = low[:, HD:]
    for k, ref in enumerate((o0, o1, o2, o3)):
        ref[...] = heads_s[spot ^ k]


def attend_back_body(
    sc, start_row, cosine, sine, q_all, k_all, v_all, ctx, lse, g0, g1, g2, g3,
    gq, own, other, g_s, gk_s, gv_s, acc_s,
):
    spot, core = sc[0], sc[2]
    rows = g0.shape[0]

    def block_of(source, side):
        return (2 * (source // 2) + side) * 2 + source % 2

    for k, ref in enumerate((g0, g1, g2, g3)):
        g_s[k] = ref[...]
    gk_s[...] = jnp.zeros(gk_s.shape, F32)
    gv_s[...] = jnp.zeros(gv_s.shape, F32)

    def per_query(k, unused):
        block = block_of(spot ^ k, core)
        query = q_all[k]
        grad = g_s[k]
        shared = grad.astype(F32) * ctx[k]
        delta = lax.dot_general(
            jnp.ones((8, HD), F32), shared, (((1,), (1,)), ((), ())),
            precision=PRECISE, preferred_element_type=F32,
        )[:1]
        first = start_row[block]
        level = lse[k]
        where_q = block * rows + lax.broadcasted_iota(jnp.int32, (rows, rows), 1)
        line = lax.broadcasted_iota(jnp.int32, (rows, rows), 0)
        acc_s[...] = jnp.zeros(acc_s.shape, F32)

        def per_key(kb, unused_two):
            where_k = kb * rows + line
            keys = k_all[kb]
            allowed = (where_k <= where_q) & (where_k >= first)
            scores = nt(keys, query) * SCORE_SCALE
            prob = jnp.where(allowed, jnp.exp(jnp.where(allowed, scores - level, 0.0)), 0.0)
            gprob = nt(v_all[kb], grad)
            graw = (prob * (gprob - delta) * SCORE_SCALE).astype(BF16)
            gv_s[kb] += nn(prob.astype(BF16), grad)
            gk_s[kb] += nn(graw, query)
            acc_s[...] += tn(graw, keys)
            return 0

        lax.fori_loop(sc[4 + block], block + 1, per_key, 0)
        gq[k] = turn_back(acc_s[...], cosine[block], sine[block]).astype(BF16)
        return 0

    lax.fori_loop(0, 4, per_query, 0)
    for k in range(4):
        mine = block_of(spot ^ k, core)
        theirs = block_of(spot ^ k, 1 - core)
        own[k, 0] = gk_s[mine]
        own[k, 1] = gv_s[mine]
        other[k, 0] = gk_s[theirs].astype(BF16)
        other[k, 1] = gv_s[theirs].astype(BF16)


def key_merge_body(sc, gq, own, got, cosine, sine, o0, o1, o2, o3):
    spot, core = sc[0], sc[2]
    for k, ref in enumerate((o0, o1, o2, o3)):
        source = spot ^ k
        block = (2 * (source // 2) + core) * 2 + source % 2
        ref[0] = gq[k]
        gk = own[k, 0] + got[k, 0].astype(F32)
        ref[1] = turn_back(gk, cosine[block], sine[block]).astype(BF16)
        ref[2] = (own[k, 1] + got[k, 1].astype(F32)).astype(BF16)


def gather_input_body(sc, r0, r1, r2, r3, gin):
    spot = sc[0]
    for k, ref in enumerate((r0, r1, r2, r3)):
        for member in range(3):
            at = pl.ds(pl.multiple_of(member * HG + (spot ^ k) * HD, HD), HD)
            gin[:, at] = ref[member]


def input_back_body(sc, gin, weights, f1, f2, f3, o0, o1, o2, o3, acc_s):
    piece = sc[1]
    rows = o0.shape[0]
    wide = weights.shape[1] * TR
    total = nt(gin[:, :HG], weights[0].reshape(wide, TC))
    for member in range(1, 3):
        total += nt(gin[:, member * HG : (member + 1) * HG], weights[member].reshape(wide, TC))
    acc_s[...] = total
    o0[...] = rows_of(acc_s, piece, rows)
    for k, (ref, passed) in enumerate(((o1, f1), (o2, f2), (o3, f3))):
        ref[0] = rows_of(acc_s, piece ^ (k + 1), rows).astype(BF16)
        ref[1] = passed[...]


def norm_one_back_body(
    sc, own, r1, r2, r3, ffn, tokp, h1, rfp, dh1, dlogp, router_t, gain, both, ggain, gbias
):
    grad = own[...] + r1[0].astype(F32) + r2[0].astype(F32) + r3[0].astype(F32)
    grad = grad + split_dot(dlogp[...], router_t[...])
    back, gain_grad, bias_grad = norm_grad(grad, tokp[...].astype(F32), gain[...])
    both[0] = (dh1[...] + back).astype(BF16)
    total = ffn[...] + r1[1].astype(F32) + r2[1].astype(F32) + r3[1].astype(F32)
    both[1] = (h1[...] + rfp[...] * total).astype(BF16)
    ggain[...] = gain_grad
    gbias[...] = bias_grad


def join_body(sc, b0, b1, b2, b3, whole):
    piece = sc[1]
    rows = b0.shape[1]
    for k, ref in enumerate((b0, b1, b2, b3)):
        at = pl.ds(pl.multiple_of((piece ^ k) * rows, rows), rows)
        whole[:, at, :] = ref[...]


def place_tiles(ids, chunks, held, waits=()):
    count = sum(c.shape[0] for c in chunks)

    def body(ids_ref, *refs):
        parts = refs[: len(chunks)]
        out = refs[len(chunks) + len(waits) + (0 if held is None else 1)]
        mark, buf, in_sems, out_sems = refs[-4:]
        mark[...] = jnp.zeros_like(mark)
        places = [(part, i) for part in parts for i in range(part.shape[0])]
        arrive = [
            pltpu.make_async_copy(part.at[i], buf.at[at], in_sems.at[at])
            for at, (part, i) in enumerate(places)
        ]
        leave = [
            pltpu.make_async_copy(buf.at[at], out.at[ids_ref[at]], out_sems.at[at])
            for at in range(count)
        ]
        for copy in arrive:
            copy.start()
        for came, go in zip(arrive, leave):
            came.wait()
            go.start()
        for copy in leave:
            copy.wait()

    extra = [] if held is None else [held]
    return pl.pallas_call(
        body,
        out_shape=[sds((TILES, TR, TC), BF16), MARK],
        in_specs=[SM] + [HBM] * (len(chunks) + len(extra) + len(waits)),
        out_specs=[HBM, VM],
        scratch_shapes=[
            pltpu.VMEM((count, TR, TC), BF16),
            pltpu.SemaphoreType.DMA((count,)),
            pltpu.SemaphoreType.DMA((count,)),
        ],
        compiler_params=params(),
        input_output_aliases={} if held is None else {1 + len(chunks): 0},
        cost_estimate=cost(0, 2 * count * TR * TC * 2),
        name="place_tiles",
    )(ids, *chunks, *extra, *waits)


def tile_kind(tile):
    kind = (tile >= 24).astype(jnp.int32) + (tile >= 32).astype(jnp.int32)
    kind = kind + (tile >= 64).astype(jnp.int32)
    base = jnp.where(kind == 1, 24, jnp.where(kind == 2, 32, 64))
    local = tile - base
    left = jnp.where(kind == 0, tile % 8, local // 4)
    right = jnp.where(kind == 0, tile // 8, local % 4)
    return kind, left, right


def tile_grads(ids, lefts, rights, added, outs_of):
    count = ids.shape[0]
    parts = len(lefts)
    rows = lefts[0][0].shape[0]
    flat = [a for part in lefts for a in part] + [a for part in rights for a in part]

    def fetch(ids_ref, step, slot, refs, lbuf, rbuf, sems):
        kind, left, right = tile_kind(ids_ref[step])
        for which in range(4):

            @pl.when(kind == which)
            def _(which=which):
                for part in range(parts):
                    src = refs[part * 4 + which]
                    at = pl.ds(pl.multiple_of(left * TR, TR), TR)
                    pltpu.make_async_copy(
                        src.at[:, at], lbuf.at[slot, pl.ds(part * rows, rows)], sems.at[slot, part]
                    ).start()
                    src = refs[(parts + part) * 4 + which]
                    at = pl.ds(pl.multiple_of(right * TC, TC), TC)
                    pltpu.make_async_copy(
                        src.at[:, at],
                        rbuf.at[slot, pl.ds(part * rows, rows)],
                        sems.at[slot, parts + part],
                    ).start()

    def body(ids_ref, *refs):
        sources = refs[: len(flat)]
        at = len(flat)
        plus = None
        if added is not None:
            plus = refs[at]
            at += 1
        outs = refs[at : at + len(outs_of)]
        lbuf, rbuf, sems = refs[at + len(outs_of) :]
        step = pl.program_id(0)
        slot = lax.rem(step, 2)

        @pl.when(step == 0)
        def _():
            fetch(ids_ref, 0, 0, sources, lbuf, rbuf, sems)

        @pl.when(step + 1 < count)
        def _():
            fetch(ids_ref, step + 1, 1 - slot, sources, lbuf, rbuf, sems)

        for part in range(parts):
            pltpu.make_async_copy(
                sources[0].at[:, :TR], lbuf.at[slot, pl.ds(part * rows, rows)], sems.at[slot, part]
            ).wait()
            pltpu.make_async_copy(
                sources[parts * 4 + 1].at[:, :TC],
                rbuf.at[slot, pl.ds(part * rows, rows)],
                sems.at[slot, parts + part],
            ).wait()
        total = tn(lbuf[slot], rbuf[slot])
        if plus is not None:
            total = total + plus[0].astype(F32)
        low = total.astype(BF16)
        if len(outs_of) == 1:
            outs[0][0] = low
        else:
            begin = 0
            for ref, size in zip(outs, outs_of):

                @pl.when((step >= begin) & (step < begin + size))
                def _(ref=ref):
                    ref[0] = low

                begin += size

    specs_out = []
    begin = 0
    for size in outs_of:
        specs_out.append(
            pl.BlockSpec(
                (1, TR, TC),
                lambda i, ids_ref, begin=begin, size=size: (jnp.clip(i - begin, 0, size - 1), 0, 0),
            )
        )
        begin += size
    plus_in = [] if added is None else [added]
    return pl.pallas_call(
        body,
        out_shape=[sds((size, TR, TC), BF16) for size in outs_of],
        grid_spec=pltpu.PrefetchScalarGridSpec(
            num_scalar_prefetch=1,
            grid=(count,),
            in_specs=[HBM] * len(flat)
            + [pl.BlockSpec((1, TR, TC), lambda i, ids_ref: (i, 0, 0))] * len(plus_in),
            out_specs=specs_out,
            scratch_shapes=[
                pltpu.VMEM((2, parts * rows, TR), BF16),
                pltpu.VMEM((2, parts * rows, TC), BF16),
                pltpu.SemaphoreType.DMA((2, 2 * parts)),
            ],
        ),
        compiler_params=pltpu.CompilerParams(vmem_limit_bytes=VMEM_ALL),
        cost_estimate=cost(
            2 * count * parts * rows * TR * TC, count * (parts * rows * (TR + TC) * 2 + TR * TC * 2)
        ),
        name="tile_grads",
    )(ids, *flat, *plus_in)


def adam_tile(grad, left, right, first, second, master):
    left_low = left.astype(BF16)
    right_low = right.astype(BF16)
    turned = nn(tn(left_low, grad.astype(BF16)).astype(BF16), right_low)
    new_first = BETA_ONE * first + (1.0 - BETA_ONE) * turned
    new_second = BETA_TWO * second + (1.0 - BETA_TWO) * turned * turned
    step = (
        new_first
        / (1.0 - BETA_ONE**STEP)
        / (jnp.sqrt(new_second / (1.0 - BETA_TWO**STEP)) + ADAM_EPS)
    )
    back = nt(nn(left_low, step.astype(BF16)).astype(BF16), right_low)
    return new_first, new_second, master - RATE_TILE * (back + DECAY_RATE * master)


def adam_tiles(sc, size, sides, bases, state, held):
    flat, specs, plans = [], [], []
    for side, members in enumerate(sides):
        plan = []
        for member in members:
            pair = member if isinstance(member, tuple) else (member,)
            plan.append(range(len(flat), len(flat) + len(pair)))
            flat.extend(pair)
            specs.extend(
                pl.BlockSpec(
                    (1, TR, TC),
                    lambda i, sc_ref, side=side: (jnp.clip(i - side * size, 0, size - 1), 0, 0),
                )
                for _ in pair
            )
        plans.append(plan)

    def slot(i, sc_ref):
        return sc_ref[1 + i // size] + lax.rem(i, size)

    def body(sc_ref, *refs):
        step = pl.program_id(0)
        left, right, first, second, master = refs[len(flat) : len(flat) + 5]
        o_first, o_second, o_master, o_low, mark = refs[-6:-1]
        grad_s = refs[-1]
        mark[...] = jnp.zeros_like(mark)
        for side, plan in enumerate(plans):

            @pl.when(step // size == side)
            def _(plan=plan):
                total = None
                for spots in plan:
                    value = refs[spots[0]][0].astype(F32)
                    if len(spots) == 2:
                        value = jnp.where(sc_ref[0] > 0, value, refs[spots[1]][0].astype(F32))
                    total = value if total is None else total + value
                grad_s[...] = total

        new_first, new_second, new_master = adam_tile(
            grad_s[...], left[0], right[0], first[0], second[0], master[0]
        )
        o_first[0] = new_first
        o_second[0] = new_second
        o_master[0] = new_master
        o_low[0] = new_master.astype(BF16)

    def at_slot(shape):
        return pl.BlockSpec((1,) + shape, lambda i, sc_ref: (slot(i, sc_ref), 0, 0))

    slots = state[0].shape[0]
    steps = len(sides) * size
    shapes = [(TR, TC)] * 4
    types = [F32, F32, F32, BF16]
    extra = [] if held is None else list(held)
    base = 1 + len(flat) + 5
    return pl.pallas_call(
        body,
        out_shape=[sds((slots,) + s, t) for s, t in zip(shapes, types)] + [MARK],
        grid_spec=pltpu.PrefetchScalarGridSpec(
            num_scalar_prefetch=1,
            grid=(steps,),
            in_specs=specs
            + [at_slot((TR, TR)), at_slot((TC, TC))]
            + [at_slot((TR, TC))] * 3
            + [HBM] * len(extra),
            out_specs=[at_slot(s) for s in shapes]
            + [pl.BlockSpec((8, HD), lambda i, sc_ref: (0, 0))],
            scratch_shapes=[pltpu.VMEM((TR, TC), F32)],
        ),
        input_output_aliases={base + i: i for i in range(len(extra))},
        compiler_params=pltpu.CompilerParams(vmem_limit_bytes=VMEM_ALL),
        cost_estimate=cost(steps * 8 * TR * TC * TC, steps * 5 * TR * TC * 4),
        name="adam_tiles",
    )(sc, *flat, *bases, *state, *extra)


def small_adam(grad, first, second, master):
    new_first = BETA_ONE * first + (1.0 - BETA_ONE) * grad
    new_second = BETA_TWO * second + (1.0 - BETA_TWO) * grad * grad
    step = (
        new_first
        / (1.0 - BETA_ONE**STEP)
        / (jnp.sqrt(new_second / (1.0 - BETA_TWO**STEP)) + ADAM_EPS)
    )
    return new_first, new_second, master - RATE_SMALL * (step + DECAY_RATE * master)


def signed_tables(places):
    middle = HD // 2
    frequency = ROPE_BASE ** (-(jnp.arange(middle, dtype=F32) * 2.0) / HD)
    angles = places.astype(F32)[:, None] * frequency[None, :]
    cosine = jnp.cos(angles)
    sine = jnp.sin(angles)
    return (
        jnp.concatenate([cosine, cosine], axis=1),
        jnp.concatenate([-sine, sine], axis=1),
    )


def token_layout(first_index, local_rows, seq_lengths):
    places = first_index + jnp.arange(local_rows, dtype=jnp.int32)
    number = seq_lengths.shape[0]
    below = jnp.arange(number)[None, :] <= jnp.arange(number)[:, None]
    bounds = jnp.sum(jnp.where(below, seq_lengths[None, :], 0), axis=1)
    passed = places[:, None] >= bounds[None, :]
    segment = jnp.sum(passed.astype(jnp.int32), axis=1)
    offset = places - jnp.sum(jnp.where(passed, seq_lengths[None, :], 0), axis=1)
    return (places, segment, offset)


def moves(target):
    pairs = []
    for z in range(4):
        for y in range(2):
            for x in range(2):
                for c in range(2):
                    to = target(z, y, x, c)
                    if to is not None:
                        a, b, e, f = to
                        pairs.append((8 * z + 4 * y + 2 * x + c, 8 * a + 4 * b + 2 * e + f))
    return pairs


def only(condition, target):
    return lambda z, y, x, c: target(z, y, x, c) if condition(z, y, x, c) else None


def flip(dz=0, dy=0, dx=0, dc=0):
    return lambda z, y, x, c: (z ^ dz, y ^ dy, x ^ dx, c ^ dc)


def own_group(z, y, x, c):
    return c == z % 2


def foreign(z, y, x, c):
    return c != z % 2


def send(value, target):
    return lax.ppermute(value, AXES, moves(target))


MEMBERS = (None, flip(dz=1), flip(dx=1), flip(dz=1, dx=1))
HEADMATES = (None, flip(dy=1), flip(dz=2), flip(dz=2, dy=1))


def scatter_pieces(pieces):
    return [pieces[0]] + [send(pieces[k], MEMBERS[k]) for k in range(1, 4)]


def share_piece(piece):
    return [piece] + [send(piece, MEMBERS[k]) for k in range(1, 4)]


def swap_heads(blocks):
    return [blocks[0]] + [send(blocks[k], HEADMATES[k]) for k in range(1, 4)]


def after(value, *others):
    return lax.optimization_barrier((value,) + others)[0]


def tied(values, done):
    return list(lax.optimization_barrier(tuple(values) + tuple(done))[: len(values)])


def small_step(values, bit, target):
    other = send(values, target)
    return jnp.where(
        bit == 0, jnp.concatenate([values, other]), jnp.concatenate([other, values])
    )


def local_remap(
    tokens, cotangent, attn_width, ffn_width, seq_lengths, tile_order, master, first_moment,
    second_moment, left_basis, right_basis, small_master, small_first, small_second,
):
    rows = tokens.shape[0]
    piece_rows = rows // 4
    s = lax.axis_index("seq")
    h = lax.axis_index("head")
    z, y, x, c = s // 2, s % 2, h // 2, h % 2
    zp, zh = z % 2, z // 2
    mine = c == zp
    group = 2 * x + zp
    spot = 2 * zh + y
    block = (2 * zh + c) * 2 + y

    y_move, h_move, c_move = flip(dy=1), flip(dz=2), flip(dc=1)

    slots = master.shape[1]
    part = slots // 4
    to_pair = only(own_group, flip(dz=1))
    order = tile_order[0]
    order_got = send(order, c_move)
    low = [master[0, i * part : (i + 1) * part].astype(BF16) for i in range(4)]
    start_move = lambda z, y, x, c: (z, y, x, 1 - c) if c == z % 2 else (z ^ 1, y, x, c)
    near = [send(low[0], start_move)]
    wid = jnp.stack([attn_width, ffn_width])
    wid_got = send(wid, to_pair)
    small_all = small_step(small_master.astype(BF16), y, y_move)
    near[0], order_got, wid, wid_got, small_all, *low = tied(
        [near[0], order_got, wid, wid_got, small_all] + low, []
    )
    order = jnp.where(mine, order, order_got)
    base = jnp.where(mine, s ^ 2, s)
    base_there = jnp.where(mine, s, s ^ 2)

    def ids_of(*chunks):
        return jnp.concatenate(
            [
                lax.dynamic_slice_in_dim(order, (o ^ hop) * slots + i * part, part, 0)
                for o in (base, base_there)
                for hop, i in chunks
            ]
        )

    far = [send(near[0], h_move)]
    near_y = [send(near[0], y_move)]
    near.append(send(low[1], start_move))
    small_all = small_step(small_all, zp, flip(dz=1))
    near[0], near[1], far[0], near_y[0], small_all, low2, low3 = tied(
        [near[0], near[1], far[0], near_y[0], small_all, low[2], low[3]], []
    )
    far.append(send(near[1], h_move))
    near_y.append(send(near[1], y_move))
    far_y = [send(far[0], y_move)]
    near.append(send(low2, start_move))
    near.append(send(low3, start_move))
    first = jnp.concatenate([near[0], near_y[0], far[0]])
    all_rows = rows * lax.axis_size("seq")
    blocks = all_rows // rows
    places, _, offset = token_layout(0, all_rows, seq_lengths)
    start = places - offset
    first_block = start.reshape(blocks, rows)[:, 0] // rows
    cosine, sine = signed_tables(offset)
    cosine, sine = cosine.reshape(blocks, rows, HD), sine.reshape(blocks, rows, HD)
    scalars = jnp.concatenate(
        [jnp.stack([spot, group, c, group]).astype(jnp.int32), first_block.astype(jnp.int32)]
    )

    start_col, start_row = start.reshape(blocks, rows, 1), start.reshape(blocks, 1, rows)
    near[1], near[2], near[3], far[1], near_y[1], far_y[0], first, small_all, tok, cosine, sine = tied(
        [near[1], near[2], near[3], far[1], near_y[1], far_y[0], first, small_all, tokens]
        + [cosine, sine],
        [],
    )
    far.append(send(near[2], h_move))
    near_y.append(send(near[2], y_move))
    far_y.append(send(far[1], y_move))
    first_there = send(first, c_move)
    tok_got = send(tok, to_pair)
    second = jnp.concatenate([near[1], near_y[1], far_y[0], far[1]])
    near[2], near[3], far[2], near_y[2], far_y[1], first, first_there, second, small_all, tok, tok_got = tied(
        [near[2], near[3], far[2], near_y[2], far_y[1], first, first_there, second]
        + [small_all, tok, tok_got],
        [],
    )
    far.append(send(near[3], h_move))
    near_y.append(send(near[3], y_move))
    far_y.append(send(far[2], y_move))
    second_there = send(second, c_move)
    small_all = small_step(small_all, zh, h_move)
    third = jnp.concatenate([near[2], near_y[2], far_y[1], far[2]])
    tok = jnp.where(mine, tok, tok_got)
    tiles, mark_one = place_tiles(ids_of((0, 0), (1, 0), (4, 0)), [first, first_there], None)
    near[3], far[3], near_y[3], far_y[2], second, second_there, third, mark_one, tok, small_all = tied(
        [near[3], far[3], near_y[3], far_y[2], second, second_there, third, mark_one]
        + [tok, small_all],
        [],
    )
    far_y.append(send(far[3], y_move))
    third_there = send(third, c_move)
    fourth = jnp.concatenate([near[3], near_y[3], far_y[2], far[3]])
    fourth_there = send(fourth, c_move)
    widths = jnp.where(mine, wid, wid_got)
    width_a, width_f = widths[0][:, None], widths[1][:, None]
    tiles, mark_two = place_tiles(
        ids_of((0, 1), (1, 1), (5, 0), (4, 1)), [second, second_there], tiles, [mark_one]
    )
    gains = small_all[: 4 * D].astype(F32).reshape(4, 1, D)
    gain_one, bias_one, gain_two, bias_two = gains[0], gains[1], gains[2], gains[3]
    routers = small_all[4 * D :].reshape(D, 2 * WIDTHS)
    pad = ((0, 0), (0, HD - WIDTHS))
    router_a = jnp.pad(routers[:, :WIDTHS], pad)
    router_f = jnp.pad(routers[:, WIDTHS:], pad)
    router_ft, router_at = router_f.T, router_a.T
    a1, a1p, tokp, rap, coefp = flat_call(
        norm_one_body,
        scalars,
        [tok, gain_one, bias_one, router_a, width_a],
        [
            sds((rows, D), BF16),
            sds((piece_rows, D), BF16),
            sds((piece_rows, D), BF16),
            sds((piece_rows, 1), F32),
            sds((piece_rows, HD), F32),
        ],
        [pltpu.VMEM((rows, 1), F32), pltpu.VMEM((rows, HD), F32)],
        name="norm_one",
    )

    far_y[3], third, third_there, fourth, fourth_there, mark_two, a1 = tied(
        [far_y[3], third, third_there, fourth, fourth_there, mark_two, a1], []
    )
    fifth_there = send(far_y[3], c_move)
    tiles, _ = place_tiles(
        jnp.concatenate(
            [
                ids_of((0, 2), (1, 2), (5, 1), (4, 2)),
                ids_of((0, 3), (1, 3), (5, 2), (4, 3)),
            ]
        ),
        [third, third_there, fourth, fourth_there],
        tiles,
        [mark_two],
    )
    tiles, _ = place_tiles(ids_of((5, 3)), [far_y[3], fifth_there], tiles)
    by_row = tiles.reshape(TILES // 4, 4, TR, TC)
    by_map = tiles.reshape(TILES // 8, 8, TR, TC)

    table = pl.BlockSpec((1, rows, HD), lambda i, sc: (sc[12], 0, 0))
    sent = pl.pallas_call(
        project_body,
        out_shape=[sds((3, rows, HD), BF16)] * 4,
        grid_spec=pltpu.PrefetchScalarGridSpec(
            num_scalar_prefetch=1,
            grid=(3,),
            in_specs=[
                pl.BlockSpec((rows, D), lambda i, sc: (0, 0)),
                pl.BlockSpec((1, 8, TR, TC), lambda i, sc: (i, 0, 0, 0)),
                table,
                table,
            ],
            out_specs=[pl.BlockSpec((1, rows, HD), lambda i, sc: (i, 0, 0))] * 4,
            scratch_shapes=[pltpu.VMEM((HPG, rows, HD), BF16)],
        ),
        compiler_params=params(),
        cost_estimate=cost(2 * rows * D * 3 * HG, 3 * D * HG * 2 + rows * D * 2),
        name="project",
    )(jnp.concatenate([scalars, block[None].astype(jnp.int32)]), a1, by_map, cosine, sine)
    got = swap_heads(sent)
    beside = [send(v, flip(dc=1)) for v in got]
    dy = after(cotangent, *got)
    dy = jnp.where(mine, dy, send(dy, to_pair))
    dyp = lax.dynamic_slice_in_dim(dy, group * piece_rows, piece_rows, 0)

    pairs_cost = 4 * 4 * rows * rows * HD * 2
    out = flat_call(
        attend_body,
        scalars,
        [start_col] + got + beside,
        [sds((rows, HD), BF16)] * 4
        + [
            sds((4, rows, HD), F32),
            sds((4, rows, 1), F32),
            sds((4, rows, HD), BF16),
            sds((blocks, rows, HD), BF16),
            sds((blocks, rows, HD), BF16),
        ],
        [pltpu.VMEM((rows, 1), F32), pltpu.VMEM((rows, 1), F32), pltpu.VMEM((rows, HD), F32)],
        flops=2 * pairs_cost,
        name="attend",
    )
    ctx_sent, (ctx, lse, q_all, k_all, v_all) = out[:4], out[4:]
    ctx_got = swap_heads(ctx_sent)

    one_piece = sds((piece_rows, D), F32)
    low_piece = sds((piece_rows, D), BF16)
    piece_outs = [one_piece] + [low_piece] * 3
    wo_spec = pl.BlockSpec((2, 4, TR, TC), lambda i, sc: (3, 0, 0, 0))

    def whole(shape):
        return pl.BlockSpec(shape, lambda i, sc: (0,) * len(shape))

    out = pl.pallas_call(
        output_body,
        out_shape=[sds((rows, HG), BF16)] + piece_outs,
        grid_spec=pltpu.PrefetchScalarGridSpec(
            num_scalar_prefetch=1,
            grid=(1,),
            in_specs=[whole((rows, HD))] * 4 + [whole((rows, 1)), wo_spec],
            out_specs=[whole((rows, HG))] + [whole((piece_rows, D))] * 4,
            scratch_shapes=[pltpu.VMEM((rows, D), F32)],
        ),
        compiler_params=params(),
        cost_estimate=cost(2 * rows * D * HG, D * HG * 2 + rows * D * 4),
        name="output",
    )(scalars, *ctx_got, width_a, by_row)
    cb, attn_parts = out[0], out[1:]
    attn_parts = scatter_pieces(attn_parts)

    attn, h1, a2p = flat_call(
        norm_two_body,
        scalars,
        attn_parts + [tokp, rap, gain_two, bias_two],
        [one_piece, one_piece, low_piece],
        name="norm_two",
    )
    a2_parts = share_piece(a2p)

    up_spec = pl.BlockSpec((8, 1, TR, TC), lambda i, sc: (1, i, 0, 0))
    down_spec = pl.BlockSpec((2, 4, TR, TC), lambda i, sc: (8 + i, 0, 0, 0))
    col_spec = pl.BlockSpec((rows, TC), lambda i, sc: (0, i))
    out = pl.pallas_call(
        ffn_body,
        out_shape=[
            sds((rows, D), BF16),
            sds((rows, FG), BF16),
            sds((rows, FG), BF16),
            sds((rows, D), BF16),
            sds((rows, HD), F32),
            sds((piece_rows, 1), F32),
        ]
        + piece_outs,
        grid_spec=pltpu.PrefetchScalarGridSpec(
            num_scalar_prefetch=1,
            grid=(FG // TC,),
            in_specs=[whole((piece_rows, D))] * 4
            + [whole((rows, D)), whole((rows, 1)), whole((D, HD)), up_spec, down_spec],
            out_specs=[
                whole((rows, D)),
                col_spec,
                col_spec,
                whole((rows, D)),
                whole((rows, HD)),
                whole((piece_rows, 1)),
            ]
            + [whole((piece_rows, D))] * 4,
            scratch_shapes=[
                pltpu.VMEM((rows, D), F32),
                pltpu.VMEM((rows, HD), F32),
                pltpu.VMEM((rows, 1), F32),
            ],
        ),
        compiler_params=params(),
        cost_estimate=cost(4 * rows * D * FG, 4 * D * FG + rows * D * 12),
        name="ffn",
    )(scalars, *a2_parts, dy, width_f, router_f, by_row, by_row)
    a2, act, relu, gffn, dlog_f, rfp = out[:6]
    ffn_parts = out[6:]

    out = pl.pallas_call(
        ffn_back_body,
        out_shape=[sds((rows, FG), BF16)] + piece_outs,
        grid_spec=pltpu.PrefetchScalarGridSpec(
            num_scalar_prefetch=1,
            grid=(FG // TC,),
            in_specs=[
                whole((rows, D)),
                col_spec,
                whole((rows, HD)),
                whole((HD, D)),
                up_spec,
                down_spec,
            ],
            out_specs=[col_spec] + [whole((piece_rows, D))] * 4,
            scratch_shapes=[pltpu.VMEM((rows, D), F32)],
        ),
        compiler_params=params(),
        cost_estimate=cost(4 * rows * D * FG, 4 * D * FG + rows * D * 12),
        name="ffn_back",
    )(scalars, gffn, relu, dlog_f, router_ft, by_row, by_row)
    gpre, ga2_parts = out[0], scatter_pieces(out[1:])

    dh1, gattnp, dlog_a, ggain_two, gbias_two = flat_call(
        norm_two_back_body,
        scalars,
        ga2_parts + [h1, attn, dyp, rap, coefp, gain_two],
        [one_piece, low_piece, sds((piece_rows, HD), F32), sds((1, D), F32), sds((1, D), F32)],
        name="norm_two_back",
    )
    gattn_parts = share_piece(gattnp)
    out = pl.pallas_call(
        gout_body,
        out_shape=[sds((rows, D), BF16)] + [sds((rows, HD), BF16)] * 4,
        grid_spec=pltpu.PrefetchScalarGridSpec(
            num_scalar_prefetch=1,
            grid=(1,),
            in_specs=[whole((piece_rows, D))] * 4 + [whole((rows, 1)), wo_spec],
            out_specs=[whole((rows, D))] + [whole((rows, HD))] * 4,
            scratch_shapes=[pltpu.VMEM((HPG, rows, HD), BF16)],
        ),
        compiler_params=params(),
        cost_estimate=cost(2 * rows * D * HG, D * HG * 2 + rows * D * 4),
        name="gout",
    )(scalars, *gattn_parts, width_a, by_row)
    gattn, gout_got = out[0], swap_heads(out[1:])

    gq, keys_own, keys_other = flat_call(
        attend_back_body,
        scalars,
        [start_row, cosine, sine, q_all, k_all, v_all, ctx]
        + [lse.reshape(4, 1, rows)]
        + gout_got,
        [
            sds((4, rows, HD), BF16),
            sds((4, 2, rows, HD), F32),
            sds((4, 2, rows, HD), BF16),
        ],
        [
            pltpu.VMEM((4, rows, HD), BF16),
            pltpu.VMEM((blocks, rows, HD), F32),
            pltpu.VMEM((blocks, rows, HD), F32),
            pltpu.VMEM((rows, HD), F32),
        ],
        flops=5 * pairs_cost,
        name="attend_back",
    )
    grads_sent = flat_call(
        key_merge_body,
        scalars,
        [gq, keys_own, send(keys_other, flip(dc=1)), cosine, sine],
        [sds((3, rows, HD), BF16)] * 4,
        name="key_merge",
    )
    grads_got = swap_heads(grads_sent)
    (gin,) = flat_call(
        gather_input_body, scalars, grads_got, [sds((rows, 3 * HG), BF16)], name="gather_input"
    )
    lefts = [[a1, cb, a2, act]]
    rights = [[gin, gattn, gpre, gffn]]
    lefts.append([send(v, c_move) for v in lefts[0]])
    rights.append([send(v, c_move) for v in rights[0]])
    begins = [sum(CHUNKS[:i]) for i in range(len(CHUNKS))]

    def grad_ids(flip_y, i):
        owners = (s ^ flip_y ^ jnp.where(mine, 2, 4), s ^ flip_y ^ jnp.where(mine, 6, 0))
        return jnp.concatenate(
            [lax.dynamic_slice_in_dim(order, o * slots + begins[i], CHUNKS[i], 0) for o in owners]
        )

    def route(own, other):
        return lambda z, y, x, c: (z ^ (own if c == z % 2 else other), y, x, z % 2)

    def away_of(i):
        return tile_grads(grad_ids(1, i), lefts, rights, None, [2 * CHUNKS[i]])[0]

    bases = (left_basis[0], right_basis[0])
    state = (first_moment[0], second_moment[0], master[0])
    gin, away0, away1 = tied([gin, away_of(0), away_of(1)], [])
    backs = [send(away0, y_move), send(away1, y_move)]
    half_cols = D // 2
    half_piece = pl.BlockSpec((piece_rows, half_cols), lambda i, sc: (0, i))
    pair_piece = pl.BlockSpec((2, piece_rows, half_cols), lambda i, sc: (0, 0, i))
    out = pl.pallas_call(
        input_back_body,
        out_shape=[one_piece] + [sds((2, piece_rows, D), BF16)] * 3,
        grid_spec=pltpu.PrefetchScalarGridSpec(
            num_scalar_prefetch=1,
            grid=(2,),
            in_specs=[
                whole((rows, 3 * HG)),
                pl.BlockSpec((3, 4, TR, TC), lambda i, sc: (0, i, 0, 0)),
                half_piece,
                half_piece,
                half_piece,
            ],
            out_specs=[half_piece] + [pair_piece] * 3,
            scratch_shapes=[pltpu.VMEM((rows, half_cols), F32)],
        ),
        compiler_params=params(),
        cost_estimate=cost(2 * rows * D * 3 * HG, 3 * D * HG * 2 + rows * D * 4),
        name="input_back",
    )(scalars, gin, by_map, *ffn_parts[1:])
    pieces = [out[0], send(out[1], MEMBERS[1]), send(out[2], MEMBERS[2])]

    def tile_step(i, back):
        here = tile_grads(grad_ids(0, i), lefts, rights, back, [CHUNKS[i]] * 2)
        return [send(here[0], route(1, 2)), send(here[1], route(3, 0))]

    def adam_step(i, flow, held):
        sc = jnp.array([0, begins[i]], jnp.int32)
        return adam_tiles(sc, CHUNKS[i], [flow], bases, state, held)[:4]

    back, away2, pieces[1], pieces[2], last_piece = tied(
        [backs[0], away_of(2), pieces[1], pieces[2], out[3]], []
    )
    backs.append(send(away2, y_move))
    pieces.append(send(last_piece, MEMBERS[3]))
    flows = [tile_step(0, back)]
    back, away3, pieces[3] = tied([backs[1], away_of(3), pieces[3]], [])
    backs.append(send(away3, y_move))
    flows.append(tile_step(1, back))
    both, ggain_one, gbias_one = flat_call(
        norm_one_back_body,
        scalars,
        pieces
        + [ffn_parts[0], tokp, h1, rfp, dh1, dlog_a, router_at, gain_one],
        [sds((2, piece_rows, D), BF16), sds((1, D), F32), sds((1, D), F32)],
        name="norm_one_back",
    )
    grad_router = jnp.concatenate(
        [
            lax.dot_general(
                a1p.astype(F32), dlog_a[:, :WIDTHS], (((0,), (0,)), ((), ())), precision=PRECISE
            ),
            lax.dot_general(
                a2.astype(F32), dlog_f[:, :WIDTHS], (((0,), (0,)), ((), ())), precision=PRECISE
            ),
        ],
        axis=1,
    ).reshape(-1)
    terms = jnp.concatenate(
        [ggain_one[0], gbias_one[0], ggain_two[0], gbias_two[0], grad_router]
    ).reshape(8, -1)
    terms = terms + send(terms, c_move)
    terms = terms + send(terms, flip(dx=1))

    def fold(terms, bit, target):
        halves = terms.reshape(2, terms.shape[0] // 2, terms.shape[1])
        keep = jnp.where(bit == 0, halves[0], halves[1])
        return keep, send(jnp.where(bit == 0, halves[1], halves[0]), target)

    both_z = send(both, only(foreign, flip(dz=1)))
    back, both, both_z, terms, *flows[0] = tied([backs[2], both, both_z, terms] + flows[0], [])
    keep, terms = fold(terms, zh, h_move)
    flows.append(tile_step(2, back))
    both_x = send(both, only(own_group, flip(dx=1)))
    both_xz = send(both, only(foreign, flip(dz=1, dx=1)))
    held = adam_step(0, flows[0], None)
    back, both_x, both_xz, keep, terms, *flows[1] = tied(
        [backs[3], both_x, both_xz, keep, terms] + flows[1], []
    )
    flows.append(tile_step(3, back))
    keep, terms = fold(keep + terms, zp, flip(dz=1))
    (joined,) = flat_call(
        join_body,
        scalars,
        [both, both_z, both_x, both_xz],
        [sds((2, rows, D), BF16)],
        name="join",
    )
    joined = jnp.where(mine, joined, send(joined, only(own_group, c_move)))
    input_grad, output = joined[0].astype(F32), joined[1]
    held = adam_step(1, flows[1], held)
    held = adam_step(2, flows[2], held)
    held = adam_step(3, flows[3], held)
    keep, terms = fold(keep + terms, y, y_move)
    terms = keep + terms
    small_outs = small_adam(terms.reshape(-1), small_first, small_second, small_master)

    return (
        output,
        input_grad,
        held[0][None],
        held[1][None],
        held[2][None],
        held[3][None],
        *small_outs,
    )


CHUNKS = (3, 3, 3, 3)


def layer_norm(values, weight_gain, weight_bias):
    center = values - jnp.mean(values, axis=1, keepdims=True)
    spread = jnp.mean(center * center, axis=1, keepdims=True)
    return center * lax.rsqrt(spread + EPS_NORM) * weight_gain + weight_bias


def rotary_tables(places):
    middle = HD // 2
    frequency = ROPE_BASE ** (-(jnp.arange(middle, dtype=jnp.float32) * 2.0) / HD)
    angles = places.astype(jnp.float32)[:, None] * frequency[None, :]
    cosine_half = jnp.cos(angles)
    sine_half = jnp.sin(angles)
    return (
        jnp.concatenate([cosine_half, cosine_half], axis=1),
        jnp.concatenate([sine_half, sine_half], axis=1),
    )


def rotary(values, cosine_table, sine_table):
    middle = HD // 2
    turned = jnp.concatenate([-values[..., middle:], values[..., :middle]], axis=-1)
    return values * cosine_table[:, None, :] + turned * sine_table[:, None, :]


def rotary_back(gradients, cosine_table, sine_table):
    middle = HD // 2
    scaled = gradients * sine_table[:, None, :]
    turned = jnp.concatenate([scaled[..., middle:], -scaled[..., :middle]], axis=-1)
    return gradients * cosine_table[:, None, :] + turned


def from_tiles(tile_stack, rows_total, cols_total):
    return (
        tile_stack.reshape(rows_total // TR, cols_total // TC, TR, TC)
        .transpose(0, 2, 1, 3)
        .reshape(rows_total, cols_total)
    )


def unpack(tile_stack):
    count_in = D // TR * (HG // TC)
    count_out = HG // TR * (D // TC)
    count_up = D // TR * (FG // TC)
    edge_out = 3 * count_in
    edge_up = edge_out + count_out
    edge_down = edge_up + count_up
    w_inputs = jnp.concatenate(
        [
            from_tiles(tile_stack[:count_in], D, HG),
            from_tiles(tile_stack[count_in : 2 * count_in], D, HG),
            from_tiles(tile_stack[2 * count_in : edge_out], D, HG),
        ],
        axis=1,
    )
    w_output = from_tiles(tile_stack[edge_out:edge_up], HG, D)
    w_up = from_tiles(tile_stack[edge_up:edge_down], D, FG)
    w_down = from_tiles(tile_stack[edge_down:], FG, D)
    return (w_inputs, w_output, w_up, w_down)


def router_scale(acts_low, router_map, chosen):
    logits = jnp.dot(acts_low.astype(jnp.float32), router_map, precision=PRECISE)
    probs_all = jax.nn.softmax(logits, axis=1)
    picked = (chosen[:, None] - 1 == jnp.arange(WIDTHS)[None, :]).astype(jnp.float32)
    return (WIDTHS * jnp.sum(probs_all * picked, axis=1), probs_all, picked)


def router_back(grad_scale, probs_all, picked):
    chosen_prob = jnp.sum(probs_all * picked, axis=1)
    return (WIDTHS * grad_scale * chosen_prob)[:, None] * (picked - probs_all)


def scores_of(queries, key_block, query_index, query_segment, key_index, key_segment):
    raw_scores = jnp.einsum(
        "qhd,khd->hqk", queries, key_block, preferred_element_type=jnp.float32
    ) * HD ** (-0.5)
    allowed = (key_segment[None, :] == query_segment[:, None]) & (
        key_index[None, :] <= query_index[:, None]
    )
    return (raw_scores, allowed[None])


def fetch_block(packed_all, all_index, all_segment, number, block_rows):
    start = number * block_rows
    piece_rows = lax.dynamic_slice_in_dim(packed_all, start, block_rows, 0)
    key_index = lax.dynamic_slice_in_dim(all_index, start, block_rows, 0)
    key_segment = lax.dynamic_slice_in_dim(all_segment, start, block_rows, 0)
    first_half = piece_rows[:, :HG].reshape(block_rows, HPG, HD)
    second_half = piece_rows[:, HG:].reshape(block_rows, HPG, HD)
    return (first_half, second_half, key_index, key_segment)


def attend_forward(queries, token_index, segment, packed_all, all_index, all_segment, block_rows):
    local_rows = queries.shape[0]
    blocks = packed_all.shape[0] // block_rows

    def first_pass(carried, number):
        running_max, running_sum = carried
        key_block, value_block, key_index, key_segment = fetch_block(
            packed_all, all_index, all_segment, number, block_rows
        )
        raw_scores, allowed = scores_of(
            queries, key_block, token_index, segment, key_index, key_segment
        )
        masked = jnp.where(allowed, raw_scores, NEG_FILL)
        fresh_max = jnp.maximum(running_max, jnp.max(masked, axis=2))
        running_sum = running_sum * jnp.exp(running_max - fresh_max) + jnp.sum(
            jnp.exp(masked - fresh_max[:, :, None]), axis=2
        )
        return ((fresh_max, running_sum), None)

    start_state = (
        jnp.full((HPG, local_rows), NEG_FILL, jnp.float32),
        jnp.zeros((HPG, local_rows), jnp.float32),
    )
    (running_max, running_sum), unused = lax.scan(first_pass, start_state, jnp.arange(blocks))
    log_sum = running_max + jnp.log(running_sum)

    def second_pass(carried, number):
        key_block, value_block, key_index, key_segment = fetch_block(
            packed_all, all_index, all_segment, number, block_rows
        )
        raw_scores, allowed = scores_of(
            queries, key_block, token_index, segment, key_index, key_segment
        )
        weights_p = jnp.where(allowed, jnp.exp(raw_scores - log_sum[:, :, None]), 0.0)
        update = jnp.einsum(
            "hqk,khd->qhd",
            weights_p.astype(jnp.bfloat16),
            value_block,
            preferred_element_type=jnp.float32,
        )
        return (carried + update, None)

    context, unused = lax.scan(
        second_pass, jnp.zeros((local_rows, HPG, HD), jnp.float32), jnp.arange(blocks)
    )
    return (log_sum, context)


def pair_grads(
    queries,
    grad_out,
    log_sum,
    delta,
    query_index,
    query_segment,
    key_block,
    value_block,
    key_index,
    key_segment,
):
    raw_scores, allowed = scores_of(
        queries, key_block, query_index, query_segment, key_index, key_segment
    )
    weights_p = jnp.where(allowed, jnp.exp(raw_scores - log_sum[:, :, None]), 0.0)
    grad_value = jnp.einsum(
        "hqk,qhd->khd", weights_p.astype(jnp.bfloat16), grad_out, preferred_element_type=jnp.float32
    )
    grad_probs = jnp.einsum(
        "qhd,khd->hqk", grad_out, value_block, preferred_element_type=jnp.float32
    )
    grad_raw = (weights_p * (grad_probs - delta[:, :, None]) * HD ** (-0.5)).astype(jnp.bfloat16)
    grad_query = jnp.einsum("hqk,khd->qhd", grad_raw, key_block, preferred_element_type=jnp.float32)
    grad_key = jnp.einsum("hqk,qhd->khd", grad_raw, queries, preferred_element_type=jnp.float32)
    return (grad_query, grad_key, grad_value)


def local_plain(
    tokens,
    cotangent,
    attn_width,
    ffn_width,
    seq_lengths,
    tile_order,
    master,
    first_moment,
    second_moment,
    left_basis,
    right_basis,
    small_master,
    small_first,
    small_second,
):
    local_rows = tokens.shape[0]
    shards = lax.axis_size("seq")
    all_rows = local_rows * shards
    block_rows = min(KB_CAP, all_rows)
    blocks = all_rows // block_rows
    group_id = lax.axis_index("head")
    slot_order = tile_order[0]
    weights_all, small_all = (
        lax.all_gather(master[0].astype(jnp.bfloat16), "seq", axis=0, tiled=True),
        lax.all_gather(small_master.astype(jnp.bfloat16), "seq", axis=0, tiled=True),
    )
    w_inputs, w_output, w_up, w_down = unpack(place_tiles(slot_order, [weights_all], None)[0])
    small_vals = small_all.astype(jnp.float32)
    gain_one = small_vals[0:D]
    bias_one = small_vals[D : 2 * D]
    gain_two = small_vals[2 * D : 3 * D]
    bias_two = small_vals[3 * D : 4 * D]
    routers = small_vals[4 * D :].reshape(D, 2 * WIDTHS)
    router_attn = routers[:, :WIDTHS]
    router_ffn = routers[:, WIDTHS:]
    first_row = lax.axis_index("seq") * local_rows
    token_index, segment, offset = token_layout(first_row, local_rows, seq_lengths)
    residual = tokens.astype(jnp.float32)
    ln_one, pull_one = jax.vjp(layer_norm, residual, gain_one, bias_one)
    act_one = ln_one.astype(jnp.bfloat16)
    scale_attn, probs_attn, picked_attn = router_scale(act_one, router_attn, attn_width)
    projected = jnp.dot(act_one, w_inputs, preferred_element_type=jnp.float32)
    cosine_table, sine_table = rotary_tables(offset)
    query_low = rotary(
        projected[:, :HG].reshape(local_rows, HPG, HD), cosine_table, sine_table
    ).astype(jnp.bfloat16)
    key_low = rotary(
        projected[:, HG : 2 * HG].reshape(local_rows, HPG, HD), cosine_table, sine_table
    ).astype(jnp.bfloat16)
    value_low = projected[:, 2 * HG :].astype(jnp.bfloat16)
    packed = jnp.concatenate([key_low.reshape(local_rows, HG), value_low], axis=1)
    packed_all = lax.all_gather(packed, "seq", axis=0, tiled=True)
    all_index, all_segment, all_offset = token_layout(0, all_rows, seq_lengths)
    log_sum, context = attend_forward(
        query_low, token_index, segment, packed_all, all_index, all_segment, block_rows
    )
    head_mask = (group_id < attn_width).astype(jnp.float32)
    ctx_low = (context * head_mask[:, None, None]).astype(jnp.bfloat16).reshape(local_rows, HG)
    attn_out = lax.psum(
        jnp.dot(ctx_low, w_output, preferred_element_type=jnp.float32).astype(jnp.bfloat16), "head"
    ).astype(jnp.float32)
    middle_res = residual + scale_attn[:, None] * attn_out
    ln_two, pull_two = jax.vjp(layer_norm, middle_res, gain_two, bias_two)
    act_two = ln_two.astype(jnp.bfloat16)
    scale_ffn, probs_ffn, picked_ffn = router_scale(act_two, router_ffn, ffn_width)
    pre_act = jnp.dot(act_two, w_up, preferred_element_type=jnp.float32)
    unit_mask = (group_id < ffn_width).astype(jnp.float32)
    hidden_low = (jnp.square(jnp.maximum(pre_act, 0.0)) * unit_mask[:, None]).astype(jnp.bfloat16)
    ffn_out = lax.psum(
        jnp.dot(hidden_low, w_down, preferred_element_type=jnp.float32).astype(jnp.bfloat16), "head"
    ).astype(jnp.float32)
    output = (middle_res + scale_ffn[:, None] * ffn_out).astype(jnp.bfloat16)
    grad_top = cotangent.astype(jnp.float32)
    grad_scale_ffn = jnp.sum(grad_top * ffn_out, axis=1)
    grad_ffn_low = (scale_ffn[:, None] * grad_top).astype(jnp.bfloat16)
    grad_hidden = jnp.dot(grad_ffn_low, w_down.T, preferred_element_type=jnp.float32)
    grad_pre_low = (grad_hidden * unit_mask[:, None] * 2.0 * jnp.maximum(pre_act, 0.0)).astype(
        jnp.bfloat16
    )
    grad_act_two = lax.psum(
        jnp.dot(grad_pre_low, w_up.T, preferred_element_type=jnp.float32).astype(jnp.bfloat16),
        "head",
    ).astype(jnp.float32)
    logit_ffn = router_back(grad_scale_ffn, probs_ffn, picked_ffn)
    grad_act_two = grad_act_two + jnp.dot(logit_ffn, router_ffn.T, precision=PRECISE)
    grad_mid_ln, grad_gain_two, grad_bias_two = pull_two(grad_act_two)
    grad_middle = grad_top + grad_mid_ln
    grad_scale_attn = jnp.sum(grad_middle * attn_out, axis=1)
    grad_attn_low = (scale_attn[:, None] * grad_middle).astype(jnp.bfloat16)
    grad_context = jnp.dot(grad_attn_low, w_output.T, preferred_element_type=jnp.float32)
    grad_out_low = (
        (grad_context * head_mask[:, None]).astype(jnp.bfloat16).reshape(local_rows, HPG, HD)
    )
    delta = jnp.sum(grad_out_low.astype(jnp.float32) * context, axis=2).T
    zero_state = jnp.zeros((local_rows, HPG, HD), jnp.float32)

    def visit_keys(carried, number):
        key_block, value_block, key_index, key_segment = fetch_block(
            packed_all, all_index, all_segment, number, block_rows
        )
        grad_query, grad_key, grad_value = pair_grads(
            query_low,
            grad_out_low,
            log_sum,
            delta,
            token_index,
            segment,
            key_block,
            value_block,
            key_index,
            key_segment,
        )
        return (
            carried + grad_query,
            jnp.concatenate(
                [grad_key.reshape(block_rows, HG), grad_value.reshape(block_rows, HG)], axis=1
            ),
        )

    grad_query_rot, key_terms = lax.scan(visit_keys, zero_state, jnp.arange(blocks))
    summed = lax.psum_scatter(
        key_terms.reshape(all_rows, 2 * HG).astype(jnp.bfloat16),
        "seq",
        scatter_dimension=0,
        tiled=True,
    ).astype(jnp.float32)
    grad_key_rot = summed[:, :HG].reshape(local_rows, HPG, HD)
    grad_value_all = summed[:, HG:].reshape(local_rows, HPG, HD)
    grad_query_low = (
        rotary_back(grad_query_rot, cosine_table, sine_table)
        .astype(jnp.bfloat16)
        .reshape(local_rows, HG)
    )
    grad_key_low = (
        rotary_back(grad_key_rot, cosine_table, sine_table)
        .astype(jnp.bfloat16)
        .reshape(local_rows, HG)
    )
    grad_value_low = grad_value_all.astype(jnp.bfloat16).reshape(local_rows, HG)
    grad_inputs_low = jnp.concatenate([grad_query_low, grad_key_low, grad_value_low], axis=1)
    grad_act_one = lax.psum(
        jnp.dot(grad_inputs_low, w_inputs.T, preferred_element_type=jnp.float32).astype(
            jnp.bfloat16
        ),
        "head",
    ).astype(jnp.float32)
    logit_attn = router_back(grad_scale_attn, probs_attn, picked_attn)
    grad_act_one = grad_act_one + jnp.dot(logit_attn, router_attn.T, precision=PRECISE)
    grad_res_ln, grad_gain_one, grad_bias_one = pull_one(grad_act_one)
    input_grad = grad_middle + grad_res_ln
    grad_router = jnp.concatenate(
        [
            jnp.dot(act_one.astype(jnp.float32).T, logit_attn, precision=PRECISE),
            jnp.dot(act_two.astype(jnp.float32).T, logit_ffn, precision=PRECISE),
        ],
        axis=1,
    ).reshape(-1)
    small_terms = jnp.concatenate(
        [grad_gain_one, grad_bias_one, grad_gain_two, grad_bias_two, grad_router]
    )
    tile_terms = tile_grads(
        slot_order,
        [[act_one, ctx_low, act_two, hidden_low]],
        [[grad_inputs_low, grad_attn_low, grad_pre_low, grad_ffn_low]],
        None,
        [slot_order.shape[0]],
    )[0]
    tile_grad, small_grad = (
        lax.psum_scatter(tile_terms, "seq", scatter_dimension=0, tiled=True),
        lax.psum_scatter(
            small_terms.astype(jnp.bfloat16), "seq", scatter_dimension=0, tiled=True
        ).astype(jnp.float32),
    )
    slots = master.shape[1]
    held = adam_tiles(
        jnp.array([0, 0], jnp.int32),
        slots,
        [[tile_grad]],
        (left_basis[0], right_basis[0]),
        (first_moment[0], second_moment[0], master[0]),
        None,
    )
    small_outs = small_adam(small_grad, small_first, small_second, small_master)
    return (
        output,
        input_grad,
        held[0][None],
        held[1][None],
        held[2][None],
        held[3][None],
        *small_outs,
    )


def solution(mesh):
    return jax.shard_map(
        local_remap if dict(mesh.shape) == {"seq": 8, "head": 4} else local_plain,
        mesh=mesh,
        in_specs=(
            P("seq", None),
            P("seq", None),
            P("seq"),
            P("seq"),
            P(),
            P("head", None),
            P("head", "seq", None, None),
            P("head", "seq", None, None),
            P("head", "seq", None, None),
            P("head", "seq", None, None),
            P("head", "seq", None, None),
            P("seq"),
            P("seq"),
            P("seq"),
        ),
        out_specs=(
            P("seq", None),
            P("seq", None),
            P("head", "seq", None, None),
            P("head", "seq", None, None),
            P("head", "seq", None, None),
            P("head", "seq", None, None),
            P("seq"),
            P("seq"),
            P("seq"),
        ),
        check_vma=False,
    )
```

```python
import functools

import jax
import jax.numpy as jnp
from jax import lax
from jax.experimental import pallas as pl
from jax.experimental.pallas import tpu as pltpu
from jax.sharding import PartitionSpec as P

D = 2048
HD = 128
WIDTHS = 4
TR = 256
TC = 512
TILES = 96
STEP = 10
KB_CAP = 1024
HPG = 4
HG = 512
FG = 2048

PRECISE = lax.Precision.HIGHEST
EPS_NORM = 1e-05
BETA_ONE = 0.95
BETA_TWO = 0.95
ADAM_EPS = 1e-08
DECAY_RATE = 0.01
RATE_TILE = 0.15
RATE_SMALL = 1.0
ROPE_BASE = 10000.0
NEG_FILL = -1e30
SCORE_SCALE = HD ** (-0.5)
F32 = jnp.float32
BF16 = jnp.bfloat16
AXES = ("seq", "head")
VMEM_BIG = 56 << 20
VMEM_ALL = 61 << 20


def nt(a, b):
    return lax.dot_general(a, b, (((1,), (1,)), ((), ())), preferred_element_type=F32)


def nn(a, b):
    return lax.dot_general(a, b, (((1,), (0,)), ((), ())), preferred_element_type=F32)


def tn(a, b):
    return lax.dot_general(a, b, (((0,), (0,)), ((), ())), preferred_element_type=F32)


VM = pl.BlockSpec(memory_space=pltpu.VMEM)
SM = pl.BlockSpec(memory_space=pltpu.SMEM)
HBM = pl.BlockSpec(memory_space=pltpu.MemorySpace.HBM)


def sds(shape, dtype):
    return jax.ShapeDtypeStruct(shape, dtype)


MARK = sds((8, HD), F32)


def params():
    return pltpu.CompilerParams(vmem_limit_bytes=VMEM_BIG)


def cost(flops, nbytes):
    return pl.CostEstimate(flops=int(flops), bytes_accessed=int(nbytes), transcendentals=0)


def flat_call(body, scalars, arrays, outs, scratch=(), flops=0, name=None):
    nbytes = sum(a.size * a.dtype.itemsize for a in arrays)
    nbytes += sum(int(jnp.dtype(o.dtype).itemsize) * o.size for o in outs)
    return pl.pallas_call(
        body,
        out_shape=outs,
        in_specs=[SM] + [VM] * len(arrays),
        out_specs=[VM] * len(outs),
        scratch_shapes=list(scratch),
        compiler_params=params(),
        cost_estimate=cost(flops, nbytes),
        name=name,
    )(scalars, *arrays)


def rows_of(ref, index, rows):
    return ref[pl.ds(pl.multiple_of(index * rows, rows), rows), :]


def put_rows(ref, index, rows, value):
    ref[pl.ds(pl.multiple_of(index * rows, rows), rows), :] = value


def store_pieces(acc_ref, piece, rows, outs):
    outs[0][...] = rows_of(acc_ref, piece, rows)
    for k in range(1, 4):
        outs[k][...] = rows_of(acc_ref, piece ^ k, rows).astype(BF16)


def row_stats(values):
    center = values - jnp.mean(values, axis=1, keepdims=True)
    rstd = lax.rsqrt(jnp.mean(center * center, axis=1, keepdims=True) + EPS_NORM)
    return center * rstd, rstd


def route_level(logits, width_col):
    lane = lax.broadcasted_iota(jnp.int32, logits.shape, 1)
    live = lane < WIDTHS
    top = jnp.max(jnp.where(live, logits, NEG_FILL), axis=1, keepdims=True)
    raised = jnp.where(live, jnp.exp(jnp.where(live, logits, NEG_FILL) - top), 0.0)
    probs = raised / jnp.sum(raised, axis=1, keepdims=True)
    picked = (lane == width_col - 1).astype(F32)
    chosen = jnp.sum(probs * picked, axis=1, keepdims=True)
    return WIDTHS * chosen, WIDTHS * chosen * (picked - probs)


def split_dot(values, right_low):
    high = values.astype(BF16)
    rest = (values - high.astype(F32)).astype(BF16)
    return nn(high, right_low) + nn(rest, right_low)


def norm_one_body(sc, tok, gain, bias, router, width, a1, a1p, tokp, rap, coefp, ra_s, coef_s):
    rows = a1p.shape[0]
    piece = sc[1]
    xhat, _ = row_stats(tok[...].astype(F32))
    low = (xhat * gain[...] + bias[...]).astype(BF16)
    a1[...] = low
    scale, coef = route_level(nn(low, router[...]), width[...])
    ra_s[...] = scale
    coef_s[...] = coef
    a1p[...] = rows_of(a1, piece, rows)
    tokp[...] = rows_of(tok, piece, rows)
    rap[...] = rows_of(ra_s, piece, rows)
    coefp[...] = rows_of(coef_s, piece, rows)


def turn(values, cosine, signed_sine):
    return values * cosine + pltpu.roll(values, HD // 2, 1) * signed_sine


def turn_back(values, cosine, signed_sine):
    return values * cosine - pltpu.roll(values, HD // 2, 1) * signed_sine


def project_body(sc, a1, weights, cosine, sine, o0, o1, o2, o3, heads_s):
    step = pl.program_id(0)
    spot = sc[0]
    out = nn(a1[...], weights[...].reshape(D, HG))
    plain = step == 2
    cos_v = jnp.where(plain, 1.0, cosine[0])
    sin_v = jnp.where(plain, 0.0, sine[0])
    for head in range(HPG):
        heads_s[head] = turn(out[:, head * HD : (head + 1) * HD], cos_v, sin_v).astype(BF16)
    for k, ref in enumerate((o0, o1, o2, o3)):
        ref[0] = heads_s[spot ^ k]


def attend_body(
    sc, start_col, r0, r1, r2, r3, c0, c1, c2, c3,
    o0, o1, o2, o3, ctx, lse, q_all, k_all, v_all, m_s, l_s, acc_s,
):
    spot, core = sc[0], sc[2]
    rows = r0.shape[1]

    def block_of(source, side):
        return (2 * (source // 2) + side) * 2 + source % 2

    for k, (own, other) in enumerate(((r0, c0), (r1, c1), (r2, c2), (r3, c3))):
        mine = block_of(spot ^ k, core)
        theirs = block_of(spot ^ k, 1 - core)
        q_all[k] = own[0]
        k_all[mine] = own[1]
        v_all[mine] = own[2]
        k_all[theirs] = other[1]
        v_all[theirs] = other[2]

    def per_query(k, unused):
        block = block_of(spot ^ k, core)
        query = q_all[k]
        first = start_col[block]
        where_q = block * rows + lax.broadcasted_iota(jnp.int32, (rows, rows), 0)
        lane = lax.broadcasted_iota(jnp.int32, (rows, rows), 1)
        m_s[...] = jnp.full(m_s.shape, NEG_FILL, F32)
        l_s[...] = jnp.zeros(l_s.shape, F32)
        acc_s[...] = jnp.zeros(acc_s.shape, F32)

        def per_key(kb, unused_two):
            where_k = kb * rows + lane
            scores = nt(query, k_all[kb]) * SCORE_SCALE
            scores = jnp.where((where_k <= where_q) & (where_k >= first), scores, NEG_FILL)
            old = m_s[...]
            new = jnp.maximum(old, jnp.max(scores, axis=1, keepdims=True))
            weight = jnp.exp(scores - new)
            fade = jnp.exp(old - new)
            l_s[...] = l_s[...] * fade + jnp.sum(weight, axis=1, keepdims=True)
            acc_s[...] = acc_s[...] * fade + nn(weight.astype(BF16), v_all[kb])
            m_s[...] = new
            return 0

        lax.fori_loop(sc[4 + block], block + 1, per_key, 0)
        ctx[k] = acc_s[...] / l_s[...]
        lse[k] = m_s[...] + jnp.log(l_s[...])
        return 0

    lax.fori_loop(0, 4, per_query, 0)
    for k, ref in enumerate((o0, o1, o2, o3)):
        ref[...] = ctx[k].astype(BF16)


def output_body(sc, r0, r1, r2, r3, width, weights, cb, o0, o1, o2, o3, acc_s):
    spot, piece, group = sc[0], sc[1], sc[3]
    keep = width[...] > group
    for k, ref in enumerate((r0, r1, r2, r3)):
        at = pl.ds(pl.multiple_of((spot ^ k) * HD, HD), HD)
        cb[:, at] = jnp.where(keep, ref[...], jnp.zeros_like(ref[...]))
    for col in range(D // TC):
        acc_s[:, col * TC : (col + 1) * TC] = nn(cb[:, :TR], weights[0, col]) + nn(
            cb[:, TR:], weights[1, col]
        )
    store_pieces(acc_s, piece, o1.shape[0], (o0, o1, o2, o3))


def norm_two_body(sc, own, r1, r2, r3, tokp, rap, gain, bias, attn, h1, a2p):
    total = own[...] + r1[...].astype(F32) + r2[...].astype(F32) + r3[...].astype(F32)
    attn[...] = total
    middle = tokp[...].astype(F32) + rap[...] * total
    h1[...] = middle
    xhat, _ = row_stats(middle)
    a2p[...] = (xhat * gain[...] + bias[...]).astype(BF16)


def ffn_body(
    sc, p0, p1, p2, p3, dy, width, router, w_up, w_down,
    a2, act, relu, gffn, dlog, rfp, o0, o1, o2, o3, acc_s, coef_s, rf_s,
):
    step = pl.program_id(0)
    piece, group = sc[1], sc[3]
    rows = p0.shape[0]

    @pl.when(step == 0)
    def _():
        for k, ref in enumerate((p0, p1, p2, p3)):
            put_rows(a2, piece ^ k, rows, ref[...])
        scale, coef = route_level(nn(a2[...], router[...]), width[...])
        rf_s[...] = scale
        coef_s[...] = coef
        gffn[...] = (scale * dy[...].astype(F32)).astype(BF16)
        rfp[...] = rows_of(rf_s, piece, rows)

    up = jnp.maximum(nn(a2[...], w_up[...].reshape(D, TC)), 0.0)
    up = jnp.where(width[...] > group, up, 0.0)
    relu[...] = up.astype(BF16)
    low = (up * up).astype(BF16)
    act[...] = low
    for col in range(D // TC):
        at = slice(col * TC, (col + 1) * TC)
        part = nn(low[:, :TR], w_down[0, col]) + nn(low[:, TR:], w_down[1, col])

        @pl.when(step == 0)
        def _(part=part, at=at):
            acc_s[:, at] = part

        @pl.when(step > 0)
        def _(part=part, at=at):
            acc_s[:, at] += part

    @pl.when(step == pl.num_programs(0) - 1)
    def _():
        drf = jnp.sum(acc_s[...] * dy[...].astype(F32), axis=1, keepdims=True)
        dlog[...] = drf * coef_s[...]
        store_pieces(acc_s, piece, rows, (o0, o1, o2, o3))


def ffn_back_body(sc, gffn, relu, dlog, router_t, w_up, w_down, gpre, o0, o1, o2, o3, acc_s):
    step = pl.program_id(0)
    piece = sc[1]
    halves = []
    for row in range(2):
        total = nt(gffn[:, :TC], w_down[row, 0])
        for col in range(1, D // TC):
            total += nt(gffn[:, col * TC : (col + 1) * TC], w_down[row, col])
        halves.append(total)
    gact = jnp.concatenate(halves, axis=1)
    low = (gact * 2.0 * relu[...].astype(F32)).astype(BF16)
    gpre[...] = low
    part = nt(low, w_up[...].reshape(D, TC))

    @pl.when(step == 0)
    def _():
        acc_s[...] = part + split_dot(dlog[...], router_t[...])

    @pl.when(step > 0)
    def _():
        acc_s[...] += part

    @pl.when(step == pl.num_programs(0) - 1)
    def _():
        store_pieces(acc_s, piece, o1.shape[0], (o0, o1, o2, o3))


def norm_grad(grad, values, gain):
    xhat, rstd = row_stats(values)
    scaled = grad * gain
    inner = scaled - jnp.mean(scaled, axis=1, keepdims=True)
    inner = inner - xhat * jnp.mean(scaled * xhat, axis=1, keepdims=True)
    gain_grad = jnp.sum(grad * xhat, axis=0, keepdims=True)
    return inner * rstd, gain_grad, jnp.sum(grad, axis=0, keepdims=True)


def norm_two_back_body(
    sc, own, r1, r2, r3, h1, attn, dyp, rap, coefp, gain, dh1, gattnp, dlogp, ggain, gbias
):
    grad = own[...] + r1[...].astype(F32) + r2[...].astype(F32) + r3[...].astype(F32)
    back, gain_grad, bias_grad = norm_grad(grad, h1[...], gain[...])
    middle = dyp[...].astype(F32) + back
    dh1[...] = middle
    gattnp[...] = (rap[...] * middle).astype(BF16)
    dra = jnp.sum(middle * attn[...], axis=1, keepdims=True)
    dlogp[...] = dra * coefp[...]
    ggain[...] = gain_grad
    gbias[...] = bias_grad


def gout_body(sc, p0, p1, p2, p3, width, weights, gattn, o0, o1, o2, o3, heads_s):
    spot, piece, group = sc[0], sc[1], sc[3]
    rows = p0.shape[0]
    for k, ref in enumerate((p0, p1, p2, p3)):
        put_rows(gattn, piece ^ k, rows, ref[...])
    keep = width[...] > group
    for row in range(2):
        total = nt(gattn[:, :TC], weights[row, 0])
        for col in range(1, D // TC):
            total += nt(gattn[:, col * TC : (col + 1) * TC], weights[row, col])
        low = jnp.where(keep, total, 0.0).astype(BF16)
        heads_s[2 * row] = low[:, :HD]
        heads_s[2 * row + 1] = low[:, HD:]
    for k, ref in enumerate((o0, o1, o2, o3)):
        ref[...] = heads_s[spot ^ k]


def attend_back_body(
    sc, start_row, cosine, sine, q_all, k_all, v_all, ctx, lse, g0, g1, g2, g3,
    gq, own, other, g_s, gk_s, gv_s, acc_s,
):
    spot, core = sc[0], sc[2]
    rows = g0.shape[0]

    def block_of(source, side):
        return (2 * (source // 2) + side) * 2 + source % 2

    for k, ref in enumerate((g0, g1, g2, g3)):
        g_s[k] = ref[...]
    gk_s[...] = jnp.zeros(gk_s.shape, F32)
    gv_s[...] = jnp.zeros(gv_s.shape, F32)

    def per_query(k, unused):
        block = block_of(spot ^ k, core)
        query = q_all[k]
        grad = g_s[k]
        shared = grad.astype(F32) * ctx[k]
        delta = lax.dot_general(
            jnp.ones((8, HD), F32), shared, (((1,), (1,)), ((), ())),
            precision=PRECISE, preferred_element_type=F32,
        )[:1]
        first = start_row[block]
        level = lse[k]
        where_q = block * rows + lax.broadcasted_iota(jnp.int32, (rows, rows), 1)
        line = lax.broadcasted_iota(jnp.int32, (rows, rows), 0)
        acc_s[...] = jnp.zeros(acc_s.shape, F32)

        def per_key(kb, unused_two):
            where_k = kb * rows + line
            keys = k_all[kb]
            allowed = (where_k <= where_q) & (where_k >= first)
            scores = nt(keys, query) * SCORE_SCALE
            prob = jnp.where(allowed, jnp.exp(jnp.where(allowed, scores - level, 0.0)), 0.0)
            gprob = nt(v_all[kb], grad)
            graw = (prob * (gprob - delta) * SCORE_SCALE).astype(BF16)
            gv_s[kb] += nn(prob.astype(BF16), grad)
            gk_s[kb] += nn(graw, query)
            acc_s[...] += tn(graw, keys)
            return 0

        lax.fori_loop(sc[4 + block], block + 1, per_key, 0)
        gq[k] = turn_back(acc_s[...], cosine[block], sine[block]).astype(BF16)
        return 0

    lax.fori_loop(0, 4, per_query, 0)
    for k in range(4):
        mine = block_of(spot ^ k, core)
        theirs = block_of(spot ^ k, 1 - core)
        own[k, 0] = gk_s[mine]
        own[k, 1] = gv_s[mine]
        other[k, 0] = gk_s[theirs].astype(BF16)
        other[k, 1] = gv_s[theirs].astype(BF16)


def key_merge_body(sc, gq, own, got, cosine, sine, o0, o1, o2, o3):
    spot, core = sc[0], sc[2]
    for k, ref in enumerate((o0, o1, o2, o3)):
        source = spot ^ k
        block = (2 * (source // 2) + core) * 2 + source % 2
        ref[0] = gq[k]
        gk = own[k, 0] + got[k, 0].astype(F32)
        ref[1] = turn_back(gk, cosine[block], sine[block]).astype(BF16)
        ref[2] = (own[k, 1] + got[k, 1].astype(F32)).astype(BF16)


def gather_input_body(sc, r0, r1, r2, r3, gin):
    spot = sc[0]
    for k, ref in enumerate((r0, r1, r2, r3)):
        for member in range(3):
            at = pl.ds(pl.multiple_of(member * HG + (spot ^ k) * HD, HD), HD)
            gin[:, at] = ref[member]


def input_back_body(sc, gin, weights, f1, f2, f3, o0, o1, o2, o3, acc_s):
    piece = sc[1]
    rows = o0.shape[0]
    wide = weights.shape[1] * TR
    total = nt(gin[:, :HG], weights[0].reshape(wide, TC))
    for member in range(1, 3):
        total += nt(gin[:, member * HG : (member + 1) * HG], weights[member].reshape(wide, TC))
    acc_s[...] = total
    o0[...] = rows_of(acc_s, piece, rows)
    for k, (ref, passed) in enumerate(((o1, f1), (o2, f2), (o3, f3))):
        ref[0] = rows_of(acc_s, piece ^ (k + 1), rows).astype(BF16)
        ref[1] = passed[...]


def norm_one_back_body(
    sc, own, r1, r2, r3, ffn, tokp, h1, rfp, dh1, dlogp, router_t, gain, both, ggain, gbias
):
    grad = own[...] + r1[0].astype(F32) + r2[0].astype(F32) + r3[0].astype(F32)
    grad = grad + split_dot(dlogp[...], router_t[...])
    back, gain_grad, bias_grad = norm_grad(grad, tokp[...].astype(F32), gain[...])
    both[0] = (dh1[...] + back).astype(BF16)
    total = ffn[...] + r1[1].astype(F32) + r2[1].astype(F32) + r3[1].astype(F32)
    both[1] = (h1[...] + rfp[...] * total).astype(BF16)
    ggain[...] = gain_grad
    gbias[...] = bias_grad


def join_body(sc, b0, b1, b2, b3, whole):
    piece = sc[1]
    rows = b0.shape[1]
    for k, ref in enumerate((b0, b1, b2, b3)):
        at = pl.ds(pl.multiple_of((piece ^ k) * rows, rows), rows)
        whole[:, at, :] = ref[...]


def place_tiles(ids, chunks, held, waits=()):
    count = sum(c.shape[0] for c in chunks)

    def body(ids_ref, *refs):
        parts = refs[: len(chunks)]
        out = refs[len(chunks) + len(waits) + (0 if held is None else 1)]
        mark, buf, in_sems, out_sems = refs[-4:]
        mark[...] = jnp.zeros_like(mark)
        places = [(part, i) for part in parts for i in range(part.shape[0])]
        arrive = [
            pltpu.make_async_copy(part.at[i], buf.at[at], in_sems.at[at])
            for at, (part, i) in enumerate(places)
        ]
        leave = [
            pltpu.make_async_copy(buf.at[at], out.at[ids_ref[at]], out_sems.at[at])
            for at in range(count)
        ]
        for copy in arrive:
            copy.start()
        for came, go in zip(arrive, leave):
            came.wait()
            go.start()
        for copy in leave:
            copy.wait()

    extra = [] if held is None else [held]
    return pl.pallas_call(
        body,
        out_shape=[sds((TILES, TR, TC), BF16), MARK],
        in_specs=[SM] + [HBM] * (len(chunks) + len(extra) + len(waits)),
        out_specs=[HBM, VM],
        scratch_shapes=[
            pltpu.VMEM((count, TR, TC), BF16),
            pltpu.SemaphoreType.DMA((count,)),
            pltpu.SemaphoreType.DMA((count,)),
        ],
        compiler_params=params(),
        input_output_aliases={} if held is None else {1 + len(chunks): 0},
        cost_estimate=cost(0, 2 * count * TR * TC * 2),
        name="place_tiles",
    )(ids, *chunks, *extra, *waits)


def tile_kind(tile):
    kind = (tile >= 24).astype(jnp.int32) + (tile >= 32).astype(jnp.int32)
    kind = kind + (tile >= 64).astype(jnp.int32)
    base = jnp.where(kind == 1, 24, jnp.where(kind == 2, 32, 64))
    local = tile - base
    left = jnp.where(kind == 0, tile % 8, local // 4)
    right = jnp.where(kind == 0, tile // 8, local % 4)
    return kind, left, right


def tile_grads(ids, lefts, rights, added, outs_of, waits=()):
    count = ids.shape[0]
    parts = len(lefts)
    rows = lefts[0][0].shape[0]
    flat = [a for part in lefts for a in part] + [a for part in rights for a in part]

    def fetch(ids_ref, step, slot, refs, lbuf, rbuf, sems):
        kind, left, right = tile_kind(ids_ref[step])
        for which in range(4):

            @pl.when(kind == which)
            def _(which=which):
                for part in range(parts):
                    src = refs[part * 4 + which]
                    at = pl.ds(pl.multiple_of(left * TR, TR), TR)
                    pltpu.make_async_copy(
                        src.at[:, at], lbuf.at[slot, pl.ds(part * rows, rows)], sems.at[slot, part]
                    ).start()
                    src = refs[(parts + part) * 4 + which]
                    at = pl.ds(pl.multiple_of(right * TC, TC), TC)
                    pltpu.make_async_copy(
                        src.at[:, at],
                        rbuf.at[slot, pl.ds(part * rows, rows)],
                        sems.at[slot, parts + part],
                    ).start()

    def body(ids_ref, *refs):
        sources = refs[: len(flat)]
        at = len(flat)
        plus = None
        if added is not None:
            plus = refs[at]
            at += 1
        at += len(waits)
        outs = refs[at : at + len(outs_of)]
        mark, lbuf, rbuf, sems = refs[at + len(outs_of) :]
        mark[...] = jnp.zeros_like(mark)
        step = pl.program_id(0)
        slot = lax.rem(step, 2)

        @pl.when(step == 0)
        def _():
            fetch(ids_ref, 0, 0, sources, lbuf, rbuf, sems)

        @pl.when(step + 1 < count)
        def _():
            fetch(ids_ref, step + 1, 1 - slot, sources, lbuf, rbuf, sems)

        for part in range(parts):
            pltpu.make_async_copy(
                sources[0].at[:, :TR], lbuf.at[slot, pl.ds(part * rows, rows)], sems.at[slot, part]
            ).wait()
            pltpu.make_async_copy(
                sources[parts * 4 + 1].at[:, :TC],
                rbuf.at[slot, pl.ds(part * rows, rows)],
                sems.at[slot, parts + part],
            ).wait()
        total = tn(lbuf[slot], rbuf[slot])
        if plus is not None:
            total = total + plus[0].astype(F32)
        low = total.astype(BF16)
        if len(outs_of) == 1:
            outs[0][0] = low
        else:
            begin = 0
            for ref, size in zip(outs, outs_of):

                @pl.when((step >= begin) & (step < begin + size))
                def _(ref=ref):
                    ref[0] = low

                begin += size

    specs_out = []
    begin = 0
    for size in outs_of:
        specs_out.append(
            pl.BlockSpec(
                (1, TR, TC),
                lambda i, ids_ref, begin=begin, size=size: (jnp.clip(i - begin, 0, size - 1), 0, 0),
            )
        )
        begin += size
    plus_in = [] if added is None else [added]
    return pl.pallas_call(
        body,
        out_shape=[sds((size, TR, TC), BF16) for size in outs_of] + [MARK],
        grid_spec=pltpu.PrefetchScalarGridSpec(
            num_scalar_prefetch=1,
            grid=(count,),
            in_specs=[HBM] * len(flat)
            + [pl.BlockSpec((1, TR, TC), lambda i, ids_ref: (i, 0, 0))] * len(plus_in)
            + [HBM] * len(waits),
            out_specs=specs_out + [pl.BlockSpec((8, HD), lambda i, ids_ref: (0, 0))],
            scratch_shapes=[
                pltpu.VMEM((2, parts * rows, TR), BF16),
                pltpu.VMEM((2, parts * rows, TC), BF16),
                pltpu.SemaphoreType.DMA((2, 2 * parts)),
            ],
        ),
        compiler_params=pltpu.CompilerParams(vmem_limit_bytes=VMEM_ALL),
        cost_estimate=cost(
            2 * count * parts * rows * TR * TC, count * (parts * rows * (TR + TC) * 2 + TR * TC * 2)
        ),
        name="tile_grads",
    )(ids, *flat, *plus_in, *waits)


def adam_tile(grad, left, right, first, second, master):
    left_low = left.astype(BF16)
    right_low = right.astype(BF16)
    turned = nn(tn(left_low, grad.astype(BF16)).astype(BF16), right_low)
    new_first = BETA_ONE * first + (1.0 - BETA_ONE) * turned
    new_second = BETA_TWO * second + (1.0 - BETA_TWO) * turned * turned
    step = (
        new_first
        / (1.0 - BETA_ONE**STEP)
        / (jnp.sqrt(new_second / (1.0 - BETA_TWO**STEP)) + ADAM_EPS)
    )
    back = nt(nn(left_low, step.astype(BF16)).astype(BF16), right_low)
    return new_first, new_second, master - RATE_TILE * (back + DECAY_RATE * master)


def adam_tiles(sc, size, sides, bases, state, held):
    flat, specs, plans = [], [], []
    for side, members in enumerate(sides):
        plan = []
        for member in members:
            pair = member if isinstance(member, tuple) else (member,)
            plan.append(range(len(flat), len(flat) + len(pair)))
            flat.extend(pair)
            specs.extend(
                pl.BlockSpec(
                    (1, TR, TC),
                    lambda i, sc_ref, side=side: (jnp.clip(i - side * size, 0, size - 1), 0, 0),
                )
                for _ in pair
            )
        plans.append(plan)

    def slot(i, sc_ref):
        return sc_ref[1 + i // size] + lax.rem(i, size)

    def body(sc_ref, *refs):
        step = pl.program_id(0)
        left, right, first, second, master = refs[len(flat) : len(flat) + 5]
        o_first, o_second, o_master, o_low, mark = refs[-6:-1]
        grad_s = refs[-1]
        mark[...] = jnp.zeros_like(mark)
        for side, plan in enumerate(plans):

            @pl.when(step // size == side)
            def _(plan=plan):
                total = None
                for spots in plan:
                    value = refs[spots[0]][0].astype(F32)
                    if len(spots) == 2:
                        value = jnp.where(sc_ref[0] > 0, value, refs[spots[1]][0].astype(F32))
                    total = value if total is None else total + value
                grad_s[...] = total

        new_first, new_second, new_master = adam_tile(
            grad_s[...], left[0], right[0], first[0], second[0], master[0]
        )
        o_first[0] = new_first
        o_second[0] = new_second
        o_master[0] = new_master
        o_low[0] = new_master.astype(BF16)

    def at_slot(shape):
        return pl.BlockSpec((1,) + shape, lambda i, sc_ref: (slot(i, sc_ref), 0, 0))

    slots = state[0].shape[0]
    steps = len(sides) * size
    shapes = [(TR, TC)] * 4
    types = [F32, F32, F32, BF16]
    extra = [] if held is None else list(held)
    base = 1 + len(flat) + 5
    return pl.pallas_call(
        body,
        out_shape=[sds((slots,) + s, t) for s, t in zip(shapes, types)] + [MARK],
        grid_spec=pltpu.PrefetchScalarGridSpec(
            num_scalar_prefetch=1,
            grid=(steps,),
            in_specs=specs
            + [at_slot((TR, TR)), at_slot((TC, TC))]
            + [at_slot((TR, TC))] * 3
            + [HBM] * len(extra),
            out_specs=[at_slot(s) for s in shapes]
            + [pl.BlockSpec((8, HD), lambda i, sc_ref: (0, 0))],
            scratch_shapes=[pltpu.VMEM((TR, TC), F32)],
        ),
        input_output_aliases={base + i: i for i in range(len(extra))},
        compiler_params=pltpu.CompilerParams(vmem_limit_bytes=VMEM_ALL),
        cost_estimate=cost(steps * 8 * TR * TC * TC, steps * 5 * TR * TC * 4),
        name="adam_tiles",
    )(sc, *flat, *bases, *state, *extra)


def small_adam(grad, first, second, master):
    new_first = BETA_ONE * first + (1.0 - BETA_ONE) * grad
    new_second = BETA_TWO * second + (1.0 - BETA_TWO) * grad * grad
    step = (
        new_first
        / (1.0 - BETA_ONE**STEP)
        / (jnp.sqrt(new_second / (1.0 - BETA_TWO**STEP)) + ADAM_EPS)
    )
    return new_first, new_second, master - RATE_SMALL * (step + DECAY_RATE * master)


def signed_tables(places):
    middle = HD // 2
    frequency = ROPE_BASE ** (-(jnp.arange(middle, dtype=F32) * 2.0) / HD)
    angles = places.astype(F32)[:, None] * frequency[None, :]
    cosine = jnp.cos(angles)
    sine = jnp.sin(angles)
    return (
        jnp.concatenate([cosine, cosine], axis=1),
        jnp.concatenate([-sine, sine], axis=1),
    )


def token_layout(first_index, local_rows, seq_lengths):
    places = first_index + jnp.arange(local_rows, dtype=jnp.int32)
    number = seq_lengths.shape[0]
    below = jnp.arange(number)[None, :] <= jnp.arange(number)[:, None]
    bounds = jnp.sum(jnp.where(below, seq_lengths[None, :], 0), axis=1)
    passed = places[:, None] >= bounds[None, :]
    segment = jnp.sum(passed.astype(jnp.int32), axis=1)
    offset = places - jnp.sum(jnp.where(passed, seq_lengths[None, :], 0), axis=1)
    return (places, segment, offset)


def moves(target):
    pairs = []
    for z in range(4):
        for y in range(2):
            for x in range(2):
                for c in range(2):
                    to = target(z, y, x, c)
                    if to is not None:
                        a, b, e, f = to
                        pairs.append((8 * z + 4 * y + 2 * x + c, 8 * a + 4 * b + 2 * e + f))
    return pairs


def only(condition, target):
    return lambda z, y, x, c: target(z, y, x, c) if condition(z, y, x, c) else None


def flip(dz=0, dy=0, dx=0, dc=0):
    return lambda z, y, x, c: (z ^ dz, y ^ dy, x ^ dx, c ^ dc)


def own_group(z, y, x, c):
    return c == z % 2


def foreign(z, y, x, c):
    return c != z % 2


def send(value, target):
    return lax.ppermute(value, AXES, moves(target))


MEMBERS = (None, flip(dz=1), flip(dx=1), flip(dz=1, dx=1))
HEADMATES = (None, flip(dy=1), flip(dz=2), flip(dz=2, dy=1))


def scatter_pieces(pieces):
    return [pieces[0]] + [send(pieces[k], MEMBERS[k]) for k in range(1, 4)]


def share_piece(piece):
    return [piece] + [send(piece, MEMBERS[k]) for k in range(1, 4)]


def swap_heads(blocks):
    return [blocks[0]] + [send(blocks[k], HEADMATES[k]) for k in range(1, 4)]


def after(value, *others):
    return lax.optimization_barrier((value,) + others)[0]


def tied(values, done):
    return list(lax.optimization_barrier(tuple(values) + tuple(done))[: len(values)])


def small_step(values, bit, target):
    other = send(values, target)
    return jnp.where(
        bit == 0, jnp.concatenate([values, other]), jnp.concatenate([other, values])
    )


def local_remap(
    tokens, cotangent, attn_width, ffn_width, seq_lengths, tile_order, master, first_moment,
    second_moment, left_basis, right_basis, small_master, small_first, small_second,
):
    rows = tokens.shape[0]
    piece_rows = rows // 4
    s = lax.axis_index("seq")
    h = lax.axis_index("head")
    z, y, x, c = s // 2, s % 2, h // 2, h % 2
    zp, zh = z % 2, z // 2
    mine = c == zp
    group = 2 * x + zp
    spot = 2 * zh + y
    block = (2 * zh + c) * 2 + y

    y_move, h_move, c_move = flip(dy=1), flip(dz=2), flip(dc=1)

    slots = master.shape[1]
    part = slots // 4
    to_pair = only(own_group, flip(dz=1))
    near_move = lambda z, y, x, c: (z, y, x, 1 - c) if c == z % 2 else (z ^ 1, y, x, c)
    far_move = lambda z, y, x, c: (z ^ 2, y, x, 1 - c) if c == z % 2 else (z ^ 3, y, x, c)
    low = [master[0, i * part : (i + 1) * part].astype(BF16) for i in range(4)]
    near, far = [send(low[0], near_move)], [send(low[0], far_move)]
    order = tile_order[0]
    order_got = send(order, c_move)
    small_all = small_step(small_master.astype(BF16), y, y_move)
    wid = jnp.stack([attn_width, ffn_width])
    wid_got = send(wid, to_pair)
    near[0], order_got, small_all, low1, low2, low3, wid, wid_got = tied(
        [near[0], order_got, small_all] + low[1:] + [wid, wid_got], []
    )
    order = jnp.where(mine, order, order_got)
    base = jnp.where(mine, s ^ 2, s)
    base_there = jnp.where(mine, s, s ^ 2)

    def ids_of(*chunks):
        return jnp.concatenate(
            [
                lax.dynamic_slice_in_dim(order, (o ^ hop) * slots + i * part, part, 0)
                for o in (base, base_there)
                for hop, i in chunks
            ]
        )

    near_y, far_y = [send(near[0], y_move)], []
    near.append(send(low1, near_move))
    small_all = small_step(small_all, zp, flip(dz=1))
    low23 = jnp.concatenate([low2, low3])
    near[0], near[1], far[0], near_y[0], small_all, low1, low2, low3, low23 = tied(
        [near[0], near[1], far[0], near_y[0], small_all, low1, low2, low3, low23], []
    )
    far.append(send(low1, far_move))
    near_y.append(send(near[1], y_move))
    far_y.append(send(far[0], y_move))
    near23 = send(low23, near_move)
    small_all = small_step(small_all, zh, h_move)
    first = jnp.concatenate([near[0], near_y[0], far[0]])
    all_rows = rows * lax.axis_size("seq")
    blocks = all_rows // rows
    places, _, offset = token_layout(0, all_rows, seq_lengths)
    start = places - offset
    first_block = start.reshape(blocks, rows)[:, 0] // rows
    cosine, sine = signed_tables(offset)
    cosine, sine = cosine.reshape(blocks, rows, HD), sine.reshape(blocks, rows, HD)
    scalars = jnp.concatenate(
        [jnp.stack([spot, group, c, group]).astype(jnp.int32), first_block.astype(jnp.int32)]
    )

    start_col, start_row = start.reshape(blocks, rows, 1), start.reshape(blocks, 1, rows)
    near[1], near23, far[1], near_y[1], far_y[0], low2, low3, small_all, first, cosine, sine, tok = tied(
        [near[1], near23, far[1], near_y[1], far_y[0], low2, low3, small_all, first]
        + [cosine, sine, tokens],
        [],
    )
    near += [near23[:part], near23[part:]]
    far.append(send(low2, far_move))
    near_y.append(send(near[2], y_move))
    far_y.append(send(far[1], y_move))
    first_there = send(first, c_move)
    tok_got = send(tok, to_pair)
    second = jnp.concatenate([near[1], near_y[1], far_y[0], far[1]])
    near[2], near[3], far[2], near_y[2], far_y[1], low3, small_all, first, first_there, second, tok, tok_got = tied(
        [near[2], near[3], far[2], near_y[2], far_y[1], low3, small_all, first, first_there]
        + [second, tok, tok_got],
        [],
    )
    far.append(send(low3, far_move))
    near_y.append(send(near[3], y_move))
    far_y.append(send(far[2], y_move))
    second_there = send(second, c_move)
    third = jnp.concatenate([near[2], near_y[2], far_y[1], far[2]])
    third_there = send(third, c_move)
    tiles, mark_one = place_tiles(ids_of((0, 0), (1, 0), (4, 0)), [first, first_there], None)
    tok = jnp.where(mine, tok, tok_got)
    widths = jnp.where(mine, wid, wid_got)
    width_a, width_f = widths[0][:, None], widths[1][:, None]
    gains = small_all[: 4 * D].astype(F32).reshape(4, 1, D)
    gain_one, bias_one, gain_two, bias_two = gains[0], gains[1], gains[2], gains[3]
    routers = small_all[4 * D :].reshape(D, 2 * WIDTHS)
    pad = ((0, 0), (0, HD - WIDTHS))
    router_a = jnp.pad(routers[:, :WIDTHS], pad)
    router_f = jnp.pad(routers[:, WIDTHS:], pad)
    router_ft, router_at = router_f.T, router_a.T
    a1, a1p, tokp, rap, coefp = flat_call(
        norm_one_body,
        scalars,
        [tok, gain_one, bias_one, router_a, width_a],
        [
            sds((rows, D), BF16),
            sds((piece_rows, D), BF16),
            sds((piece_rows, D), BF16),
            sds((piece_rows, 1), F32),
            sds((piece_rows, HD), F32),
        ],
        [pltpu.VMEM((rows, 1), F32), pltpu.VMEM((rows, HD), F32)],
        name="norm_one",
    )

    tiles, mark_two = place_tiles(
        ids_of((0, 1), (1, 1), (5, 0), (4, 1)), [second, second_there], tiles, [mark_one]
    )
    near[3], far[3], near_y[3], far_y[2], third, third_there, mark_two, a1, router_ft, router_at = tied(
        [near[3], far[3], near_y[3], far_y[2], third, third_there, mark_two, a1]
        + [router_ft, router_at],
        [],
    )
    far_y.append(send(far[3], y_move))
    fourth = jnp.concatenate([near[3], near_y[3], far_y[2], far[3]])
    fourth_there = send(fourth, c_move)
    tiles, mark_three = place_tiles(
        ids_of((0, 2), (1, 2), (5, 1), (4, 2)), [third, third_there], tiles, [mark_two]
    )
    far_y[3], fourth, fourth_there, mark_three = tied(
        [far_y[3], fourth, fourth_there, mark_three], []
    )
    fifth_there = send(far_y[3], c_move)
    tiles, _ = place_tiles(
        ids_of((0, 3), (1, 3), (5, 2), (4, 3)), [fourth, fourth_there], tiles, [mark_three]
    )
    tiles, _ = place_tiles(ids_of((5, 3)), [far_y[3], fifth_there], tiles)
    by_row = tiles.reshape(TILES // 4, 4, TR, TC)
    by_map = tiles.reshape(TILES // 8, 8, TR, TC)

    table = pl.BlockSpec((1, rows, HD), lambda i, sc: (sc[12], 0, 0))
    sent = pl.pallas_call(
        project_body,
        out_shape=[sds((3, rows, HD), BF16)] * 4,
        grid_spec=pltpu.PrefetchScalarGridSpec(
            num_scalar_prefetch=1,
            grid=(3,),
            in_specs=[
                pl.BlockSpec((rows, D), lambda i, sc: (0, 0)),
                pl.BlockSpec((1, 8, TR, TC), lambda i, sc: (i, 0, 0, 0)),
                table,
                table,
            ],
            out_specs=[pl.BlockSpec((1, rows, HD), lambda i, sc: (i, 0, 0))] * 4,
            scratch_shapes=[pltpu.VMEM((HPG, rows, HD), BF16)],
        ),
        compiler_params=params(),
        cost_estimate=cost(2 * rows * D * 3 * HG, 3 * D * HG * 2 + rows * D * 2),
        name="project",
    )(jnp.concatenate([scalars, block[None].astype(jnp.int32)]), a1, by_map, cosine, sine)
    got = swap_heads(sent)
    beside = [send(v, flip(dc=1)) for v in got]
    dy = after(cotangent, *got)
    dy = jnp.where(mine, dy, send(dy, to_pair))
    dyp = lax.dynamic_slice_in_dim(dy, group * piece_rows, piece_rows, 0)

    pairs_cost = 4 * 4 * rows * rows * HD * 2
    out = flat_call(
        attend_body,
        scalars,
        [start_col] + got + beside,
        [sds((rows, HD), BF16)] * 4
        + [
            sds((4, rows, HD), F32),
            sds((4, rows, 1), F32),
            sds((4, rows, HD), BF16),
            sds((blocks, rows, HD), BF16),
            sds((blocks, rows, HD), BF16),
        ],
        [pltpu.VMEM((rows, 1), F32), pltpu.VMEM((rows, 1), F32), pltpu.VMEM((rows, HD), F32)],
        flops=2 * pairs_cost,
        name="attend",
    )
    ctx_sent, (ctx, lse, q_all, k_all, v_all) = out[:4], out[4:]
    ctx_got = swap_heads(ctx_sent)

    one_piece = sds((piece_rows, D), F32)
    low_piece = sds((piece_rows, D), BF16)
    piece_outs = [one_piece] + [low_piece] * 3
    wo_spec = pl.BlockSpec((2, 4, TR, TC), lambda i, sc: (3, 0, 0, 0))

    def whole(shape):
        return pl.BlockSpec(shape, lambda i, sc: (0,) * len(shape))

    out = pl.pallas_call(
        output_body,
        out_shape=[sds((rows, HG), BF16)] + piece_outs,
        grid_spec=pltpu.PrefetchScalarGridSpec(
            num_scalar_prefetch=1,
            grid=(1,),
            in_specs=[whole((rows, HD))] * 4 + [whole((rows, 1)), wo_spec],
            out_specs=[whole((rows, HG))] + [whole((piece_rows, D))] * 4,
            scratch_shapes=[pltpu.VMEM((rows, D), F32)],
        ),
        compiler_params=params(),
        cost_estimate=cost(2 * rows * D * HG, D * HG * 2 + rows * D * 4),
        name="output",
    )(scalars, *ctx_got, width_a, by_row)
    cb, attn_parts = out[0], out[1:]
    attn_parts = scatter_pieces(attn_parts)

    attn, h1, a2p = flat_call(
        norm_two_body,
        scalars,
        attn_parts + [tokp, rap, gain_two, bias_two],
        [one_piece, one_piece, low_piece],
        name="norm_two",
    )
    a2_parts = share_piece(a2p)

    up_spec = pl.BlockSpec((8, 1, TR, TC), lambda i, sc: (1, i, 0, 0))
    down_spec = pl.BlockSpec((2, 4, TR, TC), lambda i, sc: (8 + i, 0, 0, 0))
    col_spec = pl.BlockSpec((rows, TC), lambda i, sc: (0, i))
    out = pl.pallas_call(
        ffn_body,
        out_shape=[
            sds((rows, D), BF16),
            sds((rows, FG), BF16),
            sds((rows, FG), BF16),
            sds((rows, D), BF16),
            sds((rows, HD), F32),
            sds((piece_rows, 1), F32),
        ]
        + piece_outs,
        grid_spec=pltpu.PrefetchScalarGridSpec(
            num_scalar_prefetch=1,
            grid=(FG // TC,),
            in_specs=[whole((piece_rows, D))] * 4
            + [whole((rows, D)), whole((rows, 1)), whole((D, HD)), up_spec, down_spec],
            out_specs=[
                whole((rows, D)),
                col_spec,
                col_spec,
                whole((rows, D)),
                whole((rows, HD)),
                whole((piece_rows, 1)),
            ]
            + [whole((piece_rows, D))] * 4,
            scratch_shapes=[
                pltpu.VMEM((rows, D), F32),
                pltpu.VMEM((rows, HD), F32),
                pltpu.VMEM((rows, 1), F32),
            ],
        ),
        compiler_params=params(),
        cost_estimate=cost(4 * rows * D * FG, 4 * D * FG + rows * D * 12),
        name="ffn",
    )(scalars, *a2_parts, dy, width_f, router_f, by_row, by_row)
    a2, act, relu, gffn, dlog_f, rfp = out[:6]
    ffn_parts = out[6:]

    out = pl.pallas_call(
        ffn_back_body,
        out_shape=[sds((rows, FG), BF16)] + piece_outs,
        grid_spec=pltpu.PrefetchScalarGridSpec(
            num_scalar_prefetch=1,
            grid=(FG // TC,),
            in_specs=[
                whole((rows, D)),
                col_spec,
                whole((rows, HD)),
                whole((HD, D)),
                up_spec,
                down_spec,
            ],
            out_specs=[col_spec] + [whole((piece_rows, D))] * 4,
            scratch_shapes=[pltpu.VMEM((rows, D), F32)],
        ),
        compiler_params=params(),
        cost_estimate=cost(4 * rows * D * FG, 4 * D * FG + rows * D * 12),
        name="ffn_back",
    )(scalars, gffn, relu, dlog_f, router_ft, by_row, by_row)
    gpre, ga2_parts = out[0], scatter_pieces(out[1:])

    dh1, gattnp, dlog_a, ggain_two, gbias_two = flat_call(
        norm_two_back_body,
        scalars,
        ga2_parts + [h1, attn, dyp, rap, coefp, gain_two],
        [one_piece, low_piece, sds((piece_rows, HD), F32), sds((1, D), F32), sds((1, D), F32)],
        name="norm_two_back",
    )
    gattn_parts = share_piece(gattnp)
    out = pl.pallas_call(
        gout_body,
        out_shape=[sds((rows, D), BF16)] + [sds((rows, HD), BF16)] * 4,
        grid_spec=pltpu.PrefetchScalarGridSpec(
            num_scalar_prefetch=1,
            grid=(1,),
            in_specs=[whole((piece_rows, D))] * 4 + [whole((rows, 1)), wo_spec],
            out_specs=[whole((rows, D))] + [whole((rows, HD))] * 4,
            scratch_shapes=[pltpu.VMEM((HPG, rows, HD), BF16)],
        ),
        compiler_params=params(),
        cost_estimate=cost(2 * rows * D * HG, D * HG * 2 + rows * D * 4),
        name="gout",
    )(scalars, *gattn_parts, width_a, by_row)
    gattn, gout_got = out[0], swap_heads(out[1:])

    gq, keys_own, keys_other = flat_call(
        attend_back_body,
        scalars,
        [start_row, cosine, sine, q_all, k_all, v_all, ctx]
        + [lse.reshape(4, 1, rows)]
        + gout_got,
        [
            sds((4, rows, HD), BF16),
            sds((4, 2, rows, HD), F32),
            sds((4, 2, rows, HD), BF16),
        ],
        [
            pltpu.VMEM((4, rows, HD), BF16),
            pltpu.VMEM((blocks, rows, HD), F32),
            pltpu.VMEM((blocks, rows, HD), F32),
            pltpu.VMEM((rows, HD), F32),
        ],
        flops=5 * pairs_cost,
        name="attend_back",
    )
    grads_sent = flat_call(
        key_merge_body,
        scalars,
        [gq, keys_own, send(keys_other, flip(dc=1)), cosine, sine],
        [sds((3, rows, HD), BF16)] * 4,
        name="key_merge",
    )
    grads_got = swap_heads(grads_sent)
    (gin,) = flat_call(
        gather_input_body, scalars, grads_got, [sds((rows, 3 * HG), BF16)], name="gather_input"
    )
    lefts = [[a1, cb, a2, act]]
    rights = [[gin, gattn, gpre, gffn]]
    lefts.append([send(v, c_move) for v in lefts[0]])
    rights.append([send(v, c_move) for v in rights[0]])
    begins = [sum(CHUNKS[:i]) for i in range(len(CHUNKS))]

    def grad_ids(flip_y, i):
        owners = (s ^ flip_y ^ jnp.where(mine, 2, 4), s ^ flip_y ^ jnp.where(mine, 6, 0))
        return jnp.concatenate(
            [lax.dynamic_slice_in_dim(order, o * slots + begins[i], CHUNKS[i], 0) for o in owners]
        )

    def route(own, other):
        return lambda z, y, x, c: (z ^ (own if c == z % 2 else other), y, x, z % 2)

    def away_of(i):
        return tile_grads(grad_ids(1, i), lefts, rights, None, [2 * CHUNKS[i]])[0]

    bases = (left_basis[0], right_basis[0])
    state = (first_moment[0], second_moment[0], master[0])
    gin, away0 = tied([gin, away_of(0)], [])
    backs = [send(away0, y_move)]
    gin, away1 = tied([gin, away_of(1)], [])
    backs.append(send(away1, y_move))
    half_cols = D // 2
    half_piece = pl.BlockSpec((piece_rows, half_cols), lambda i, sc: (0, i))
    pair_piece = pl.BlockSpec((2, piece_rows, half_cols), lambda i, sc: (0, 0, i))
    out = pl.pallas_call(
        input_back_body,
        out_shape=[one_piece] + [sds((2, piece_rows, D), BF16)] * 3,
        grid_spec=pltpu.PrefetchScalarGridSpec(
            num_scalar_prefetch=1,
            grid=(2,),
            in_specs=[
                whole((rows, 3 * HG)),
                pl.BlockSpec((3, 4, TR, TC), lambda i, sc: (0, i, 0, 0)),
                half_piece,
                half_piece,
                half_piece,
            ],
            out_specs=[half_piece] + [pair_piece] * 3,
            scratch_shapes=[pltpu.VMEM((rows, half_cols), F32)],
        ),
        compiler_params=params(),
        cost_estimate=cost(2 * rows * D * 3 * HG, 3 * D * HG * 2 + rows * D * 4),
        name="input_back",
    )(scalars, gin, by_map, *ffn_parts[1:])
    pieces = [out[0], send(out[1], MEMBERS[1]), send(out[2], MEMBERS[2])]

    def tile_step(i, back, waits):
        first, second, mark = tile_grads(
            grad_ids(0, i), lefts, rights, back, [CHUNKS[i]] * 2, waits
        )
        return [send(first, route(1, 2)), send(second, route(3, 0))], [mark]

    def adam_step(i, flow, held):
        sc = jnp.array([0, begins[i]], jnp.int32)
        return adam_tiles(sc, CHUNKS[i], [flow], bases, state, held)[:4]

    back, away2, pieces[1], pieces[2], last_piece = tied(
        [backs[0], away_of(2), pieces[1], pieces[2], out[3]], []
    )
    backs.append(send(away2, y_move))
    pieces.append(send(last_piece, MEMBERS[3]))
    flow, mark = tile_step(0, back, [])
    flows = [flow]
    back, away3, pieces[3], *mark = tied([backs[1], away_of(3), pieces[3]] + mark, [])
    backs.append(send(away3, y_move))
    flow, mark = tile_step(1, back, mark)
    flows.append(flow)
    both, ggain_one, gbias_one = flat_call(
        norm_one_back_body,
        scalars,
        pieces
        + [ffn_parts[0], tokp, h1, rfp, dh1, dlog_a, router_at, gain_one],
        [sds((2, piece_rows, D), BF16), sds((1, D), F32), sds((1, D), F32)],
        name="norm_one_back",
    )
    grad_router = jnp.concatenate(
        [
            lax.dot_general(
                a1p.astype(F32), dlog_a[:, :WIDTHS], (((0,), (0,)), ((), ())), precision=PRECISE
            ),
            lax.dot_general(
                a2.astype(F32), dlog_f[:, :WIDTHS], (((0,), (0,)), ((), ())), precision=PRECISE
            ),
        ],
        axis=1,
    ).reshape(-1)
    terms = jnp.concatenate(
        [ggain_one[0], gbias_one[0], ggain_two[0], gbias_two[0], grad_router]
    ).reshape(8, -1)
    terms = terms + send(terms, c_move)
    terms = terms + send(terms, flip(dx=1))

    def fold(terms, bit, target):
        halves = terms.reshape(2, terms.shape[0] // 2, terms.shape[1])
        keep = jnp.where(bit == 0, halves[0], halves[1])
        return keep, send(jnp.where(bit == 0, halves[1], halves[0]), target)

    both_z = send(both, only(foreign, flip(dz=1)))
    back, both, both_z, terms, *rest = tied([backs[2], both, both_z, terms] + flows[0] + mark, [])
    flows[0], mark = rest[:2], rest[2:]
    keep, terms = fold(terms, zh, h_move)
    flow, mark = tile_step(2, back, mark)
    flows.append(flow)
    both_x = send(both, only(own_group, flip(dx=1)))
    both_xz = send(both, only(foreign, flip(dz=1, dx=1)))
    held = adam_step(0, flows[0], None)
    back, both_x, both_xz, keep, terms, *rest = tied(
        [backs[3], both_x, both_xz, keep, terms] + flows[1] + mark, []
    )
    flows[1], mark = rest[:2], rest[2:]
    flow, mark = tile_step(3, back, mark)
    flows.append(flow)
    keep, terms = fold(keep + terms, zp, flip(dz=1))
    (joined,) = flat_call(
        join_body,
        scalars,
        [both, both_z, both_x, both_xz],
        [sds((2, rows, D), BF16)],
        name="join",
    )
    joined = jnp.where(mine, joined, send(joined, only(own_group, c_move)))
    input_grad, output = joined[0].astype(F32), joined[1]
    held = adam_step(1, flows[1], held)
    held = adam_step(2, flows[2], held)
    input_grad, output, *flows[3] = tied([input_grad, output] + flows[3], [])
    held = adam_step(3, flows[3], held)
    keep, terms = fold(keep + terms, y, y_move)
    terms = keep + terms
    small_outs = small_adam(terms.reshape(-1), small_first, small_second, small_master)

    return (
        output,
        input_grad,
        held[0][None],
        held[1][None],
        held[2][None],
        held[3][None],
        *small_outs,
    )


CHUNKS = (4, 3, 3, 2)


def layer_norm(values, weight_gain, weight_bias):
    center = values - jnp.mean(values, axis=1, keepdims=True)
    spread = jnp.mean(center * center, axis=1, keepdims=True)
    return center * lax.rsqrt(spread + EPS_NORM) * weight_gain + weight_bias


def rotary_tables(places):
    middle = HD // 2
    frequency = ROPE_BASE ** (-(jnp.arange(middle, dtype=jnp.float32) * 2.0) / HD)
    angles = places.astype(jnp.float32)[:, None] * frequency[None, :]
    cosine_half = jnp.cos(angles)
    sine_half = jnp.sin(angles)
    return (
        jnp.concatenate([cosine_half, cosine_half], axis=1),
        jnp.concatenate([sine_half, sine_half], axis=1),
    )


def rotary(values, cosine_table, sine_table):
    middle = HD // 2
    turned = jnp.concatenate([-values[..., middle:], values[..., :middle]], axis=-1)
    return values * cosine_table[:, None, :] + turned * sine_table[:, None, :]


def rotary_back(gradients, cosine_table, sine_table):
    middle = HD // 2
    scaled = gradients * sine_table[:, None, :]
    turned = jnp.concatenate([scaled[..., middle:], -scaled[..., :middle]], axis=-1)
    return gradients * cosine_table[:, None, :] + turned


def from_tiles(tile_stack, rows_total, cols_total):
    return (
        tile_stack.reshape(rows_total // TR, cols_total // TC, TR, TC)
        .transpose(0, 2, 1, 3)
        .reshape(rows_total, cols_total)
    )


def unpack(tile_stack):
    count_in = D // TR * (HG // TC)
    count_out = HG // TR * (D // TC)
    count_up = D // TR * (FG // TC)
    edge_out = 3 * count_in
    edge_up = edge_out + count_out
    edge_down = edge_up + count_up
    w_inputs = jnp.concatenate(
        [
            from_tiles(tile_stack[:count_in], D, HG),
            from_tiles(tile_stack[count_in : 2 * count_in], D, HG),
            from_tiles(tile_stack[2 * count_in : edge_out], D, HG),
        ],
        axis=1,
    )
    w_output = from_tiles(tile_stack[edge_out:edge_up], HG, D)
    w_up = from_tiles(tile_stack[edge_up:edge_down], D, FG)
    w_down = from_tiles(tile_stack[edge_down:], FG, D)
    return (w_inputs, w_output, w_up, w_down)


def router_scale(acts_low, router_map, chosen):
    logits = jnp.dot(acts_low.astype(jnp.float32), router_map, precision=PRECISE)
    probs_all = jax.nn.softmax(logits, axis=1)
    picked = (chosen[:, None] - 1 == jnp.arange(WIDTHS)[None, :]).astype(jnp.float32)
    return (WIDTHS * jnp.sum(probs_all * picked, axis=1), probs_all, picked)


def router_back(grad_scale, probs_all, picked):
    chosen_prob = jnp.sum(probs_all * picked, axis=1)
    return (WIDTHS * grad_scale * chosen_prob)[:, None] * (picked - probs_all)


def scores_of(queries, key_block, query_index, query_segment, key_index, key_segment):
    raw_scores = jnp.einsum(
        "qhd,khd->hqk", queries, key_block, preferred_element_type=jnp.float32
    ) * HD ** (-0.5)
    allowed = (key_segment[None, :] == query_segment[:, None]) & (
        key_index[None, :] <= query_index[:, None]
    )
    return (raw_scores, allowed[None])


def fetch_block(packed_all, all_index, all_segment, number, block_rows):
    start = number * block_rows
    piece_rows = lax.dynamic_slice_in_dim(packed_all, start, block_rows, 0)
    key_index = lax.dynamic_slice_in_dim(all_index, start, block_rows, 0)
    key_segment = lax.dynamic_slice_in_dim(all_segment, start, block_rows, 0)
    first_half = piece_rows[:, :HG].reshape(block_rows, HPG, HD)
    second_half = piece_rows[:, HG:].reshape(block_rows, HPG, HD)
    return (first_half, second_half, key_index, key_segment)


def attend_forward(queries, token_index, segment, packed_all, all_index, all_segment, block_rows):
    local_rows = queries.shape[0]
    blocks = packed_all.shape[0] // block_rows

    def first_pass(carried, number):
        running_max, running_sum = carried
        key_block, value_block, key_index, key_segment = fetch_block(
            packed_all, all_index, all_segment, number, block_rows
        )
        raw_scores, allowed = scores_of(
            queries, key_block, token_index, segment, key_index, key_segment
        )
        masked = jnp.where(allowed, raw_scores, NEG_FILL)
        fresh_max = jnp.maximum(running_max, jnp.max(masked, axis=2))
        running_sum = running_sum * jnp.exp(running_max - fresh_max) + jnp.sum(
            jnp.exp(masked - fresh_max[:, :, None]), axis=2
        )
        return ((fresh_max, running_sum), None)

    start_state = (
        jnp.full((HPG, local_rows), NEG_FILL, jnp.float32),
        jnp.zeros((HPG, local_rows), jnp.float32),
    )
    (running_max, running_sum), unused = lax.scan(first_pass, start_state, jnp.arange(blocks))
    log_sum = running_max + jnp.log(running_sum)

    def second_pass(carried, number):
        key_block, value_block, key_index, key_segment = fetch_block(
            packed_all, all_index, all_segment, number, block_rows
        )
        raw_scores, allowed = scores_of(
            queries, key_block, token_index, segment, key_index, key_segment
        )
        weights_p = jnp.where(allowed, jnp.exp(raw_scores - log_sum[:, :, None]), 0.0)
        update = jnp.einsum(
            "hqk,khd->qhd",
            weights_p.astype(jnp.bfloat16),
            value_block,
            preferred_element_type=jnp.float32,
        )
        return (carried + update, None)

    context, unused = lax.scan(
        second_pass, jnp.zeros((local_rows, HPG, HD), jnp.float32), jnp.arange(blocks)
    )
    return (log_sum, context)


def pair_grads(
    queries,
    grad_out,
    log_sum,
    delta,
    query_index,
    query_segment,
    key_block,
    value_block,
    key_index,
    key_segment,
):
    raw_scores, allowed = scores_of(
        queries, key_block, query_index, query_segment, key_index, key_segment
    )
    weights_p = jnp.where(allowed, jnp.exp(raw_scores - log_sum[:, :, None]), 0.0)
    grad_value = jnp.einsum(
        "hqk,qhd->khd", weights_p.astype(jnp.bfloat16), grad_out, preferred_element_type=jnp.float32
    )
    grad_probs = jnp.einsum(
        "qhd,khd->hqk", grad_out, value_block, preferred_element_type=jnp.float32
    )
    grad_raw = (weights_p * (grad_probs - delta[:, :, None]) * HD ** (-0.5)).astype(jnp.bfloat16)
    grad_query = jnp.einsum("hqk,khd->qhd", grad_raw, key_block, preferred_element_type=jnp.float32)
    grad_key = jnp.einsum("hqk,qhd->khd", grad_raw, queries, preferred_element_type=jnp.float32)
    return (grad_query, grad_key, grad_value)


def local_plain(
    tokens,
    cotangent,
    attn_width,
    ffn_width,
    seq_lengths,
    tile_order,
    master,
    first_moment,
    second_moment,
    left_basis,
    right_basis,
    small_master,
    small_first,
    small_second,
):
    local_rows = tokens.shape[0]
    shards = lax.axis_size("seq")
    all_rows = local_rows * shards
    block_rows = min(KB_CAP, all_rows)
    blocks = all_rows // block_rows
    group_id = lax.axis_index("head")
    slot_order = tile_order[0]
    weights_all, small_all = (
        lax.all_gather(master[0].astype(jnp.bfloat16), "seq", axis=0, tiled=True),
        lax.all_gather(small_master.astype(jnp.bfloat16), "seq", axis=0, tiled=True),
    )
    w_inputs, w_output, w_up, w_down = unpack(place_tiles(slot_order, [weights_all], None)[0])
    small_vals = small_all.astype(jnp.float32)
    gain_one = small_vals[0:D]
    bias_one = small_vals[D : 2 * D]
    gain_two = small_vals[2 * D : 3 * D]
    bias_two = small_vals[3 * D : 4 * D]
    routers = small_vals[4 * D :].reshape(D, 2 * WIDTHS)
    router_attn = routers[:, :WIDTHS]
    router_ffn = routers[:, WIDTHS:]
    first_row = lax.axis_index("seq") * local_rows
    token_index, segment, offset = token_layout(first_row, local_rows, seq_lengths)
    residual = tokens.astype(jnp.float32)
    ln_one, pull_one = jax.vjp(layer_norm, residual, gain_one, bias_one)
    act_one = ln_one.astype(jnp.bfloat16)
    scale_attn, probs_attn, picked_attn = router_scale(act_one, router_attn, attn_width)
    projected = jnp.dot(act_one, w_inputs, preferred_element_type=jnp.float32)
    cosine_table, sine_table = rotary_tables(offset)
    query_low = rotary(
        projected[:, :HG].reshape(local_rows, HPG, HD), cosine_table, sine_table
    ).astype(jnp.bfloat16)
    key_low = rotary(
        projected[:, HG : 2 * HG].reshape(local_rows, HPG, HD), cosine_table, sine_table
    ).astype(jnp.bfloat16)
    value_low = projected[:, 2 * HG :].astype(jnp.bfloat16)
    packed = jnp.concatenate([key_low.reshape(local_rows, HG), value_low], axis=1)
    packed_all = lax.all_gather(packed, "seq", axis=0, tiled=True)
    all_index, all_segment, all_offset = token_layout(0, all_rows, seq_lengths)
    log_sum, context = attend_forward(
        query_low, token_index, segment, packed_all, all_index, all_segment, block_rows
    )
    head_mask = (group_id < attn_width).astype(jnp.float32)
    ctx_low = (context * head_mask[:, None, None]).astype(jnp.bfloat16).reshape(local_rows, HG)
    attn_out = lax.psum(
        jnp.dot(ctx_low, w_output, preferred_element_type=jnp.float32).astype(jnp.bfloat16), "head"
    ).astype(jnp.float32)
    middle_res = residual + scale_attn[:, None] * attn_out
    ln_two, pull_two = jax.vjp(layer_norm, middle_res, gain_two, bias_two)
    act_two = ln_two.astype(jnp.bfloat16)
    scale_ffn, probs_ffn, picked_ffn = router_scale(act_two, router_ffn, ffn_width)
    pre_act = jnp.dot(act_two, w_up, preferred_element_type=jnp.float32)
    unit_mask = (group_id < ffn_width).astype(jnp.float32)
    hidden_low = (jnp.square(jnp.maximum(pre_act, 0.0)) * unit_mask[:, None]).astype(jnp.bfloat16)
    ffn_out = lax.psum(
        jnp.dot(hidden_low, w_down, preferred_element_type=jnp.float32).astype(jnp.bfloat16), "head"
    ).astype(jnp.float32)
    output = (middle_res + scale_ffn[:, None] * ffn_out).astype(jnp.bfloat16)
    grad_top = cotangent.astype(jnp.float32)
    grad_scale_ffn = jnp.sum(grad_top * ffn_out, axis=1)
    grad_ffn_low = (scale_ffn[:, None] * grad_top).astype(jnp.bfloat16)
    grad_hidden = jnp.dot(grad_ffn_low, w_down.T, preferred_element_type=jnp.float32)
    grad_pre_low = (grad_hidden * unit_mask[:, None] * 2.0 * jnp.maximum(pre_act, 0.0)).astype(
        jnp.bfloat16
    )
    grad_act_two = lax.psum(
        jnp.dot(grad_pre_low, w_up.T, preferred_element_type=jnp.float32).astype(jnp.bfloat16),
        "head",
    ).astype(jnp.float32)
    logit_ffn = router_back(grad_scale_ffn, probs_ffn, picked_ffn)
    grad_act_two = grad_act_two + jnp.dot(logit_ffn, router_ffn.T, precision=PRECISE)
    grad_mid_ln, grad_gain_two, grad_bias_two = pull_two(grad_act_two)
    grad_middle = grad_top + grad_mid_ln
    grad_scale_attn = jnp.sum(grad_middle * attn_out, axis=1)
    grad_attn_low = (scale_attn[:, None] * grad_middle).astype(jnp.bfloat16)
    grad_context = jnp.dot(grad_attn_low, w_output.T, preferred_element_type=jnp.float32)
    grad_out_low = (
        (grad_context * head_mask[:, None]).astype(jnp.bfloat16).reshape(local_rows, HPG, HD)
    )
    delta = jnp.sum(grad_out_low.astype(jnp.float32) * context, axis=2).T
    zero_state = jnp.zeros((local_rows, HPG, HD), jnp.float32)

    def visit_keys(carried, number):
        key_block, value_block, key_index, key_segment = fetch_block(
            packed_all, all_index, all_segment, number, block_rows
        )
        grad_query, grad_key, grad_value = pair_grads(
            query_low,
            grad_out_low,
            log_sum,
            delta,
            token_index,
            segment,
            key_block,
            value_block,
            key_index,
            key_segment,
        )
        return (
            carried + grad_query,
            jnp.concatenate(
                [grad_key.reshape(block_rows, HG), grad_value.reshape(block_rows, HG)], axis=1
            ),
        )

    grad_query_rot, key_terms = lax.scan(visit_keys, zero_state, jnp.arange(blocks))
    summed = lax.psum_scatter(
        key_terms.reshape(all_rows, 2 * HG).astype(jnp.bfloat16),
        "seq",
        scatter_dimension=0,
        tiled=True,
    ).astype(jnp.float32)
    grad_key_rot = summed[:, :HG].reshape(local_rows, HPG, HD)
    grad_value_all = summed[:, HG:].reshape(local_rows, HPG, HD)
    grad_query_low = (
        rotary_back(grad_query_rot, cosine_table, sine_table)
        .astype(jnp.bfloat16)
        .reshape(local_rows, HG)
    )
    grad_key_low = (
        rotary_back(grad_key_rot, cosine_table, sine_table)
        .astype(jnp.bfloat16)
        .reshape(local_rows, HG)
    )
    grad_value_low = grad_value_all.astype(jnp.bfloat16).reshape(local_rows, HG)
    grad_inputs_low = jnp.concatenate([grad_query_low, grad_key_low, grad_value_low], axis=1)
    grad_act_one = lax.psum(
        jnp.dot(grad_inputs_low, w_inputs.T, preferred_element_type=jnp.float32).astype(
            jnp.bfloat16
        ),
        "head",
    ).astype(jnp.float32)
    logit_attn = router_back(grad_scale_attn, probs_attn, picked_attn)
    grad_act_one = grad_act_one + jnp.dot(logit_attn, router_attn.T, precision=PRECISE)
    grad_res_ln, grad_gain_one, grad_bias_one = pull_one(grad_act_one)
    input_grad = grad_middle + grad_res_ln
    grad_router = jnp.concatenate(
        [
            jnp.dot(act_one.astype(jnp.float32).T, logit_attn, precision=PRECISE),
            jnp.dot(act_two.astype(jnp.float32).T, logit_ffn, precision=PRECISE),
        ],
        axis=1,
    ).reshape(-1)
    small_terms = jnp.concatenate(
        [grad_gain_one, grad_bias_one, grad_gain_two, grad_bias_two, grad_router]
    )
    tile_terms = tile_grads(
        slot_order,
        [[act_one, ctx_low, act_two, hidden_low]],
        [[grad_inputs_low, grad_attn_low, grad_pre_low, grad_ffn_low]],
        None,
        [slot_order.shape[0]],
    )[0]
    tile_grad, small_grad = (
        lax.psum_scatter(tile_terms, "seq", scatter_dimension=0, tiled=True),
        lax.psum_scatter(
            small_terms.astype(jnp.bfloat16), "seq", scatter_dimension=0, tiled=True
        ).astype(jnp.float32),
    )
    slots = master.shape[1]
    held = adam_tiles(
        jnp.array([0, 0], jnp.int32),
        slots,
        [[tile_grad]],
        (left_basis[0], right_basis[0]),
        (first_moment[0], second_moment[0], master[0]),
        None,
    )
    small_outs = small_adam(small_grad, small_first, small_second, small_master)
    return (
        output,
        input_grad,
        held[0][None],
        held[1][None],
        held[2][None],
        held[3][None],
        *small_outs,
    )


def solution(mesh):
    return jax.shard_map(
        local_remap if dict(mesh.shape) == {"seq": 8, "head": 4} else local_plain,
        mesh=mesh,
        in_specs=(
            P("seq", None),
            P("seq", None),
            P("seq"),
            P("seq"),
            P(),
            P("head", None),
            P("head", "seq", None, None),
            P("head", "seq", None, None),
            P("head", "seq", None, None),
            P("head", "seq", None, None),
            P("head", "seq", None, None),
            P("seq"),
            P("seq"),
            P("seq"),
        ),
        out_specs=(
            P("seq", None),
            P("seq", None),
            P("head", "seq", None, None),
            P("head", "seq", None, None),
            P("head", "seq", None, None),
            P("head", "seq", None, None),
            P("seq"),
            P("seq"),
            P("seq"),
        ),
        check_vma=False,
    )
```

```python
import functools

import jax
import jax.numpy as jnp
from jax import lax
from jax.experimental import pallas as pl
from jax.experimental.pallas import tpu as pltpu
from jax.sharding import PartitionSpec as P

D = 2048
HD = 128
WIDTHS = 4
TR = 256
TC = 512
TILES = 96
STEP = 10
KB_CAP = 1024
HPG = 4
HG = 512
FG = 2048

PRECISE = lax.Precision.HIGHEST
EPS_NORM = 1e-05
BETA_ONE = 0.95
BETA_TWO = 0.95
ADAM_EPS = 1e-08
DECAY_RATE = 0.01
RATE_TILE = 0.15
RATE_SMALL = 1.0
ROPE_BASE = 10000.0
NEG_FILL = -1e30
SCORE_SCALE = HD ** (-0.5)
F32 = jnp.float32
BF16 = jnp.bfloat16
AXES = ("seq", "head")
VMEM_BIG = 56 << 20
VMEM_ALL = 61 << 20


def nt(a, b):
    return lax.dot_general(a, b, (((1,), (1,)), ((), ())), preferred_element_type=F32)


def nn(a, b):
    return lax.dot_general(a, b, (((1,), (0,)), ((), ())), preferred_element_type=F32)


def tn(a, b):
    return lax.dot_general(a, b, (((0,), (0,)), ((), ())), preferred_element_type=F32)


VM = pl.BlockSpec(memory_space=pltpu.VMEM)
SM = pl.BlockSpec(memory_space=pltpu.SMEM)
HBM = pl.BlockSpec(memory_space=pltpu.MemorySpace.HBM)


def sds(shape, dtype):
    return jax.ShapeDtypeStruct(shape, dtype)


MARK = sds((8, HD), F32)


def params():
    return pltpu.CompilerParams(vmem_limit_bytes=VMEM_BIG)


def cost(flops, nbytes):
    return pl.CostEstimate(flops=int(flops), bytes_accessed=int(nbytes), transcendentals=0)


def flat_call(body, scalars, arrays, outs, scratch=(), flops=0, name=None):
    nbytes = sum(a.size * a.dtype.itemsize for a in arrays)
    nbytes += sum(int(jnp.dtype(o.dtype).itemsize) * o.size for o in outs)
    return pl.pallas_call(
        body,
        out_shape=outs,
        in_specs=[SM] + [VM] * len(arrays),
        out_specs=[VM] * len(outs),
        scratch_shapes=list(scratch),
        compiler_params=params(),
        cost_estimate=cost(flops, nbytes),
        name=name,
    )(scalars, *arrays)


def rows_of(ref, index, rows):
    return ref[pl.ds(pl.multiple_of(index * rows, rows), rows), :]


def put_rows(ref, index, rows, value):
    ref[pl.ds(pl.multiple_of(index * rows, rows), rows), :] = value


def store_pieces(acc_ref, piece, rows, outs):
    outs[0][...] = rows_of(acc_ref, piece, rows)
    for k in range(1, 4):
        outs[k][...] = rows_of(acc_ref, piece ^ k, rows).astype(BF16)


def row_stats(values):
    center = values - jnp.mean(values, axis=1, keepdims=True)
    rstd = lax.rsqrt(jnp.mean(center * center, axis=1, keepdims=True) + EPS_NORM)
    return center * rstd, rstd


def route_level(logits, width_col):
    lane = lax.broadcasted_iota(jnp.int32, logits.shape, 1)
    live = lane < WIDTHS
    top = jnp.max(jnp.where(live, logits, NEG_FILL), axis=1, keepdims=True)
    raised = jnp.where(live, jnp.exp(jnp.where(live, logits, NEG_FILL) - top), 0.0)
    probs = raised / jnp.sum(raised, axis=1, keepdims=True)
    picked = (lane == width_col - 1).astype(F32)
    chosen = jnp.sum(probs * picked, axis=1, keepdims=True)
    return WIDTHS * chosen, WIDTHS * chosen * (picked - probs)


def split_dot(values, right_low):
    high = values.astype(BF16)
    rest = (values - high.astype(F32)).astype(BF16)
    return nn(high, right_low) + nn(rest, right_low)


def norm_one_body(sc, tok, gain, bias, router, width, a1, a1p, tokp, rap, coefp, ra_s, coef_s):
    rows = a1p.shape[0]
    piece = sc[1]
    xhat, _ = row_stats(tok[...].astype(F32))
    low = (xhat * gain[...] + bias[...]).astype(BF16)
    a1[...] = low
    scale, coef = route_level(nn(low, router[...]), width[...])
    ra_s[...] = scale
    coef_s[...] = coef
    a1p[...] = rows_of(a1, piece, rows)
    tokp[...] = rows_of(tok, piece, rows)
    rap[...] = rows_of(ra_s, piece, rows)
    coefp[...] = rows_of(coef_s, piece, rows)


def turn(values, cosine, signed_sine):
    return values * cosine + pltpu.roll(values, HD // 2, 1) * signed_sine


def turn_back(values, cosine, signed_sine):
    return values * cosine - pltpu.roll(values, HD // 2, 1) * signed_sine


def project_body(sc, a1, weights, cosine, sine, o0, o1, o2, o3, heads_s):
    step = pl.program_id(0)
    spot = sc[0]
    out = nn(a1[...], weights[...].reshape(D, HG))
    plain = step == 2
    cos_v = jnp.where(plain, 1.0, cosine[0])
    sin_v = jnp.where(plain, 0.0, sine[0])
    for head in range(HPG):
        heads_s[head] = turn(out[:, head * HD : (head + 1) * HD], cos_v, sin_v).astype(BF16)
    for k, ref in enumerate((o0, o1, o2, o3)):
        ref[0] = heads_s[spot ^ k]


def attend_body(
    sc, start_col, r0, r1, r2, r3, c0, c1, c2, c3,
    o0, o1, o2, o3, ctx, lse, q_all, k_all, v_all, m_s, l_s, acc_s,
):
    spot, core = sc[0], sc[2]
    rows = r0.shape[1]

    def block_of(source, side):
        return (2 * (source // 2) + side) * 2 + source % 2

    for k, (own, other) in enumerate(((r0, c0), (r1, c1), (r2, c2), (r3, c3))):
        mine = block_of(spot ^ k, core)
        theirs = block_of(spot ^ k, 1 - core)
        q_all[k] = own[0]
        k_all[mine] = own[1]
        v_all[mine] = own[2]
        k_all[theirs] = other[1]
        v_all[theirs] = other[2]

    def per_query(k, unused):
        block = block_of(spot ^ k, core)
        query = q_all[k]
        first = start_col[block]
        where_q = block * rows + lax.broadcasted_iota(jnp.int32, (rows, rows), 0)
        lane = lax.broadcasted_iota(jnp.int32, (rows, rows), 1)
        m_s[...] = jnp.full(m_s.shape, NEG_FILL, F32)
        l_s[...] = jnp.zeros(l_s.shape, F32)
        acc_s[...] = jnp.zeros(acc_s.shape, F32)

        def per_key(kb, unused_two):
            where_k = kb * rows + lane
            scores = nt(query, k_all[kb]) * SCORE_SCALE
            scores = jnp.where((where_k <= where_q) & (where_k >= first), scores, NEG_FILL)
            old = m_s[...]
            new = jnp.maximum(old, jnp.max(scores, axis=1, keepdims=True))
            weight = jnp.exp(scores - new)
            fade = jnp.exp(old - new)
            l_s[...] = l_s[...] * fade + jnp.sum(weight, axis=1, keepdims=True)
            acc_s[...] = acc_s[...] * fade + nn(weight.astype(BF16), v_all[kb])
            m_s[...] = new
            return 0

        lax.fori_loop(sc[4 + block], block + 1, per_key, 0)
        ctx[k] = acc_s[...] / l_s[...]
        lse[k] = m_s[...] + jnp.log(l_s[...])
        return 0

    lax.fori_loop(0, 4, per_query, 0)
    for k, ref in enumerate((o0, o1, o2, o3)):
        ref[...] = ctx[k].astype(BF16)


def output_body(sc, r0, r1, r2, r3, width, weights, cb, o0, o1, o2, o3, acc_s):
    spot, piece, group = sc[0], sc[1], sc[3]
    keep = width[...] > group
    for k, ref in enumerate((r0, r1, r2, r3)):
        at = pl.ds(pl.multiple_of((spot ^ k) * HD, HD), HD)
        cb[:, at] = jnp.where(keep, ref[...], jnp.zeros_like(ref[...]))
    for col in range(D // TC):
        acc_s[:, col * TC : (col + 1) * TC] = nn(cb[:, :TR], weights[0, col]) + nn(
            cb[:, TR:], weights[1, col]
        )
    store_pieces(acc_s, piece, o1.shape[0], (o0, o1, o2, o3))


def norm_two_body(sc, own, r1, r2, r3, tokp, rap, gain, bias, attn, h1, a2p):
    total = own[...] + r1[...].astype(F32) + r2[...].astype(F32) + r3[...].astype(F32)
    attn[...] = total
    middle = tokp[...].astype(F32) + rap[...] * total
    h1[...] = middle
    xhat, _ = row_stats(middle)
    a2p[...] = (xhat * gain[...] + bias[...]).astype(BF16)


def ffn_body(
    sc, p0, p1, p2, p3, dy, width, router, w_up, w_down,
    a2, act, relu, gffn, dlog, rfp, o0, o1, o2, o3, acc_s, coef_s, rf_s,
):
    step = pl.program_id(0)
    piece, group = sc[1], sc[3]
    rows = p0.shape[0]

    @pl.when(step == 0)
    def _():
        for k, ref in enumerate((p0, p1, p2, p3)):
            put_rows(a2, piece ^ k, rows, ref[...])
        scale, coef = route_level(nn(a2[...], router[...]), width[...])
        rf_s[...] = scale
        coef_s[...] = coef
        gffn[...] = (scale * dy[...].astype(F32)).astype(BF16)
        rfp[...] = rows_of(rf_s, piece, rows)

    up = jnp.maximum(nn(a2[...], w_up[...].reshape(D, TC)), 0.0)
    up = jnp.where(width[...] > group, up, 0.0)
    relu[...] = up.astype(BF16)
    low = (up * up).astype(BF16)
    act[...] = low
    for col in range(D // TC):
        at = slice(col * TC, (col + 1) * TC)
        part = nn(low[:, :TR], w_down[0, col]) + nn(low[:, TR:], w_down[1, col])

        @pl.when(step == 0)
        def _(part=part, at=at):
            acc_s[:, at] = part

        @pl.when(step > 0)
        def _(part=part, at=at):
            acc_s[:, at] += part

    @pl.when(step == pl.num_programs(0) - 1)
    def _():
        drf = jnp.sum(acc_s[...] * dy[...].astype(F32), axis=1, keepdims=True)
        dlog[...] = drf * coef_s[...]
        store_pieces(acc_s, piece, rows, (o0, o1, o2, o3))


def ffn_back_body(sc, gffn, relu, dlog, router_t, w_up, w_down, gpre, o0, o1, o2, o3, acc_s):
    step = pl.program_id(0)
    piece = sc[1]
    halves = []
    for row in range(2):
        total = nt(gffn[:, :TC], w_down[row, 0])
        for col in range(1, D // TC):
            total += nt(gffn[:, col * TC : (col + 1) * TC], w_down[row, col])
        halves.append(total)
    gact = jnp.concatenate(halves, axis=1)
    low = (gact * 2.0 * relu[...].astype(F32)).astype(BF16)
    gpre[...] = low
    part = nt(low, w_up[...].reshape(D, TC))

    @pl.when(step == 0)
    def _():
        acc_s[...] = part + split_dot(dlog[...], router_t[...])

    @pl.when(step > 0)
    def _():
        acc_s[...] += part

    @pl.when(step == pl.num_programs(0) - 1)
    def _():
        store_pieces(acc_s, piece, o1.shape[0], (o0, o1, o2, o3))


def norm_grad(grad, values, gain):
    xhat, rstd = row_stats(values)
    scaled = grad * gain
    inner = scaled - jnp.mean(scaled, axis=1, keepdims=True)
    inner = inner - xhat * jnp.mean(scaled * xhat, axis=1, keepdims=True)
    gain_grad = jnp.sum(grad * xhat, axis=0, keepdims=True)
    return inner * rstd, gain_grad, jnp.sum(grad, axis=0, keepdims=True)


def norm_two_back_body(
    sc, own, r1, r2, r3, h1, attn, dyp, rap, coefp, gain, dh1, gattnp, dlogp, ggain, gbias
):
    grad = own[...] + r1[...].astype(F32) + r2[...].astype(F32) + r3[...].astype(F32)
    back, gain_grad, bias_grad = norm_grad(grad, h1[...], gain[...])
    middle = dyp[...].astype(F32) + back
    dh1[...] = middle
    gattnp[...] = (rap[...] * middle).astype(BF16)
    dra = jnp.sum(middle * attn[...], axis=1, keepdims=True)
    dlogp[...] = dra * coefp[...]
    ggain[...] = gain_grad
    gbias[...] = bias_grad


def gout_body(sc, p0, p1, p2, p3, width, weights, gattn, o0, o1, o2, o3, heads_s):
    spot, piece, group = sc[0], sc[1], sc[3]
    rows = p0.shape[0]
    for k, ref in enumerate((p0, p1, p2, p3)):
        put_rows(gattn, piece ^ k, rows, ref[...])
    keep = width[...] > group
    for row in range(2):
        total = nt(gattn[:, :TC], weights[row, 0])
        for col in range(1, D // TC):
            total += nt(gattn[:, col * TC : (col + 1) * TC], weights[row, col])
        low = jnp.where(keep, total, 0.0).astype(BF16)
        heads_s[2 * row] = low[:, :HD]
        heads_s[2 * row + 1] = low[:, HD:]
    for k, ref in enumerate((o0, o1, o2, o3)):
        ref[...] = heads_s[spot ^ k]


def attend_back_body(
    sc, start_row, cosine, sine, q_all, k_all, v_all, ctx, lse, g0, g1, g2, g3,
    gq, own, other, g_s, gk_s, gv_s, acc_s,
):
    spot, core = sc[0], sc[2]
    rows = g0.shape[0]

    def block_of(source, side):
        return (2 * (source // 2) + side) * 2 + source % 2

    for k, ref in enumerate((g0, g1, g2, g3)):
        g_s[k] = ref[...]
    gk_s[...] = jnp.zeros(gk_s.shape, F32)
    gv_s[...] = jnp.zeros(gv_s.shape, F32)

    def per_query(k, unused):
        block = block_of(spot ^ k, core)
        query = q_all[k]
        grad = g_s[k]
        shared = grad.astype(F32) * ctx[k]
        delta = lax.dot_general(
            jnp.ones((8, HD), F32), shared, (((1,), (1,)), ((), ())),
            precision=PRECISE, preferred_element_type=F32,
        )[:1]
        first = start_row[block]
        level = lse[k]
        where_q = block * rows + lax.broadcasted_iota(jnp.int32, (rows, rows), 1)
        line = lax.broadcasted_iota(jnp.int32, (rows, rows), 0)
        acc_s[...] = jnp.zeros(acc_s.shape, F32)

        def per_key(kb, unused_two):
            where_k = kb * rows + line
            keys = k_all[kb]
            allowed = (where_k <= where_q) & (where_k >= first)
            scores = nt(keys, query) * SCORE_SCALE
            prob = jnp.where(allowed, jnp.exp(jnp.where(allowed, scores - level, 0.0)), 0.0)
            gprob = nt(v_all[kb], grad)
            graw = (prob * (gprob - delta) * SCORE_SCALE).astype(BF16)
            gv_s[kb] += nn(prob.astype(BF16), grad)
            gk_s[kb] += nn(graw, query)
            acc_s[...] += tn(graw, keys)
            return 0

        lax.fori_loop(sc[4 + block], block + 1, per_key, 0)
        gq[k] = turn_back(acc_s[...], cosine[block], sine[block]).astype(BF16)
        return 0

    lax.fori_loop(0, 4, per_query, 0)
    for k in range(4):
        mine = block_of(spot ^ k, core)
        theirs = block_of(spot ^ k, 1 - core)
        own[k, 0] = gk_s[mine]
        own[k, 1] = gv_s[mine]
        other[k, 0] = gk_s[theirs].astype(BF16)
        other[k, 1] = gv_s[theirs].astype(BF16)


def key_merge_body(sc, gq, own, got, cosine, sine, o0, o1, o2, o3):
    spot, core = sc[0], sc[2]
    for k, ref in enumerate((o0, o1, o2, o3)):
        source = spot ^ k
        block = (2 * (source // 2) + core) * 2 + source % 2
        ref[0] = gq[k]
        gk = own[k, 0] + got[k, 0].astype(F32)
        ref[1] = turn_back(gk, cosine[block], sine[block]).astype(BF16)
        ref[2] = (own[k, 1] + got[k, 1].astype(F32)).astype(BF16)


def gather_input_body(sc, r0, r1, r2, r3, gin):
    spot = sc[0]
    for k, ref in enumerate((r0, r1, r2, r3)):
        for member in range(3):
            at = pl.ds(pl.multiple_of(member * HG + (spot ^ k) * HD, HD), HD)
            gin[:, at] = ref[member]


def input_back_body(sc, gin, weights, f1, f2, f3, o0, o1, o2, o3, acc_s):
    piece = sc[1]
    rows = o0.shape[0]
    wide = weights.shape[1] * TR
    total = nt(gin[:, :HG], weights[0].reshape(wide, TC))
    for member in range(1, 3):
        total += nt(gin[:, member * HG : (member + 1) * HG], weights[member].reshape(wide, TC))
    acc_s[...] = total
    o0[...] = rows_of(acc_s, piece, rows)
    for k, (ref, passed) in enumerate(((o1, f1), (o2, f2), (o3, f3))):
        ref[0] = rows_of(acc_s, piece ^ (k + 1), rows).astype(BF16)
        ref[1] = passed[...]


def norm_one_back_body(
    sc, own, r1, r2, r3, ffn, tokp, h1, rfp, dh1, dlogp, router_t, gain, both, ggain, gbias
):
    grad = own[...] + r1[0].astype(F32) + r2[0].astype(F32) + r3[0].astype(F32)
    grad = grad + split_dot(dlogp[...], router_t[...])
    back, gain_grad, bias_grad = norm_grad(grad, tokp[...].astype(F32), gain[...])
    both[0] = (dh1[...] + back).astype(BF16)
    total = ffn[...] + r1[1].astype(F32) + r2[1].astype(F32) + r3[1].astype(F32)
    both[1] = (h1[...] + rfp[...] * total).astype(BF16)
    ggain[...] = gain_grad
    gbias[...] = bias_grad


def join_body(sc, b0, b1, b2, b3, whole):
    piece = sc[1]
    rows = b0.shape[1]
    for k, ref in enumerate((b0, b1, b2, b3)):
        at = pl.ds(pl.multiple_of((piece ^ k) * rows, rows), rows)
        whole[:, at, :] = ref[...]


def place_tiles(ids, chunks, held, waits=()):
    count = sum(c.shape[0] for c in chunks)

    def body(ids_ref, *refs):
        parts = refs[: len(chunks)]
        out = refs[len(chunks) + len(waits) + (0 if held is None else 1)]
        mark, buf, in_sems, out_sems = refs[-4:]
        mark[...] = jnp.zeros_like(mark)
        places = [(part, i) for part in parts for i in range(part.shape[0])]
        arrive = [
            pltpu.make_async_copy(part.at[i], buf.at[at], in_sems.at[at])
            for at, (part, i) in enumerate(places)
        ]
        leave = [
            pltpu.make_async_copy(buf.at[at], out.at[ids_ref[at]], out_sems.at[at])
            for at in range(count)
        ]
        for copy in arrive:
            copy.start()
        for came, go in zip(arrive, leave):
            came.wait()
            go.start()
        for copy in leave:
            copy.wait()

    extra = [] if held is None else [held]
    return pl.pallas_call(
        body,
        out_shape=[sds((TILES, TR, TC), BF16), MARK],
        in_specs=[SM] + [HBM] * (len(chunks) + len(extra) + len(waits)),
        out_specs=[HBM, VM],
        scratch_shapes=[
            pltpu.VMEM((count, TR, TC), BF16),
            pltpu.SemaphoreType.DMA((count,)),
            pltpu.SemaphoreType.DMA((count,)),
        ],
        compiler_params=params(),
        input_output_aliases={} if held is None else {1 + len(chunks): 0},
        cost_estimate=cost(0, 2 * count * TR * TC * 2),
        name="place_tiles",
    )(ids, *chunks, *extra, *waits)


def tile_kind(tile):
    kind = (tile >= 24).astype(jnp.int32) + (tile >= 32).astype(jnp.int32)
    kind = kind + (tile >= 64).astype(jnp.int32)
    base = jnp.where(kind == 1, 24, jnp.where(kind == 2, 32, 64))
    local = tile - base
    left = jnp.where(kind == 0, tile % 8, local // 4)
    right = jnp.where(kind == 0, tile // 8, local % 4)
    return kind, left, right


def tile_grads(ids, lefts, rights, added, outs_of, waits=()):
    count = ids.shape[0]
    parts = len(lefts)
    rows = lefts[0][0].shape[0]
    flat = [a for part in lefts for a in part] + [a for part in rights for a in part]

    def fetch(ids_ref, step, slot, refs, lbuf, rbuf, sems):
        kind, left, right = tile_kind(ids_ref[step])
        for which in range(4):

            @pl.when(kind == which)
            def _(which=which):
                for part in range(parts):
                    src = refs[part * 4 + which]
                    at = pl.ds(pl.multiple_of(left * TR, TR), TR)
                    pltpu.make_async_copy(
                        src.at[:, at], lbuf.at[slot, pl.ds(part * rows, rows)], sems.at[slot, part]
                    ).start()
                    src = refs[(parts + part) * 4 + which]
                    at = pl.ds(pl.multiple_of(right * TC, TC), TC)
                    pltpu.make_async_copy(
                        src.at[:, at],
                        rbuf.at[slot, pl.ds(part * rows, rows)],
                        sems.at[slot, parts + part],
                    ).start()

    def body(ids_ref, *refs):
        sources = refs[: len(flat)]
        at = len(flat)
        plus = None
        if added is not None:
            plus = refs[at]
            at += 1
        at += len(waits)
        outs = refs[at : at + len(outs_of)]
        mark, lbuf, rbuf, sems = refs[at + len(outs_of) :]
        mark[...] = jnp.zeros_like(mark)
        step = pl.program_id(0)
        slot = lax.rem(step, 2)

        @pl.when(step == 0)
        def _():
            fetch(ids_ref, 0, 0, sources, lbuf, rbuf, sems)

        @pl.when(step + 1 < count)
        def _():
            fetch(ids_ref, step + 1, 1 - slot, sources, lbuf, rbuf, sems)

        for part in range(parts):
            pltpu.make_async_copy(
                sources[0].at[:, :TR], lbuf.at[slot, pl.ds(part * rows, rows)], sems.at[slot, part]
            ).wait()
            pltpu.make_async_copy(
                sources[parts * 4 + 1].at[:, :TC],
                rbuf.at[slot, pl.ds(part * rows, rows)],
                sems.at[slot, parts + part],
            ).wait()
        total = tn(lbuf[slot], rbuf[slot])
        if plus is not None:
            total = total + plus[0].astype(F32)
        low = total.astype(BF16)
        if len(outs_of) == 1:
            outs[0][0] = low
        else:
            begin = 0
            for ref, size in zip(outs, outs_of):

                @pl.when((step >= begin) & (step < begin + size))
                def _(ref=ref):
                    ref[0] = low

                begin += size

    specs_out = []
    begin = 0
    for size in outs_of:
        specs_out.append(
            pl.BlockSpec(
                (1, TR, TC),
                lambda i, ids_ref, begin=begin, size=size: (jnp.clip(i - begin, 0, size - 1), 0, 0),
            )
        )
        begin += size
    plus_in = [] if added is None else [added]
    return pl.pallas_call(
        body,
        out_shape=[sds((size, TR, TC), BF16) for size in outs_of] + [MARK],
        grid_spec=pltpu.PrefetchScalarGridSpec(
            num_scalar_prefetch=1,
            grid=(count,),
            in_specs=[HBM] * len(flat)
            + [pl.BlockSpec((1, TR, TC), lambda i, ids_ref: (i, 0, 0))] * len(plus_in)
            + [HBM] * len(waits),
            out_specs=specs_out + [pl.BlockSpec((8, HD), lambda i, ids_ref: (0, 0))],
            scratch_shapes=[
                pltpu.VMEM((2, parts * rows, TR), BF16),
                pltpu.VMEM((2, parts * rows, TC), BF16),
                pltpu.SemaphoreType.DMA((2, 2 * parts)),
            ],
        ),
        compiler_params=pltpu.CompilerParams(vmem_limit_bytes=VMEM_ALL),
        cost_estimate=cost(
            2 * count * parts * rows * TR * TC, count * (parts * rows * (TR + TC) * 2 + TR * TC * 2)
        ),
        name="tile_grads",
    )(ids, *flat, *plus_in, *waits)


def adam_tile(grad, left, right, first, second, master):
    left_low = left.astype(BF16)
    right_low = right.astype(BF16)
    turned = nn(tn(left_low, grad.astype(BF16)).astype(BF16), right_low)
    new_first = BETA_ONE * first + (1.0 - BETA_ONE) * turned
    new_second = BETA_TWO * second + (1.0 - BETA_TWO) * turned * turned
    step = (
        new_first
        / (1.0 - BETA_ONE**STEP)
        / (jnp.sqrt(new_second / (1.0 - BETA_TWO**STEP)) + ADAM_EPS)
    )
    back = nt(nn(left_low, step.astype(BF16)).astype(BF16), right_low)
    return new_first, new_second, master - RATE_TILE * (back + DECAY_RATE * master)


def adam_tiles(slot_list, flows, bases, state, held, waits=()):
    steps = slot_list.shape[0]

    def body(sc_ref, *refs):
        grads = refs[: len(flows)]
        left, right, first, second, master = refs[len(flows) : len(flows) + 5]
        o_first, o_second, o_master, o_low, mark = refs[-5:]
        mark[...] = jnp.zeros_like(mark)
        total = grads[0][0].astype(F32)
        for ref in grads[1:]:
            total = total + ref[0].astype(F32)
        new_first, new_second, new_master = adam_tile(
            total, left[0], right[0], first[0], second[0], master[0]
        )
        o_first[0] = new_first
        o_second[0] = new_second
        o_master[0] = new_master
        o_low[0] = new_master.astype(BF16)

    def at_slot(shape):
        return pl.BlockSpec((1,) + shape, lambda i, sc_ref: (sc_ref[i], 0, 0))

    slots = state[0].shape[0]
    shapes = [(TR, TC)] * 4
    types = [F32, F32, F32, BF16]
    extra = [] if held is None else list(held)
    base = 1 + len(flows) + 5
    return pl.pallas_call(
        body,
        out_shape=[sds((slots,) + s, t) for s, t in zip(shapes, types)] + [MARK],
        grid_spec=pltpu.PrefetchScalarGridSpec(
            num_scalar_prefetch=1,
            grid=(steps,),
            in_specs=[pl.BlockSpec((1, TR, TC), lambda i, sc_ref: (i, 0, 0))] * len(flows)
            + [at_slot((TR, TR)), at_slot((TC, TC))]
            + [at_slot((TR, TC))] * 3
            + [HBM] * (len(extra) + len(waits)),
            out_specs=[at_slot(s) for s in shapes]
            + [pl.BlockSpec((8, HD), lambda i, sc_ref: (0, 0))],
        ),
        input_output_aliases={base + i: i for i in range(len(extra))},
        compiler_params=pltpu.CompilerParams(vmem_limit_bytes=VMEM_ALL),
        cost_estimate=cost(steps * 8 * TR * TC * TC, steps * 5 * TR * TC * 4),
        name="adam_tiles",
    )(slot_list, *flows, *bases, *state, *extra, *waits)


def small_adam(grad, first, second, master):
    new_first = BETA_ONE * first + (1.0 - BETA_ONE) * grad
    new_second = BETA_TWO * second + (1.0 - BETA_TWO) * grad * grad
    step = (
        new_first
        / (1.0 - BETA_ONE**STEP)
        / (jnp.sqrt(new_second / (1.0 - BETA_TWO**STEP)) + ADAM_EPS)
    )
    return new_first, new_second, master - RATE_SMALL * (step + DECAY_RATE * master)


def signed_tables(places):
    middle = HD // 2
    frequency = ROPE_BASE ** (-(jnp.arange(middle, dtype=F32) * 2.0) / HD)
    angles = places.astype(F32)[:, None] * frequency[None, :]
    cosine = jnp.cos(angles)
    sine = jnp.sin(angles)
    return (
        jnp.concatenate([cosine, cosine], axis=1),
        jnp.concatenate([-sine, sine], axis=1),
    )


def token_layout(first_index, local_rows, seq_lengths):
    places = first_index + jnp.arange(local_rows, dtype=jnp.int32)
    number = seq_lengths.shape[0]
    below = jnp.arange(number)[None, :] <= jnp.arange(number)[:, None]
    bounds = jnp.sum(jnp.where(below, seq_lengths[None, :], 0), axis=1)
    passed = places[:, None] >= bounds[None, :]
    segment = jnp.sum(passed.astype(jnp.int32), axis=1)
    offset = places - jnp.sum(jnp.where(passed, seq_lengths[None, :], 0), axis=1)
    return (places, segment, offset)


def moves(target):
    pairs = []
    for z in range(4):
        for y in range(2):
            for x in range(2):
                for c in range(2):
                    to = target(z, y, x, c)
                    if to is not None:
                        a, b, e, f = to
                        pairs.append((8 * z + 4 * y + 2 * x + c, 8 * a + 4 * b + 2 * e + f))
    return pairs


def only(condition, target):
    return lambda z, y, x, c: target(z, y, x, c) if condition(z, y, x, c) else None


def flip(dz=0, dy=0, dx=0, dc=0):
    return lambda z, y, x, c: (z ^ dz, y ^ dy, x ^ dx, c ^ dc)


def own_group(z, y, x, c):
    return c == z % 2


def foreign(z, y, x, c):
    return c != z % 2


def send(value, target):
    return lax.ppermute(value, AXES, moves(target))


MEMBERS = (None, flip(dz=1), flip(dx=1), flip(dz=1, dx=1))
HEADMATES = (None, flip(dy=1), flip(dz=2), flip(dz=2, dy=1))


def scatter_pieces(pieces):
    return [pieces[0]] + [send(pieces[k], MEMBERS[k]) for k in range(1, 4)]


def share_piece(piece):
    return [piece] + [send(piece, MEMBERS[k]) for k in range(1, 4)]


def swap_heads(blocks):
    return [blocks[0]] + [send(blocks[k], HEADMATES[k]) for k in range(1, 4)]


def after(value, *others):
    return lax.optimization_barrier((value,) + others)[0]


def tied(values, done):
    return list(lax.optimization_barrier(tuple(values) + tuple(done))[: len(values)])


def small_step(values, bit, target):
    other = send(values, target)
    return jnp.where(
        bit == 0, jnp.concatenate([values, other]), jnp.concatenate([other, values])
    )


def local_remap(
    tokens, cotangent, attn_width, ffn_width, seq_lengths, tile_order, master, first_moment,
    second_moment, left_basis, right_basis, small_master, small_first, small_second,
):
    rows = tokens.shape[0]
    piece_rows = rows // 4
    s = lax.axis_index("seq")
    h = lax.axis_index("head")
    z, y, x, c = s // 2, s % 2, h // 2, h % 2
    zp, zh = z % 2, z // 2
    mine = c == zp
    group = 2 * x + zp
    spot = 2 * zh + y
    block = (2 * zh + c) * 2 + y

    y_move, h_move, c_move = flip(dy=1), flip(dz=2), flip(dc=1)

    slots = master.shape[1]
    part = slots // 4
    to_pair = only(own_group, flip(dz=1))
    near_move = lambda z, y, x, c: (z, y, x, 1 - c) if c == z % 2 else (z ^ 1, y, x, c)
    far_move = lambda z, y, x, c: (z ^ 2, y, x, 1 - c) if c == z % 2 else (z ^ 3, y, x, c)
    low = [master[0, i * part : (i + 1) * part].astype(BF16) for i in range(4)]
    near, far = [send(low[0], near_move)], [send(low[0], far_move)]
    order = tile_order[0]
    order_got = send(order, c_move)
    small_all = small_step(small_master.astype(BF16), y, y_move)
    wid = jnp.stack([attn_width, ffn_width])
    wid_got = send(wid, to_pair)
    near[0], order_got, small_all, low1, low2, low3, wid, wid_got = tied(
        [near[0], order_got, small_all] + low[1:] + [wid, wid_got], []
    )
    order = jnp.where(mine, order, order_got)
    base = jnp.where(mine, s ^ 2, s)
    base_there = jnp.where(mine, s, s ^ 2)

    def ids_of(*chunks):
        return jnp.concatenate(
            [
                lax.dynamic_slice_in_dim(order, (o ^ hop) * slots + i * part, part, 0)
                for o in (base, base_there)
                for hop, i in chunks
            ]
        )

    def by_kind(row):
        place = jnp.arange(slots, dtype=jnp.int32)
        key = jnp.where(row < FFN_TILE, slots, 0) + place
        rank = jnp.sum((key[:, None, :] < key[:, :, None]).astype(jnp.int32), axis=2)
        spot_of = rank[:, :, None] == place
        return jnp.sum(jnp.where(spot_of, row[:, :, None], 0), axis=1), jnp.sum(
            jnp.where(spot_of, place[:, None], 0), axis=1
        )

    sorted_order = by_kind(order.reshape(-1, slots))[0].reshape(-1)
    own_row = lax.dynamic_slice_in_dim(tile_order[0], s * slots, slots, 0)
    own_slots = by_kind(own_row[None])[1][0]
    enough = jnp.min(
        jnp.sum(
            (jnp.stack([tile_order[0], order_got]).reshape(-1, slots) >= FFN_TILE).astype(jnp.int32),
            axis=1,
        )
    )
    enough = jnp.full((HD,), enough, jnp.int32)
    enough = jnp.minimum(enough, send(enough, flip(dx=1)))
    near_y, far_y = [send(near[0], y_move)], []
    near.append(send(low1, near_move))
    small_all = small_step(small_all, zp, flip(dz=1))
    low23 = jnp.concatenate([low2, low3])
    near[0], near[1], far[0], near_y[0], small_all, low1, low2, low3, low23, enough = tied(
        [near[0], near[1], far[0], near_y[0], small_all, low1, low2, low3, low23, enough], []
    )
    far.append(send(low1, far_move))
    near_y.append(send(near[1], y_move))
    far_y.append(send(far[0], y_move))
    near23 = send(low23, near_move)
    small_all = small_step(small_all, zh, h_move)
    first = jnp.concatenate([near[0], near_y[0], far[0]])
    all_rows = rows * lax.axis_size("seq")
    blocks = all_rows // rows
    places, _, offset = token_layout(0, all_rows, seq_lengths)
    start = places - offset
    first_block = start.reshape(blocks, rows)[:, 0] // rows
    cosine, sine = signed_tables(offset)
    cosine, sine = cosine.reshape(blocks, rows, HD), sine.reshape(blocks, rows, HD)
    scalars = jnp.concatenate(
        [jnp.stack([spot, group, c, group]).astype(jnp.int32), first_block.astype(jnp.int32)]
    )

    start_col, start_row = start.reshape(blocks, rows, 1), start.reshape(blocks, 1, rows)
    near[1], near23, far[1], near_y[1], far_y[0], low2, low3, small_all, first, cosine, sine, tok = tied(
        [near[1], near23, far[1], near_y[1], far_y[0], low2, low3, small_all, first]
        + [cosine, sine, tokens],
        [],
    )
    near += [near23[:part], near23[part:]]
    far.append(send(low2, far_move))
    near_y.append(send(near[2], y_move))
    far_y.append(send(far[1], y_move))
    first_there = send(first, c_move)
    tok_got = send(tok, to_pair)
    second = jnp.concatenate([near[1], near_y[1], far_y[0], far[1]])
    near[2], near[3], far[2], near_y[2], far_y[1], low3, small_all, first, first_there, second, tok, tok_got = tied(
        [near[2], near[3], far[2], near_y[2], far_y[1], low3, small_all, first, first_there]
        + [second, tok, tok_got],
        [],
    )
    far.append(send(low3, far_move))
    near_y.append(send(near[3], y_move))
    far_y.append(send(far[2], y_move))
    second_there = send(second, c_move)
    third = jnp.concatenate([near[2], near_y[2], far_y[1], far[2]])
    third_there = send(third, c_move)
    tiles, mark_one = place_tiles(ids_of((0, 0), (1, 0), (4, 0)), [first, first_there], None)
    tok = jnp.where(mine, tok, tok_got)
    widths = jnp.where(mine, wid, wid_got)
    width_a, width_f = widths[0][:, None], widths[1][:, None]
    gains = small_all[: 4 * D].astype(F32).reshape(4, 1, D)
    gain_one, bias_one, gain_two, bias_two = gains[0], gains[1], gains[2], gains[3]
    routers = small_all[4 * D :].reshape(D, 2 * WIDTHS)
    pad = ((0, 0), (0, HD - WIDTHS))
    router_a = jnp.pad(routers[:, :WIDTHS], pad)
    router_f = jnp.pad(routers[:, WIDTHS:], pad)
    router_ft, router_at = router_f.T, router_a.T
    a1, a1p, tokp, rap, coefp = flat_call(
        norm_one_body,
        scalars,
        [tok, gain_one, bias_one, router_a, width_a],
        [
            sds((rows, D), BF16),
            sds((piece_rows, D), BF16),
            sds((piece_rows, D), BF16),
            sds((piece_rows, 1), F32),
            sds((piece_rows, HD), F32),
        ],
        [pltpu.VMEM((rows, 1), F32), pltpu.VMEM((rows, HD), F32)],
        name="norm_one",
    )

    tiles, mark_two = place_tiles(
        ids_of((0, 1), (1, 1), (5, 0), (4, 1)), [second, second_there], tiles, [mark_one]
    )
    near[3], far[3], near_y[3], far_y[2], third, third_there, mark_two, a1, router_ft, router_at = tied(
        [near[3], far[3], near_y[3], far_y[2], third, third_there, mark_two, a1]
        + [router_ft, router_at],
        [],
    )
    far_y.append(send(far[3], y_move))
    fourth = jnp.concatenate([near[3], near_y[3], far_y[2], far[3]])
    fourth_there = send(fourth, c_move)
    tiles, mark_three = place_tiles(
        ids_of((0, 2), (1, 2), (5, 1), (4, 2)), [third, third_there], tiles, [mark_two]
    )
    far_y[3], fourth, fourth_there, mark_three = tied(
        [far_y[3], fourth, fourth_there, mark_three], []
    )
    fifth_there = send(far_y[3], c_move)
    tiles, _ = place_tiles(
        ids_of((0, 3), (1, 3), (5, 2), (4, 3)), [fourth, fourth_there], tiles, [mark_three]
    )
    tiles, _ = place_tiles(ids_of((5, 3)), [far_y[3], fifth_there], tiles)
    by_row = tiles.reshape(TILES // 4, 4, TR, TC)
    by_map = tiles.reshape(TILES // 8, 8, TR, TC)

    table = pl.BlockSpec((1, rows, HD), lambda i, sc: (sc[12], 0, 0))
    sent = pl.pallas_call(
        project_body,
        out_shape=[sds((3, rows, HD), BF16)] * 4,
        grid_spec=pltpu.PrefetchScalarGridSpec(
            num_scalar_prefetch=1,
            grid=(3,),
            in_specs=[
                pl.BlockSpec((rows, D), lambda i, sc: (0, 0)),
                pl.BlockSpec((1, 8, TR, TC), lambda i, sc: (i, 0, 0, 0)),
                table,
                table,
            ],
            out_specs=[pl.BlockSpec((1, rows, HD), lambda i, sc: (i, 0, 0))] * 4,
            scratch_shapes=[pltpu.VMEM((HPG, rows, HD), BF16)],
        ),
        compiler_params=params(),
        cost_estimate=cost(2 * rows * D * 3 * HG, 3 * D * HG * 2 + rows * D * 2),
        name="project",
    )(jnp.concatenate([scalars, block[None].astype(jnp.int32)]), a1, by_map, cosine, sine)
    got = swap_heads(sent)
    beside = [send(v, flip(dc=1)) for v in got]
    dy = after(cotangent, *got)
    dy = jnp.where(mine, dy, send(dy, to_pair))
    dyp = lax.dynamic_slice_in_dim(dy, group * piece_rows, piece_rows, 0)

    pairs_cost = 4 * 4 * rows * rows * HD * 2
    out = flat_call(
        attend_body,
        scalars,
        [start_col] + got + beside,
        [sds((rows, HD), BF16)] * 4
        + [
            sds((4, rows, HD), F32),
            sds((4, rows, 1), F32),
            sds((4, rows, HD), BF16),
            sds((blocks, rows, HD), BF16),
            sds((blocks, rows, HD), BF16),
        ],
        [pltpu.VMEM((rows, 1), F32), pltpu.VMEM((rows, 1), F32), pltpu.VMEM((rows, HD), F32)],
        flops=2 * pairs_cost,
        name="attend",
    )
    ctx_sent, (ctx, lse, q_all, k_all, v_all) = out[:4], out[4:]
    ctx_got = swap_heads(ctx_sent)

    one_piece = sds((piece_rows, D), F32)
    low_piece = sds((piece_rows, D), BF16)
    piece_outs = [one_piece] + [low_piece] * 3
    wo_spec = pl.BlockSpec((2, 4, TR, TC), lambda i, sc: (3, 0, 0, 0))

    def whole(shape):
        return pl.BlockSpec(shape, lambda i, sc: (0,) * len(shape))

    out = pl.pallas_call(
        output_body,
        out_shape=[sds((rows, HG), BF16)] + piece_outs,
        grid_spec=pltpu.PrefetchScalarGridSpec(
            num_scalar_prefetch=1,
            grid=(1,),
            in_specs=[whole((rows, HD))] * 4 + [whole((rows, 1)), wo_spec],
            out_specs=[whole((rows, HG))] + [whole((piece_rows, D))] * 4,
            scratch_shapes=[pltpu.VMEM((rows, D), F32)],
        ),
        compiler_params=params(),
        cost_estimate=cost(2 * rows * D * HG, D * HG * 2 + rows * D * 4),
        name="output",
    )(scalars, *ctx_got, width_a, by_row)
    cb, attn_parts = out[0], out[1:]
    attn_parts = scatter_pieces(attn_parts)

    attn, h1, a2p = flat_call(
        norm_two_body,
        scalars,
        attn_parts + [tokp, rap, gain_two, bias_two],
        [one_piece, one_piece, low_piece],
        name="norm_two",
    )
    a2_parts = share_piece(a2p)

    up_spec = pl.BlockSpec((8, 1, TR, TC), lambda i, sc: (1, i, 0, 0))
    down_spec = pl.BlockSpec((2, 4, TR, TC), lambda i, sc: (8 + i, 0, 0, 0))
    col_spec = pl.BlockSpec((rows, TC), lambda i, sc: (0, i))
    out = pl.pallas_call(
        ffn_body,
        out_shape=[
            sds((rows, D), BF16),
            sds((rows, FG), BF16),
            sds((rows, FG), BF16),
            sds((rows, D), BF16),
            sds((rows, HD), F32),
            sds((piece_rows, 1), F32),
        ]
        + piece_outs,
        grid_spec=pltpu.PrefetchScalarGridSpec(
            num_scalar_prefetch=1,
            grid=(FG // TC,),
            in_specs=[whole((piece_rows, D))] * 4
            + [whole((rows, D)), whole((rows, 1)), whole((D, HD)), up_spec, down_spec],
            out_specs=[
                whole((rows, D)),
                col_spec,
                col_spec,
                whole((rows, D)),
                whole((rows, HD)),
                whole((piece_rows, 1)),
            ]
            + [whole((piece_rows, D))] * 4,
            scratch_shapes=[
                pltpu.VMEM((rows, D), F32),
                pltpu.VMEM((rows, HD), F32),
                pltpu.VMEM((rows, 1), F32),
            ],
        ),
        compiler_params=params(),
        cost_estimate=cost(4 * rows * D * FG, 4 * D * FG + rows * D * 12),
        name="ffn",
    )(scalars, *a2_parts, dy, width_f, router_f, by_row, by_row)
    a2, act, relu, gffn, dlog_f, rfp = out[:6]
    ffn_parts = out[6:]

    out = pl.pallas_call(
        ffn_back_body,
        out_shape=[sds((rows, FG), BF16)] + piece_outs,
        grid_spec=pltpu.PrefetchScalarGridSpec(
            num_scalar_prefetch=1,
            grid=(FG // TC,),
            in_specs=[
                whole((rows, D)),
                col_spec,
                whole((rows, HD)),
                whole((HD, D)),
                up_spec,
                down_spec,
            ],
            out_specs=[col_spec] + [whole((piece_rows, D))] * 4,
            scratch_shapes=[pltpu.VMEM((rows, D), F32)],
        ),
        compiler_params=params(),
        cost_estimate=cost(4 * rows * D * FG, 4 * D * FG + rows * D * 12),
        name="ffn_back",
    )(scalars, gffn, relu, dlog_f, router_ft, by_row, by_row)
    gpre, ga2_parts = out[0], scatter_pieces(out[1:])

    begins = [sum(CHUNKS[:i]) for i in range(len(CHUNKS))]

    def grad_ids(flip_y, i):
        owners = (s ^ flip_y ^ jnp.where(mine, 2, 4), s ^ flip_y ^ jnp.where(mine, 6, 0))
        return jnp.concatenate(
            [
                lax.dynamic_slice_in_dim(sorted_order, o * slots + begins[i], CHUNKS[i], 0)
                for o in owners
            ]
        )

    def route(own, other):
        return lambda z, y, x, c: (z ^ (own if c == z % 2 else other), y, x, z % 2)

    def to_owners(first, second):
        return [send(first, route(1, 2)), send(second, route(3, 0))]

    a2_there, act_there, gffn_there = [send(v, c_move) for v in (a2, act, gffn)]
    gpre_there = send(gpre, c_move)
    early_lefts = [[a2, act, a2, act], [a2_there, act_there, a2_there, act_there]]
    early_rights = [[gffn, gffn, gpre, gffn], [gffn_there, gffn_there, gpre_there, gffn_there]]
    early_away = tile_grads(grad_ids(1, 0), early_lefts, early_rights, None, [2 * CHUNKS[0]])[0]
    early_away, *ga2_parts = tied([early_away] + ga2_parts, [])
    early_back = send(early_away, y_move)

    dh1, gattnp, dlog_a, ggain_two, gbias_two = flat_call(
        norm_two_back_body,
        scalars,
        ga2_parts + [h1, attn, dyp, rap, coefp, gain_two],
        [one_piece, low_piece, sds((piece_rows, HD), F32), sds((1, D), F32), sds((1, D), F32)],
        name="norm_two_back",
    )
    gattn_parts = share_piece(gattnp)
    out = pl.pallas_call(
        gout_body,
        out_shape=[sds((rows, D), BF16)] + [sds((rows, HD), BF16)] * 4,
        grid_spec=pltpu.PrefetchScalarGridSpec(
            num_scalar_prefetch=1,
            grid=(1,),
            in_specs=[whole((piece_rows, D))] * 4 + [whole((rows, 1)), wo_spec],
            out_specs=[whole((rows, D))] + [whole((rows, HD))] * 4,
            scratch_shapes=[pltpu.VMEM((HPG, rows, HD), BF16)],
        ),
        compiler_params=params(),
        cost_estimate=cost(2 * rows * D * HG, D * HG * 2 + rows * D * 4),
        name="gout",
    )(scalars, *gattn_parts, width_a, by_row)
    gattn, *gout_sent, early_back = tied(list(out) + [early_back], [])
    gout_got = swap_heads(gout_sent)
    early_here = tile_grads(
        grad_ids(0, 0), early_lefts, early_rights, early_back, [CHUNKS[0]] * 2
    )[:2]
    *early_here, gout_got[0] = tied(list(early_here) + [gout_got[0]], [])
    early_flow = [send(early_here[0], route(1, 2))]

    gq, keys_own, keys_other = flat_call(
        attend_back_body,
        scalars,
        [start_row, cosine, sine, q_all, k_all, v_all, ctx]
        + [lse.reshape(4, 1, rows)]
        + gout_got,
        [
            sds((4, rows, HD), BF16),
            sds((4, 2, rows, HD), F32),
            sds((4, 2, rows, HD), BF16),
        ],
        [
            pltpu.VMEM((4, rows, HD), BF16),
            pltpu.VMEM((blocks, rows, HD), F32),
            pltpu.VMEM((blocks, rows, HD), F32),
            pltpu.VMEM((rows, HD), F32),
        ],
        flops=5 * pairs_cost,
        name="attend_back",
    )
    gq, early_flow[0] = tied([gq, early_flow[0]], [])
    grads_sent = flat_call(
        key_merge_body,
        scalars,
        [gq, keys_own, send(keys_other, flip(dc=1)), cosine, sine],
        [sds((3, rows, HD), BF16)] * 4,
        name="key_merge",
    )
    grads_got = swap_heads(grads_sent)
    (gin,) = flat_call(
        gather_input_body, scalars, grads_got, [sds((rows, 3 * HG), BF16)], name="gather_input"
    )
    a1_there, cb_there, gattn_there = [send(v, c_move) for v in (a1, cb, gattn)]
    lefts = [[a1, cb, a2, act], [a1_there, cb_there, a2_there, act_there]]
    rights = [
        [gin, gattn, gpre, gffn],
        [send(gin, c_move), gattn_there, gpre_there, gffn_there],
    ]

    def away_of(i):
        return tile_grads(grad_ids(1, i), lefts, rights, None, [2 * CHUNKS[i]])[0]

    bases = (left_basis[0], right_basis[0])
    state = (first_moment[0], second_moment[0], master[0])
    gin, away1, early_last = tied([gin, away_of(1), early_here[1]], [])
    back1 = send(away1, y_move)
    early_flow.append(send(early_last, route(3, 0)))
    gin, away2, away3 = tied([gin, away_of(2), away_of(3)], [])
    back2 = send(away2, y_move)
    half_cols = D // 2
    half_piece = pl.BlockSpec((piece_rows, half_cols), lambda i, sc: (0, i))
    pair_piece = pl.BlockSpec((2, piece_rows, half_cols), lambda i, sc: (0, 0, i))
    out = pl.pallas_call(
        input_back_body,
        out_shape=[one_piece] + [sds((2, piece_rows, D), BF16)] * 3,
        grid_spec=pltpu.PrefetchScalarGridSpec(
            num_scalar_prefetch=1,
            grid=(2,),
            in_specs=[
                whole((rows, 3 * HG)),
                pl.BlockSpec((3, 4, TR, TC), lambda i, sc: (0, i, 0, 0)),
                half_piece,
                half_piece,
                half_piece,
            ],
            out_specs=[half_piece] + [pair_piece] * 3,
            scratch_shapes=[pltpu.VMEM((rows, half_cols), F32)],
        ),
        compiler_params=params(),
        cost_estimate=cost(2 * rows * D * 3 * HG, 3 * D * HG * 2 + rows * D * 4),
        name="input_back",
    )(scalars, gin, by_map, *ffn_parts[1:])
    pieces = [out[0], send(out[1], MEMBERS[1]), send(out[2], MEMBERS[2])]
    pieces[1], pieces[2], last_piece = tied([pieces[1], pieces[2], out[3]], [])
    pieces.append(send(last_piece, MEMBERS[3]))

    def tile_step(i, back, waits):
        first, second, mark = tile_grads(
            grad_ids(0, i), lefts, rights, back, [CHUNKS[i]] * 2, waits
        )
        return to_owners(first, second), [mark]

    def adam_step(i, flow, held, waits=()):
        chosen = own_slots[begins[i] : begins[i] + CHUNKS[i]]
        return adam_tiles(chosen, flow, bases, state, held, waits)

    back, away3, *early_flow = tied([back1, away3] + early_flow, [])
    back3 = send(away3, y_move)
    flow1, mark = tile_step(1, back, [])
    *pieces, mark = tied(pieces + mark, [])
    mark = [mark]
    both, ggain_one, gbias_one = flat_call(
        norm_one_back_body,
        scalars,
        pieces
        + [ffn_parts[0], tokp, h1, rfp, dh1, dlog_a, router_at, gain_one],
        [sds((2, piece_rows, D), BF16), sds((1, D), F32), sds((1, D), F32)],
        name="norm_one_back",
    )
    grad_router = jnp.concatenate(
        [
            lax.dot_general(
                a1p.astype(F32), dlog_a[:, :WIDTHS], (((0,), (0,)), ((), ())), precision=PRECISE
            ),
            lax.dot_general(
                a2.astype(F32), dlog_f[:, :WIDTHS], (((0,), (0,)), ((), ())), precision=PRECISE
            ),
        ],
        axis=1,
    ).reshape(-1)
    terms = jnp.concatenate(
        [ggain_one[0], gbias_one[0], ggain_two[0], gbias_two[0], grad_router]
    ).reshape(8, -1)
    terms = terms + send(terms, c_move)
    terms = terms + send(terms, flip(dx=1))

    def fold(terms, axis, bit, target):
        low_half = lax.index_in_dim(terms, 0, axis, keepdims=False)
        high_half = lax.index_in_dim(terms, 1, axis, keepdims=False)
        keep = jnp.where(bit == 0, low_half, high_half)
        return keep, send(jnp.where(bit == 0, high_half, low_half), target)


    def again():
        once_more = send(away_of(0), y_move)
        return to_owners(
            *tile_grads(grad_ids(0, 0), lefts, rights, once_more, [CHUNKS[0]] * 2)[:2]
        )

    flow0 = lax.cond(enough[0] >= CHUNKS[0], lambda: early_flow, again)
    back, both, terms, *mark = tied([back2, both, terms] + mark, [])
    flow2, mark = tile_step(2, back, mark)
    both_z = send(both, only(foreign, flip(dz=1)))
    keep, terms = fold(terms.reshape(2, 2, 2, -1), 0, zh, h_move)
    *held, adam_mark = adam_step(0, flow0, None)
    back, both, both_z, *rest = tied([back3, both, both_z, adam_mark] + mark + flow1, [])
    mark, flow1 = rest[:2], rest[2:]
    flow3, mark = tile_step(3, back, mark)
    both_x = send(both, only(own_group, flip(dx=1)))
    both_xz = send(both, only(foreign, flip(dz=1, dx=1)))
    *held, adam_mark = adam_step(1, flow1, held, mark)
    both_x, both_xz, keep, terms, *flow2 = tied(
        [both_x, both_xz, keep, terms] + flow2 + [adam_mark], []
    )
    flow2, marks = flow2[:2], flow2[2:]
    keep, terms = fold(keep + terms, 0, zp, flip(dz=1))
    keep, terms = fold(keep + terms, 0, y, y_move)
    (joined,) = flat_call(
        join_body,
        scalars,
        [both, both_z, both_x, both_xz],
        [sds((2, rows, D), BF16)],
        name="join",
    )
    joined = jnp.where(mine, joined, send(joined, only(own_group, c_move)))
    input_grad, output = joined[0].astype(F32), joined[1]
    held = adam_step(2, flow2, held, marks)[:4]
    input_grad, output, *flow3 = tied([input_grad, output] + flow3, [])
    held = adam_step(3, flow3, held)
    terms = keep + terms
    small_outs = small_adam(terms.reshape(-1), small_first, small_second, small_master)

    return (
        output,
        input_grad,
        held[0][None],
        held[1][None],
        held[2][None],
        held[3][None],
        *small_outs,
    )


CHUNKS = (3, 4, 3, 2)
FFN_TILE = 32


def layer_norm(values, weight_gain, weight_bias):
    center = values - jnp.mean(values, axis=1, keepdims=True)
    spread = jnp.mean(center * center, axis=1, keepdims=True)
    return center * lax.rsqrt(spread + EPS_NORM) * weight_gain + weight_bias


def rotary_tables(places):
    middle = HD // 2
    frequency = ROPE_BASE ** (-(jnp.arange(middle, dtype=jnp.float32) * 2.0) / HD)
    angles = places.astype(jnp.float32)[:, None] * frequency[None, :]
    cosine_half = jnp.cos(angles)
    sine_half = jnp.sin(angles)
    return (
        jnp.concatenate([cosine_half, cosine_half], axis=1),
        jnp.concatenate([sine_half, sine_half], axis=1),
    )


def rotary(values, cosine_table, sine_table):
    middle = HD // 2
    turned = jnp.concatenate([-values[..., middle:], values[..., :middle]], axis=-1)
    return values * cosine_table[:, None, :] + turned * sine_table[:, None, :]


def rotary_back(gradients, cosine_table, sine_table):
    middle = HD // 2
    scaled = gradients * sine_table[:, None, :]
    turned = jnp.concatenate([scaled[..., middle:], -scaled[..., :middle]], axis=-1)
    return gradients * cosine_table[:, None, :] + turned


def from_tiles(tile_stack, rows_total, cols_total):
    return (
        tile_stack.reshape(rows_total // TR, cols_total // TC, TR, TC)
        .transpose(0, 2, 1, 3)
        .reshape(rows_total, cols_total)
    )


def unpack(tile_stack):
    count_in = D // TR * (HG // TC)
    count_out = HG // TR * (D // TC)
    count_up = D // TR * (FG // TC)
    edge_out = 3 * count_in
    edge_up = edge_out + count_out
    edge_down = edge_up + count_up
    w_inputs = jnp.concatenate(
        [
            from_tiles(tile_stack[:count_in], D, HG),
            from_tiles(tile_stack[count_in : 2 * count_in], D, HG),
            from_tiles(tile_stack[2 * count_in : edge_out], D, HG),
        ],
        axis=1,
    )
    w_output = from_tiles(tile_stack[edge_out:edge_up], HG, D)
    w_up = from_tiles(tile_stack[edge_up:edge_down], D, FG)
    w_down = from_tiles(tile_stack[edge_down:], FG, D)
    return (w_inputs, w_output, w_up, w_down)


def router_scale(acts_low, router_map, chosen):
    logits = jnp.dot(acts_low.astype(jnp.float32), router_map, precision=PRECISE)
    probs_all = jax.nn.softmax(logits, axis=1)
    picked = (chosen[:, None] - 1 == jnp.arange(WIDTHS)[None, :]).astype(jnp.float32)
    return (WIDTHS * jnp.sum(probs_all * picked, axis=1), probs_all, picked)


def router_back(grad_scale, probs_all, picked):
    chosen_prob = jnp.sum(probs_all * picked, axis=1)
    return (WIDTHS * grad_scale * chosen_prob)[:, None] * (picked - probs_all)


def scores_of(queries, key_block, query_index, query_segment, key_index, key_segment):
    raw_scores = jnp.einsum(
        "qhd,khd->hqk", queries, key_block, preferred_element_type=jnp.float32
    ) * HD ** (-0.5)
    allowed = (key_segment[None, :] == query_segment[:, None]) & (
        key_index[None, :] <= query_index[:, None]
    )
    return (raw_scores, allowed[None])


def fetch_block(packed_all, all_index, all_segment, number, block_rows):
    start = number * block_rows
    piece_rows = lax.dynamic_slice_in_dim(packed_all, start, block_rows, 0)
    key_index = lax.dynamic_slice_in_dim(all_index, start, block_rows, 0)
    key_segment = lax.dynamic_slice_in_dim(all_segment, start, block_rows, 0)
    first_half = piece_rows[:, :HG].reshape(block_rows, HPG, HD)
    second_half = piece_rows[:, HG:].reshape(block_rows, HPG, HD)
    return (first_half, second_half, key_index, key_segment)


def attend_forward(queries, token_index, segment, packed_all, all_index, all_segment, block_rows):
    local_rows = queries.shape[0]
    blocks = packed_all.shape[0] // block_rows

    def first_pass(carried, number):
        running_max, running_sum = carried
        key_block, value_block, key_index, key_segment = fetch_block(
            packed_all, all_index, all_segment, number, block_rows
        )
        raw_scores, allowed = scores_of(
            queries, key_block, token_index, segment, key_index, key_segment
        )
        masked = jnp.where(allowed, raw_scores, NEG_FILL)
        fresh_max = jnp.maximum(running_max, jnp.max(masked, axis=2))
        running_sum = running_sum * jnp.exp(running_max - fresh_max) + jnp.sum(
            jnp.exp(masked - fresh_max[:, :, None]), axis=2
        )
        return ((fresh_max, running_sum), None)

    start_state = (
        jnp.full((HPG, local_rows), NEG_FILL, jnp.float32),
        jnp.zeros((HPG, local_rows), jnp.float32),
    )
    (running_max, running_sum), unused = lax.scan(first_pass, start_state, jnp.arange(blocks))
    log_sum = running_max + jnp.log(running_sum)

    def second_pass(carried, number):
        key_block, value_block, key_index, key_segment = fetch_block(
            packed_all, all_index, all_segment, number, block_rows
        )
        raw_scores, allowed = scores_of(
            queries, key_block, token_index, segment, key_index, key_segment
        )
        weights_p = jnp.where(allowed, jnp.exp(raw_scores - log_sum[:, :, None]), 0.0)
        update = jnp.einsum(
            "hqk,khd->qhd",
            weights_p.astype(jnp.bfloat16),
            value_block,
            preferred_element_type=jnp.float32,
        )
        return (carried + update, None)

    context, unused = lax.scan(
        second_pass, jnp.zeros((local_rows, HPG, HD), jnp.float32), jnp.arange(blocks)
    )
    return (log_sum, context)


def pair_grads(
    queries,
    grad_out,
    log_sum,
    delta,
    query_index,
    query_segment,
    key_block,
    value_block,
    key_index,
    key_segment,
):
    raw_scores, allowed = scores_of(
        queries, key_block, query_index, query_segment, key_index, key_segment
    )
    weights_p = jnp.where(allowed, jnp.exp(raw_scores - log_sum[:, :, None]), 0.0)
    grad_value = jnp.einsum(
        "hqk,qhd->khd", weights_p.astype(jnp.bfloat16), grad_out, preferred_element_type=jnp.float32
    )
    grad_probs = jnp.einsum(
        "qhd,khd->hqk", grad_out, value_block, preferred_element_type=jnp.float32
    )
    grad_raw = (weights_p * (grad_probs - delta[:, :, None]) * HD ** (-0.5)).astype(jnp.bfloat16)
    grad_query = jnp.einsum("hqk,khd->qhd", grad_raw, key_block, preferred_element_type=jnp.float32)
    grad_key = jnp.einsum("hqk,qhd->khd", grad_raw, queries, preferred_element_type=jnp.float32)
    return (grad_query, grad_key, grad_value)


def local_plain(
    tokens,
    cotangent,
    attn_width,
    ffn_width,
    seq_lengths,
    tile_order,
    master,
    first_moment,
    second_moment,
    left_basis,
    right_basis,
    small_master,
    small_first,
    small_second,
):
    local_rows = tokens.shape[0]
    shards = lax.axis_size("seq")
    all_rows = local_rows * shards
    block_rows = min(KB_CAP, all_rows)
    blocks = all_rows // block_rows
    group_id = lax.axis_index("head")
    slot_order = tile_order[0]
    weights_all, small_all = (
        lax.all_gather(master[0].astype(jnp.bfloat16), "seq", axis=0, tiled=True),
        lax.all_gather(small_master.astype(jnp.bfloat16), "seq", axis=0, tiled=True),
    )
    w_inputs, w_output, w_up, w_down = unpack(place_tiles(slot_order, [weights_all], None)[0])
    small_vals = small_all.astype(jnp.float32)
    gain_one = small_vals[0:D]
    bias_one = small_vals[D : 2 * D]
    gain_two = small_vals[2 * D : 3 * D]
    bias_two = small_vals[3 * D : 4 * D]
    routers = small_vals[4 * D :].reshape(D, 2 * WIDTHS)
    router_attn = routers[:, :WIDTHS]
    router_ffn = routers[:, WIDTHS:]
    first_row = lax.axis_index("seq") * local_rows
    token_index, segment, offset = token_layout(first_row, local_rows, seq_lengths)
    residual = tokens.astype(jnp.float32)
    ln_one, pull_one = jax.vjp(layer_norm, residual, gain_one, bias_one)
    act_one = ln_one.astype(jnp.bfloat16)
    scale_attn, probs_attn, picked_attn = router_scale(act_one, router_attn, attn_width)
    projected = jnp.dot(act_one, w_inputs, preferred_element_type=jnp.float32)
    cosine_table, sine_table = rotary_tables(offset)
    query_low = rotary(
        projected[:, :HG].reshape(local_rows, HPG, HD), cosine_table, sine_table
    ).astype(jnp.bfloat16)
    key_low = rotary(
        projected[:, HG : 2 * HG].reshape(local_rows, HPG, HD), cosine_table, sine_table
    ).astype(jnp.bfloat16)
    value_low = projected[:, 2 * HG :].astype(jnp.bfloat16)
    packed = jnp.concatenate([key_low.reshape(local_rows, HG), value_low], axis=1)
    packed_all = lax.all_gather(packed, "seq", axis=0, tiled=True)
    all_index, all_segment, all_offset = token_layout(0, all_rows, seq_lengths)
    log_sum, context = attend_forward(
        query_low, token_index, segment, packed_all, all_index, all_segment, block_rows
    )
    head_mask = (group_id < attn_width).astype(jnp.float32)
    ctx_low = (context * head_mask[:, None, None]).astype(jnp.bfloat16).reshape(local_rows, HG)
    attn_out = lax.psum(
        jnp.dot(ctx_low, w_output, preferred_element_type=jnp.float32).astype(jnp.bfloat16), "head"
    ).astype(jnp.float32)
    middle_res = residual + scale_attn[:, None] * attn_out
    ln_two, pull_two = jax.vjp(layer_norm, middle_res, gain_two, bias_two)
    act_two = ln_two.astype(jnp.bfloat16)
    scale_ffn, probs_ffn, picked_ffn = router_scale(act_two, router_ffn, ffn_width)
    pre_act = jnp.dot(act_two, w_up, preferred_element_type=jnp.float32)
    unit_mask = (group_id < ffn_width).astype(jnp.float32)
    hidden_low = (jnp.square(jnp.maximum(pre_act, 0.0)) * unit_mask[:, None]).astype(jnp.bfloat16)
    ffn_out = lax.psum(
        jnp.dot(hidden_low, w_down, preferred_element_type=jnp.float32).astype(jnp.bfloat16), "head"
    ).astype(jnp.float32)
    output = (middle_res + scale_ffn[:, None] * ffn_out).astype(jnp.bfloat16)
    grad_top = cotangent.astype(jnp.float32)
    grad_scale_ffn = jnp.sum(grad_top * ffn_out, axis=1)
    grad_ffn_low = (scale_ffn[:, None] * grad_top).astype(jnp.bfloat16)
    grad_hidden = jnp.dot(grad_ffn_low, w_down.T, preferred_element_type=jnp.float32)
    grad_pre_low = (grad_hidden * unit_mask[:, None] * 2.0 * jnp.maximum(pre_act, 0.0)).astype(
        jnp.bfloat16
    )
    grad_act_two = lax.psum(
        jnp.dot(grad_pre_low, w_up.T, preferred_element_type=jnp.float32).astype(jnp.bfloat16),
        "head",
    ).astype(jnp.float32)
    logit_ffn = router_back(grad_scale_ffn, probs_ffn, picked_ffn)
    grad_act_two = grad_act_two + jnp.dot(logit_ffn, router_ffn.T, precision=PRECISE)
    grad_mid_ln, grad_gain_two, grad_bias_two = pull_two(grad_act_two)
    grad_middle = grad_top + grad_mid_ln
    grad_scale_attn = jnp.sum(grad_middle * attn_out, axis=1)
    grad_attn_low = (scale_attn[:, None] * grad_middle).astype(jnp.bfloat16)
    grad_context = jnp.dot(grad_attn_low, w_output.T, preferred_element_type=jnp.float32)
    grad_out_low = (
        (grad_context * head_mask[:, None]).astype(jnp.bfloat16).reshape(local_rows, HPG, HD)
    )
    delta = jnp.sum(grad_out_low.astype(jnp.float32) * context, axis=2).T
    zero_state = jnp.zeros((local_rows, HPG, HD), jnp.float32)

    def visit_keys(carried, number):
        key_block, value_block, key_index, key_segment = fetch_block(
            packed_all, all_index, all_segment, number, block_rows
        )
        grad_query, grad_key, grad_value = pair_grads(
            query_low,
            grad_out_low,
            log_sum,
            delta,
            token_index,
            segment,
            key_block,
            value_block,
            key_index,
            key_segment,
        )
        return (
            carried + grad_query,
            jnp.concatenate(
                [grad_key.reshape(block_rows, HG), grad_value.reshape(block_rows, HG)], axis=1
            ),
        )

    grad_query_rot, key_terms = lax.scan(visit_keys, zero_state, jnp.arange(blocks))
    summed = lax.psum_scatter(
        key_terms.reshape(all_rows, 2 * HG).astype(jnp.bfloat16),
        "seq",
        scatter_dimension=0,
        tiled=True,
    ).astype(jnp.float32)
    grad_key_rot = summed[:, :HG].reshape(local_rows, HPG, HD)
    grad_value_all = summed[:, HG:].reshape(local_rows, HPG, HD)
    grad_query_low = (
        rotary_back(grad_query_rot, cosine_table, sine_table)
        .astype(jnp.bfloat16)
        .reshape(local_rows, HG)
    )
    grad_key_low = (
        rotary_back(grad_key_rot, cosine_table, sine_table)
        .astype(jnp.bfloat16)
        .reshape(local_rows, HG)
    )
    grad_value_low = grad_value_all.astype(jnp.bfloat16).reshape(local_rows, HG)
    grad_inputs_low = jnp.concatenate([grad_query_low, grad_key_low, grad_value_low], axis=1)
    grad_act_one = lax.psum(
        jnp.dot(grad_inputs_low, w_inputs.T, preferred_element_type=jnp.float32).astype(
            jnp.bfloat16
        ),
        "head",
    ).astype(jnp.float32)
    logit_attn = router_back(grad_scale_attn, probs_attn, picked_attn)
    grad_act_one = grad_act_one + jnp.dot(logit_attn, router_attn.T, precision=PRECISE)
    grad_res_ln, grad_gain_one, grad_bias_one = pull_one(grad_act_one)
    input_grad = grad_middle + grad_res_ln
    grad_router = jnp.concatenate(
        [
            jnp.dot(act_one.astype(jnp.float32).T, logit_attn, precision=PRECISE),
            jnp.dot(act_two.astype(jnp.float32).T, logit_ffn, precision=PRECISE),
        ],
        axis=1,
    ).reshape(-1)
    small_terms = jnp.concatenate(
        [grad_gain_one, grad_bias_one, grad_gain_two, grad_bias_two, grad_router]
    )
    tile_terms = tile_grads(
        slot_order,
        [[act_one, ctx_low, act_two, hidden_low]],
        [[grad_inputs_low, grad_attn_low, grad_pre_low, grad_ffn_low]],
        None,
        [slot_order.shape[0]],
    )[0]
    tile_grad, small_grad = (
        lax.psum_scatter(tile_terms, "seq", scatter_dimension=0, tiled=True),
        lax.psum_scatter(
            small_terms.astype(jnp.bfloat16), "seq", scatter_dimension=0, tiled=True
        ).astype(jnp.float32),
    )
    slots = master.shape[1]
    held = adam_tiles(
        jnp.arange(slots, dtype=jnp.int32),
        [tile_grad],
        (left_basis[0], right_basis[0]),
        (first_moment[0], second_moment[0], master[0]),
        None,
    )
    small_outs = small_adam(small_grad, small_first, small_second, small_master)
    return (
        output,
        input_grad,
        held[0][None],
        held[1][None],
        held[2][None],
        held[3][None],
        *small_outs,
    )


def solution(mesh):
    return jax.shard_map(
        local_remap if dict(mesh.shape) == {"seq": 8, "head": 4} else local_plain,
        mesh=mesh,
        in_specs=(
            P("seq", None),
            P("seq", None),
            P("seq"),
            P("seq"),
            P(),
            P("head", None),
            P("head", "seq", None, None),
            P("head", "seq", None, None),
            P("head", "seq", None, None),
            P("head", "seq", None, None),
            P("head", "seq", None, None),
            P("seq"),
            P("seq"),
            P("seq"),
        ),
        out_specs=(
            P("seq", None),
            P("seq", None),
            P("head", "seq", None, None),
            P("head", "seq", None, None),
            P("head", "seq", None, None),
            P("head", "seq", None, None),
            P("seq"),
            P("seq"),
            P("seq"),
        ),
        check_vma=False,
    )
```

```python
import functools

import jax
import jax.numpy as jnp
from jax import lax
from jax.experimental import pallas as pl
from jax.experimental.pallas import tpu as pltpu
from jax.sharding import PartitionSpec as P

D = 2048
HD = 128
WIDTHS = 4
TR = 256
TC = 512
TILES = 96
STEP = 10
KB_CAP = 1024
HPG = 4
HG = 512
FG = 2048

PRECISE = lax.Precision.HIGHEST
EPS_NORM = 1e-05
BETA_ONE = 0.95
BETA_TWO = 0.95
ADAM_EPS = 1e-08
DECAY_RATE = 0.01
RATE_TILE = 0.15
RATE_SMALL = 1.0
ROPE_BASE = 10000.0
NEG_FILL = -1e30
SCORE_SCALE = HD ** (-0.5)
F32 = jnp.float32
BF16 = jnp.bfloat16
AXES = ("seq", "head")
VMEM_BIG = 56 << 20
VMEM_ALL = 61 << 20


def nt(a, b):
    return lax.dot_general(a, b, (((1,), (1,)), ((), ())), preferred_element_type=F32)


def nn(a, b):
    return lax.dot_general(a, b, (((1,), (0,)), ((), ())), preferred_element_type=F32)


def tn(a, b):
    return lax.dot_general(a, b, (((0,), (0,)), ((), ())), preferred_element_type=F32)


VM = pl.BlockSpec(memory_space=pltpu.VMEM)
SM = pl.BlockSpec(memory_space=pltpu.SMEM)
HBM = pl.BlockSpec(memory_space=pltpu.MemorySpace.HBM)


def sds(shape, dtype):
    return jax.ShapeDtypeStruct(shape, dtype)


MARK = sds((8, HD), F32)


def params():
    return pltpu.CompilerParams(vmem_limit_bytes=VMEM_BIG)


def cost(flops, nbytes):
    return pl.CostEstimate(flops=int(flops), bytes_accessed=int(nbytes), transcendentals=0)


def flat_call(body, scalars, arrays, outs, scratch=(), flops=0, name=None):
    nbytes = sum(a.size * a.dtype.itemsize for a in arrays)
    nbytes += sum(int(jnp.dtype(o.dtype).itemsize) * o.size for o in outs)
    return pl.pallas_call(
        body,
        out_shape=outs,
        in_specs=[SM] + [VM] * len(arrays),
        out_specs=[VM] * len(outs),
        scratch_shapes=list(scratch),
        compiler_params=params(),
        cost_estimate=cost(flops, nbytes),
        name=name,
    )(scalars, *arrays)


def rows_of(ref, index, rows):
    return ref[pl.ds(pl.multiple_of(index * rows, rows), rows), :]


def put_rows(ref, index, rows, value):
    ref[pl.ds(pl.multiple_of(index * rows, rows), rows), :] = value


def store_pieces(acc_ref, piece, rows, outs):
    outs[0][...] = rows_of(acc_ref, piece, rows)
    for k in range(1, 4):
        outs[k][...] = rows_of(acc_ref, piece ^ k, rows).astype(BF16)


def row_stats(values):
    center = values - jnp.mean(values, axis=1, keepdims=True)
    rstd = lax.rsqrt(jnp.mean(center * center, axis=1, keepdims=True) + EPS_NORM)
    return center * rstd, rstd


def route_level(logits, width_col):
    lane = lax.broadcasted_iota(jnp.int32, logits.shape, 1)
    live = lane < WIDTHS
    top = jnp.max(jnp.where(live, logits, NEG_FILL), axis=1, keepdims=True)
    raised = jnp.where(live, jnp.exp(jnp.where(live, logits, NEG_FILL) - top), 0.0)
    probs = raised / jnp.sum(raised, axis=1, keepdims=True)
    picked = (lane == width_col - 1).astype(F32)
    chosen = jnp.sum(probs * picked, axis=1, keepdims=True)
    return WIDTHS * chosen, WIDTHS * chosen * (picked - probs)


def split_dot(values, right_low):
    high = values.astype(BF16)
    rest = (values - high.astype(F32)).astype(BF16)
    return nn(high, right_low) + nn(rest, right_low)


def norm_one_body(sc, tok, gain, bias, router, width, a1, a1p, tokp, rap, coefp, ra_s, coef_s):
    rows = a1p.shape[0]
    piece = sc[1]
    xhat, _ = row_stats(tok[...].astype(F32))
    low = (xhat * gain[...] + bias[...]).astype(BF16)
    a1[...] = low
    scale, coef = route_level(nn(low, router[...]), width[...])
    ra_s[...] = scale
    coef_s[...] = coef
    a1p[...] = rows_of(a1, piece, rows)
    tokp[...] = rows_of(tok, piece, rows)
    rap[...] = rows_of(ra_s, piece, rows)
    coefp[...] = rows_of(coef_s, piece, rows)


def turn(values, cosine, signed_sine):
    return values * cosine + pltpu.roll(values, HD // 2, 1) * signed_sine


def turn_back(values, cosine, signed_sine):
    return values * cosine - pltpu.roll(values, HD // 2, 1) * signed_sine


def project_body(sc, a1, weights, cosine, sine, o0, o1, o2, o3, heads_s):
    step = pl.program_id(0)
    spot = sc[0]
    out = nn(a1[...], weights[...].reshape(D, HG))
    plain = step == 2
    cos_v = jnp.where(plain, 1.0, cosine[0])
    sin_v = jnp.where(plain, 0.0, sine[0])
    for head in range(HPG):
        heads_s[head] = turn(out[:, head * HD : (head + 1) * HD], cos_v, sin_v).astype(BF16)
    for k, ref in enumerate((o0, o1, o2, o3)):
        ref[0] = heads_s[spot ^ k]


def sequence_start(sc, places):
    first = jnp.zeros_like(places)
    for i in range(13, sc.shape[0]):
        first = jnp.where(places >= sc[i], sc[i], first)
    return first


def attend_body(
    sc, r0, r1, r2, r3, c0, c1, c2, c3,
    o0, o1, o2, o3, ctx, lse, q_all, k_all, v_all, m_s, l_s, acc_s,
):
    spot, core = sc[0], sc[2]
    rows = r0.shape[1]

    def block_of(source, side):
        return (2 * (source // 2) + side) * 2 + source % 2

    for k, (own, other) in enumerate(((r0, c0), (r1, c1), (r2, c2), (r3, c3))):
        mine = block_of(spot ^ k, core)
        theirs = block_of(spot ^ k, 1 - core)
        q_all[k] = own[0]
        k_all[mine] = own[1]
        v_all[mine] = own[2]
        k_all[theirs] = other[1]
        v_all[theirs] = other[2]

    def per_query(k, unused):
        block = block_of(spot ^ k, core)
        query = q_all[k]
        first = sequence_start(
            sc, block * rows + lax.broadcasted_iota(jnp.int32, (rows, 1), 0)
        )
        where_q = block * rows + lax.broadcasted_iota(jnp.int32, (rows, rows), 0)
        lane = lax.broadcasted_iota(jnp.int32, (rows, rows), 1)
        m_s[...] = jnp.full(m_s.shape, NEG_FILL, F32)
        l_s[...] = jnp.zeros(l_s.shape, F32)
        acc_s[...] = jnp.zeros(acc_s.shape, F32)

        def per_key(kb, unused_two):
            where_k = kb * rows + lane
            scores = nt(query, k_all[kb]) * SCORE_SCALE
            scores = jnp.where((where_k <= where_q) & (where_k >= first), scores, NEG_FILL)
            old = m_s[...]
            new = jnp.maximum(old, jnp.max(scores, axis=1, keepdims=True))
            weight = jnp.exp(scores - new)
            fade = jnp.exp(old - new)
            l_s[...] = l_s[...] * fade + jnp.sum(weight, axis=1, keepdims=True)
            acc_s[...] = acc_s[...] * fade + nn(weight.astype(BF16), v_all[kb])
            m_s[...] = new
            return 0

        lax.fori_loop(sc[4 + block], block + 1, per_key, 0)
        ctx[k] = acc_s[...] / l_s[...]
        lse[k] = m_s[...] + jnp.log(l_s[...])
        return 0

    lax.fori_loop(0, 4, per_query, 0)
    for k, ref in enumerate((o0, o1, o2, o3)):
        ref[...] = ctx[k].astype(BF16)


def output_body(sc, r0, r1, r2, r3, width, weights, cb, o0, o1, o2, o3, acc_s):
    spot, piece, group = sc[0], sc[1], sc[3]
    keep = width[...] > group
    for k, ref in enumerate((r0, r1, r2, r3)):
        at = pl.ds(pl.multiple_of((spot ^ k) * HD, HD), HD)
        cb[:, at] = jnp.where(keep, ref[...], jnp.zeros_like(ref[...]))
    for col in range(D // TC):
        acc_s[:, col * TC : (col + 1) * TC] = nn(cb[:, :TR], weights[0, col]) + nn(
            cb[:, TR:], weights[1, col]
        )
    store_pieces(acc_s, piece, o1.shape[0], (o0, o1, o2, o3))


def norm_two_body(sc, own, r1, r2, r3, tokp, rap, gain, bias, attn, h1, a2p):
    total = own[...] + r1[...].astype(F32) + r2[...].astype(F32) + r3[...].astype(F32)
    attn[...] = total
    middle = tokp[...].astype(F32) + rap[...] * total
    h1[...] = middle
    xhat, _ = row_stats(middle)
    a2p[...] = (xhat * gain[...] + bias[...]).astype(BF16)


def ffn_body(
    sc, p0, p1, p2, p3, dy, width, router, w_up, w_down,
    a2, act, relu, gffn, dlog, rfp, o0, o1, o2, o3, acc_s, coef_s, rf_s,
):
    step = pl.program_id(0)
    piece, group = sc[1], sc[3]
    rows = p0.shape[0]

    @pl.when(step == 0)
    def _():
        for k, ref in enumerate((p0, p1, p2, p3)):
            put_rows(a2, piece ^ k, rows, ref[...])
        scale, coef = route_level(nn(a2[...], router[...]), width[...])
        rf_s[...] = scale
        coef_s[...] = coef
        gffn[...] = (scale * dy[...].astype(F32)).astype(BF16)
        rfp[...] = rows_of(rf_s, piece, rows)

    up = jnp.maximum(nn(a2[...], w_up[...].reshape(D, TC)), 0.0)
    up = jnp.where(width[...] > group, up, 0.0)
    relu[...] = up.astype(BF16)
    low = (up * up).astype(BF16)
    act[...] = low
    for col in range(D // TC):
        at = slice(col * TC, (col + 1) * TC)
        part = nn(low[:, :TR], w_down[0, col]) + nn(low[:, TR:], w_down[1, col])

        @pl.when(step == 0)
        def _(part=part, at=at):
            acc_s[:, at] = part

        @pl.when(step > 0)
        def _(part=part, at=at):
            acc_s[:, at] += part

    @pl.when(step == pl.num_programs(0) - 1)
    def _():
        drf = jnp.sum(acc_s[...] * dy[...].astype(F32), axis=1, keepdims=True)
        dlog[...] = drf * coef_s[...]
        store_pieces(acc_s, piece, rows, (o0, o1, o2, o3))


def ffn_back_body(sc, gffn, relu, dlog, router_t, w_up, w_down, gpre, o0, o1, o2, o3, acc_s):
    step = pl.program_id(0)
    piece = sc[1]
    halves = []
    for row in range(2):
        total = nt(gffn[:, :TC], w_down[row, 0])
        for col in range(1, D // TC):
            total += nt(gffn[:, col * TC : (col + 1) * TC], w_down[row, col])
        halves.append(total)
    gact = jnp.concatenate(halves, axis=1)
    low = (gact * 2.0 * relu[...].astype(F32)).astype(BF16)
    gpre[...] = low
    part = nt(low, w_up[...].reshape(D, TC))

    @pl.when(step == 0)
    def _():
        acc_s[...] = part + split_dot(dlog[...], router_t[...])

    @pl.when(step > 0)
    def _():
        acc_s[...] += part

    @pl.when(step == pl.num_programs(0) - 1)
    def _():
        store_pieces(acc_s, piece, o1.shape[0], (o0, o1, o2, o3))


def norm_grad(grad, values, gain):
    xhat, rstd = row_stats(values)
    scaled = grad * gain
    inner = scaled - jnp.mean(scaled, axis=1, keepdims=True)
    inner = inner - xhat * jnp.mean(scaled * xhat, axis=1, keepdims=True)
    gain_grad = jnp.sum(grad * xhat, axis=0, keepdims=True)
    return inner * rstd, gain_grad, jnp.sum(grad, axis=0, keepdims=True)


def norm_two_back_body(
    sc, own, r1, r2, r3, h1, attn, dy, rap, coefp, gain, dh1, gattnp, dlogp, ggain, gbias
):
    grad = own[...] + r1[...].astype(F32) + r2[...].astype(F32) + r3[...].astype(F32)
    back, gain_grad, bias_grad = norm_grad(grad, h1[...], gain[...])
    middle = rows_of(dy, sc[1], dh1.shape[0]).astype(F32) + back
    dh1[...] = middle
    gattnp[...] = (rap[...] * middle).astype(BF16)
    dra = jnp.sum(middle * attn[...], axis=1, keepdims=True)
    dlogp[...] = dra * coefp[...]
    ggain[...] = gain_grad
    gbias[...] = bias_grad


def gout_body(sc, p0, p1, p2, p3, width, weights, gattn, o0, o1, o2, o3, heads_s):
    spot, piece, group = sc[0], sc[1], sc[3]
    rows = p0.shape[0]
    for k, ref in enumerate((p0, p1, p2, p3)):
        put_rows(gattn, piece ^ k, rows, ref[...])
    keep = width[...] > group
    for row in range(2):
        total = nt(gattn[:, :TC], weights[row, 0])
        for col in range(1, D // TC):
            total += nt(gattn[:, col * TC : (col + 1) * TC], weights[row, col])
        low = jnp.where(keep, total, 0.0).astype(BF16)
        heads_s[2 * row] = low[:, :HD]
        heads_s[2 * row + 1] = low[:, HD:]
    for k, ref in enumerate((o0, o1, o2, o3)):
        ref[...] = heads_s[spot ^ k]


def attend_back_body(
    sc, cosine, sine, q_all, k_all, v_all, ctx, lse, g0, g1, g2, g3,
    gq, own, other, g_s, gk_s, gv_s, acc_s,
):
    spot, core = sc[0], sc[2]
    rows = g0.shape[0]

    def block_of(source, side):
        return (2 * (source // 2) + side) * 2 + source % 2

    for k, ref in enumerate((g0, g1, g2, g3)):
        g_s[k] = ref[...]
    gk_s[...] = jnp.zeros(gk_s.shape, F32)
    gv_s[...] = jnp.zeros(gv_s.shape, F32)

    def per_query(k, unused):
        block = block_of(spot ^ k, core)
        query = q_all[k]
        grad = g_s[k]
        shared = grad.astype(F32) * ctx[k]
        delta = lax.dot_general(
            jnp.ones((8, HD), F32), shared, (((1,), (1,)), ((), ())),
            precision=PRECISE, preferred_element_type=F32,
        )[:1]
        first = sequence_start(
            sc, block * rows + lax.broadcasted_iota(jnp.int32, (1, rows), 1)
        )
        level = lse[k]
        where_q = block * rows + lax.broadcasted_iota(jnp.int32, (rows, rows), 1)
        line = lax.broadcasted_iota(jnp.int32, (rows, rows), 0)
        acc_s[...] = jnp.zeros(acc_s.shape, F32)

        def per_key(kb, unused_two):
            where_k = kb * rows + line
            keys = k_all[kb]
            allowed = (where_k <= where_q) & (where_k >= first)
            scores = nt(keys, query) * SCORE_SCALE
            prob = jnp.where(allowed, jnp.exp(jnp.where(allowed, scores - level, 0.0)), 0.0)
            gprob = nt(v_all[kb], grad)
            graw = (prob * (gprob - delta) * SCORE_SCALE).astype(BF16)
            gv_s[kb] += nn(prob.astype(BF16), grad)
            gk_s[kb] += nn(graw, query)
            acc_s[...] += tn(graw, keys)
            return 0

        lax.fori_loop(sc[4 + block], block + 1, per_key, 0)
        gq[k] = turn_back(acc_s[...], cosine[block], sine[block]).astype(BF16)
        return 0

    lax.fori_loop(0, 4, per_query, 0)
    for k in range(4):
        mine = block_of(spot ^ k, core)
        theirs = block_of(spot ^ k, 1 - core)
        own[k, 0] = gk_s[mine]
        own[k, 1] = gv_s[mine]
        other[k, 0] = gk_s[theirs].astype(BF16)
        other[k, 1] = gv_s[theirs].astype(BF16)


def key_merge_body(sc, gq, own, got, cosine, sine, o0, o1, o2, o3):
    spot, core = sc[0], sc[2]
    for k, ref in enumerate((o0, o1, o2, o3)):
        source = spot ^ k
        block = (2 * (source // 2) + core) * 2 + source % 2
        ref[0] = gq[k]
        gk = own[k, 0] + got[k, 0].astype(F32)
        ref[1] = turn_back(gk, cosine[block], sine[block]).astype(BF16)
        ref[2] = (own[k, 1] + got[k, 1].astype(F32)).astype(BF16)


def gather_input_body(sc, r0, r1, r2, r3, gin):
    spot = sc[0]
    for k, ref in enumerate((r0, r1, r2, r3)):
        for member in range(3):
            at = pl.ds(pl.multiple_of(member * HG + (spot ^ k) * HD, HD), HD)
            gin[:, at] = ref[member]


def input_back_body(sc, gin, weights, f1, f2, f3, o0, o1, o2, o3, acc_s):
    piece = sc[1]
    rows = o0.shape[0]
    wide = weights.shape[1] * TR
    total = nt(gin[:, :HG], weights[0].reshape(wide, TC))
    for member in range(1, 3):
        total += nt(gin[:, member * HG : (member + 1) * HG], weights[member].reshape(wide, TC))
    acc_s[...] = total
    o0[...] = rows_of(acc_s, piece, rows)
    for k, (ref, passed) in enumerate(((o1, f1), (o2, f2), (o3, f3))):
        ref[0] = rows_of(acc_s, piece ^ (k + 1), rows).astype(BF16)
        ref[1] = passed[...]


def norm_one_back_body(
    sc, own, r1, r2, r3, ffn, tokp, h1, rfp, dh1, dlogp, router_t, gain, both, ggain, gbias
):
    grad = own[...] + r1[0].astype(F32) + r2[0].astype(F32) + r3[0].astype(F32)
    grad = grad + split_dot(dlogp[...], router_t[...])
    back, gain_grad, bias_grad = norm_grad(grad, tokp[...].astype(F32), gain[...])
    both[0] = (dh1[...] + back).astype(BF16)
    total = ffn[...] + r1[1].astype(F32) + r2[1].astype(F32) + r3[1].astype(F32)
    both[1] = (h1[...] + rfp[...] * total).astype(BF16)
    ggain[...] = gain_grad
    gbias[...] = bias_grad


def join_body(sc, b0, b1, b2, b3, whole):
    piece = sc[1]
    rows = b0.shape[1]
    for k, ref in enumerate((b0, b1, b2, b3)):
        at = pl.ds(pl.multiple_of((piece ^ k) * rows, rows), rows)
        whole[:, at, :] = ref[...]


def place_tiles(ids, chunks, held, waits=()):
    count = sum(c.shape[0] for c in chunks)

    def body(ids_ref, *refs):
        parts = refs[: len(chunks)]
        out = refs[len(chunks) + len(waits) + (0 if held is None else 1)]
        mark, buf, in_sems, out_sems = refs[-4:]
        mark[...] = jnp.zeros_like(mark)
        places = [(part, i) for part in parts for i in range(part.shape[0])]
        arrive = [
            pltpu.make_async_copy(part.at[i], buf.at[at], in_sems.at[at])
            for at, (part, i) in enumerate(places)
        ]
        leave = [
            pltpu.make_async_copy(buf.at[at], out.at[ids_ref[at]], out_sems.at[at])
            for at in range(count)
        ]
        for copy in arrive:
            copy.start()
        for came, go in zip(arrive, leave):
            came.wait()
            go.start()
        for copy in leave:
            copy.wait()

    extra = [] if held is None else [held]
    return pl.pallas_call(
        body,
        out_shape=[sds((TILES, TR, TC), BF16), MARK],
        in_specs=[SM] + [HBM] * (len(chunks) + len(extra) + len(waits)),
        out_specs=[HBM, VM],
        scratch_shapes=[
            pltpu.VMEM((count, TR, TC), BF16),
            pltpu.SemaphoreType.DMA((count,)),
            pltpu.SemaphoreType.DMA((count,)),
        ],
        compiler_params=params(),
        input_output_aliases={} if held is None else {1 + len(chunks): 0},
        cost_estimate=cost(0, 2 * count * TR * TC * 2),
        name="place_tiles",
    )(ids, *chunks, *extra, *waits)


def tile_kind(tile):
    kind = (tile >= 24).astype(jnp.int32) + (tile >= 32).astype(jnp.int32)
    kind = kind + (tile >= 64).astype(jnp.int32)
    base = jnp.where(kind == 1, 24, jnp.where(kind == 2, 32, 64))
    local = tile - base
    left = jnp.where(kind == 0, tile % 8, local // 4)
    right = jnp.where(kind == 0, tile // 8, local % 4)
    return kind, left, right


def tile_grads(ids, lefts, rights, added, outs_of, waits=()):
    count = ids.shape[0]
    parts = len(lefts)
    rows = lefts[0][0].shape[0]
    flat = [a for part in lefts for a in part] + [a for part in rights for a in part]

    def fetch(ids_ref, step, slot, refs, lbuf, rbuf, sems):
        kind, left, right = tile_kind(ids_ref[step])
        for which in range(4):

            @pl.when(kind == which)
            def _(which=which):
                for part in range(parts):
                    src = refs[part * 4 + which]
                    at = pl.ds(pl.multiple_of(left * TR, TR), TR)
                    pltpu.make_async_copy(
                        src.at[:, at], lbuf.at[slot, pl.ds(part * rows, rows)], sems.at[slot, part]
                    ).start()
                    src = refs[(parts + part) * 4 + which]
                    at = pl.ds(pl.multiple_of(right * TC, TC), TC)
                    pltpu.make_async_copy(
                        src.at[:, at],
                        rbuf.at[slot, pl.ds(part * rows, rows)],
                        sems.at[slot, parts + part],
                    ).start()

    def body(ids_ref, *refs):
        sources = refs[: len(flat)]
        at = len(flat)
        plus = None
        if added is not None:
            plus = refs[at]
            at += 1
        at += len(waits)
        outs = refs[at : at + len(outs_of)]
        mark, lbuf, rbuf, sems = refs[at + len(outs_of) :]
        mark[...] = jnp.zeros_like(mark)
        step = pl.program_id(0)
        slot = lax.rem(step, 2)

        @pl.when(step == 0)
        def _():
            fetch(ids_ref, 0, 0, sources, lbuf, rbuf, sems)

        @pl.when(step + 1 < count)
        def _():
            fetch(ids_ref, step + 1, 1 - slot, sources, lbuf, rbuf, sems)

        for part in range(parts):
            pltpu.make_async_copy(
                sources[0].at[:, :TR], lbuf.at[slot, pl.ds(part * rows, rows)], sems.at[slot, part]
            ).wait()
            pltpu.make_async_copy(
                sources[parts * 4 + 1].at[:, :TC],
                rbuf.at[slot, pl.ds(part * rows, rows)],
                sems.at[slot, parts + part],
            ).wait()
        total = tn(lbuf[slot], rbuf[slot])
        if plus is not None:
            total = total + plus[0].astype(F32)
        low = total.astype(BF16)
        if len(outs_of) == 1:
            outs[0][0] = low
        else:
            begin = 0
            for ref, size in zip(outs, outs_of):

                @pl.when((step >= begin) & (step < begin + size))
                def _(ref=ref):
                    ref[0] = low

                begin += size

    specs_out = []
    begin = 0
    for size in outs_of:
        specs_out.append(
            pl.BlockSpec(
                (1, TR, TC),
                lambda i, ids_ref, begin=begin, size=size: (jnp.clip(i - begin, 0, size - 1), 0, 0),
            )
        )
        begin += size
    plus_in = [] if added is None else [added]
    return pl.pallas_call(
        body,
        out_shape=[sds((size, TR, TC), BF16) for size in outs_of] + [MARK],
        grid_spec=pltpu.PrefetchScalarGridSpec(
            num_scalar_prefetch=1,
            grid=(count,),
            in_specs=[HBM] * len(flat)
            + [pl.BlockSpec((1, TR, TC), lambda i, ids_ref: (i, 0, 0))] * len(plus_in)
            + [HBM] * len(waits),
            out_specs=specs_out + [pl.BlockSpec((8, HD), lambda i, ids_ref: (0, 0))],
            scratch_shapes=[
                pltpu.VMEM((2, parts * rows, TR), BF16),
                pltpu.VMEM((2, parts * rows, TC), BF16),
                pltpu.SemaphoreType.DMA((2, 2 * parts)),
            ],
        ),
        compiler_params=pltpu.CompilerParams(vmem_limit_bytes=VMEM_ALL),
        cost_estimate=cost(
            2 * count * parts * rows * TR * TC, count * (parts * rows * (TR + TC) * 2 + TR * TC * 2)
        ),
        name="tile_grads",
    )(ids, *flat, *plus_in, *waits)


def adam_tile(grad, left, right, first, second, master):
    left_low = left.astype(BF16)
    right_low = right.astype(BF16)
    turned = nn(tn(left_low, grad.astype(BF16)).astype(BF16), right_low)
    new_first = BETA_ONE * first + (1.0 - BETA_ONE) * turned
    new_second = BETA_TWO * second + (1.0 - BETA_TWO) * turned * turned
    step = (
        new_first
        / (1.0 - BETA_ONE**STEP)
        / (jnp.sqrt(new_second / (1.0 - BETA_TWO**STEP)) + ADAM_EPS)
    )
    back = nt(nn(left_low, step.astype(BF16)).astype(BF16), right_low)
    return new_first, new_second, master - RATE_TILE * (back + DECAY_RATE * master)


def adam_tiles(slot_list, flows, bases, state, held, waits=()):
    steps = slot_list.shape[0]

    def body(sc_ref, *refs):
        grads = refs[: len(flows)]
        left, right, first, second, master = refs[len(flows) : len(flows) + 5]
        o_first, o_second, o_master, o_low, mark = refs[-5:]
        mark[...] = jnp.zeros_like(mark)
        total = grads[0][0].astype(F32)
        for ref in grads[1:]:
            total = total + ref[0].astype(F32)
        new_first, new_second, new_master = adam_tile(
            total, left[0], right[0], first[0], second[0], master[0]
        )
        o_first[0] = new_first
        o_second[0] = new_second
        o_master[0] = new_master
        o_low[0] = new_master.astype(BF16)

    def at_slot(shape):
        return pl.BlockSpec((1,) + shape, lambda i, sc_ref: (sc_ref[i], 0, 0))

    slots = state[0].shape[0]
    shapes = [(TR, TC)] * 4
    types = [F32, F32, F32, BF16]
    extra = [] if held is None else list(held)
    base = 1 + len(flows) + 5
    return pl.pallas_call(
        body,
        out_shape=[sds((slots,) + s, t) for s, t in zip(shapes, types)] + [MARK],
        grid_spec=pltpu.PrefetchScalarGridSpec(
            num_scalar_prefetch=1,
            grid=(steps,),
            in_specs=[pl.BlockSpec((1, TR, TC), lambda i, sc_ref: (i, 0, 0))] * len(flows)
            + [at_slot((TR, TR)), at_slot((TC, TC))]
            + [at_slot((TR, TC))] * 3
            + [HBM] * (len(extra) + len(waits)),
            out_specs=[at_slot(s) for s in shapes]
            + [pl.BlockSpec((8, HD), lambda i, sc_ref: (0, 0))],
        ),
        input_output_aliases={base + i: i for i in range(len(extra))},
        compiler_params=pltpu.CompilerParams(vmem_limit_bytes=VMEM_ALL),
        cost_estimate=cost(steps * 8 * TR * TC * TC, steps * 5 * TR * TC * 4),
        name="adam_tiles",
    )(slot_list, *flows, *bases, *state, *extra, *waits)


def small_adam(grad, first, second, master):
    new_first = BETA_ONE * first + (1.0 - BETA_ONE) * grad
    new_second = BETA_TWO * second + (1.0 - BETA_TWO) * grad * grad
    step = (
        new_first
        / (1.0 - BETA_ONE**STEP)
        / (jnp.sqrt(new_second / (1.0 - BETA_TWO**STEP)) + ADAM_EPS)
    )
    return new_first, new_second, master - RATE_SMALL * (step + DECAY_RATE * master)


def signed_tables(places):
    middle = HD // 2
    frequency = ROPE_BASE ** (-(jnp.arange(middle, dtype=F32) * 2.0) / HD)
    angles = places.astype(F32)[:, None] * frequency[None, :]
    cosine = jnp.cos(angles)
    sine = jnp.sin(angles)
    return (
        jnp.concatenate([cosine, cosine], axis=1),
        jnp.concatenate([-sine, sine], axis=1),
    )


def token_layout(first_index, local_rows, seq_lengths):
    places = first_index + jnp.arange(local_rows, dtype=jnp.int32)
    number = seq_lengths.shape[0]
    below = jnp.arange(number)[None, :] <= jnp.arange(number)[:, None]
    bounds = jnp.sum(jnp.where(below, seq_lengths[None, :], 0), axis=1)
    passed = places[:, None] >= bounds[None, :]
    segment = jnp.sum(passed.astype(jnp.int32), axis=1)
    offset = places - jnp.sum(jnp.where(passed, seq_lengths[None, :], 0), axis=1)
    return (places, segment, offset)


def moves(target):
    pairs = []
    for z in range(4):
        for y in range(2):
            for x in range(2):
                for c in range(2):
                    to = target(z, y, x, c)
                    if to is not None:
                        a, b, e, f = to
                        pairs.append((8 * z + 4 * y + 2 * x + c, 8 * a + 4 * b + 2 * e + f))
    return pairs


def only(condition, target):
    return lambda z, y, x, c: target(z, y, x, c) if condition(z, y, x, c) else None


def flip(dz=0, dy=0, dx=0, dc=0):
    return lambda z, y, x, c: (z ^ dz, y ^ dy, x ^ dx, c ^ dc)


def own_group(z, y, x, c):
    return c == z % 2


def foreign(z, y, x, c):
    return c != z % 2


def send(value, target):
    return lax.ppermute(value, AXES, moves(target))


MEMBERS = (None, flip(dz=1), flip(dx=1), flip(dz=1, dx=1))
HEADMATES = (None, flip(dy=1), flip(dz=2), flip(dz=2, dy=1))


def scatter_pieces(pieces):
    return [pieces[0]] + [send(pieces[k], MEMBERS[k]) for k in range(1, 4)]


def share_piece(piece):
    return [piece] + [send(piece, MEMBERS[k]) for k in range(1, 4)]


def swap_heads(blocks):
    return [blocks[0]] + [send(blocks[k], HEADMATES[k]) for k in range(1, 4)]


def after(value, *others):
    return lax.optimization_barrier((value,) + others)[0]


def tied(values, done):
    return list(lax.optimization_barrier(tuple(values) + tuple(done))[: len(values)])


def small_step(values, bit, target):
    other = send(values, target)
    return jnp.where(
        bit == 0, jnp.concatenate([values, other]), jnp.concatenate([other, values])
    )


def local_remap(
    tokens, cotangent, attn_width, ffn_width, seq_lengths, tile_order, master, first_moment,
    second_moment, left_basis, right_basis, small_master, small_first, small_second,
):
    rows = tokens.shape[0]
    piece_rows = rows // 4
    s = lax.axis_index("seq")
    h = lax.axis_index("head")
    z, y, x, c = s // 2, s % 2, h // 2, h % 2
    zp, zh = z % 2, z // 2
    mine = c == zp
    group = 2 * x + zp
    spot = 2 * zh + y
    block = (2 * zh + c) * 2 + y

    y_move, h_move, c_move = flip(dy=1), flip(dz=2), flip(dc=1)

    slots = master.shape[1]
    part = slots // 4
    to_pair = only(own_group, flip(dz=1))
    near_move = lambda z, y, x, c: (z, y, x, 1 - c) if c == z % 2 else (z ^ 1, y, x, c)
    far_move = lambda z, y, x, c: (z ^ 2, y, x, 1 - c) if c == z % 2 else (z ^ 3, y, x, c)
    low = [master[0, i * part : (i + 1) * part].astype(BF16) for i in range(4)]
    near, far = [send(low[0], near_move)], [send(low[0], far_move)]
    order = tile_order[0]
    order_got = send(order, c_move)
    small_all = small_step(small_master.astype(BF16), y, y_move)
    wid = jnp.stack([attn_width, ffn_width])
    wid_got = send(wid, to_pair)
    near[0], order_got, small_all, low1, low2, low3, wid, wid_got = tied(
        [near[0], order_got, small_all] + low[1:] + [wid, wid_got], []
    )
    order = jnp.where(mine, order, order_got)
    base = jnp.where(mine, s ^ 2, s)
    base_there = jnp.where(mine, s, s ^ 2)

    def ids_of(*chunks):
        return jnp.concatenate(
            [
                lax.dynamic_slice_in_dim(order, (o ^ hop) * slots + i * part, part, 0)
                for o in (base, base_there)
                for hop, i in chunks
            ]
        )

    def by_kind(row):
        place = jnp.arange(slots, dtype=jnp.int32)
        key = jnp.where(row < FFN_TILE, slots, 0) + place
        rank = jnp.sum((key[:, None, :] < key[:, :, None]).astype(jnp.int32), axis=2)
        spot_of = rank[:, :, None] == place
        return jnp.sum(jnp.where(spot_of, row[:, :, None], 0), axis=1), jnp.sum(
            jnp.where(spot_of, place[:, None], 0), axis=1
        )

    sorted_order = by_kind(order.reshape(-1, slots))[0].reshape(-1)
    own_row = lax.dynamic_slice_in_dim(tile_order[0], s * slots, slots, 0)
    own_slots = by_kind(own_row[None])[1][0]
    enough = jnp.min(
        jnp.sum(
            (jnp.stack([tile_order[0], order_got]).reshape(-1, slots) >= FFN_TILE).astype(jnp.int32),
            axis=1,
        )
    )
    enough = jnp.full((HD,), enough, jnp.int32)
    enough = jnp.minimum(enough, send(enough, flip(dx=1)))
    near_y, far_y = [send(near[0], y_move)], []
    near.append(send(low1, near_move))
    small_all = small_step(small_all, zp, flip(dz=1))
    low23 = jnp.concatenate([low2, low3])
    near[0], near[1], far[0], near_y[0], small_all, low1, low2, low3, low23, enough = tied(
        [near[0], near[1], far[0], near_y[0], small_all, low1, low2, low3, low23, enough], []
    )
    far.append(send(low1, far_move))
    near_y.append(send(near[1], y_move))
    far_y.append(send(far[0], y_move))
    near23 = send(low23, near_move)
    small_all = small_step(small_all, zh, h_move)
    first = jnp.concatenate([near[0], near_y[0], far[0]])
    all_rows = rows * lax.axis_size("seq")
    blocks = all_rows // rows
    places, _, offset = token_layout(0, all_rows, seq_lengths)
    start = places - offset
    first_block = start.reshape(blocks, rows)[:, 0] // rows
    cosine, sine = signed_tables(offset)
    cosine, sine = cosine.reshape(blocks, rows, HD), sine.reshape(blocks, rows, HD)
    number = seq_lengths.shape[0]
    below = jnp.arange(number)[None, :] <= jnp.arange(number)[:, None]
    ends = jnp.sum(jnp.where(below, seq_lengths[None, :], 0), axis=1)
    scalars = jnp.concatenate(
        [
            jnp.stack([spot, group, c, group]).astype(jnp.int32),
            first_block.astype(jnp.int32),
            block[None].astype(jnp.int32),
            ends.astype(jnp.int32),
        ]
    )
    near[1], near23, far[1], near_y[1], far_y[0], low2, low3, small_all, first, cosine, sine, tok = tied(
        [near[1], near23, far[1], near_y[1], far_y[0], low2, low3, small_all, first]
        + [cosine, sine, tokens],
        [],
    )
    near += [near23[:part], near23[part:]]
    far.append(send(low2, far_move))
    near_y.append(send(near[2], y_move))
    far_y.append(send(far[1], y_move))
    first_there = send(first, c_move)
    tok_got = send(tok, to_pair)
    second = jnp.concatenate([near[1], near_y[1], far_y[0], far[1]])
    near[2], near[3], far[2], near_y[2], far_y[1], low3, small_all, first, first_there, second, tok, tok_got = tied(
        [near[2], near[3], far[2], near_y[2], far_y[1], low3, small_all, first, first_there]
        + [second, tok, tok_got],
        [],
    )
    far.append(send(low3, far_move))
    near_y.append(send(near[3], y_move))
    far_y.append(send(far[2], y_move))
    second_there = send(second, c_move)
    third = jnp.concatenate([near[2], near_y[2], far_y[1], far[2]])
    third_there = send(third, c_move)
    tiles, mark_one = place_tiles(ids_of((0, 0), (1, 0), (4, 0)), [first, first_there], None)
    tok = jnp.where(mine, tok, tok_got)
    widths = jnp.where(mine, wid, wid_got)
    width_a, width_f = widths[0][:, None], widths[1][:, None]
    gains = small_all[: 4 * D].astype(F32).reshape(4, 1, D)
    gain_one, bias_one, gain_two, bias_two = gains[0], gains[1], gains[2], gains[3]
    routers = small_all[4 * D :].reshape(D, 2 * WIDTHS)
    pad = ((0, 0), (0, HD - WIDTHS))
    router_a = jnp.pad(routers[:, :WIDTHS], pad)
    router_f = jnp.pad(routers[:, WIDTHS:], pad)
    router_ft, router_at = router_f.T, router_a.T
    a1, a1p, tokp, rap, coefp = flat_call(
        norm_one_body,
        scalars,
        [tok, gain_one, bias_one, router_a, width_a],
        [
            sds((rows, D), BF16),
            sds((piece_rows, D), BF16),
            sds((piece_rows, D), BF16),
            sds((piece_rows, 1), F32),
            sds((piece_rows, HD), F32),
        ],
        [pltpu.VMEM((rows, 1), F32), pltpu.VMEM((rows, HD), F32)],
        name="norm_one",
    )

    tiles, mark_two = place_tiles(
        ids_of((0, 1), (1, 1), (5, 0), (4, 1)), [second, second_there], tiles, [mark_one]
    )
    near[3], far[3], near_y[3], far_y[2], third, third_there, mark_two, a1, router_ft, router_at = tied(
        [near[3], far[3], near_y[3], far_y[2], third, third_there, mark_two, a1]
        + [router_ft, router_at],
        [],
    )
    far_y.append(send(far[3], y_move))
    fourth = [near[3], near_y[3], far_y[2], far[3]]
    fourth_there = [send(v, c_move) for v in fourth]
    tiles, mark_three = place_tiles(
        ids_of((0, 2), (1, 2), (5, 1), (4, 2)), [third, third_there], tiles, [mark_two]
    )
    tiles, mark_four = place_tiles(
        ids_of((0, 3), (1, 3), (5, 2), (4, 3)), fourth + fourth_there, tiles, [mark_three]
    )
    far_y[3], mark_four = tied([far_y[3], mark_four], [])
    fifth_there = send(far_y[3], c_move)
    tiles, _ = place_tiles(ids_of((5, 3)), [far_y[3], fifth_there], tiles, [mark_four])
    by_row = tiles.reshape(TILES // 4, 4, TR, TC)
    by_map = tiles.reshape(TILES // 8, 8, TR, TC)

    table = pl.BlockSpec((1, rows, HD), lambda i, sc: (sc[12], 0, 0))
    sent = pl.pallas_call(
        project_body,
        out_shape=[sds((3, rows, HD), BF16)] * 4,
        grid_spec=pltpu.PrefetchScalarGridSpec(
            num_scalar_prefetch=1,
            grid=(3,),
            in_specs=[
                pl.BlockSpec((rows, D), lambda i, sc: (0, 0)),
                pl.BlockSpec((1, 8, TR, TC), lambda i, sc: (i, 0, 0, 0)),
                table,
                table,
            ],
            out_specs=[pl.BlockSpec((1, rows, HD), lambda i, sc: (i, 0, 0))] * 4,
            scratch_shapes=[pltpu.VMEM((HPG, rows, HD), BF16)],
        ),
        compiler_params=params(),
        cost_estimate=cost(2 * rows * D * 3 * HG, 3 * D * HG * 2 + rows * D * 2),
        name="project",
    )(scalars, a1, by_map, cosine, sine)
    got = swap_heads(sent)
    beside = [send(v, flip(dc=1)) for v in got]
    dy = after(cotangent, *got)
    dy = jnp.where(mine, dy, send(dy, to_pair))

    pairs_cost = 4 * 4 * rows * rows * HD * 2
    out = flat_call(
        attend_body,
        scalars,
        got + beside,
        [sds((rows, HD), BF16)] * 4
        + [
            sds((4, rows, HD), F32),
            sds((4, rows, 1), F32),
            sds((4, rows, HD), BF16),
            sds((blocks, rows, HD), BF16),
            sds((blocks, rows, HD), BF16),
        ],
        [pltpu.VMEM((rows, 1), F32), pltpu.VMEM((rows, 1), F32), pltpu.VMEM((rows, HD), F32)],
        flops=2 * pairs_cost,
        name="attend",
    )
    ctx_sent, (ctx, lse, q_all, k_all, v_all) = out[:4], out[4:]
    ctx_got = swap_heads(ctx_sent)

    one_piece = sds((piece_rows, D), F32)
    low_piece = sds((piece_rows, D), BF16)
    piece_outs = [one_piece] + [low_piece] * 3
    wo_spec = pl.BlockSpec((2, 4, TR, TC), lambda i, sc: (3, 0, 0, 0))

    def whole(shape):
        return pl.BlockSpec(shape, lambda i, sc: (0,) * len(shape))

    out = pl.pallas_call(
        output_body,
        out_shape=[sds((rows, HG), BF16)] + piece_outs,
        grid_spec=pltpu.PrefetchScalarGridSpec(
            num_scalar_prefetch=1,
            grid=(1,),
            in_specs=[whole((rows, HD))] * 4 + [whole((rows, 1)), wo_spec],
            out_specs=[whole((rows, HG))] + [whole((piece_rows, D))] * 4,
            scratch_shapes=[pltpu.VMEM((rows, D), F32)],
        ),
        compiler_params=params(),
        cost_estimate=cost(2 * rows * D * HG, D * HG * 2 + rows * D * 4),
        name="output",
    )(scalars, *ctx_got, width_a, by_row)
    cb, attn_parts = out[0], out[1:]
    attn_parts = scatter_pieces(attn_parts)

    attn, h1, a2p = flat_call(
        norm_two_body,
        scalars,
        attn_parts + [tokp, rap, gain_two, bias_two],
        [one_piece, one_piece, low_piece],
        name="norm_two",
    )
    a2_parts = share_piece(a2p)

    up_spec = pl.BlockSpec((8, 1, TR, TC), lambda i, sc: (1, i, 0, 0))
    down_spec = pl.BlockSpec((2, 4, TR, TC), lambda i, sc: (8 + i, 0, 0, 0))
    col_spec = pl.BlockSpec((rows, TC), lambda i, sc: (0, i))
    out = pl.pallas_call(
        ffn_body,
        out_shape=[
            sds((rows, D), BF16),
            sds((rows, FG), BF16),
            sds((rows, FG), BF16),
            sds((rows, D), BF16),
            sds((rows, HD), F32),
            sds((piece_rows, 1), F32),
        ]
        + piece_outs,
        grid_spec=pltpu.PrefetchScalarGridSpec(
            num_scalar_prefetch=1,
            grid=(FG // TC,),
            in_specs=[whole((piece_rows, D))] * 4
            + [whole((rows, D)), whole((rows, 1)), whole((D, HD)), up_spec, down_spec],
            out_specs=[
                whole((rows, D)),
                col_spec,
                col_spec,
                whole((rows, D)),
                whole((rows, HD)),
                whole((piece_rows, 1)),
            ]
            + [whole((piece_rows, D))] * 4,
            scratch_shapes=[
                pltpu.VMEM((rows, D), F32),
                pltpu.VMEM((rows, HD), F32),
                pltpu.VMEM((rows, 1), F32),
            ],
        ),
        compiler_params=params(),
        cost_estimate=cost(4 * rows * D * FG, 4 * D * FG + rows * D * 12),
        name="ffn",
    )(scalars, *a2_parts, dy, width_f, router_f, by_row, by_row)
    a2, act, relu, gffn, dlog_f, rfp = out[:6]
    ffn_parts = out[6:]

    out = pl.pallas_call(
        ffn_back_body,
        out_shape=[sds((rows, FG), BF16)] + piece_outs,
        grid_spec=pltpu.PrefetchScalarGridSpec(
            num_scalar_prefetch=1,
            grid=(FG // TC,),
            in_specs=[
                whole((rows, D)),
                col_spec,
                whole((rows, HD)),
                whole((HD, D)),
                up_spec,
                down_spec,
            ],
            out_specs=[col_spec] + [whole((piece_rows, D))] * 4,
            scratch_shapes=[pltpu.VMEM((rows, D), F32)],
        ),
        compiler_params=params(),
        cost_estimate=cost(4 * rows * D * FG, 4 * D * FG + rows * D * 12),
        name="ffn_back",
    )(scalars, gffn, relu, dlog_f, router_ft, by_row, by_row)
    gpre, ga2_parts = out[0], scatter_pieces(out[1:])

    begins = [sum(CHUNKS[:i]) for i in range(len(CHUNKS))]

    def grad_ids(flip_y, i):
        owners = (s ^ flip_y ^ jnp.where(mine, 2, 4), s ^ flip_y ^ jnp.where(mine, 6, 0))
        return jnp.concatenate(
            [
                lax.dynamic_slice_in_dim(sorted_order, o * slots + begins[i], CHUNKS[i], 0)
                for o in owners
            ]
        )

    def route(own, other):
        return lambda z, y, x, c: (z ^ (own if c == z % 2 else other), y, x, z % 2)

    def to_owners(first, second):
        return [send(first, route(1, 2)), send(second, route(3, 0))]

    a2_there, act_there, gffn_there = [send(v, c_move) for v in (a2, act, gffn)]
    gpre_there = send(gpre, c_move)
    early_lefts = [[a2, act, a2, act], [a2_there, act_there, a2_there, act_there]]
    early_rights = [[gffn, gffn, gpre, gffn], [gffn_there, gffn_there, gpre_there, gffn_there]]
    early_away = tile_grads(grad_ids(1, 0), early_lefts, early_rights, None, [2 * CHUNKS[0]])[0]
    early_away, *ga2_parts = tied([early_away] + ga2_parts, [])
    early_back = send(early_away, y_move)

    dh1, gattnp, dlog_a, ggain_two, gbias_two = flat_call(
        norm_two_back_body,
        scalars,
        ga2_parts + [h1, attn, dy, rap, coefp, gain_two],
        [one_piece, low_piece, sds((piece_rows, HD), F32), sds((1, D), F32), sds((1, D), F32)],
        name="norm_two_back",
    )
    gattn_parts = share_piece(gattnp)
    out = pl.pallas_call(
        gout_body,
        out_shape=[sds((rows, D), BF16)] + [sds((rows, HD), BF16)] * 4,
        grid_spec=pltpu.PrefetchScalarGridSpec(
            num_scalar_prefetch=1,
            grid=(1,),
            in_specs=[whole((piece_rows, D))] * 4 + [whole((rows, 1)), wo_spec],
            out_specs=[whole((rows, D))] + [whole((rows, HD))] * 4,
            scratch_shapes=[pltpu.VMEM((HPG, rows, HD), BF16)],
        ),
        compiler_params=params(),
        cost_estimate=cost(2 * rows * D * HG, D * HG * 2 + rows * D * 4),
        name="gout",
    )(scalars, *gattn_parts, width_a, by_row)
    gattn, *gout_sent, early_back = tied(list(out) + [early_back], [])
    gout_got = swap_heads(gout_sent)
    early_here = tile_grads(
        grad_ids(0, 0), early_lefts, early_rights, early_back, [CHUNKS[0]] * 2
    )[:2]
    *early_here, gout_got[0] = tied(list(early_here) + [gout_got[0]], [])
    early_flow = [send(early_here[0], route(1, 2))]

    gq, keys_own, keys_other = flat_call(
        attend_back_body,
        scalars,
        [cosine, sine, q_all, k_all, v_all, ctx]
        + [lse.reshape(4, 1, rows)]
        + gout_got,
        [
            sds((4, rows, HD), BF16),
            sds((4, 2, rows, HD), F32),
            sds((4, 2, rows, HD), BF16),
        ],
        [
            pltpu.VMEM((4, rows, HD), BF16),
            pltpu.VMEM((blocks, rows, HD), F32),
            pltpu.VMEM((blocks, rows, HD), F32),
            pltpu.VMEM((rows, HD), F32),
        ],
        flops=5 * pairs_cost,
        name="attend_back",
    )
    gq, early_flow[0] = tied([gq, early_flow[0]], [])
    grads_sent = flat_call(
        key_merge_body,
        scalars,
        [gq, keys_own, send(keys_other, flip(dc=1)), cosine, sine],
        [sds((3, rows, HD), BF16)] * 4,
        name="key_merge",
    )
    grads_got = swap_heads(grads_sent)
    (gin,) = flat_call(
        gather_input_body, scalars, grads_got, [sds((rows, 3 * HG), BF16)], name="gather_input"
    )
    a1_there, cb_there, gattn_there = [send(v, c_move) for v in (a1, cb, gattn)]
    lefts = [[a1, cb, a2, act], [a1_there, cb_there, a2_there, act_there]]
    rights = [
        [gin, gattn, gpre, gffn],
        [send(gin, c_move), gattn_there, gpre_there, gffn_there],
    ]

    def away_of(i):
        return tile_grads(grad_ids(1, i), lefts, rights, None, [2 * CHUNKS[i]])[0]

    bases = (left_basis[0], right_basis[0])
    state = (first_moment[0], second_moment[0], master[0])
    gin, away1, early_last = tied([gin, away_of(1), early_here[1]], [])
    back1 = send(away1, y_move)
    early_flow.append(send(early_last, route(3, 0)))
    gin, away2, away3 = tied([gin, away_of(2), away_of(3)], [])
    back2 = send(away2, y_move)
    half_cols = D // 2
    half_piece = pl.BlockSpec((piece_rows, half_cols), lambda i, sc: (0, i))
    pair_piece = pl.BlockSpec((2, piece_rows, half_cols), lambda i, sc: (0, 0, i))
    out = pl.pallas_call(
        input_back_body,
        out_shape=[one_piece] + [sds((2, piece_rows, D), BF16)] * 3,
        grid_spec=pltpu.PrefetchScalarGridSpec(
            num_scalar_prefetch=1,
            grid=(2,),
            in_specs=[
                whole((rows, 3 * HG)),
                pl.BlockSpec((3, 4, TR, TC), lambda i, sc: (0, i, 0, 0)),
                half_piece,
                half_piece,
                half_piece,
            ],
            out_specs=[half_piece] + [pair_piece] * 3,
            scratch_shapes=[pltpu.VMEM((rows, half_cols), F32)],
        ),
        compiler_params=params(),
        cost_estimate=cost(2 * rows * D * 3 * HG, 3 * D * HG * 2 + rows * D * 4),
        name="input_back",
    )(scalars, gin, by_map, *ffn_parts[1:])
    pieces = [out[0], send(out[1], MEMBERS[1]), send(out[2], MEMBERS[2])]
    pieces[1], pieces[2], last_piece = tied([pieces[1], pieces[2], out[3]], [])
    pieces.append(send(last_piece, MEMBERS[3]))

    def tile_step(i, back, waits):
        first, second, mark = tile_grads(
            grad_ids(0, i), lefts, rights, back, [CHUNKS[i]] * 2, waits
        )
        return to_owners(first, second), [mark]

    def adam_step(i, flow, held, waits=()):
        chosen = own_slots[begins[i] : begins[i] + CHUNKS[i]]
        return adam_tiles(chosen, flow, bases, state, held, waits)

    back, away3, *early_flow = tied([back1, away3] + early_flow, [])
    back3 = send(away3, y_move)
    flow1, mark = tile_step(1, back, [])
    *pieces, mark = tied(pieces + mark, [])
    mark = [mark]
    both, ggain_one, gbias_one = flat_call(
        norm_one_back_body,
        scalars,
        pieces
        + [ffn_parts[0], tokp, h1, rfp, dh1, dlog_a, router_at, gain_one],
        [sds((2, piece_rows, D), BF16), sds((1, D), F32), sds((1, D), F32)],
        name="norm_one_back",
    )
    grad_router = jnp.concatenate(
        [
            lax.dot_general(
                a1p.astype(F32), dlog_a[:, :WIDTHS], (((0,), (0,)), ((), ())), precision=PRECISE
            ),
            lax.dot_general(
                a2.astype(F32), dlog_f[:, :WIDTHS], (((0,), (0,)), ((), ())), precision=PRECISE
            ),
        ],
        axis=1,
    ).reshape(-1)
    terms = jnp.concatenate(
        [ggain_one[0], gbias_one[0], ggain_two[0], gbias_two[0], grad_router]
    ).reshape(8, -1)
    terms = terms + send(terms, c_move)
    terms = terms + send(terms, flip(dx=1))

    def fold(terms, axis, bit, target):
        low_half = lax.index_in_dim(terms, 0, axis, keepdims=False)
        high_half = lax.index_in_dim(terms, 1, axis, keepdims=False)
        keep = jnp.where(bit == 0, low_half, high_half)
        return keep, send(jnp.where(bit == 0, high_half, low_half), target)


    def again():
        once_more = send(away_of(0), y_move)
        return to_owners(
            *tile_grads(grad_ids(0, 0), lefts, rights, once_more, [CHUNKS[0]] * 2)[:2]
        )

    flow0 = lax.cond(enough[0] >= CHUNKS[0], lambda: early_flow, again)
    back, both, terms, *mark = tied([back2, both, terms] + mark, [])
    flow2, mark = tile_step(2, back, mark)
    both_z = send(both, only(foreign, flip(dz=1)))
    keep, terms = fold(terms.reshape(2, 2, 2, -1), 0, zh, h_move)
    *held, adam_mark = adam_step(0, flow0, None)
    back, both, both_z, *rest = tied([back3, both, both_z, adam_mark] + mark + flow1, [])
    mark, flow1 = rest[:2], rest[2:]
    flow3, mark = tile_step(3, back, mark)
    both_x = send(both, only(own_group, flip(dx=1)))
    both_xz = send(both, only(foreign, flip(dz=1, dx=1)))
    *held, adam_mark = adam_step(1, flow1, held, mark)
    both_x, both_xz, keep, terms, *flow2 = tied(
        [both_x, both_xz, keep, terms] + flow2 + [adam_mark], []
    )
    flow2, marks = flow2[:2], flow2[2:]
    keep, terms = fold(keep + terms, 0, zp, flip(dz=1))
    keep, terms = fold(keep + terms, 0, y, y_move)
    (joined,) = flat_call(
        join_body,
        scalars,
        [both, both_z, both_x, both_xz],
        [sds((2, rows, D), BF16)],
        name="join",
    )
    joined = jnp.where(mine, joined, send(joined, only(own_group, c_move)))
    input_grad, output = joined[0].astype(F32), joined[1]
    held = adam_step(2, flow2, held, marks)[:4]
    input_grad, output, *flow3 = tied([input_grad, output] + flow3, [])
    held = adam_step(3, flow3, held)
    terms = keep + terms
    small_outs = small_adam(terms.reshape(-1), small_first, small_second, small_master)

    return (
        output,
        input_grad,
        held[0][None],
        held[1][None],
        held[2][None],
        held[3][None],
        *small_outs,
    )


CHUNKS = (3, 4, 3, 2)
FFN_TILE = 32


def layer_norm(values, weight_gain, weight_bias):
    center = values - jnp.mean(values, axis=1, keepdims=True)
    spread = jnp.mean(center * center, axis=1, keepdims=True)
    return center * lax.rsqrt(spread + EPS_NORM) * weight_gain + weight_bias


def rotary_tables(places):
    middle = HD // 2
    frequency = ROPE_BASE ** (-(jnp.arange(middle, dtype=jnp.float32) * 2.0) / HD)
    angles = places.astype(jnp.float32)[:, None] * frequency[None, :]
    cosine_half = jnp.cos(angles)
    sine_half = jnp.sin(angles)
    return (
        jnp.concatenate([cosine_half, cosine_half], axis=1),
        jnp.concatenate([sine_half, sine_half], axis=1),
    )


def rotary(values, cosine_table, sine_table):
    middle = HD // 2
    turned = jnp.concatenate([-values[..., middle:], values[..., :middle]], axis=-1)
    return values * cosine_table[:, None, :] + turned * sine_table[:, None, :]


def rotary_back(gradients, cosine_table, sine_table):
    middle = HD // 2
    scaled = gradients * sine_table[:, None, :]
    turned = jnp.concatenate([scaled[..., middle:], -scaled[..., :middle]], axis=-1)
    return gradients * cosine_table[:, None, :] + turned


def from_tiles(tile_stack, rows_total, cols_total):
    return (
        tile_stack.reshape(rows_total // TR, cols_total // TC, TR, TC)
        .transpose(0, 2, 1, 3)
        .reshape(rows_total, cols_total)
    )


def unpack(tile_stack):
    count_in = D // TR * (HG // TC)
    count_out = HG // TR * (D // TC)
    count_up = D // TR * (FG // TC)
    edge_out = 3 * count_in
    edge_up = edge_out + count_out
    edge_down = edge_up + count_up
    w_inputs = jnp.concatenate(
        [
            from_tiles(tile_stack[:count_in], D, HG),
            from_tiles(tile_stack[count_in : 2 * count_in], D, HG),
            from_tiles(tile_stack[2 * count_in : edge_out], D, HG),
        ],
        axis=1,
    )
    w_output = from_tiles(tile_stack[edge_out:edge_up], HG, D)
    w_up = from_tiles(tile_stack[edge_up:edge_down], D, FG)
    w_down = from_tiles(tile_stack[edge_down:], FG, D)
    return (w_inputs, w_output, w_up, w_down)


def router_scale(acts_low, router_map, chosen):
    logits = jnp.dot(acts_low.astype(jnp.float32), router_map, precision=PRECISE)
    probs_all = jax.nn.softmax(logits, axis=1)
    picked = (chosen[:, None] - 1 == jnp.arange(WIDTHS)[None, :]).astype(jnp.float32)
    return (WIDTHS * jnp.sum(probs_all * picked, axis=1), probs_all, picked)


def router_back(grad_scale, probs_all, picked):
    chosen_prob = jnp.sum(probs_all * picked, axis=1)
    return (WIDTHS * grad_scale * chosen_prob)[:, None] * (picked - probs_all)


def scores_of(queries, key_block, query_index, query_segment, key_index, key_segment):
    raw_scores = jnp.einsum(
        "qhd,khd->hqk", queries, key_block, preferred_element_type=jnp.float32
    ) * HD ** (-0.5)
    allowed = (key_segment[None, :] == query_segment[:, None]) & (
        key_index[None, :] <= query_index[:, None]
    )
    return (raw_scores, allowed[None])


def fetch_block(packed_all, all_index, all_segment, number, block_rows):
    start = number * block_rows
    piece_rows = lax.dynamic_slice_in_dim(packed_all, start, block_rows, 0)
    key_index = lax.dynamic_slice_in_dim(all_index, start, block_rows, 0)
    key_segment = lax.dynamic_slice_in_dim(all_segment, start, block_rows, 0)
    first_half = piece_rows[:, :HG].reshape(block_rows, HPG, HD)
    second_half = piece_rows[:, HG:].reshape(block_rows, HPG, HD)
    return (first_half, second_half, key_index, key_segment)


def attend_forward(queries, token_index, segment, packed_all, all_index, all_segment, block_rows):
    local_rows = queries.shape[0]
    blocks = packed_all.shape[0] // block_rows

    def first_pass(carried, number):
        running_max, running_sum = carried
        key_block, value_block, key_index, key_segment = fetch_block(
            packed_all, all_index, all_segment, number, block_rows
        )
        raw_scores, allowed = scores_of(
            queries, key_block, token_index, segment, key_index, key_segment
        )
        masked = jnp.where(allowed, raw_scores, NEG_FILL)
        fresh_max = jnp.maximum(running_max, jnp.max(masked, axis=2))
        running_sum = running_sum * jnp.exp(running_max - fresh_max) + jnp.sum(
            jnp.exp(masked - fresh_max[:, :, None]), axis=2
        )
        return ((fresh_max, running_sum), None)

    start_state = (
        jnp.full((HPG, local_rows), NEG_FILL, jnp.float32),
        jnp.zeros((HPG, local_rows), jnp.float32),
    )
    (running_max, running_sum), unused = lax.scan(first_pass, start_state, jnp.arange(blocks))
    log_sum = running_max + jnp.log(running_sum)

    def second_pass(carried, number):
        key_block, value_block, key_index, key_segment = fetch_block(
            packed_all, all_index, all_segment, number, block_rows
        )
        raw_scores, allowed = scores_of(
            queries, key_block, token_index, segment, key_index, key_segment
        )
        weights_p = jnp.where(allowed, jnp.exp(raw_scores - log_sum[:, :, None]), 0.0)
        update = jnp.einsum(
            "hqk,khd->qhd",
            weights_p.astype(jnp.bfloat16),
            value_block,
            preferred_element_type=jnp.float32,
        )
        return (carried + update, None)

    context, unused = lax.scan(
        second_pass, jnp.zeros((local_rows, HPG, HD), jnp.float32), jnp.arange(blocks)
    )
    return (log_sum, context)


def pair_grads(
    queries,
    grad_out,
    log_sum,
    delta,
    query_index,
    query_segment,
    key_block,
    value_block,
    key_index,
    key_segment,
):
    raw_scores, allowed = scores_of(
        queries, key_block, query_index, query_segment, key_index, key_segment
    )
    weights_p = jnp.where(allowed, jnp.exp(raw_scores - log_sum[:, :, None]), 0.0)
    grad_value = jnp.einsum(
        "hqk,qhd->khd", weights_p.astype(jnp.bfloat16), grad_out, preferred_element_type=jnp.float32
    )
    grad_probs = jnp.einsum(
        "qhd,khd->hqk", grad_out, value_block, preferred_element_type=jnp.float32
    )
    grad_raw = (weights_p * (grad_probs - delta[:, :, None]) * HD ** (-0.5)).astype(jnp.bfloat16)
    grad_query = jnp.einsum("hqk,khd->qhd", grad_raw, key_block, preferred_element_type=jnp.float32)
    grad_key = jnp.einsum("hqk,qhd->khd", grad_raw, queries, preferred_element_type=jnp.float32)
    return (grad_query, grad_key, grad_value)


def local_plain(
    tokens,
    cotangent,
    attn_width,
    ffn_width,
    seq_lengths,
    tile_order,
    master,
    first_moment,
    second_moment,
    left_basis,
    right_basis,
    small_master,
    small_first,
    small_second,
):
    local_rows = tokens.shape[0]
    shards = lax.axis_size("seq")
    all_rows = local_rows * shards
    block_rows = min(KB_CAP, all_rows)
    blocks = all_rows // block_rows
    group_id = lax.axis_index("head")
    slot_order = tile_order[0]
    weights_all, small_all = (
        lax.all_gather(master[0].astype(jnp.bfloat16), "seq", axis=0, tiled=True),
        lax.all_gather(small_master.astype(jnp.bfloat16), "seq", axis=0, tiled=True),
    )
    w_inputs, w_output, w_up, w_down = unpack(place_tiles(slot_order, [weights_all], None)[0])
    small_vals = small_all.astype(jnp.float32)
    gain_one = small_vals[0:D]
    bias_one = small_vals[D : 2 * D]
    gain_two = small_vals[2 * D : 3 * D]
    bias_two = small_vals[3 * D : 4 * D]
    routers = small_vals[4 * D :].reshape(D, 2 * WIDTHS)
    router_attn = routers[:, :WIDTHS]
    router_ffn = routers[:, WIDTHS:]
    first_row = lax.axis_index("seq") * local_rows
    token_index, segment, offset = token_layout(first_row, local_rows, seq_lengths)
    residual = tokens.astype(jnp.float32)
    ln_one, pull_one = jax.vjp(layer_norm, residual, gain_one, bias_one)
    act_one = ln_one.astype(jnp.bfloat16)
    scale_attn, probs_attn, picked_attn = router_scale(act_one, router_attn, attn_width)
    projected = jnp.dot(act_one, w_inputs, preferred_element_type=jnp.float32)
    cosine_table, sine_table = rotary_tables(offset)
    query_low = rotary(
        projected[:, :HG].reshape(local_rows, HPG, HD), cosine_table, sine_table
    ).astype(jnp.bfloat16)
    key_low = rotary(
        projected[:, HG : 2 * HG].reshape(local_rows, HPG, HD), cosine_table, sine_table
    ).astype(jnp.bfloat16)
    value_low = projected[:, 2 * HG :].astype(jnp.bfloat16)
    packed = jnp.concatenate([key_low.reshape(local_rows, HG), value_low], axis=1)
    packed_all = lax.all_gather(packed, "seq", axis=0, tiled=True)
    all_index, all_segment, all_offset = token_layout(0, all_rows, seq_lengths)
    log_sum, context = attend_forward(
        query_low, token_index, segment, packed_all, all_index, all_segment, block_rows
    )
    head_mask = (group_id < attn_width).astype(jnp.float32)
    ctx_low = (context * head_mask[:, None, None]).astype(jnp.bfloat16).reshape(local_rows, HG)
    attn_out = lax.psum(
        jnp.dot(ctx_low, w_output, preferred_element_type=jnp.float32).astype(jnp.bfloat16), "head"
    ).astype(jnp.float32)
    middle_res = residual + scale_attn[:, None] * attn_out
    ln_two, pull_two = jax.vjp(layer_norm, middle_res, gain_two, bias_two)
    act_two = ln_two.astype(jnp.bfloat16)
    scale_ffn, probs_ffn, picked_ffn = router_scale(act_two, router_ffn, ffn_width)
    pre_act = jnp.dot(act_two, w_up, preferred_element_type=jnp.float32)
    unit_mask = (group_id < ffn_width).astype(jnp.float32)
    hidden_low = (jnp.square(jnp.maximum(pre_act, 0.0)) * unit_mask[:, None]).astype(jnp.bfloat16)
    ffn_out = lax.psum(
        jnp.dot(hidden_low, w_down, preferred_element_type=jnp.float32).astype(jnp.bfloat16), "head"
    ).astype(jnp.float32)
    output = (middle_res + scale_ffn[:, None] * ffn_out).astype(jnp.bfloat16)
    grad_top = cotangent.astype(jnp.float32)
    grad_scale_ffn = jnp.sum(grad_top * ffn_out, axis=1)
    grad_ffn_low = (scale_ffn[:, None] * grad_top).astype(jnp.bfloat16)
    grad_hidden = jnp.dot(grad_ffn_low, w_down.T, preferred_element_type=jnp.float32)
    grad_pre_low = (grad_hidden * unit_mask[:, None] * 2.0 * jnp.maximum(pre_act, 0.0)).astype(
        jnp.bfloat16
    )
    grad_act_two = lax.psum(
        jnp.dot(grad_pre_low, w_up.T, preferred_element_type=jnp.float32).astype(jnp.bfloat16),
        "head",
    ).astype(jnp.float32)
    logit_ffn = router_back(grad_scale_ffn, probs_ffn, picked_ffn)
    grad_act_two = grad_act_two + jnp.dot(logit_ffn, router_ffn.T, precision=PRECISE)
    grad_mid_ln, grad_gain_two, grad_bias_two = pull_two(grad_act_two)
    grad_middle = grad_top + grad_mid_ln
    grad_scale_attn = jnp.sum(grad_middle * attn_out, axis=1)
    grad_attn_low = (scale_attn[:, None] * grad_middle).astype(jnp.bfloat16)
    grad_context = jnp.dot(grad_attn_low, w_output.T, preferred_element_type=jnp.float32)
    grad_out_low = (
        (grad_context * head_mask[:, None]).astype(jnp.bfloat16).reshape(local_rows, HPG, HD)
    )
    delta = jnp.sum(grad_out_low.astype(jnp.float32) * context, axis=2).T
    zero_state = jnp.zeros((local_rows, HPG, HD), jnp.float32)

    def visit_keys(carried, number):
        key_block, value_block, key_index, key_segment = fetch_block(
            packed_all, all_index, all_segment, number, block_rows
        )
        grad_query, grad_key, grad_value = pair_grads(
            query_low,
            grad_out_low,
            log_sum,
            delta,
            token_index,
            segment,
            key_block,
            value_block,
            key_index,
            key_segment,
        )
        return (
            carried + grad_query,
            jnp.concatenate(
                [grad_key.reshape(block_rows, HG), grad_value.reshape(block_rows, HG)], axis=1
            ),
        )

    grad_query_rot, key_terms = lax.scan(visit_keys, zero_state, jnp.arange(blocks))
    summed = lax.psum_scatter(
        key_terms.reshape(all_rows, 2 * HG).astype(jnp.bfloat16),
        "seq",
        scatter_dimension=0,
        tiled=True,
    ).astype(jnp.float32)
    grad_key_rot = summed[:, :HG].reshape(local_rows, HPG, HD)
    grad_value_all = summed[:, HG:].reshape(local_rows, HPG, HD)
    grad_query_low = (
        rotary_back(grad_query_rot, cosine_table, sine_table)
        .astype(jnp.bfloat16)
        .reshape(local_rows, HG)
    )
    grad_key_low = (
        rotary_back(grad_key_rot, cosine_table, sine_table)
        .astype(jnp.bfloat16)
        .reshape(local_rows, HG)
    )
    grad_value_low = grad_value_all.astype(jnp.bfloat16).reshape(local_rows, HG)
    grad_inputs_low = jnp.concatenate([grad_query_low, grad_key_low, grad_value_low], axis=1)
    grad_act_one = lax.psum(
        jnp.dot(grad_inputs_low, w_inputs.T, preferred_element_type=jnp.float32).astype(
            jnp.bfloat16
        ),
        "head",
    ).astype(jnp.float32)
    logit_attn = router_back(grad_scale_attn, probs_attn, picked_attn)
    grad_act_one = grad_act_one + jnp.dot(logit_attn, router_attn.T, precision=PRECISE)
    grad_res_ln, grad_gain_one, grad_bias_one = pull_one(grad_act_one)
    input_grad = grad_middle + grad_res_ln
    grad_router = jnp.concatenate(
        [
            jnp.dot(act_one.astype(jnp.float32).T, logit_attn, precision=PRECISE),
            jnp.dot(act_two.astype(jnp.float32).T, logit_ffn, precision=PRECISE),
        ],
        axis=1,
    ).reshape(-1)
    small_terms = jnp.concatenate(
        [grad_gain_one, grad_bias_one, grad_gain_two, grad_bias_two, grad_router]
    )
    tile_terms = tile_grads(
        slot_order,
        [[act_one, ctx_low, act_two, hidden_low]],
        [[grad_inputs_low, grad_attn_low, grad_pre_low, grad_ffn_low]],
        None,
        [slot_order.shape[0]],
    )[0]
    tile_grad, small_grad = (
        lax.psum_scatter(tile_terms, "seq", scatter_dimension=0, tiled=True),
        lax.psum_scatter(
            small_terms.astype(jnp.bfloat16), "seq", scatter_dimension=0, tiled=True
        ).astype(jnp.float32),
    )
    slots = master.shape[1]
    held = adam_tiles(
        jnp.arange(slots, dtype=jnp.int32),
        [tile_grad],
        (left_basis[0], right_basis[0]),
        (first_moment[0], second_moment[0], master[0]),
        None,
    )
    small_outs = small_adam(small_grad, small_first, small_second, small_master)
    return (
        output,
        input_grad,
        held[0][None],
        held[1][None],
        held[2][None],
        held[3][None],
        *small_outs,
    )


def solution(mesh):
    return jax.shard_map(
        local_remap if dict(mesh.shape) == {"seq": 8, "head": 4} else local_plain,
        mesh=mesh,
        in_specs=(
            P("seq", None),
            P("seq", None),
            P("seq"),
            P("seq"),
            P(),
            P("head", None),
            P("head", "seq", None, None),
            P("head", "seq", None, None),
            P("head", "seq", None, None),
            P("head", "seq", None, None),
            P("head", "seq", None, None),
            P("seq"),
            P("seq"),
            P("seq"),
        ),
        out_specs=(
            P("seq", None),
            P("seq", None),
            P("head", "seq", None, None),
            P("head", "seq", None, None),
            P("head", "seq", None, None),
            P("head", "seq", None, None),
            P("seq"),
            P("seq"),
            P("seq"),
        ),
        check_vma=False,
    )
```

```python
import functools

import jax
import jax.numpy as jnp
from jax import lax
from jax.experimental import pallas as pl
from jax.experimental.pallas import tpu as pltpu
from jax.sharding import PartitionSpec as P

D = 2048
HD = 128
WIDTHS = 4
TR = 256
TC = 512
TILES = 96
STEP = 10
KB_CAP = 1024
HPG = 4
HG = 512
FG = 2048

PRECISE = lax.Precision.HIGHEST
EPS_NORM = 1e-05
BETA_ONE = 0.95
BETA_TWO = 0.95
ADAM_EPS = 1e-08
DECAY_RATE = 0.01
RATE_TILE = 0.15
RATE_SMALL = 1.0
ROPE_BASE = 10000.0
NEG_FILL = -1e30
SCORE_SCALE = HD ** (-0.5)
F32 = jnp.float32
BF16 = jnp.bfloat16
AXES = ("seq", "head")
VMEM_BIG = 56 << 20
VMEM_ALL = 61 << 20


def nt(a, b):
    return lax.dot_general(a, b, (((1,), (1,)), ((), ())), preferred_element_type=F32)


def nn(a, b):
    return lax.dot_general(a, b, (((1,), (0,)), ((), ())), preferred_element_type=F32)


def tn(a, b):
    return lax.dot_general(a, b, (((0,), (0,)), ((), ())), preferred_element_type=F32)


VM = pl.BlockSpec(memory_space=pltpu.VMEM)
SM = pl.BlockSpec(memory_space=pltpu.SMEM)
HBM = pl.BlockSpec(memory_space=pltpu.MemorySpace.HBM)


def sds(shape, dtype):
    return jax.ShapeDtypeStruct(shape, dtype)


MARK = sds((8, HD), F32)


def params():
    return pltpu.CompilerParams(vmem_limit_bytes=VMEM_BIG)


def cost(flops, nbytes):
    return pl.CostEstimate(flops=int(flops), bytes_accessed=int(nbytes), transcendentals=0)


def flat_call(body, scalars, arrays, outs, scratch=(), flops=0, name=None):
    nbytes = sum(a.size * a.dtype.itemsize for a in arrays)
    nbytes += sum(int(jnp.dtype(o.dtype).itemsize) * o.size for o in outs)
    return pl.pallas_call(
        body,
        out_shape=outs,
        in_specs=[SM] + [VM] * len(arrays),
        out_specs=[VM] * len(outs),
        scratch_shapes=list(scratch),
        compiler_params=params(),
        cost_estimate=cost(flops, nbytes),
        name=name,
    )(scalars, *arrays)


def rows_of(ref, index, rows):
    return ref[pl.ds(pl.multiple_of(index * rows, rows), rows), :]


def put_rows(ref, index, rows, value):
    ref[pl.ds(pl.multiple_of(index * rows, rows), rows), :] = value


def store_pieces(acc_ref, piece, rows, outs):
    outs[0][...] = rows_of(acc_ref, piece, rows)
    for k in range(1, 4):
        outs[k][...] = rows_of(acc_ref, piece ^ k, rows).astype(BF16)


def row_stats(values):
    center = values - jnp.mean(values, axis=1, keepdims=True)
    rstd = lax.rsqrt(jnp.mean(center * center, axis=1, keepdims=True) + EPS_NORM)
    return center * rstd, rstd


def route_level(logits, width_col):
    lane = lax.broadcasted_iota(jnp.int32, logits.shape, 1)
    live = lane < WIDTHS
    top = jnp.max(jnp.where(live, logits, NEG_FILL), axis=1, keepdims=True)
    raised = jnp.where(live, jnp.exp(jnp.where(live, logits, NEG_FILL) - top), 0.0)
    probs = raised / jnp.sum(raised, axis=1, keepdims=True)
    picked = (lane == width_col - 1).astype(F32)
    chosen = jnp.sum(probs * picked, axis=1, keepdims=True)
    return WIDTHS * chosen, WIDTHS * chosen * (picked - probs)


def split_dot(values, right_low):
    high = values.astype(BF16)
    rest = (values - high.astype(F32)).astype(BF16)
    return nn(high, right_low) + nn(rest, right_low)


def norm_one_body(sc, tok, gain, bias, router, width, a1, a1p, tokp, rap, coefp, ra_s, coef_s):
    rows = a1p.shape[0]
    piece = sc[1]
    xhat, _ = row_stats(tok[...].astype(F32))
    low = (xhat * gain[...] + bias[...]).astype(BF16)
    a1[...] = low
    scale, coef = route_level(nn(low, router[...]), width[...])
    ra_s[...] = scale
    coef_s[...] = coef
    a1p[...] = rows_of(a1, piece, rows)
    tokp[...] = rows_of(tok, piece, rows)
    rap[...] = rows_of(ra_s, piece, rows)
    coefp[...] = rows_of(coef_s, piece, rows)


def turn(values, cosine, signed_sine):
    return values * cosine + pltpu.roll(values, HD // 2, 1) * signed_sine


def turn_back(values, cosine, signed_sine):
    return values * cosine - pltpu.roll(values, HD // 2, 1) * signed_sine


def project_body(sc, a1, weights, cosine, sine, o0, o1, o2, o3, heads_s):
    step = pl.program_id(0)
    spot = sc[0]
    out = nn(a1[...], weights[...].reshape(D, HG))
    plain = step == 2
    cos_v = jnp.where(plain, 1.0, cosine[0])
    sin_v = jnp.where(plain, 0.0, sine[0])
    for head in range(HPG):
        heads_s[head] = turn(out[:, head * HD : (head + 1) * HD], cos_v, sin_v).astype(BF16)
    for k, ref in enumerate((o0, o1, o2, o3)):
        ref[0] = heads_s[spot ^ k]


def sequence_start(sc, places):
    first = jnp.zeros_like(places)
    for i in range(13, sc.shape[0]):
        first = jnp.where(places >= sc[i], sc[i], first)
    return first


def key_ranges(sc, block, rows, per_key):
    last = block * rows + rows - 1
    begin = jnp.int32(0)
    for i in range(13, sc.shape[0]):
        begin = jnp.where(last >= sc[i], sc[i], begin)
    clear = jnp.minimum((begin + rows - 1) // rows, block)
    lax.fori_loop(sc[4 + block], clear, functools.partial(per_key, masked=True), 0)
    lax.fori_loop(clear, block, functools.partial(per_key, masked=False), 0)
    per_key(block, 0, masked=True)


def attend_body(
    sc, r0, r1, r2, r3, c0, c1, c2, c3,
    o0, o1, o2, o3, ctx, lse, q_all, k_all, v_all, m_s, l_s, acc_s,
):
    spot, core = sc[0], sc[2]
    rows = r0.shape[1]

    def block_of(source, side):
        return (2 * (source // 2) + side) * 2 + source % 2

    for k, (own, other) in enumerate(((r0, c0), (r1, c1), (r2, c2), (r3, c3))):
        mine = block_of(spot ^ k, core)
        theirs = block_of(spot ^ k, 1 - core)
        q_all[k] = own[0]
        k_all[mine] = own[1]
        v_all[mine] = own[2]
        k_all[theirs] = other[1]
        v_all[theirs] = other[2]

    def per_query(k, unused):
        block = block_of(spot ^ k, core)
        query = q_all[k]
        first = sequence_start(
            sc, block * rows + lax.broadcasted_iota(jnp.int32, (rows, 1), 0)
        )
        where_q = block * rows + lax.broadcasted_iota(jnp.int32, (rows, rows), 0)
        lane = lax.broadcasted_iota(jnp.int32, (rows, rows), 1)
        m_s[...] = jnp.full(m_s.shape, NEG_FILL, F32)
        l_s[...] = jnp.zeros(l_s.shape, F32)
        acc_s[...] = jnp.zeros(acc_s.shape, F32)

        def per_key(kb, unused_two):
            where_k = kb * rows + lane
            scores = nt(query, k_all[kb]) * SCORE_SCALE
            scores = jnp.where((where_k <= where_q) & (where_k >= first), scores, NEG_FILL)
            old = m_s[...]
            new = jnp.maximum(old, jnp.max(scores, axis=1, keepdims=True))
            weight = jnp.exp(scores - new)
            fade = jnp.exp(old - new)
            l_s[...] = l_s[...] * fade + jnp.sum(weight, axis=1, keepdims=True)
            acc_s[...] = acc_s[...] * fade + nn(weight.astype(BF16), v_all[kb])
            m_s[...] = new
            return 0

        lax.fori_loop(sc[4 + block], block + 1, per_key, 0)
        ctx[k] = acc_s[...] / l_s[...]
        lse[k] = m_s[...] + jnp.log(l_s[...])
        return 0

    lax.fori_loop(0, 4, per_query, 0)
    for k, ref in enumerate((o0, o1, o2, o3)):
        ref[...] = ctx[k].astype(BF16)


def output_body(sc, r0, r1, r2, r3, width, weights, cb, o0, o1, o2, o3, acc_s):
    spot, piece, group = sc[0], sc[1], sc[3]
    keep = width[...] > group
    for k, ref in enumerate((r0, r1, r2, r3)):
        at = pl.ds(pl.multiple_of((spot ^ k) * HD, HD), HD)
        cb[:, at] = jnp.where(keep, ref[...], jnp.zeros_like(ref[...]))
    for col in range(D // TC):
        acc_s[:, col * TC : (col + 1) * TC] = nn(cb[:, :TR], weights[0, col]) + nn(
            cb[:, TR:], weights[1, col]
        )
    store_pieces(acc_s, piece, o1.shape[0], (o0, o1, o2, o3))


def norm_two_body(sc, own, r1, r2, r3, tokp, rap, gain, bias, attn, h1, a2p):
    total = own[...] + r1[...].astype(F32) + r2[...].astype(F32) + r3[...].astype(F32)
    attn[...] = total
    middle = tokp[...].astype(F32) + rap[...] * total
    h1[...] = middle
    xhat, _ = row_stats(middle)
    a2p[...] = (xhat * gain[...] + bias[...]).astype(BF16)


def ffn_body(
    sc, p0, p1, p2, p3, dy, width, router, w_up, w_down,
    a2, act, relu, gffn, dlog, rfp, o0, o1, o2, o3, acc_s, coef_s, rf_s,
):
    step = pl.program_id(0)
    piece, group = sc[1], sc[3]
    rows = p0.shape[0]

    @pl.when(step == 0)
    def _():
        for k, ref in enumerate((p0, p1, p2, p3)):
            put_rows(a2, piece ^ k, rows, ref[...])
        scale, coef = route_level(nn(a2[...], router[...]), width[...])
        rf_s[...] = scale
        coef_s[...] = coef
        gffn[...] = (scale * dy[...].astype(F32)).astype(BF16)
        rfp[...] = rows_of(rf_s, piece, rows)

    up = jnp.maximum(nn(a2[...], w_up[...].reshape(D, TC)), 0.0)
    up = jnp.where(width[...] > group, up, 0.0)
    relu[...] = up.astype(BF16)
    low = (up * up).astype(BF16)
    act[...] = low
    for col in range(D // TC):
        at = slice(col * TC, (col + 1) * TC)
        part = nn(low[:, :TR], w_down[0, col]) + nn(low[:, TR:], w_down[1, col])

        @pl.when(step == 0)
        def _(part=part, at=at):
            acc_s[:, at] = part

        @pl.when(step > 0)
        def _(part=part, at=at):
            acc_s[:, at] += part

    @pl.when(step == pl.num_programs(0) - 1)
    def _():
        drf = jnp.sum(acc_s[...] * dy[...].astype(F32), axis=1, keepdims=True)
        dlog[...] = drf * coef_s[...]
        store_pieces(acc_s, piece, rows, (o0, o1, o2, o3))


def ffn_back_body(sc, gffn, relu, dlog, router_t, w_up, w_down, gpre, o0, o1, o2, o3, acc_s):
    step = pl.program_id(0)
    piece = sc[1]
    halves = []
    for row in range(2):
        total = nt(gffn[:, :TC], w_down[row, 0])
        for col in range(1, D // TC):
            total += nt(gffn[:, col * TC : (col + 1) * TC], w_down[row, col])
        halves.append(total)
    gact = jnp.concatenate(halves, axis=1)
    low = (gact * 2.0 * relu[...].astype(F32)).astype(BF16)
    gpre[...] = low
    part = nt(low, w_up[...].reshape(D, TC))

    @pl.when(step == 0)
    def _():
        acc_s[...] = part + split_dot(dlog[...], router_t[...])

    @pl.when(step > 0)
    def _():
        acc_s[...] += part

    @pl.when(step == pl.num_programs(0) - 1)
    def _():
        store_pieces(acc_s, piece, o1.shape[0], (o0, o1, o2, o3))


def norm_grad(grad, values, gain):
    xhat, rstd = row_stats(values)
    scaled = grad * gain
    inner = scaled - jnp.mean(scaled, axis=1, keepdims=True)
    inner = inner - xhat * jnp.mean(scaled * xhat, axis=1, keepdims=True)
    gain_grad = jnp.sum(grad * xhat, axis=0, keepdims=True)
    return inner * rstd, gain_grad, jnp.sum(grad, axis=0, keepdims=True)


def norm_two_back_body(
    sc, own, r1, r2, r3, h1, attn, dy, rap, coefp, gain, dh1, gattnp, dlogp, ggain, gbias
):
    grad = own[...] + r1[...].astype(F32) + r2[...].astype(F32) + r3[...].astype(F32)
    back, gain_grad, bias_grad = norm_grad(grad, h1[...], gain[...])
    middle = rows_of(dy, sc[1], dh1.shape[0]).astype(F32) + back
    dh1[...] = middle
    gattnp[...] = (rap[...] * middle).astype(BF16)
    dra = jnp.sum(middle * attn[...], axis=1, keepdims=True)
    dlogp[...] = dra * coefp[...]
    ggain[...] = gain_grad
    gbias[...] = bias_grad


def gout_body(sc, p0, p1, p2, p3, width, weights, gattn, o0, o1, o2, o3, heads_s):
    spot, piece, group = sc[0], sc[1], sc[3]
    rows = p0.shape[0]
    for k, ref in enumerate((p0, p1, p2, p3)):
        put_rows(gattn, piece ^ k, rows, ref[...])
    keep = width[...] > group
    for row in range(2):
        total = nt(gattn[:, :TC], weights[row, 0])
        for col in range(1, D // TC):
            total += nt(gattn[:, col * TC : (col + 1) * TC], weights[row, col])
        low = jnp.where(keep, total, 0.0).astype(BF16)
        heads_s[2 * row] = low[:, :HD]
        heads_s[2 * row + 1] = low[:, HD:]
    for k, ref in enumerate((o0, o1, o2, o3)):
        ref[...] = heads_s[spot ^ k]


def attend_back_body(
    sc, cosine, sine, q_all, k_all, v_all, ctx, lse, g0, g1, g2, g3,
    gq, own, other, g_s, gk_s, gv_s, acc_s,
):
    spot, core = sc[0], sc[2]
    rows = g0.shape[0]

    def block_of(source, side):
        return (2 * (source // 2) + side) * 2 + source % 2

    for k, ref in enumerate((g0, g1, g2, g3)):
        g_s[k] = ref[...]
    gk_s[...] = jnp.zeros(gk_s.shape, F32)
    gv_s[...] = jnp.zeros(gv_s.shape, F32)

    def per_query(k, unused):
        block = block_of(spot ^ k, core)
        query = q_all[k]
        grad = g_s[k]
        shared = grad.astype(F32) * ctx[k]
        delta = lax.dot_general(
            jnp.ones((8, HD), F32), shared, (((1,), (1,)), ((), ())),
            precision=PRECISE, preferred_element_type=F32,
        )[:1]
        first = sequence_start(
            sc, block * rows + lax.broadcasted_iota(jnp.int32, (1, rows), 1)
        )
        level = lse[k]
        where_q = block * rows + lax.broadcasted_iota(jnp.int32, (rows, rows), 1)
        line = lax.broadcasted_iota(jnp.int32, (rows, rows), 0)
        acc_s[...] = jnp.zeros(acc_s.shape, F32)

        def per_key(kb, unused_two, masked):
            keys = k_all[kb]
            scores = nt(keys, query) * SCORE_SCALE - level
            if masked:
                where_k = kb * rows + line
                allowed = (where_k <= where_q) & (where_k >= first)
                prob = jnp.where(allowed, jnp.exp(jnp.where(allowed, scores, 0.0)), 0.0)
            else:
                prob = jnp.exp(scores)
            gprob = nt(v_all[kb], grad)
            graw = (prob * (gprob - delta) * SCORE_SCALE).astype(BF16)
            gv_s[kb] += nn(prob.astype(BF16), grad)
            gk_s[kb] += nn(graw, query)
            acc_s[...] += tn(graw, keys)
            return 0

        key_ranges(sc, block, rows, per_key)
        gq[k] = turn_back(acc_s[...], cosine[block], sine[block]).astype(BF16)
        return 0

    lax.fori_loop(0, 4, per_query, 0)
    for k in range(4):
        mine = block_of(spot ^ k, core)
        theirs = block_of(spot ^ k, 1 - core)
        own[k, 0] = gk_s[mine]
        own[k, 1] = gv_s[mine]
        other[k, 0] = gk_s[theirs].astype(BF16)
        other[k, 1] = gv_s[theirs].astype(BF16)


def key_merge_body(sc, gq, own, got, cosine, sine, o0, o1, o2, o3):
    spot, core = sc[0], sc[2]
    for k, ref in enumerate((o0, o1, o2, o3)):
        source = spot ^ k
        block = (2 * (source // 2) + core) * 2 + source % 2
        ref[0] = gq[k]
        gk = own[k, 0] + got[k, 0].astype(F32)
        ref[1] = turn_back(gk, cosine[block], sine[block]).astype(BF16)
        ref[2] = (own[k, 1] + got[k, 1].astype(F32)).astype(BF16)


def gather_input_body(sc, r0, r1, r2, r3, gin):
    spot = sc[0]
    for k, ref in enumerate((r0, r1, r2, r3)):
        for member in range(3):
            at = pl.ds(pl.multiple_of(member * HG + (spot ^ k) * HD, HD), HD)
            gin[:, at] = ref[member]


def input_back_body(sc, gin, weights, f1, f2, f3, o0, o1, o2, o3, acc_s):
    piece = sc[1]
    rows = o0.shape[0]
    wide = weights.shape[1] * TR
    total = nt(gin[:, :HG], weights[0].reshape(wide, TC))
    for member in range(1, 3):
        total += nt(gin[:, member * HG : (member + 1) * HG], weights[member].reshape(wide, TC))
    acc_s[...] = total
    o0[...] = rows_of(acc_s, piece, rows)
    for k, (ref, passed) in enumerate(((o1, f1), (o2, f2), (o3, f3))):
        ref[0] = rows_of(acc_s, piece ^ (k + 1), rows).astype(BF16)
        ref[1] = passed[...]


def norm_one_back_body(
    sc, own, r1, r2, r3, ffn, tokp, h1, rfp, dh1, dlogp, router_t, gain, both, ggain, gbias
):
    grad = own[...] + r1[0].astype(F32) + r2[0].astype(F32) + r3[0].astype(F32)
    grad = grad + split_dot(dlogp[...], router_t[...])
    back, gain_grad, bias_grad = norm_grad(grad, tokp[...].astype(F32), gain[...])
    both[0] = (dh1[...] + back).astype(BF16)
    total = ffn[...] + r1[1].astype(F32) + r2[1].astype(F32) + r3[1].astype(F32)
    both[1] = (h1[...] + rfp[...] * total).astype(BF16)
    ggain[...] = gain_grad
    gbias[...] = bias_grad


def join_body(sc, b0, b1, b2, b3, whole):
    piece = sc[1]
    rows = b0.shape[1]
    for k, ref in enumerate((b0, b1, b2, b3)):
        at = pl.ds(pl.multiple_of((piece ^ k) * rows, rows), rows)
        whole[:, at, :] = ref[...]


def place_tiles(ids, chunks, held, waits=()):
    count = sum(c.shape[0] for c in chunks)

    def body(ids_ref, *refs):
        parts = refs[: len(chunks)]
        out = refs[len(chunks) + len(waits) + (0 if held is None else 1)]
        mark, buf, in_sems, out_sems = refs[-4:]
        mark[...] = jnp.zeros_like(mark)
        places = [(part, i) for part in parts for i in range(part.shape[0])]
        arrive = [
            pltpu.make_async_copy(part.at[i], buf.at[at], in_sems.at[at])
            for at, (part, i) in enumerate(places)
        ]
        leave = [
            pltpu.make_async_copy(buf.at[at], out.at[ids_ref[at]], out_sems.at[at])
            for at in range(count)
        ]
        for copy in arrive:
            copy.start()
        for came, go in zip(arrive, leave):
            came.wait()
            go.start()
        for copy in leave:
            copy.wait()

    extra = [] if held is None else [held]
    return pl.pallas_call(
        body,
        out_shape=[sds((TILES, TR, TC), BF16), MARK],
        in_specs=[SM] + [HBM] * (len(chunks) + len(extra) + len(waits)),
        out_specs=[HBM, VM],
        scratch_shapes=[
            pltpu.VMEM((count, TR, TC), BF16),
            pltpu.SemaphoreType.DMA((count,)),
            pltpu.SemaphoreType.DMA((count,)),
        ],
        compiler_params=params(),
        input_output_aliases={} if held is None else {1 + len(chunks): 0},
        cost_estimate=cost(0, 2 * count * TR * TC * 2),
        name="place_tiles",
    )(ids, *chunks, *extra, *waits)


def tile_kind(tile):
    kind = (tile >= 24).astype(jnp.int32) + (tile >= 32).astype(jnp.int32)
    kind = kind + (tile >= 64).astype(jnp.int32)
    base = jnp.where(kind == 1, 24, jnp.where(kind == 2, 32, 64))
    local = tile - base
    left = jnp.where(kind == 0, tile % 8, local // 4)
    right = jnp.where(kind == 0, tile // 8, local % 4)
    return kind, left, right


def tile_grads(ids, lefts, rights, added, outs_of, waits=()):
    count = ids.shape[0]
    parts = len(lefts)
    rows = lefts[0][0].shape[0]
    flat = [a for part in lefts for a in part] + [a for part in rights for a in part]

    def fetch(ids_ref, step, slot, refs, lbuf, rbuf, sems):
        kind, left, right = tile_kind(ids_ref[step])
        for which in range(4):

            @pl.when(kind == which)
            def _(which=which):
                for part in range(parts):
                    src = refs[part * 4 + which]
                    at = pl.ds(pl.multiple_of(left * TR, TR), TR)
                    pltpu.make_async_copy(
                        src.at[:, at], lbuf.at[slot, pl.ds(part * rows, rows)], sems.at[slot, part]
                    ).start()
                    src = refs[(parts + part) * 4 + which]
                    at = pl.ds(pl.multiple_of(right * TC, TC), TC)
                    pltpu.make_async_copy(
                        src.at[:, at],
                        rbuf.at[slot, pl.ds(part * rows, rows)],
                        sems.at[slot, parts + part],
                    ).start()

    def body(ids_ref, *refs):
        sources = refs[: len(flat)]
        at = len(flat)
        plus = None
        if added is not None:
            plus = refs[at]
            at += 1
        at += len(waits)
        outs = refs[at : at + len(outs_of)]
        mark, lbuf, rbuf, sems = refs[at + len(outs_of) :]
        mark[...] = jnp.zeros_like(mark)
        step = pl.program_id(0)
        slot = lax.rem(step, 2)

        @pl.when(step == 0)
        def _():
            fetch(ids_ref, 0, 0, sources, lbuf, rbuf, sems)

        @pl.when(step + 1 < count)
        def _():
            fetch(ids_ref, step + 1, 1 - slot, sources, lbuf, rbuf, sems)

        for part in range(parts):
            pltpu.make_async_copy(
                sources[0].at[:, :TR], lbuf.at[slot, pl.ds(part * rows, rows)], sems.at[slot, part]
            ).wait()
            pltpu.make_async_copy(
                sources[parts * 4 + 1].at[:, :TC],
                rbuf.at[slot, pl.ds(part * rows, rows)],
                sems.at[slot, parts + part],
            ).wait()
        total = tn(lbuf[slot], rbuf[slot])
        if plus is not None:
            total = total + plus[0].astype(F32)
        low = total.astype(BF16)
        if len(outs_of) == 1:
            outs[0][0] = low
        else:
            begin = 0
            for ref, size in zip(outs, outs_of):

                @pl.when((step >= begin) & (step < begin + size))
                def _(ref=ref):
                    ref[0] = low

                begin += size

    specs_out = []
    begin = 0
    for size in outs_of:
        specs_out.append(
            pl.BlockSpec(
                (1, TR, TC),
                lambda i, ids_ref, begin=begin, size=size: (jnp.clip(i - begin, 0, size - 1), 0, 0),
            )
        )
        begin += size
    plus_in = [] if added is None else [added]
    return pl.pallas_call(
        body,
        out_shape=[sds((size, TR, TC), BF16) for size in outs_of] + [MARK],
        grid_spec=pltpu.PrefetchScalarGridSpec(
            num_scalar_prefetch=1,
            grid=(count,),
            in_specs=[HBM] * len(flat)
            + [pl.BlockSpec((1, TR, TC), lambda i, ids_ref: (i, 0, 0))] * len(plus_in)
            + [HBM] * len(waits),
            out_specs=specs_out + [pl.BlockSpec((8, HD), lambda i, ids_ref: (0, 0))],
            scratch_shapes=[
                pltpu.VMEM((2, parts * rows, TR), BF16),
                pltpu.VMEM((2, parts * rows, TC), BF16),
                pltpu.SemaphoreType.DMA((2, 2 * parts)),
            ],
        ),
        compiler_params=pltpu.CompilerParams(vmem_limit_bytes=VMEM_ALL),
        cost_estimate=cost(
            2 * count * parts * rows * TR * TC, count * (parts * rows * (TR + TC) * 2 + TR * TC * 2)
        ),
        name="tile_grads",
    )(ids, *flat, *plus_in, *waits)


def adam_tile(grad, left, right, first, second, master):
    left_low = left.astype(BF16)
    right_low = right.astype(BF16)
    turned = nn(tn(left_low, grad.astype(BF16)).astype(BF16), right_low)
    new_first = BETA_ONE * first + (1.0 - BETA_ONE) * turned
    new_second = BETA_TWO * second + (1.0 - BETA_TWO) * turned * turned
    step = (
        new_first
        / (1.0 - BETA_ONE**STEP)
        / (jnp.sqrt(new_second / (1.0 - BETA_TWO**STEP)) + ADAM_EPS)
    )
    back = nt(nn(left_low, step.astype(BF16)).astype(BF16), right_low)
    return new_first, new_second, master - RATE_TILE * (back + DECAY_RATE * master)


def adam_tiles(slot_list, flows, bases, state, held, waits=()):
    steps = slot_list.shape[0]

    def body(sc_ref, *refs):
        grads = refs[: len(flows)]
        left, right, first, second, master = refs[len(flows) : len(flows) + 5]
        o_first, o_second, o_master, o_low, mark = refs[-5:]
        mark[...] = jnp.zeros_like(mark)
        total = grads[0][0].astype(F32)
        for ref in grads[1:]:
            total = total + ref[0].astype(F32)
        new_first, new_second, new_master = adam_tile(
            total, left[0], right[0], first[0], second[0], master[0]
        )
        o_first[0] = new_first
        o_second[0] = new_second
        o_master[0] = new_master
        o_low[0] = new_master.astype(BF16)

    def at_slot(shape):
        return pl.BlockSpec((1,) + shape, lambda i, sc_ref: (sc_ref[i], 0, 0))

    slots = state[0].shape[0]
    shapes = [(TR, TC)] * 4
    types = [F32, F32, F32, BF16]
    extra = [] if held is None else list(held)
    base = 1 + len(flows) + 5
    return pl.pallas_call(
        body,
        out_shape=[sds((slots,) + s, t) for s, t in zip(shapes, types)] + [MARK],
        grid_spec=pltpu.PrefetchScalarGridSpec(
            num_scalar_prefetch=1,
            grid=(steps,),
            in_specs=[pl.BlockSpec((1, TR, TC), lambda i, sc_ref: (i, 0, 0))] * len(flows)
            + [at_slot((TR, TR)), at_slot((TC, TC))]
            + [at_slot((TR, TC))] * 3
            + [HBM] * (len(extra) + len(waits)),
            out_specs=[at_slot(s) for s in shapes]
            + [pl.BlockSpec((8, HD), lambda i, sc_ref: (0, 0))],
        ),
        input_output_aliases={base + i: i for i in range(len(extra))},
        compiler_params=pltpu.CompilerParams(vmem_limit_bytes=VMEM_ALL),
        cost_estimate=cost(steps * 8 * TR * TC * TC, steps * 5 * TR * TC * 4),
        name="adam_tiles",
    )(slot_list, *flows, *bases, *state, *extra, *waits)


def small_adam(grad, first, second, master):
    new_first = BETA_ONE * first + (1.0 - BETA_ONE) * grad
    new_second = BETA_TWO * second + (1.0 - BETA_TWO) * grad * grad
    step = (
        new_first
        / (1.0 - BETA_ONE**STEP)
        / (jnp.sqrt(new_second / (1.0 - BETA_TWO**STEP)) + ADAM_EPS)
    )
    return new_first, new_second, master - RATE_SMALL * (step + DECAY_RATE * master)


def signed_tables(places):
    middle = HD // 2
    frequency = ROPE_BASE ** (-(jnp.arange(middle, dtype=F32) * 2.0) / HD)
    angles = places.astype(F32)[:, None] * frequency[None, :]
    cosine = jnp.cos(angles)
    sine = jnp.sin(angles)
    return (
        jnp.concatenate([cosine, cosine], axis=1),
        jnp.concatenate([-sine, sine], axis=1),
    )


def token_layout(first_index, local_rows, seq_lengths):
    places = first_index + jnp.arange(local_rows, dtype=jnp.int32)
    number = seq_lengths.shape[0]
    below = jnp.arange(number)[None, :] <= jnp.arange(number)[:, None]
    bounds = jnp.sum(jnp.where(below, seq_lengths[None, :], 0), axis=1)
    passed = places[:, None] >= bounds[None, :]
    segment = jnp.sum(passed.astype(jnp.int32), axis=1)
    offset = places - jnp.sum(jnp.where(passed, seq_lengths[None, :], 0), axis=1)
    return (places, segment, offset)


def moves(target):
    pairs = []
    for z in range(4):
        for y in range(2):
            for x in range(2):
                for c in range(2):
                    to = target(z, y, x, c)
                    if to is not None:
                        a, b, e, f = to
                        pairs.append((8 * z + 4 * y + 2 * x + c, 8 * a + 4 * b + 2 * e + f))
    return pairs


def only(condition, target):
    return lambda z, y, x, c: target(z, y, x, c) if condition(z, y, x, c) else None


def flip(dz=0, dy=0, dx=0, dc=0):
    return lambda z, y, x, c: (z ^ dz, y ^ dy, x ^ dx, c ^ dc)


def own_group(z, y, x, c):
    return c == z % 2


def foreign(z, y, x, c):
    return c != z % 2


def send(value, target):
    return lax.ppermute(value, AXES, moves(target))


MEMBERS = (None, flip(dz=1), flip(dx=1), flip(dz=1, dx=1))
HEADMATES = (None, flip(dy=1), flip(dz=2), flip(dz=2, dy=1))


def scatter_pieces(pieces):
    return [pieces[0]] + [send(pieces[k], MEMBERS[k]) for k in range(1, 4)]


def share_piece(piece):
    return [piece] + [send(piece, MEMBERS[k]) for k in range(1, 4)]


def swap_heads(blocks):
    return [blocks[0]] + [send(blocks[k], HEADMATES[k]) for k in range(1, 4)]


def after(value, *others):
    return lax.optimization_barrier((value,) + others)[0]


def tied(values, done):
    return list(lax.optimization_barrier(tuple(values) + tuple(done))[: len(values)])


def small_step(values, bit, target):
    other = send(values, target)
    return jnp.where(
        bit == 0, jnp.concatenate([values, other]), jnp.concatenate([other, values])
    )


def local_remap(
    tokens, cotangent, attn_width, ffn_width, seq_lengths, tile_order, master, first_moment,
    second_moment, left_basis, right_basis, small_master, small_first, small_second,
):
    rows = tokens.shape[0]
    piece_rows = rows // 4
    s = lax.axis_index("seq")
    h = lax.axis_index("head")
    z, y, x, c = s // 2, s % 2, h // 2, h % 2
    zp, zh = z % 2, z // 2
    mine = c == zp
    group = 2 * x + zp
    spot = 2 * zh + y
    block = (2 * zh + c) * 2 + y

    y_move, h_move, c_move = flip(dy=1), flip(dz=2), flip(dc=1)

    slots = master.shape[1]
    part = slots // 4
    to_pair = only(own_group, flip(dz=1))
    near_move = lambda z, y, x, c: (z, y, x, 1 - c) if c == z % 2 else (z ^ 1, y, x, c)
    far_move = lambda z, y, x, c: (z ^ 2, y, x, 1 - c) if c == z % 2 else (z ^ 3, y, x, c)
    low = [master[0, i * part : (i + 1) * part].astype(BF16) for i in range(4)]
    near, far = [send(low[0], near_move)], [send(low[0], far_move)]
    order = tile_order[0]
    order_got = send(order, c_move)
    small_all = small_step(small_master.astype(BF16), y, y_move)
    near[0], order_got, small_all, low1, low2, low3, wid = tied(
        [near[0], order_got, small_all] + low[1:] + [jnp.stack([attn_width, ffn_width])], []
    )
    order = jnp.where(mine, order, order_got)
    base = jnp.where(mine, s ^ 2, s)
    base_there = jnp.where(mine, s, s ^ 2)

    def ids_of(*chunks):
        return jnp.concatenate(
            [
                lax.dynamic_slice_in_dim(order, (o ^ hop) * slots + i * part, part, 0)
                for o in (base, base_there)
                for hop, i in chunks
            ]
        )

    def by_kind(row):
        place = jnp.arange(slots, dtype=jnp.int32)
        key = jnp.where(row < FFN_TILE, slots, 0) + place
        rank = jnp.sum((key[:, None, :] < key[:, :, None]).astype(jnp.int32), axis=2)
        spot_of = rank[:, :, None] == place
        return jnp.sum(jnp.where(spot_of, row[:, :, None], 0), axis=1), jnp.sum(
            jnp.where(spot_of, place[:, None], 0), axis=1
        )

    sorted_order = by_kind(order.reshape(-1, slots))[0].reshape(-1)
    own_row = lax.dynamic_slice_in_dim(tile_order[0], s * slots, slots, 0)
    own_slots = by_kind(own_row[None])[1][0]
    enough = jnp.min(
        jnp.sum(
            (jnp.stack([tile_order[0], order_got]).reshape(-1, slots) >= FFN_TILE).astype(jnp.int32),
            axis=1,
        )
    )
    enough = jnp.full((HD,), enough, jnp.int32)
    wid_got = send(wid, to_pair)
    near_y, far_y = [send(near[0], y_move)], []
    near.append(send(low1, near_move))
    small_all = small_step(small_all, zp, flip(dz=1))
    low23 = jnp.concatenate([low2, low3])
    near[0], near[1], far[0], near_y[0], small_all, low1, low2, low3, low23, wid, wid_got = tied(
        [near[0], near[1], far[0], near_y[0], small_all, low1, low2, low3, low23, wid, wid_got], []
    )
    far.append(send(low1, far_move))
    near_y.append(send(near[1], y_move))
    far_y.append(send(far[0], y_move))
    near23 = send(low23, near_move)
    small_all = small_step(small_all, zh, h_move)
    first = jnp.concatenate([near[0], near_y[0], far[0]])
    all_rows = rows * lax.axis_size("seq")
    blocks = all_rows // rows
    places, _, offset = token_layout(0, all_rows, seq_lengths)
    start = places - offset
    first_block = start.reshape(blocks, rows)[:, 0] // rows
    cosine, sine = signed_tables(offset)
    cosine, sine = cosine.reshape(blocks, rows, HD), sine.reshape(blocks, rows, HD)
    number = seq_lengths.shape[0]
    below = jnp.arange(number)[None, :] <= jnp.arange(number)[:, None]
    ends = jnp.sum(jnp.where(below, seq_lengths[None, :], 0), axis=1)
    scalars = jnp.concatenate(
        [
            jnp.stack([spot, group, c, group]).astype(jnp.int32),
            first_block.astype(jnp.int32),
            block[None].astype(jnp.int32),
            ends.astype(jnp.int32),
        ]
    )
    near[1], near23, far[1], near_y[1], far_y[0], low2, low3, small_all, first, cosine, sine, tok = tied(
        [near[1], near23, far[1], near_y[1], far_y[0], low2, low3, small_all, first]
        + [cosine, sine, tokens],
        [],
    )
    near += [near23[:part], near23[part:]]
    far.append(send(low2, far_move))
    near_y.append(send(near[2], y_move))
    far_y.append(send(far[1], y_move))
    first_there = send(first, c_move)
    tok_got = send(tok, to_pair)
    second = jnp.concatenate([near[1], near_y[1], far_y[0], far[1]])
    near[2], near[3], far[2], near_y[2], far_y[1], low3, small_all, first, first_there, second, tok, tok_got = tied(
        [near[2], near[3], far[2], near_y[2], far_y[1], low3, small_all, first, first_there]
        + [second, tok, tok_got],
        [],
    )
    far.append(send(low3, far_move))
    near_y.append(send(near[3], y_move))
    far_y.append(send(far[2], y_move))
    second_there = send(second, c_move)
    *third, small_all, second_there = tied(
        [near[2], near_y[2], far_y[1], far[2], small_all, second_there], []
    )
    third = jnp.concatenate(third)
    third_there = send(third, c_move)
    tiles, mark_one = place_tiles(ids_of((0, 0), (1, 0), (4, 0)), [first, first_there], None)
    tok = jnp.where(mine, tok, tok_got)
    widths = jnp.where(mine, wid, wid_got)
    width_a, width_f = widths[0][:, None], widths[1][:, None]
    gains = small_all[: 4 * D].astype(F32).reshape(4, 1, D)
    gain_one, bias_one, gain_two, bias_two = gains[0], gains[1], gains[2], gains[3]
    routers = small_all[4 * D :].reshape(D, 2 * WIDTHS)
    pad = ((0, 0), (0, HD - WIDTHS))
    router_a = jnp.pad(routers[:, :WIDTHS], pad)
    router_f = jnp.pad(routers[:, WIDTHS:], pad)
    router_ft, router_at = router_f.T, router_a.T
    a1, a1p, tokp, rap, coefp = flat_call(
        norm_one_body,
        scalars,
        [tok, gain_one, bias_one, router_a, width_a],
        [
            sds((rows, D), BF16),
            sds((piece_rows, D), BF16),
            sds((piece_rows, D), BF16),
            sds((piece_rows, 1), F32),
            sds((piece_rows, HD), F32),
        ],
        [pltpu.VMEM((rows, 1), F32), pltpu.VMEM((rows, HD), F32)],
        name="norm_one",
    )

    tiles, mark_two = place_tiles(
        ids_of((0, 1), (1, 1), (5, 0), (4, 1)), [second, second_there], tiles, [mark_one]
    )
    near[3], far[3], near_y[3], far_y[2], third, third_there, mark_two, a1, router_ft, router_at = tied(
        [near[3], far[3], near_y[3], far_y[2], third, third_there, mark_two, a1]
        + [router_ft, router_at],
        [],
    )
    far_y.append(send(far[3], y_move))
    fourth = [near[3], near_y[3], far_y[2], far[3]]
    fourth_there = [send(v, c_move) for v in fourth]
    tiles, mark_three = place_tiles(
        ids_of((0, 2), (1, 2), (5, 1), (4, 2)), [third, third_there], tiles, [mark_two]
    )
    tiles, mark_four = place_tiles(
        ids_of((0, 3), (1, 3), (5, 2), (4, 3)), fourth + fourth_there, tiles, [mark_three]
    )
    far_y[3], mark_four = tied([far_y[3], mark_four], [])
    fifth_there = send(far_y[3], c_move)
    tiles, _ = place_tiles(ids_of((5, 3)), [far_y[3], fifth_there], tiles, [mark_four])
    by_row = tiles.reshape(TILES // 4, 4, TR, TC)
    by_map = tiles.reshape(TILES // 8, 8, TR, TC)

    table = pl.BlockSpec((1, rows, HD), lambda i, sc: (sc[12], 0, 0))
    sent = pl.pallas_call(
        project_body,
        out_shape=[sds((3, rows, HD), BF16)] * 4,
        grid_spec=pltpu.PrefetchScalarGridSpec(
            num_scalar_prefetch=1,
            grid=(3,),
            in_specs=[
                pl.BlockSpec((rows, D), lambda i, sc: (0, 0)),
                pl.BlockSpec((1, 8, TR, TC), lambda i, sc: (i, 0, 0, 0)),
                table,
                table,
            ],
            out_specs=[pl.BlockSpec((1, rows, HD), lambda i, sc: (i, 0, 0))] * 4,
            scratch_shapes=[pltpu.VMEM((HPG, rows, HD), BF16)],
        ),
        compiler_params=params(),
        cost_estimate=cost(2 * rows * D * 3 * HG, 3 * D * HG * 2 + rows * D * 2),
        name="project",
    )(scalars, a1, by_map, cosine, sine)
    got = swap_heads(sent)
    beside = [send(v, flip(dc=1)) for v in got]
    dy, enough = tied([cotangent, enough], got)
    enough = jnp.minimum(enough, send(enough, flip(dx=1)))
    dy = jnp.where(mine, dy, send(dy, to_pair))

    pairs_cost = 4 * 4 * rows * rows * HD * 2
    out = flat_call(
        attend_body,
        scalars,
        got + beside,
        [sds((rows, HD), BF16)] * 4
        + [
            sds((4, rows, HD), F32),
            sds((4, rows, 1), F32),
            sds((4, rows, HD), BF16),
            sds((blocks, rows, HD), BF16),
            sds((blocks, rows, HD), BF16),
        ],
        [pltpu.VMEM((rows, 1), F32), pltpu.VMEM((rows, 1), F32), pltpu.VMEM((rows, HD), F32)],
        flops=2 * pairs_cost,
        name="attend",
    )
    ctx_sent, (ctx, lse, q_all, k_all, v_all) = out[:4], out[4:]
    ctx_got = swap_heads(ctx_sent)

    one_piece = sds((piece_rows, D), F32)
    low_piece = sds((piece_rows, D), BF16)
    piece_outs = [one_piece] + [low_piece] * 3
    wo_spec = pl.BlockSpec((2, 4, TR, TC), lambda i, sc: (3, 0, 0, 0))

    def whole(shape):
        return pl.BlockSpec(shape, lambda i, sc: (0,) * len(shape))

    out = pl.pallas_call(
        output_body,
        out_shape=[sds((rows, HG), BF16)] + piece_outs,
        grid_spec=pltpu.PrefetchScalarGridSpec(
            num_scalar_prefetch=1,
            grid=(1,),
            in_specs=[whole((rows, HD))] * 4 + [whole((rows, 1)), wo_spec],
            out_specs=[whole((rows, HG))] + [whole((piece_rows, D))] * 4,
            scratch_shapes=[pltpu.VMEM((rows, D), F32)],
        ),
        compiler_params=params(),
        cost_estimate=cost(2 * rows * D * HG, D * HG * 2 + rows * D * 4),
        name="output",
    )(scalars, *ctx_got, width_a, by_row)
    cb, attn_parts = out[0], out[1:]
    attn_parts = scatter_pieces(attn_parts)

    attn, h1, a2p = flat_call(
        norm_two_body,
        scalars,
        attn_parts + [tokp, rap, gain_two, bias_two],
        [one_piece, one_piece, low_piece],
        name="norm_two",
    )
    a2_parts = share_piece(a2p)

    up_spec = pl.BlockSpec((8, 1, TR, TC), lambda i, sc: (1, i, 0, 0))
    down_spec = pl.BlockSpec((2, 4, TR, TC), lambda i, sc: (8 + i, 0, 0, 0))
    col_spec = pl.BlockSpec((rows, TC), lambda i, sc: (0, i))
    out = pl.pallas_call(
        ffn_body,
        out_shape=[
            sds((rows, D), BF16),
            sds((rows, FG), BF16),
            sds((rows, FG), BF16),
            sds((rows, D), BF16),
            sds((rows, HD), F32),
            sds((piece_rows, 1), F32),
        ]
        + piece_outs,
        grid_spec=pltpu.PrefetchScalarGridSpec(
            num_scalar_prefetch=1,
            grid=(FG // TC,),
            in_specs=[whole((piece_rows, D))] * 4
            + [whole((rows, D)), whole((rows, 1)), whole((D, HD)), up_spec, down_spec],
            out_specs=[
                whole((rows, D)),
                col_spec,
                col_spec,
                whole((rows, D)),
                whole((rows, HD)),
                whole((piece_rows, 1)),
            ]
            + [whole((piece_rows, D))] * 4,
            scratch_shapes=[
                pltpu.VMEM((rows, D), F32),
                pltpu.VMEM((rows, HD), F32),
                pltpu.VMEM((rows, 1), F32),
            ],
        ),
        compiler_params=params(),
        cost_estimate=cost(4 * rows * D * FG, 4 * D * FG + rows * D * 12),
        name="ffn",
    )(scalars, *a2_parts, dy, width_f, router_f, by_row, by_row)
    a2, act, relu, gffn, dlog_f, rfp = out[:6]
    ffn_parts = out[6:]

    out = pl.pallas_call(
        ffn_back_body,
        out_shape=[sds((rows, FG), BF16)] + piece_outs,
        grid_spec=pltpu.PrefetchScalarGridSpec(
            num_scalar_prefetch=1,
            grid=(FG // TC,),
            in_specs=[
                whole((rows, D)),
                col_spec,
                whole((rows, HD)),
                whole((HD, D)),
                up_spec,
                down_spec,
            ],
            out_specs=[col_spec] + [whole((piece_rows, D))] * 4,
            scratch_shapes=[pltpu.VMEM((rows, D), F32)],
        ),
        compiler_params=params(),
        cost_estimate=cost(4 * rows * D * FG, 4 * D * FG + rows * D * 12),
        name="ffn_back",
    )(scalars, gffn, relu, dlog_f, router_ft, by_row, by_row)
    gpre, ga2_parts = out[0], scatter_pieces(out[1:])

    begins = [sum(CHUNKS[:i]) for i in range(len(CHUNKS))]

    def grad_ids(flip_y, i):
        owners = (s ^ flip_y ^ jnp.where(mine, 2, 4), s ^ flip_y ^ jnp.where(mine, 6, 0))
        return jnp.concatenate(
            [
                lax.dynamic_slice_in_dim(sorted_order, o * slots + begins[i], CHUNKS[i], 0)
                for o in owners
            ]
        )

    def route(own, other):
        return lambda z, y, x, c: (z ^ (own if c == z % 2 else other), y, x, z % 2)

    def to_owners(first, second):
        return [send(first, route(1, 2)), send(second, route(3, 0))]

    a2_there, act_there, gffn_there = [send(v, c_move) for v in (a2, act, gffn)]
    gpre_there = send(gpre, c_move)
    early_lefts = [[a2, act, a2, act], [a2_there, act_there, a2_there, act_there]]
    early_rights = [[gffn, gffn, gpre, gffn], [gffn_there, gffn_there, gpre_there, gffn_there]]
    early_away = tile_grads(grad_ids(1, 0), early_lefts, early_rights, None, [2 * CHUNKS[0]])[0]
    early_away, *ga2_parts = tied([early_away] + ga2_parts, [])
    early_back = send(early_away, y_move)

    dh1, gattnp, dlog_a, ggain_two, gbias_two = flat_call(
        norm_two_back_body,
        scalars,
        ga2_parts + [h1, attn, dy, rap, coefp, gain_two],
        [one_piece, low_piece, sds((piece_rows, HD), F32), sds((1, D), F32), sds((1, D), F32)],
        name="norm_two_back",
    )
    gattn_parts = share_piece(gattnp)
    out = pl.pallas_call(
        gout_body,
        out_shape=[sds((rows, D), BF16)] + [sds((rows, HD), BF16)] * 4,
        grid_spec=pltpu.PrefetchScalarGridSpec(
            num_scalar_prefetch=1,
            grid=(1,),
            in_specs=[whole((piece_rows, D))] * 4 + [whole((rows, 1)), wo_spec],
            out_specs=[whole((rows, D))] + [whole((rows, HD))] * 4,
            scratch_shapes=[pltpu.VMEM((HPG, rows, HD), BF16)],
        ),
        compiler_params=params(),
        cost_estimate=cost(2 * rows * D * HG, D * HG * 2 + rows * D * 4),
        name="gout",
    )(scalars, *gattn_parts, width_a, by_row)
    gattn, *gout_sent, early_back = tied(list(out) + [early_back], [])
    gout_got = swap_heads(gout_sent)
    early_here = tile_grads(
        grad_ids(0, 0), early_lefts, early_rights, early_back, [CHUNKS[0]] * 2
    )[:2]
    *early_here, gout_got[0] = tied(list(early_here) + [gout_got[0]], [])
    early_flow = [send(early_here[0], route(1, 2))]

    gq, keys_own, keys_other = flat_call(
        attend_back_body,
        scalars,
        [cosine, sine, q_all, k_all, v_all, ctx]
        + [lse.reshape(4, 1, rows)]
        + gout_got,
        [
            sds((4, rows, HD), BF16),
            sds((4, 2, rows, HD), F32),
            sds((4, 2, rows, HD), BF16),
        ],
        [
            pltpu.VMEM((4, rows, HD), BF16),
            pltpu.VMEM((blocks, rows, HD), F32),
            pltpu.VMEM((blocks, rows, HD), F32),
            pltpu.VMEM((rows, HD), F32),
        ],
        flops=5 * pairs_cost,
        name="attend_back",
    )
    gq, early_flow[0] = tied([gq, early_flow[0]], [])
    grads_sent = flat_call(
        key_merge_body,
        scalars,
        [gq, keys_own, send(keys_other, flip(dc=1)), cosine, sine],
        [sds((3, rows, HD), BF16)] * 4,
        name="key_merge",
    )
    grads_got = swap_heads(grads_sent)
    (gin,) = flat_call(
        gather_input_body, scalars, grads_got, [sds((rows, 3 * HG), BF16)], name="gather_input"
    )
    a1_there, cb_there, gattn_there = [send(v, c_move) for v in (a1, cb, gattn)]
    lefts = [[a1, cb, a2, act], [a1_there, cb_there, a2_there, act_there]]
    rights = [
        [gin, gattn, gpre, gffn],
        [send(gin, c_move), gattn_there, gpre_there, gffn_there],
    ]

    def away_of(i):
        return tile_grads(grad_ids(1, i), lefts, rights, None, [2 * CHUNKS[i]])[0]

    bases = (left_basis[0], right_basis[0])
    state = (first_moment[0], second_moment[0], master[0])
    gin, away1, early_last = tied([gin, away_of(1), early_here[1]], [])
    back1 = send(away1, y_move)
    early_flow.append(send(early_last, route(3, 0)))
    gin, away2, away3 = tied([gin, away_of(2), away_of(3)], [])
    back2 = send(away2, y_move)
    half_cols = D // 2
    half_piece = pl.BlockSpec((piece_rows, half_cols), lambda i, sc: (0, i))
    pair_piece = pl.BlockSpec((2, piece_rows, half_cols), lambda i, sc: (0, 0, i))
    out = pl.pallas_call(
        input_back_body,
        out_shape=[one_piece] + [sds((2, piece_rows, D), BF16)] * 3,
        grid_spec=pltpu.PrefetchScalarGridSpec(
            num_scalar_prefetch=1,
            grid=(2,),
            in_specs=[
                whole((rows, 3 * HG)),
                pl.BlockSpec((3, 4, TR, TC), lambda i, sc: (0, i, 0, 0)),
                half_piece,
                half_piece,
                half_piece,
            ],
            out_specs=[half_piece] + [pair_piece] * 3,
            scratch_shapes=[pltpu.VMEM((rows, half_cols), F32)],
        ),
        compiler_params=params(),
        cost_estimate=cost(2 * rows * D * 3 * HG, 3 * D * HG * 2 + rows * D * 4),
        name="input_back",
    )(scalars, gin, by_map, *ffn_parts[1:])
    pieces = [out[0], send(out[1], MEMBERS[1]), send(out[2], MEMBERS[2])]
    pieces[1], pieces[2], last_piece = tied([pieces[1], pieces[2], out[3]], [])
    pieces.append(send(last_piece, MEMBERS[3]))

    def tile_step(i, back, waits):
        first, second, mark = tile_grads(
            grad_ids(0, i), lefts, rights, back, [CHUNKS[i]] * 2, waits
        )
        return to_owners(first, second), [mark]

    def adam_step(i, flow, held, waits=()):
        chosen = own_slots[begins[i] : begins[i] + CHUNKS[i]]
        return adam_tiles(chosen, flow, bases, state, held, waits)

    back, away3, *early_flow = tied([back1, away3] + early_flow, [])
    back3 = send(away3, y_move)
    flow1, mark = tile_step(1, back, [])
    *pieces, mark = tied(pieces + mark, [])
    mark = [mark]
    both, ggain_one, gbias_one = flat_call(
        norm_one_back_body,
        scalars,
        pieces
        + [ffn_parts[0], tokp, h1, rfp, dh1, dlog_a, router_at, gain_one],
        [sds((2, piece_rows, D), BF16), sds((1, D), F32), sds((1, D), F32)],
        name="norm_one_back",
    )
    grad_router = jnp.concatenate(
        [
            lax.dot_general(
                a1p.astype(F32), dlog_a[:, :WIDTHS], (((0,), (0,)), ((), ())), precision=PRECISE
            ),
            lax.dot_general(
                a2.astype(F32), dlog_f[:, :WIDTHS], (((0,), (0,)), ((), ())), precision=PRECISE
            ),
        ],
        axis=1,
    ).reshape(-1)
    terms = jnp.concatenate(
        [ggain_one[0], gbias_one[0], ggain_two[0], gbias_two[0], grad_router]
    ).reshape(8, -1)
    terms = terms + send(terms, c_move)
    terms = terms + send(terms, flip(dx=1))

    def fold(terms, axis, bit, target):
        low_half = lax.index_in_dim(terms, 0, axis, keepdims=False)
        high_half = lax.index_in_dim(terms, 1, axis, keepdims=False)
        keep = jnp.where(bit == 0, low_half, high_half)
        return keep, send(jnp.where(bit == 0, high_half, low_half), target)


    def again():
        once_more = send(away_of(0), y_move)
        return to_owners(
            *tile_grads(grad_ids(0, 0), lefts, rights, once_more, [CHUNKS[0]] * 2)[:2]
        )

    flow0 = lax.cond(enough[0] >= CHUNKS[0], lambda: early_flow, again)
    back, both, terms, *mark = tied([back2, both, terms] + mark, [])
    flow2, mark = tile_step(2, back, mark)
    both_z = send(both, only(foreign, flip(dz=1)))
    keep, terms = fold(terms.reshape(2, 2, 2, -1), 0, zh, h_move)
    *held, adam_mark = adam_step(0, flow0, None)
    back, both, both_z, *rest = tied([back3, both, both_z, adam_mark] + mark + flow1, [])
    mark, flow1 = rest[:2], rest[2:]
    flow3, mark = tile_step(3, back, mark)
    both_x = send(both, only(own_group, flip(dx=1)))
    both_xz = send(both, only(foreign, flip(dz=1, dx=1)))
    *held, adam_mark = adam_step(1, flow1, held, mark)
    both_x, both_xz, keep, terms, *flow2 = tied(
        [both_x, both_xz, keep, terms] + flow2 + [adam_mark], []
    )
    flow2, marks = flow2[:2], flow2[2:]
    keep, terms = fold(keep + terms, 0, zp, flip(dz=1))
    keep, terms = fold(keep + terms, 0, y, y_move)
    (joined,) = flat_call(
        join_body,
        scalars,
        [both, both_z, both_x, both_xz],
        [sds((2, rows, D), BF16)],
        name="join",
    )
    joined = jnp.where(mine, joined, send(joined, only(own_group, c_move)))
    input_grad, output = joined[0].astype(F32), joined[1]
    held = adam_step(2, flow2, held, marks)[:4]
    input_grad, output, *flow3 = tied([input_grad, output] + flow3, [])
    held = adam_step(3, flow3, held)
    terms = keep + terms
    small_outs = small_adam(terms.reshape(-1), small_first, small_second, small_master)

    return (
        output,
        input_grad,
        held[0][None],
        held[1][None],
        held[2][None],
        held[3][None],
        *small_outs,
    )


CHUNKS = (3, 4, 3, 2)
FFN_TILE = 32


def layer_norm(values, weight_gain, weight_bias):
    center = values - jnp.mean(values, axis=1, keepdims=True)
    spread = jnp.mean(center * center, axis=1, keepdims=True)
    return center * lax.rsqrt(spread + EPS_NORM) * weight_gain + weight_bias


def rotary_tables(places):
    middle = HD // 2
    frequency = ROPE_BASE ** (-(jnp.arange(middle, dtype=jnp.float32) * 2.0) / HD)
    angles = places.astype(jnp.float32)[:, None] * frequency[None, :]
    cosine_half = jnp.cos(angles)
    sine_half = jnp.sin(angles)
    return (
        jnp.concatenate([cosine_half, cosine_half], axis=1),
        jnp.concatenate([sine_half, sine_half], axis=1),
    )


def rotary(values, cosine_table, sine_table):
    middle = HD // 2
    turned = jnp.concatenate([-values[..., middle:], values[..., :middle]], axis=-1)
    return values * cosine_table[:, None, :] + turned * sine_table[:, None, :]


def rotary_back(gradients, cosine_table, sine_table):
    middle = HD // 2
    scaled = gradients * sine_table[:, None, :]
    turned = jnp.concatenate([scaled[..., middle:], -scaled[..., :middle]], axis=-1)
    return gradients * cosine_table[:, None, :] + turned


def from_tiles(tile_stack, rows_total, cols_total):
    return (
        tile_stack.reshape(rows_total // TR, cols_total // TC, TR, TC)
        .transpose(0, 2, 1, 3)
        .reshape(rows_total, cols_total)
    )


def unpack(tile_stack):
    count_in = D // TR * (HG // TC)
    count_out = HG // TR * (D // TC)
    count_up = D // TR * (FG // TC)
    edge_out = 3 * count_in
    edge_up = edge_out + count_out
    edge_down = edge_up + count_up
    w_inputs = jnp.concatenate(
        [
            from_tiles(tile_stack[:count_in], D, HG),
            from_tiles(tile_stack[count_in : 2 * count_in], D, HG),
            from_tiles(tile_stack[2 * count_in : edge_out], D, HG),
        ],
        axis=1,
    )
    w_output = from_tiles(tile_stack[edge_out:edge_up], HG, D)
    w_up = from_tiles(tile_stack[edge_up:edge_down], D, FG)
    w_down = from_tiles(tile_stack[edge_down:], FG, D)
    return (w_inputs, w_output, w_up, w_down)


def router_scale(acts_low, router_map, chosen):
    logits = jnp.dot(acts_low.astype(jnp.float32), router_map, precision=PRECISE)
    probs_all = jax.nn.softmax(logits, axis=1)
    picked = (chosen[:, None] - 1 == jnp.arange(WIDTHS)[None, :]).astype(jnp.float32)
    return (WIDTHS * jnp.sum(probs_all * picked, axis=1), probs_all, picked)


def router_back(grad_scale, probs_all, picked):
    chosen_prob = jnp.sum(probs_all * picked, axis=1)
    return (WIDTHS * grad_scale * chosen_prob)[:, None] * (picked - probs_all)


def scores_of(queries, key_block, query_index, query_segment, key_index, key_segment):
    raw_scores = jnp.einsum(
        "qhd,khd->hqk", queries, key_block, preferred_element_type=jnp.float32
    ) * HD ** (-0.5)
    allowed = (key_segment[None, :] == query_segment[:, None]) & (
        key_index[None, :] <= query_index[:, None]
    )
    return (raw_scores, allowed[None])


def fetch_block(packed_all, all_index, all_segment, number, block_rows):
    start = number * block_rows
    piece_rows = lax.dynamic_slice_in_dim(packed_all, start, block_rows, 0)
    key_index = lax.dynamic_slice_in_dim(all_index, start, block_rows, 0)
    key_segment = lax.dynamic_slice_in_dim(all_segment, start, block_rows, 0)
    first_half = piece_rows[:, :HG].reshape(block_rows, HPG, HD)
    second_half = piece_rows[:, HG:].reshape(block_rows, HPG, HD)
    return (first_half, second_half, key_index, key_segment)


def attend_forward(queries, token_index, segment, packed_all, all_index, all_segment, block_rows):
    local_rows = queries.shape[0]
    blocks = packed_all.shape[0] // block_rows

    def first_pass(carried, number):
        running_max, running_sum = carried
        key_block, value_block, key_index, key_segment = fetch_block(
            packed_all, all_index, all_segment, number, block_rows
        )
        raw_scores, allowed = scores_of(
            queries, key_block, token_index, segment, key_index, key_segment
        )
        masked = jnp.where(allowed, raw_scores, NEG_FILL)
        fresh_max = jnp.maximum(running_max, jnp.max(masked, axis=2))
        running_sum = running_sum * jnp.exp(running_max - fresh_max) + jnp.sum(
            jnp.exp(masked - fresh_max[:, :, None]), axis=2
        )
        return ((fresh_max, running_sum), None)

    start_state = (
        jnp.full((HPG, local_rows), NEG_FILL, jnp.float32),
        jnp.zeros((HPG, local_rows), jnp.float32),
    )
    (running_max, running_sum), unused = lax.scan(first_pass, start_state, jnp.arange(blocks))
    log_sum = running_max + jnp.log(running_sum)

    def second_pass(carried, number):
        key_block, value_block, key_index, key_segment = fetch_block(
            packed_all, all_index, all_segment, number, block_rows
        )
        raw_scores, allowed = scores_of(
            queries, key_block, token_index, segment, key_index, key_segment
        )
        weights_p = jnp.where(allowed, jnp.exp(raw_scores - log_sum[:, :, None]), 0.0)
        update = jnp.einsum(
            "hqk,khd->qhd",
            weights_p.astype(jnp.bfloat16),
            value_block,
            preferred_element_type=jnp.float32,
        )
        return (carried + update, None)

    context, unused = lax.scan(
        second_pass, jnp.zeros((local_rows, HPG, HD), jnp.float32), jnp.arange(blocks)
    )
    return (log_sum, context)


def pair_grads(
    queries,
    grad_out,
    log_sum,
    delta,
    query_index,
    query_segment,
    key_block,
    value_block,
    key_index,
    key_segment,
):
    raw_scores, allowed = scores_of(
        queries, key_block, query_index, query_segment, key_index, key_segment
    )
    weights_p = jnp.where(allowed, jnp.exp(raw_scores - log_sum[:, :, None]), 0.0)
    grad_value = jnp.einsum(
        "hqk,qhd->khd", weights_p.astype(jnp.bfloat16), grad_out, preferred_element_type=jnp.float32
    )
    grad_probs = jnp.einsum(
        "qhd,khd->hqk", grad_out, value_block, preferred_element_type=jnp.float32
    )
    grad_raw = (weights_p * (grad_probs - delta[:, :, None]) * HD ** (-0.5)).astype(jnp.bfloat16)
    grad_query = jnp.einsum("hqk,khd->qhd", grad_raw, key_block, preferred_element_type=jnp.float32)
    grad_key = jnp.einsum("hqk,qhd->khd", grad_raw, queries, preferred_element_type=jnp.float32)
    return (grad_query, grad_key, grad_value)


def local_plain(
    tokens,
    cotangent,
    attn_width,
    ffn_width,
    seq_lengths,
    tile_order,
    master,
    first_moment,
    second_moment,
    left_basis,
    right_basis,
    small_master,
    small_first,
    small_second,
):
    local_rows = tokens.shape[0]
    shards = lax.axis_size("seq")
    all_rows = local_rows * shards
    block_rows = min(KB_CAP, all_rows)
    blocks = all_rows // block_rows
    group_id = lax.axis_index("head")
    slot_order = tile_order[0]
    weights_all, small_all = (
        lax.all_gather(master[0].astype(jnp.bfloat16), "seq", axis=0, tiled=True),
        lax.all_gather(small_master.astype(jnp.bfloat16), "seq", axis=0, tiled=True),
    )
    w_inputs, w_output, w_up, w_down = unpack(place_tiles(slot_order, [weights_all], None)[0])
    small_vals = small_all.astype(jnp.float32)
    gain_one = small_vals[0:D]
    bias_one = small_vals[D : 2 * D]
    gain_two = small_vals[2 * D : 3 * D]
    bias_two = small_vals[3 * D : 4 * D]
    routers = small_vals[4 * D :].reshape(D, 2 * WIDTHS)
    router_attn = routers[:, :WIDTHS]
    router_ffn = routers[:, WIDTHS:]
    first_row = lax.axis_index("seq") * local_rows
    token_index, segment, offset = token_layout(first_row, local_rows, seq_lengths)
    residual = tokens.astype(jnp.float32)
    ln_one, pull_one = jax.vjp(layer_norm, residual, gain_one, bias_one)
    act_one = ln_one.astype(jnp.bfloat16)
    scale_attn, probs_attn, picked_attn = router_scale(act_one, router_attn, attn_width)
    projected = jnp.dot(act_one, w_inputs, preferred_element_type=jnp.float32)
    cosine_table, sine_table = rotary_tables(offset)
    query_low = rotary(
        projected[:, :HG].reshape(local_rows, HPG, HD), cosine_table, sine_table
    ).astype(jnp.bfloat16)
    key_low = rotary(
        projected[:, HG : 2 * HG].reshape(local_rows, HPG, HD), cosine_table, sine_table
    ).astype(jnp.bfloat16)
    value_low = projected[:, 2 * HG :].astype(jnp.bfloat16)
    packed = jnp.concatenate([key_low.reshape(local_rows, HG), value_low], axis=1)
    packed_all = lax.all_gather(packed, "seq", axis=0, tiled=True)
    all_index, all_segment, all_offset = token_layout(0, all_rows, seq_lengths)
    log_sum, context = attend_forward(
        query_low, token_index, segment, packed_all, all_index, all_segment, block_rows
    )
    head_mask = (group_id < attn_width).astype(jnp.float32)
    ctx_low = (context * head_mask[:, None, None]).astype(jnp.bfloat16).reshape(local_rows, HG)
    attn_out = lax.psum(
        jnp.dot(ctx_low, w_output, preferred_element_type=jnp.float32).astype(jnp.bfloat16), "head"
    ).astype(jnp.float32)
    middle_res = residual + scale_attn[:, None] * attn_out
    ln_two, pull_two = jax.vjp(layer_norm, middle_res, gain_two, bias_two)
    act_two = ln_two.astype(jnp.bfloat16)
    scale_ffn, probs_ffn, picked_ffn = router_scale(act_two, router_ffn, ffn_width)
    pre_act = jnp.dot(act_two, w_up, preferred_element_type=jnp.float32)
    unit_mask = (group_id < ffn_width).astype(jnp.float32)
    hidden_low = (jnp.square(jnp.maximum(pre_act, 0.0)) * unit_mask[:, None]).astype(jnp.bfloat16)
    ffn_out = lax.psum(
        jnp.dot(hidden_low, w_down, preferred_element_type=jnp.float32).astype(jnp.bfloat16), "head"
    ).astype(jnp.float32)
    output = (middle_res + scale_ffn[:, None] * ffn_out).astype(jnp.bfloat16)
    grad_top = cotangent.astype(jnp.float32)
    grad_scale_ffn = jnp.sum(grad_top * ffn_out, axis=1)
    grad_ffn_low = (scale_ffn[:, None] * grad_top).astype(jnp.bfloat16)
    grad_hidden = jnp.dot(grad_ffn_low, w_down.T, preferred_element_type=jnp.float32)
    grad_pre_low = (grad_hidden * unit_mask[:, None] * 2.0 * jnp.maximum(pre_act, 0.0)).astype(
        jnp.bfloat16
    )
    grad_act_two = lax.psum(
        jnp.dot(grad_pre_low, w_up.T, preferred_element_type=jnp.float32).astype(jnp.bfloat16),
        "head",
    ).astype(jnp.float32)
    logit_ffn = router_back(grad_scale_ffn, probs_ffn, picked_ffn)
    grad_act_two = grad_act_two + jnp.dot(logit_ffn, router_ffn.T, precision=PRECISE)
    grad_mid_ln, grad_gain_two, grad_bias_two = pull_two(grad_act_two)
    grad_middle = grad_top + grad_mid_ln
    grad_scale_attn = jnp.sum(grad_middle * attn_out, axis=1)
    grad_attn_low = (scale_attn[:, None] * grad_middle).astype(jnp.bfloat16)
    grad_context = jnp.dot(grad_attn_low, w_output.T, preferred_element_type=jnp.float32)
    grad_out_low = (
        (grad_context * head_mask[:, None]).astype(jnp.bfloat16).reshape(local_rows, HPG, HD)
    )
    delta = jnp.sum(grad_out_low.astype(jnp.float32) * context, axis=2).T
    zero_state = jnp.zeros((local_rows, HPG, HD), jnp.float32)

    def visit_keys(carried, number):
        key_block, value_block, key_index, key_segment = fetch_block(
            packed_all, all_index, all_segment, number, block_rows
        )
        grad_query, grad_key, grad_value = pair_grads(
            query_low,
            grad_out_low,
            log_sum,
            delta,
            token_index,
            segment,
            key_block,
            value_block,
            key_index,
            key_segment,
        )
        return (
            carried + grad_query,
            jnp.concatenate(
                [grad_key.reshape(block_rows, HG), grad_value.reshape(block_rows, HG)], axis=1
            ),
        )

    grad_query_rot, key_terms = lax.scan(visit_keys, zero_state, jnp.arange(blocks))
    summed = lax.psum_scatter(
        key_terms.reshape(all_rows, 2 * HG).astype(jnp.bfloat16),
        "seq",
        scatter_dimension=0,
        tiled=True,
    ).astype(jnp.float32)
    grad_key_rot = summed[:, :HG].reshape(local_rows, HPG, HD)
    grad_value_all = summed[:, HG:].reshape(local_rows, HPG, HD)
    grad_query_low = (
        rotary_back(grad_query_rot, cosine_table, sine_table)
        .astype(jnp.bfloat16)
        .reshape(local_rows, HG)
    )
    grad_key_low = (
        rotary_back(grad_key_rot, cosine_table, sine_table)
        .astype(jnp.bfloat16)
        .reshape(local_rows, HG)
    )
    grad_value_low = grad_value_all.astype(jnp.bfloat16).reshape(local_rows, HG)
    grad_inputs_low = jnp.concatenate([grad_query_low, grad_key_low, grad_value_low], axis=1)
    grad_act_one = lax.psum(
        jnp.dot(grad_inputs_low, w_inputs.T, preferred_element_type=jnp.float32).astype(
            jnp.bfloat16
        ),
        "head",
    ).astype(jnp.float32)
    logit_attn = router_back(grad_scale_attn, probs_attn, picked_attn)
    grad_act_one = grad_act_one + jnp.dot(logit_attn, router_attn.T, precision=PRECISE)
    grad_res_ln, grad_gain_one, grad_bias_one = pull_one(grad_act_one)
    input_grad = grad_middle + grad_res_ln
    grad_router = jnp.concatenate(
        [
            jnp.dot(act_one.astype(jnp.float32).T, logit_attn, precision=PRECISE),
            jnp.dot(act_two.astype(jnp.float32).T, logit_ffn, precision=PRECISE),
        ],
        axis=1,
    ).reshape(-1)
    small_terms = jnp.concatenate(
        [grad_gain_one, grad_bias_one, grad_gain_two, grad_bias_two, grad_router]
    )
    tile_terms = tile_grads(
        slot_order,
        [[act_one, ctx_low, act_two, hidden_low]],
        [[grad_inputs_low, grad_attn_low, grad_pre_low, grad_ffn_low]],
        None,
        [slot_order.shape[0]],
    )[0]
    tile_grad, small_grad = (
        lax.psum_scatter(tile_terms, "seq", scatter_dimension=0, tiled=True),
        lax.psum_scatter(
            small_terms.astype(jnp.bfloat16), "seq", scatter_dimension=0, tiled=True
        ).astype(jnp.float32),
    )
    slots = master.shape[1]
    held = adam_tiles(
        jnp.arange(slots, dtype=jnp.int32),
        [tile_grad],
        (left_basis[0], right_basis[0]),
        (first_moment[0], second_moment[0], master[0]),
        None,
    )
    small_outs = small_adam(small_grad, small_first, small_second, small_master)
    return (
        output,
        input_grad,
        held[0][None],
        held[1][None],
        held[2][None],
        held[3][None],
        *small_outs,
    )


def solution(mesh):
    return jax.shard_map(
        local_remap if dict(mesh.shape) == {"seq": 8, "head": 4} else local_plain,
        mesh=mesh,
        in_specs=(
            P("seq", None),
            P("seq", None),
            P("seq"),
            P("seq"),
            P(),
            P("head", None),
            P("head", "seq", None, None),
            P("head", "seq", None, None),
            P("head", "seq", None, None),
            P("head", "seq", None, None),
            P("head", "seq", None, None),
            P("seq"),
            P("seq"),
            P("seq"),
        ),
        out_specs=(
            P("seq", None),
            P("seq", None),
            P("head", "seq", None, None),
            P("head", "seq", None, None),
            P("head", "seq", None, None),
            P("head", "seq", None, None),
            P("seq"),
            P("seq"),
            P("seq"),
        ),
        check_vma=False,
    )
```
